32 devices in a mesh: ctx: 16 (over z, y, x), ws: 2 (over core).
Axes of the slice: x: 2, y: 2, z: 4, core: 2. Of those that a mesh axis runs over, the one named last changes fastest.
Arguments:
- tokens: bfloat16 [2, 4096, 512], P('ws', 'ctx'), may hold values from -6 to 6
- segment_ids: int32 [2, 4096], P('ws', 'ctx'), may hold values from 0 to 7, never falling along the last dimension, each value on 1 to 2048 neighbouring positions
- out_grad: bfloat16 [2, 4096, 512], P('ws', 'ctx'), may hold values from -6 to 6
- ln1_gain: float32 [512], P('ws'), may hold values from 0.5 to 1.5
- ln1_bias: float32 [512], P('ws'), may hold values from -3 to 3
- glu_weight: float32 [512, 1024], P('ws'), may hold values from -0.25 to 0.25
- glu_bias: float32 [1024], P('ws'), may hold values from -3 to 3
- ln2_gain: float32 [512], P('ws'), may hold values from 0.5 to 1.5
- ln2_bias: float32 [512], P('ws'), may hold values from -3 to 3
- left_weight: float32 [512, 2048], P('ws'), may hold values from -0.25 to 0.25
- left_bias: float32 [2048], P('ws'), may hold values from -3 to 3
- conv_weight: float32 [3, 512, 256], P(None, 'ws'), may hold values from -0.15625 to 0.15625
- conv_bias: float32 [256], P('ws'), may hold values from -3 to 3
- ln3_gain: float32 [2048], P('ws'), may hold values from 0.5 to 1.5
- ln3_bias: float32 [2048], P('ws'), may hold values from -3 to 3
- depth_weight: float32 [9, 2048], P(None, 'ws'), may hold values from -2 to 2
- point_weight: float32 [2048, 256], P('ws'), may hold values from -0.125 to 0.125
- point_bias: float32 [256], P('ws'), may hold values from -3 to 3
- ln4_gain: float32 [512], P('ws'), may hold values from 0.5 to 1.5
- ln4_bias: float32 [512], P('ws'), may hold values from -3 to 3
- qkv_weight: float32 [512, 1536], P('ws'), may hold values from -0.25 to 0.25
- attn_out_weight: float32 [512, 512], P('ws'), may hold values from -0.75 to 0.75
- attn_out_bias: float32 [512], P('ws'), may hold values from -3 to 3
- ln5_gain: float32 [512], P('ws'), may hold values from 0.5 to 1.5
- ln5_bias: float32 [512], P('ws'), may hold values from -3 to 3
- expand_weight: float32 [512, 2048], P('ws'), may hold values from -0.25 to 0.25
- expand_bias: float32 [2048], P('ws'), may hold values from -3 to 3
- shrink_weight: float32 [2048, 512], P('ws'), may hold values from -0.125 to 0.125
- shrink_bias: float32 [512], P('ws'), may hold values from -3 to 3
Outputs:
- output: bfloat16 [2, 4096, 512], P('ws', 'ctx')
- input_grad: float32 [2, 4096, 512], P('ws', 'ctx')
- d_ln1_gain: float32 [512], P('ws')
- d_ln1_bias: float32 [512], P('ws')
- d_glu_weight: float32 [512, 1024], P('ws')
- d_glu_bias: float32 [1024], P('ws')
- d_ln2_gain: float32 [512], P('ws')
- d_ln2_bias: float32 [512], P('ws')
- d_left_weight: float32 [512, 2048], P('ws')
- d_left_bias: float32 [2048], P('ws')
- d_conv_weight: float32 [3, 512, 256], P(None, 'ws')
- d_conv_bias: float32 [256], P('ws')
- d_ln3_gain: float32 [2048], P('ws')
- d_ln3_bias: float32 [2048], P('ws')
- d_depth_weight: float32 [9, 2048], P(None, 'ws')
- d_point_weight: float32 [2048, 256], P('ws')
- d_point_bias: float32 [256], P('ws')
- d_ln4_gain: float32 [512], P('ws')
- d_ln4_bias: float32 [512], P('ws')
- d_qkv_weight: float32 [512, 1536], P('ws')
- d_attn_out_weight: float32 [512, 512], P('ws')
- d_attn_out_bias: float32 [512], P('ws')
- d_ln5_gain: float32 [512], P('ws')
- d_ln5_bias: float32 [512], P('ws')
- d_expand_weight: float32 [512, 2048], P('ws')
- d_expand_bias: float32 [2048], P('ws')
- d_shrink_weight: float32 [2048, 512], P('ws')
- d_shrink_bias: float32 [512], P('ws')
The draws below stay inside these ranges and needn't reach their ends.
Inputs may be any that keep to these rules, and one draw needn't show every extreme that they name: `segment_ids`: segment numbers never fall along a sequence; each document is a run of 1 to 2048 positions, and some document has exactly that many.
All inputs are finite; a program needn't handle non-finite values.
Results may differ from the reference program's by a relative error of at most 0.015.
Values may be sent and summed in bfloat16 or wider, within the bound.
A program may use at most 192 MiB of HBM per device.

```python
import math
import jax
import jax.numpy as jnp
import numpy as np
from jax import lax

D = 512
HEADS = 8
HEAD_DIM = 64
FF = 2048
HALF = 256
TOK_DEV = 256
LENGTH = 4096
SEQS = 2
N_CTX = 16


def block_scale(stream_key, shape, cuts, low, largest):
    factor_of, own = 1.0, jax.random.fold_in(stream_key, 6)
    for axis_at, shards_of in cuts:
        draws = jnp.exp(jax.random.uniform(jax.random.fold_in(own, axis_at), (shards_of,), jnp.float32, low / len(cuts), largest / len(cuts)))
        factor_of = factor_of * jnp.repeat(draws, shape[axis_at] // shards_of).reshape([-1 if axis == axis_at else 1 for axis in range(len(shape))])
    return factor_of


def profile(number_of, total, bound, lean):
    portions = [(1 << 20) // math.isqrt(grade ** lean) + 1 for grade in range(2, number_of + 1)]
    spare, counts = total - bound - (number_of - 1), [1] * (number_of - 1)
    while spare > 0:
        free = [i for i in range(number_of - 1) if counts[i] < bound]
        whole, budget = sum([portions[i] for i in free]), spare
        for i in free:
            more = min(bound - counts[i], max(1, budget * portions[i] // whole), spare)
            counts[i] = counts[i] + more
            spare = spare - more
    return np.array([bound] + counts)


def uneven(rng, count, total, bound, skew):
    if count == 2:
        one = jax.random.randint(rng, (), max(1, total - bound), min(bound, total - 1) + 1)
        return jnp.stack([one, total - one])
    sizes = jnp.asarray(profile(count, total, bound, skew), jnp.int32)
    twos = (count - 1) // 2
    source_of, receiver = sizes[1:1 + 2 * twos:2], sizes[2:2 + 2 * twos:2]
    slack = jnp.minimum(source_of - 1, bound - receiver)
    moved = jax.random.randint(jax.random.fold_in(rng, 1), (twos,), 0, 1 << 20) % (slack + 1)
    sizes = sizes.at[1:1 + 2 * twos:2].set(source_of - moved).at[2:2 + 2 * twos:2].set(receiver + moved)
    return sizes[jax.random.permutation(jax.random.fold_in(rng, 2), count)]


def bell_draw(stream_key, dims, width, most, pieces=(), kind=jnp.bfloat16):
    entries = jax.random.normal(stream_key, dims, jnp.float32) * width
    if len(pieces) > 0:
        entries = block_scale(stream_key, dims, pieces, -0.22, 0.18) * entries
    return jnp.clip(entries, min=-most, max=most).astype(kind)


def setup_inputs(seed: int = 0) -> dict:
    splits = jax.random.split(jax.random.key(seed), 30)
    return {
        "tokens": bell_draw(splits[0], (SEQS, LENGTH, D), 1.0, 6.0, ((0, 2), (1, 16))),
        "segment_ids": jax.vmap(lambda own: jnp.searchsorted(jnp.cumsum(uneven(own, max(LENGTH // 512, 8), LENGTH, LENGTH // 2, 2)), jnp.arange(LENGTH), side="right"))(jax.random.split(splits[1], SEQS)).reshape((SEQS, LENGTH)).astype(jnp.int32),
        "out_grad": bell_draw(splits[2], (SEQS, LENGTH, D), 1.0, 6.0, ((0, 2), (1, 16))),
        "ln1_gain": jnp.clip(1.0 + 0.1 * jax.random.normal(splits[3], (D,), jnp.float32), 0.5, 1.5),
        "ln1_bias": bell_draw(splits[4], (D,), 0.3, 3.0, ((0, 2),), jnp.float32),
        "glu_weight": bell_draw(splits[5], (D, 2 * D), D ** -0.5, 0.25, ((0, 2),), jnp.float32),
        "glu_bias": bell_draw(splits[6], (2 * D,), 0.5, 3.0, ((0, 2),), jnp.float32),
        "ln2_gain": jnp.clip(1.0 + 0.1 * jax.random.normal(splits[7], (D,), jnp.float32), 0.5, 1.5),
        "ln2_bias": bell_draw(splits[8], (D,), 0.3, 3.0, ((0, 2),), jnp.float32),
        "left_weight": bell_draw(splits[9], (D, FF), D ** -0.5, 0.25, ((0, 2),), jnp.float32),
        "left_bias": bell_draw(splits[10], (FF,), 0.5, 3.0, ((0, 2),), jnp.float32),
        "conv_weight": bell_draw(splits[11], (3, D, HALF), (3 * D) ** -0.5, 0.15625, ((1, 2),), jnp.float32),
        "conv_bias": bell_draw(splits[12], (HALF,), 0.5, 3.0, ((0, 2),), jnp.float32),
        "ln3_gain": jnp.clip(1.0 + 0.1 * jax.random.normal(splits[13], (FF,), jnp.float32), 0.5, 1.5),
        "ln3_bias": bell_draw(splits[14], (FF,), 0.3, 3.0, ((0, 2),), jnp.float32),
        "depth_weight": bell_draw(splits[15], (9, FF), 9 ** -0.5, 2.0, ((1, 2),), jnp.float32),
        "point_weight": bell_draw(splits[16], (FF, HALF), FF ** -0.5, 0.125, ((0, 2),), jnp.float32),
        "point_bias": bell_draw(splits[17], (HALF,), 0.5, 3.0, ((0, 2),), jnp.float32),
        "ln4_gain": jnp.clip(1.0 + 0.1 * jax.random.normal(splits[18], (D,), jnp.float32), 0.5, 1.5),
        "ln4_bias": bell_draw(splits[19], (D,), 0.3, 3.0, ((0, 2),), jnp.float32),
        "qkv_weight": bell_draw(splits[20], (D, 3 * D), D ** -0.5, 0.25, ((0, 2),), jnp.float32),
        "attn_out_weight": bell_draw(splits[21], (D, D), HEAD_DIM ** -0.5, 0.75, ((0, 2),), jnp.float32),
        "attn_out_bias": bell_draw(splits[22], (D,), 0.5, 3.0, ((0, 2),), jnp.float32),
        "ln5_gain": jnp.clip(1.0 + 0.1 * jax.random.normal(splits[23], (D,), jnp.float32), 0.5, 1.5),
        "ln5_bias": bell_draw(splits[24], (D,), 0.3, 3.0, ((0, 2),), jnp.float32),
        "expand_weight": bell_draw(splits[25], (D, FF), D ** -0.5, 0.25, ((0, 2),), jnp.float32),
        "expand_bias": bell_draw(splits[26], (FF,), 0.5, 3.0, ((0, 2),), jnp.float32),
        "shrink_weight": bell_draw(splits[27], (FF, D), FF ** -0.5, 0.125, ((0, 2),), jnp.float32),
        "shrink_bias": bell_draw(splits[28], (D,), 0.5, 3.0, ((0, 2),), jnp.float32),
    }


@jax.custom_vjp
def low(v):
    return lax.optimization_barrier(v.astype(jnp.bfloat16)).astype(jnp.float32)

@jax.custom_vjp
def low_back(v):
    return v

def low_keep(v):
    return (low(v), None)

def low_pass(kept, grad):
    return (grad,)

def back_keep(v):
    return (v, None)

def back_low(kept, grad):
    return (low(grad),)
low.defvjp(low_keep, low_pass)
low_back.defvjp(back_keep, back_low)
NORM_EPS = 1e-06
MASK_FILL = -1e+30

def matmul(left_op, right_op):
    return jnp.dot(left_op, right_op, precision=lax.Precision.HIGHEST, preferred_element_type=jnp.float32)

def layer_norm(array_in, gain_vec, shift_vec):
    average = lax.optimization_barrier(jnp.mean(array_in, axis=-1, keepdims=True))
    centred = array_in - average
    inv_std = lax.rsqrt(lax.optimization_barrier(jnp.mean(centred * centred, axis=-1, keepdims=True)) + NORM_EPS)
    return centred * inv_std * gain_vec + shift_vec

def taps_of(array_in, seg_ids, reach):
    length_all = array_in.shape[0]
    padded = jnp.pad(array_in, ((reach, reach), (0, 0)))
    seg_int = seg_ids.astype(jnp.int32)
    seg_pad = jnp.pad(seg_int, reach, constant_values=jnp.int32(-1)).astype(jnp.int32)
    zero_val = jnp.zeros((), array_in.dtype)
    result_list = []
    for tap_no in range(2 * reach + 1):
        keep_mask = (seg_pad[tap_no:tap_no + length_all] == seg_int)[:, None]
        result_list.append(jnp.where(keep_mask, padded[tap_no:tap_no + length_all], zero_val))
    return result_list

def attend(queries, key_heads, value_heads, seg_ids):
    length_all = queries.shape[0]
    seg_int = seg_ids.astype(jnp.int32)
    block_q = queries.reshape(N_CTX, TOK_DEV, HEADS, HEAD_DIM)
    block_s = seg_int.reshape(N_CTX, TOK_DEV)
    scale_val = jnp.asarray(HEAD_DIM ** (-0.5), queries.dtype)

    def one_block(seq_pair):
        query_blk, seg_blk = seq_pair
        scores = low_back(jnp.einsum('qhd,khd->hqk', query_blk, key_heads, precision=lax.Precision.HIGHEST) * scale_val)
        same_doc = (seg_blk[:, None] == seg_int[None, :])[None]
        fill_val = jnp.asarray(MASK_FILL, scores.dtype)
        attn_prob = jax.nn.softmax(jnp.where(same_doc, scores, fill_val), axis=-1)
        return jnp.einsum('hqk,khd->qhd', low(attn_prob), value_heads, precision=lax.Precision.HIGHEST)
    result = lax.map(jax.checkpoint(one_block), (block_q, block_s))
    return result.reshape(length_all, HEADS * HEAD_DIM)

def layer(state_in, seg_ids, params):
    n1_gain, n1_shift, glu_w, glu_b, n2_gain, n2_shift, left_w, left_b, conv_w, conv_b, n3_gain, n3_shift, depth_w, point_w, point_b, n4_gain, n4_shift, qkv_w, attn_w, attn_b, n5_gain, n5_shift, expand_w, expand_b, shrink_w, shrink_b = params
    length_all = state_in.shape[0]
    h_one = low(layer_norm(state_in, n1_gain, n1_shift))
    glu_pre = low_back(matmul(h_one, glu_w) + glu_b)
    state_one = state_in + glu_pre[:, :D] * jax.nn.sigmoid(glu_pre[:, D:])
    h_two = low(layer_norm(state_one, n2_gain, n2_shift))
    left_pre = low_back(matmul(h_two, left_w) + left_b)
    conv_taps = taps_of(h_two, seg_ids, 1)
    conv_sum = conv_b + matmul(conv_taps[0], conv_w[0])
    for tap_no in range(1, 3):
        conv_sum = conv_sum + matmul(conv_taps[tap_no], conv_w[tap_no])
    conv_pre = low_back(conv_sum)
    mixed_sum = jax.nn.silu(left_pre) + jnp.pad(jax.nn.silu(conv_pre), ((0, 0), (0, FF - HALF)))
    g_three = low(layer_norm(mixed_sum, n3_gain, n3_shift))
    sep_taps = taps_of(g_three, seg_ids, 4)
    depth_acc = sep_taps[0] * depth_w[0]
    for tap_no in range(1, 9):
        depth_acc = depth_acc + sep_taps[tap_no] * depth_w[tap_no]
    depth_out = low(low_back(depth_acc))
    sep_out = low_back(matmul(depth_out, point_w) + point_b)
    state_two = state_one + jnp.pad(sep_out, ((0, 0), (0, D - HALF)))
    h_four = low(layer_norm(state_two, n4_gain, n4_shift))
    qkv_all = matmul(h_four, qkv_w)
    queries = low(low_back(qkv_all[:, :D])).reshape(length_all, HEADS, HEAD_DIM)
    key_heads = low(low_back(qkv_all[:, D:2 * D])).reshape(length_all, HEADS, HEAD_DIM)
    value_heads = low(low_back(qkv_all[:, 2 * D:])).reshape(length_all, HEADS, HEAD_DIM)
    attn_out = low(low_back(attend(queries, key_heads, value_heads, seg_ids)))
    state_three = state_two + low_back(matmul(attn_out, attn_w) + attn_b)
    h_five = low(layer_norm(state_three, n5_gain, n5_shift))
    expand_pre = low_back(matmul(h_five, expand_w) + expand_b)
    hidden = low(jax.nn.silu(expand_pre))
    return state_three + low_back(matmul(hidden, shrink_w) + shrink_b)

def reference(tokens, segment_ids, out_grad, ln1_gain, ln1_bias, glu_weight, glu_bias, ln2_gain, ln2_bias, left_weight, left_bias, conv_weight, conv_bias, ln3_gain, ln3_bias, depth_weight, point_weight, point_bias, ln4_gain, ln4_bias, qkv_weight, attn_out_weight, attn_out_bias, ln5_gain, ln5_bias, expand_weight, expand_bias, shrink_weight, shrink_bias):
    params = (ln1_gain, ln1_bias, glu_weight, glu_bias, ln2_gain, ln2_bias, left_weight, left_bias, conv_weight, conv_bias, ln3_gain, ln3_bias, depth_weight, point_weight, point_bias, ln4_gain, ln4_bias, qkv_weight, attn_out_weight, attn_out_bias, ln5_gain, ln5_bias, expand_weight, expand_bias, shrink_weight, shrink_bias)
    params = jax.tree.map(lambda item: item.astype(jnp.float32), params)
    state_in = tokens.astype(jnp.float32)
    seg_int = segment_ids.astype(jnp.int32)

    def whole(state_all, param_all):
        low_params = jax.tree.map(low, param_all)
        return lax.map(lambda seq_pair: layer(seq_pair[0], seq_pair[1], low_params), (state_all, seg_int))
    result, pull_back = jax.vjp(whole, state_in, params)
    input_grad, grads = pull_back(out_grad.astype(jnp.float32))
    return (result.astype(jnp.bfloat16), input_grad, grads[0], grads[1], grads[2], grads[3], grads[4], grads[5], grads[6], grads[7], grads[8], grads[9], grads[10], grads[11], grads[12], grads[13], grads[14], grads[15], grads[16], grads[17], grads[18], grads[19], grads[20], grads[21], grads[22], grads[23], grads[24], grads[25])
```

```python
import functools
import math

import jax
import jax.numpy as jnp
from jax import lax
from jax.experimental import pallas as pl
from jax.experimental.pallas import tpu as pltpu
from jax.sharding import PartitionSpec as P

HEAD_DIM = 64


NORM_EPS = 1e-06
MASK_FILL = -1e30


def extended(block, sides, width):
    for axis, dim in sides:
        count = lax.axis_size(axis)
        forward = [(i, i + 1) for i in range(count - 1)]
        backward = [(target, source) for source, target in forward]
        low = lax.ppermute(
            lax.slice_in_dim(block, block.shape[dim] - width, None, axis=dim), axis, forward
        )
        high = lax.ppermute(lax.slice_in_dim(block, 0, width, axis=dim), axis, backward)
        block = jnp.concatenate([low, block, high], axis=dim)
    return block


def to_low(array_in):
    return array_in.astype(jnp.bfloat16)


def smooth_slope(array_in):
    sigma = jax.nn.sigmoid(array_in)
    return sigma * (1.0 + array_in * (1.0 - sigma))


def matmul(left_op, right_op):
    return jnp.dot(left_op, right_op, preferred_element_type=jnp.float32)


def outer_sum(left_op, right_op):
    return lax.dot_general(
        left_op, right_op, (((0,), (0,)), ((), ())), preferred_element_type=jnp.float32
    )


def back_mul(grad_in, weight):
    return lax.dot_general(
        grad_in, weight, (((1,), (1,)), ((), ())), preferred_element_type=jnp.float32
    )


def col_sum(grad_in):
    return jnp.sum(grad_in.astype(jnp.float32), axis=0)


def norm_fwd(array_in, gain_vec, shift_vec):
    average = jnp.mean(array_in, axis=-1, keepdims=True)
    centred = array_in - average
    inv_std = lax.rsqrt(jnp.mean(centred * centred, axis=-1, keepdims=True) + NORM_EPS)
    normed = centred * inv_std
    return (normed * gain_vec + shift_vec, normed, inv_std)


def norm_back(grad_in, normed, inv_std, gain_vec):
    scaled = grad_in * gain_vec
    inner_term = jnp.mean(scaled, axis=-1, keepdims=True)
    cross_term = jnp.mean(scaled * normed, axis=-1, keepdims=True)
    return (
        inv_std * (scaled - inner_term - normed * cross_term),
        jnp.sum(grad_in * normed, axis=0),
        jnp.sum(grad_in, axis=0),
    )


def masked_rows(rim_rows, seg_rim, seg_own, first_row, row_count):
    keep_mask = (lax.slice_in_dim(seg_rim, first_row, first_row + row_count) == seg_own)[:, None]
    return jnp.where(
        keep_mask,
        lax.slice_in_dim(rim_rows, first_row, first_row + row_count),
        jnp.zeros((), rim_rows.dtype),
    )


def head_view(flat_rows):
    return flat_rows.reshape(flat_rows.shape[0], -1, HEAD_DIM)


MESH_ID = pl.DeviceIdType.MESH
LANES = 128
ROW_BLOCK = 16
KEY_TILE = 512
VMEM_MOST = 56 * 1024 * 1024


def vmem_spec():
    return pl.BlockSpec(memory_space=pltpu.VMEM)


def any_spec():
    return pl.BlockSpec(memory_space=pl.ANY)


def comm_params(number):
    return pltpu.CompilerParams(
        collective_id=number, has_side_effects=True, vmem_limit_bytes=VMEM_MOST
    )


def greet(peers):
    barrier = pltpu.get_barrier_semaphore()
    for peer in peers:
        pl.semaphore_signal(barrier, inc=1, device_id=peer, device_id_type=MESH_ID)
    pl.semaphore_wait(barrier, len(peers))


def push(src, dst, sems, at, peer):
    copy = pltpu.make_async_remote_copy(
        src_ref=src,
        dst_ref=dst,
        send_sem=sems[0].at[at],
        recv_sem=sems[1].at[at],
        device_id=peer,
        device_id_type=MESH_ID,
    )
    copy.start()
    return copy


def sem_pair(count):
    return [pltpu.SemaphoreType.DMA((count,)), pltpu.SemaphoreType.DMA((count,))]


def bound(value, step):
    return pl.multiple_of(value, step)


def seg_body(count, row_ref, out_ref, local_sem, send_sem, recv_sem):
    own, core = lax.axis_index("ctx"), lax.axis_index("ws")
    peers = [(lax.rem(own + gap, count), core) for gap in range(1, count)]
    greet(peers)
    keep = pltpu.make_async_copy(row_ref, out_ref.at[own], local_sem)
    keep.start()
    copies = [
        push(row_ref, out_ref.at[own], (send_sem, recv_sem), gap, peer)
        for gap, peer in enumerate(peers)
    ]
    keep.wait()
    for copy in copies:
        copy.wait()


def gather_segments(row, count):
    return pl.pallas_call(
        functools.partial(seg_body, count),
        out_shape=jax.ShapeDtypeStruct((count,) + row.shape, row.dtype),
        in_specs=[vmem_spec()],
        out_specs=vmem_spec(),
        scratch_shapes=[pltpu.SemaphoreType.DMA] + sem_pair(count - 1),
        compiler_params=comm_params(1),
        name="gather_segments",
    )(row)


def spread_body(count, heads, q_ref, kv_ref, qo_ref, kvo_ref, local_sem, qs, qr, ks, kr):
    own, core = lax.axis_index("ctx"), lax.axis_index("ws")
    parts = count // heads
    rows = kv_ref.shape[0]
    head, part = own // parts, lax.rem(own, parts)
    peers = [lax.rem(own + gap, count) for gap in range(1, count)]
    greet([(peer, core) for peer in peers])

    def q_piece(which):
        return q_ref.at[pl.ds(bound(which * HEAD_DIM, HEAD_DIM), HEAD_DIM), :]

    def kv_piece(which):
        return kv_ref.at[:, pl.ds(bound(which * LANES, LANES), LANES)]

    q_slot = qo_ref.at[:, pl.ds(bound(head * rows, rows), rows)]
    kv_slot = kvo_ref.at[pl.ds(bound(own * rows, rows), rows), :]
    copies = []
    for gap in range(1, heads):
        other = lax.rem(head + gap, heads)
        copies.append(
            push(q_piece(other), q_slot, (qs, qr), gap - 1, (other * parts + part, core))
        )
    for gap, peer in enumerate(peers):
        copies.append(push(kv_piece(peer // parts), kv_slot, (ks, kr), gap, (peer, core)))
    keep_q = pltpu.make_async_copy(q_piece(head), q_slot, local_sem.at[0])
    keep_kv = pltpu.make_async_copy(kv_piece(head), kv_slot, local_sem.at[1])
    keep_q.start()
    keep_kv.start()
    keep_q.wait()
    keep_kv.wait()
    for copy in copies:
        copy.wait()


def spread_heads(q_t, kv, count, heads):
    rows = kv.shape[0]
    return pl.pallas_call(
        functools.partial(spread_body, count, heads),
        out_shape=(
            jax.ShapeDtypeStruct((HEAD_DIM, heads * rows), q_t.dtype),
            jax.ShapeDtypeStruct((count * rows, LANES), kv.dtype),
        ),
        in_specs=[vmem_spec(), vmem_spec()],
        out_specs=(vmem_spec(), vmem_spec()),
        scratch_shapes=[pltpu.SemaphoreType.DMA((2,))]
        + sem_pair(heads - 1)
        + sem_pair(count - 1),
        compiler_params=comm_params(2),
        name="spread_heads",
    )(q_t, kv)


def swap_body(count, heads, outward, in_ref, out_ref, local_sem, send_sem, recv_sem):
    own, core = lax.axis_index("ctx"), lax.axis_index("ws")
    parts = count // heads
    head, part = own // parts, lax.rem(own, parts)
    rows = in_ref.shape[1] if outward else out_ref.shape[1]
    others = [lax.rem(head + gap, heads) for gap in range(heads)]
    greet([(other * parts + part, core) for other in others[1:]])

    def tall(ref, which):
        return ref.at[pl.ds(bound(which * HEAD_DIM, HEAD_DIM), HEAD_DIM), :]

    def wide(ref, which):
        return ref.at[:, pl.ds(bound(which * rows, rows), rows)]

    take, put = (tall, wide) if outward else (wide, tall)
    copies = [
        push(
            take(in_ref, other),
            put(out_ref, head),
            (send_sem, recv_sem),
            gap,
            (other * parts + part, core),
        )
        for gap, other in enumerate(others[1:])
    ]
    keep = pltpu.make_async_copy(take(in_ref, head), put(out_ref, head), local_sem)
    keep.start()
    keep.wait()
    for copy in copies:
        copy.wait()


def swap_heads(block, count, heads, outward, number):
    if outward:
        shape = (HEAD_DIM, heads * block.shape[1])
    else:
        shape = (heads * HEAD_DIM, block.shape[1] // heads)
    return pl.pallas_call(
        functools.partial(swap_body, count, heads, outward),
        out_shape=jax.ShapeDtypeStruct(shape, block.dtype),
        in_specs=[vmem_spec()],
        out_specs=vmem_spec(),
        scratch_shapes=[pltpu.SemaphoreType.DMA] + sem_pair(heads - 1),
        compiler_params=comm_params(number),
        name="swap_heads",
    )(block)


def collect_body(count, heads, dq_ref, dkv_ref, dqo_ref, dkvo_ref, local_sem, qs, qr, ks, kr):
    own, core = lax.axis_index("ctx"), lax.axis_index("ws")
    parts = count // heads
    rows = dqo_ref.shape[1]
    head, part = own // parts, lax.rem(own, parts)
    peers = [lax.rem(own + gap, count) for gap in range(1, count)]
    greet([(peer, core) for peer in peers])

    def dq_piece(which):
        return dq_ref.at[:, pl.ds(bound(which * rows, rows), rows)]

    def dkv_piece(which):
        return dkv_ref.at[pl.ds(bound(which * rows, rows), rows), :]

    dq_slot = dqo_ref.at[pl.ds(bound(head * HEAD_DIM, HEAD_DIM), HEAD_DIM), :]
    dkv_slot = dkvo_ref.at[part, :, pl.ds(bound(head * LANES, LANES), LANES)]
    copies = []
    for gap in range(1, heads):
        other = lax.rem(head + gap, heads)
        copies.append(
            push(dq_piece(other), dq_slot, (qs, qr), gap - 1, (other * parts + part, core))
        )
    for gap, peer in enumerate(peers):
        copies.append(push(dkv_piece(peer), dkv_slot, (ks, kr), gap, (peer, core)))
    keep_q = pltpu.make_async_copy(dq_piece(head), dq_slot, local_sem.at[0])
    keep_kv = pltpu.make_async_copy(dkv_piece(own), dkv_slot, local_sem.at[1])
    keep_q.start()
    keep_kv.start()
    keep_q.wait()
    keep_kv.wait()
    for copy in copies:
        copy.wait()


def collect_heads(dq_t, dkv, count, heads):
    rows = dkv.shape[0] // count
    return pl.pallas_call(
        functools.partial(collect_body, count, heads),
        out_shape=(
            jax.ShapeDtypeStruct((heads * HEAD_DIM, rows), dq_t.dtype),
            jax.ShapeDtypeStruct((count // heads, rows, heads * LANES), dkv.dtype),
        ),
        in_specs=[vmem_spec(), vmem_spec()],
        out_specs=(vmem_spec(), vmem_spec()),
        scratch_shapes=[pltpu.SemaphoreType.DMA((2,))]
        + sem_pair(heads - 1)
        + sem_pair(count - 1),
        compiler_params=comm_params(3),
        name="collect_heads",
    )(dq_t, dkv)


def same_doc(segk_ref, seg_q, first):
    seg_k = segk_ref[pl.ds(first, KEY_TILE), :]
    return jnp.concatenate([seg_k] * (seg_q.shape[1] // LANES), axis=1) == seg_q


def turn_keys(kv_ref, turned):
    @pl.loop(0, kv_ref.shape[0] // KEY_TILE)
    def _(tile):
        first = bound(tile * KEY_TILE, KEY_TILE)
        turned[:, pl.ds(first, KEY_TILE)] = (
            kv_ref[pl.ds(first, KEY_TILE), :].astype(jnp.float32).T.astype(jnp.bfloat16)
        )


def attend_body(rows, range_ref, q_ref, kv_ref, segq_ref, segk_ref, o_ref, low_ref, lse_ref, turned):
    turn_keys(kv_ref, turned)

    @pl.loop(0, q_ref.shape[1] // rows)
    def _(tile):
        at = bound(tile * rows, rows)
        q = q_ref[:, pl.ds(at, rows)] * jnp.bfloat16(HEAD_DIM**-0.5)
        q_pad = jnp.concatenate([q, jnp.zeros_like(q)], axis=0)
        seg_q = segq_ref[:, pl.ds(at, rows)]

        def block(key_tile, carry):
            top, total, acc = carry
            first = bound(key_tile * KEY_TILE, KEY_TILE)
            scores = matmul(kv_ref[pl.ds(first, KEY_TILE), :], q_pad)
            scores = jnp.where(same_doc(segk_ref, seg_q, first), scores, MASK_FILL)
            new_top = jnp.maximum(top, jnp.max(scores, axis=0, keepdims=True))
            probs = jnp.exp(scores - new_top)
            shrink = jnp.exp(top - new_top)
            total = total * shrink + jnp.sum(probs, axis=0, keepdims=True)
            values = turned[HEAD_DIM:, pl.ds(first, KEY_TILE)]
            acc = acc * shrink + matmul(values, probs.astype(jnp.bfloat16))
            return (new_top, total, acc)

        top, total, acc = lax.fori_loop(
            range_ref[0, tile],
            range_ref[1, tile],
            block,
            (
                jnp.full((1, rows), MASK_FILL, jnp.float32),
                jnp.zeros((1, rows), jnp.float32),
                jnp.zeros((HEAD_DIM, rows), jnp.float32),
            ),
        )
        out = acc / total
        o_ref[:, pl.ds(at, rows)] = out
        low_ref[:, pl.ds(at, rows)] = out.astype(jnp.bfloat16)
        lse_ref[:, pl.ds(at, rows)] = top + jnp.log(total)


def attend(ranges, q_t, kv, seg_q, seg_k, rows):
    return pl.pallas_call(
        functools.partial(attend_body, rows),
        out_shape=(
            jax.ShapeDtypeStruct(q_t.shape, jnp.float32),
            jax.ShapeDtypeStruct(q_t.shape, jnp.bfloat16),
            jax.ShapeDtypeStruct((1, q_t.shape[1]), jnp.float32),
        ),
        in_specs=[pl.BlockSpec(memory_space=pltpu.SMEM)] + [vmem_spec()] * 4,
        out_specs=(vmem_spec(),) * 3,
        scratch_shapes=[pltpu.VMEM(kv.shape[::-1], jnp.bfloat16)],
        compiler_params=pltpu.CompilerParams(vmem_limit_bytes=VMEM_MOST),
        name="attend",
    )(ranges, q_t, kv, seg_q, seg_k)


def attend_back_body(
    rows,
    range_ref,
    q_ref,
    do_ref,
    o_ref,
    lse_ref,
    kv_ref,
    segq_ref,
    segk_ref,
    dq_ref,
    dkv_ref,
    turned,
    dkv_acc,
):
    turn_keys(kv_ref, turned)
    dkv_acc[...] = jnp.zeros_like(dkv_acc)
    scale = HEAD_DIM**-0.5

    @pl.loop(0, q_ref.shape[1] // rows)
    def _(tile):
        at = bound(tile * rows, rows)
        q = q_ref[:, pl.ds(at, rows)] * jnp.bfloat16(scale)
        do = do_ref[:, pl.ds(at, rows)]
        none = jnp.zeros_like(q)
        both = jnp.concatenate(
            [jnp.concatenate([q, none], axis=1), jnp.concatenate([none, do], axis=1)], axis=0
        )
        delta = jnp.sum(o_ref[:, pl.ds(at, rows)] * do.astype(jnp.float32), axis=0, keepdims=True)
        lse = lse_ref[:, pl.ds(at, rows)]
        seg_q = segq_ref[:, pl.ds(at, rows)]

        def block(key_tile, dq):
            first = bound(key_tile * KEY_TILE, KEY_TILE)
            pair = matmul(kv_ref[pl.ds(first, KEY_TILE), :], both)
            scores, prob_grad = pair[:, :rows], pair[:, rows:]
            scores = jnp.where(same_doc(segk_ref, seg_q, first), scores, MASK_FILL)
            probs = jnp.exp(scores - lse)
            score_grad = (probs * (prob_grad - delta)).astype(jnp.bfloat16)
            joined = jnp.concatenate([score_grad, probs.astype(jnp.bfloat16)], axis=1)
            dkv_acc[pl.ds(first, KEY_TILE), :] += back_mul(joined, both)
            return dq + matmul(turned[:HEAD_DIM, pl.ds(first, KEY_TILE)], score_grad)

        dq = lax.fori_loop(
            range_ref[0, tile],
            range_ref[1, tile],
            block,
            jnp.zeros((HEAD_DIM, rows), jnp.float32),
        )
        dq_ref[:, pl.ds(at, rows)] = (dq * scale).astype(jnp.bfloat16)

    dkv_ref[...] = dkv_acc[...].astype(jnp.bfloat16)


def attend_back(ranges, q_t, do_t, o_t, lse, kv, seg_q, seg_k, rows):
    return pl.pallas_call(
        functools.partial(attend_back_body, rows),
        out_shape=(
            jax.ShapeDtypeStruct(q_t.shape, jnp.bfloat16),
            jax.ShapeDtypeStruct(kv.shape, jnp.bfloat16),
        ),
        in_specs=[pl.BlockSpec(memory_space=pltpu.SMEM)] + [vmem_spec()] * 7,
        out_specs=(vmem_spec(),) * 2,
        scratch_shapes=[
            pltpu.VMEM(kv.shape[::-1], jnp.bfloat16),
            pltpu.VMEM(kv.shape, jnp.float32),
        ],
        compiler_params=pltpu.CompilerParams(vmem_limit_bytes=VMEM_MOST),
        name="attend_back",
    )(ranges, q_t, do_t, o_t, lse, kv, seg_q, seg_k)


def column_groups(width, bits):
    tiles = width // LANES
    unit = 2 ** max(0, bits - 4)
    shares = [0.182, 0.182, 0.136] * 2
    sizes = [max(1, round(tiles * share / unit)) * unit for share in shares]
    sizes[-1] += tiles - sum(sizes)
    orders = [
        list(range(bits)),
        [1, 0] + list(range(2, bits)),
        list(range(2, bits)) + [0, 1],
    ] * 2
    groups, first = [], 0
    for size, order in zip(sizes, orders):
        groups.append((first * LANES, size * LANES, order))
        first += size
    return groups


def add_rows(dst, own, other, place, spot, first):
    row, tall, col, wide = place

    @pl.loop(0, tall // ROW_BLOCK)
    def _(step):
        gap = step * ROW_BLOCK
        here = (
            pl.ds(bound(row + gap, ROW_BLOCK), ROW_BLOCK),
            pl.ds(col if isinstance(col, int) else bound(col, LANES), wide),
        )
        there = (pl.ds(bound(spot + gap, ROW_BLOCK), ROW_BLOCK), pl.ds(first, wide))
        mine, got = own[here].astype(jnp.float32), other[there].astype(jnp.float32)
        dst[here] = (mine + got).astype(jnp.bfloat16)


def reduce_body(count, groups, g_ref, out_ref, buf, got_pair, got, ls, ws, wr, rs, rr, gs, gr):
    own, core = lax.axis_index("ctx"), lax.axis_index("ws")
    bits = count.bit_length() - 1
    rows = buf.shape[0]
    sibling = (own, 1 - core)
    bit_of = [lax.rem(own // 2**bit, 2) for bit in range(bits)]
    partner = [
        (own + 2**bit - 2 * 2**bit * bit_of[bit], core) for bit in range(bits)
    ]
    greet([sibling] + partner)

    sends, state, waiting = [], [], []
    for at, (first, width, order) in enumerate(groups):
        cols = pl.ds(first, width)
        waiting.append(
            push(
                g_ref.at[1 - core, :, cols], got_pair.at[:, cols], (ws, wr), at, sibling
            )
        )
        keep = pltpu.make_async_copy(g_ref.at[core, :, cols], buf.at[:, cols], ls.at[at])
        keep.start()
        state.append(keep)

    def start_step(at, step, place):
        first, width, order = groups[at]
        row, tall, col, wide, spot = place
        bit = order[step]
        if tall > ROW_BLOCK:
            half = tall // 2
            kept = (row + half * bit_of[bit], half, col, wide)
            sent = (row + half * (1 - bit_of[bit]), half, col, wide)
        else:
            half = wide // 2
            kept = (row, tall, col + half * bit_of[bit], half)
            sent = (row, tall, col + half * (1 - bit_of[bit]), half)
        copy = push(
            view(buf, sent),
            got.at[pl.ds(spot, sent[1]), pl.ds(first, sent[3])],
            (rs, rr),
            at * bits + step,
            partner[bit],
        )
        return copy, kept, spot

    def view(ref, place):
        row, tall, col, wide = place
        if not isinstance(row, int):
            row = bound(row, ROW_BLOCK)
        if not isinstance(col, int):
            col = bound(col, LANES)
        return ref.at[pl.ds(row, tall), pl.ds(col, wide)]

    places = [None] * len(groups)
    for at, (first, width, order) in enumerate(groups):
        state[at].wait()
        waiting[at].wait()
        add_rows(buf, buf, got_pair, (0, rows, first, width), 0, first)
        copy, kept, spot = start_step(at, 0, (0, rows, first, width, 0))
        places[at] = (copy, kept, spot)
    trail = [[] for _ in groups]
    for step in range(bits):
        for at, (first, width, order) in enumerate(groups):
            copy, kept, spot = places[at]
            copy.wait()
            trail[at].append(kept)
            row, tall, col, wide = kept
            last = step == bits - 1
            target = out_ref if last else buf
            add_rows(target, buf, got, kept, spot, first)
            if not last:
                places[at] = start_step(
                    at, step + 1, (row, tall, col, wide, spot + tall)
                )
    for step in reversed(range(bits)):
        for at, (first, width, order) in enumerate(groups):
            place = view(out_ref, trail[at][step])
            if step < bits - 1:
                places[at].wait()
            places[at] = push(
                place, place, (gs, gr), at * bits + step, partner[order[step]]
            )
    for at in range(len(groups)):
        places[at].wait()


def reduce_grads(packed, count):
    rows, width = packed.shape[1:]
    bits = count.bit_length() - 1
    groups = column_groups(width, bits)
    spots = len(groups)
    return pl.pallas_call(
        functools.partial(reduce_body, count, groups),
        out_shape=jax.ShapeDtypeStruct((rows, width), packed.dtype),
        in_specs=[any_spec()],
        out_specs=vmem_spec(),
        scratch_shapes=[
            pltpu.VMEM((rows, width), packed.dtype),
            pltpu.VMEM((rows, width), packed.dtype),
            pltpu.VMEM((rows + ROW_BLOCK * max(0, bits - 4), width), packed.dtype),
            pltpu.SemaphoreType.DMA((spots,)),
        ]
        + sem_pair(spots)
        + sem_pair(spots * bits)
        + sem_pair(spots * bits),
        compiler_params=comm_params(5),
        name="reduce_grads",
    )(packed)


def half_shape(grad):
    axis = 1 if grad.shape[0] in (3, 9) and grad.ndim > 1 else 0
    return axis, grad.shape[:axis] + (grad.shape[axis] // 2,) + grad.shape[axis + 1 :]


def is_small(grad):
    return grad.ndim == 1 or (grad.ndim == 2 and grad.shape[0] == 9)


SMALL_ROWS = 32
SMALL_WIDTH = 1024
BLOCK = 256


def pack_grads(grads):
    halves = []
    for half in range(2):
        columns, vectors = [], []
        for grad in grads:
            axis, shape = half_shape(grad)
            piece = lax.slice_in_dim(
                to_low(grad), half * shape[axis], (half + 1) * shape[axis], axis=axis
            )
            if is_small(grad):
                piece = piece.reshape(-1, shape[-1])
                vectors.append(jnp.pad(piece, ((0, 0), (0, SMALL_WIDTH - shape[-1]))))
            else:
                piece = piece.reshape(-1, BLOCK, shape[-1])
                columns.extend(piece[at] for at in range(piece.shape[0]))
        small = jnp.concatenate(vectors, axis=0)
        small = jnp.pad(small, ((0, SMALL_ROWS - small.shape[0]), (0, 0)))
        small = jnp.concatenate(jnp.split(small, SMALL_WIDTH // BLOCK, axis=1), axis=0)
        columns.append(jnp.pad(small, ((0, BLOCK - small.shape[0]), (0, 0))))
        halves.append(jnp.concatenate(columns, axis=1))
    return jnp.stack(halves)


def unpack_grads(packed, grads):
    results, first, row = [], 0, 0
    small = packed[: SMALL_ROWS * SMALL_WIDTH // BLOCK, packed.shape[1] - BLOCK :]
    small = jnp.concatenate(jnp.split(small, SMALL_WIDTH // BLOCK, axis=0), axis=1)
    for grad in grads:
        axis, shape = half_shape(grad)
        if is_small(grad):
            count = 1 if grad.ndim == 1 else grad.shape[0]
            piece = small[row : row + count, : shape[-1]].reshape(shape)
            row += count
        else:
            blocks = math.prod(shape) // (BLOCK * shape[-1])
            piece = jnp.concatenate(
                [
                    packed[:, first + at * shape[-1] : first + (at + 1) * shape[-1]]
                    for at in range(blocks)
                ],
                axis=0,
            ).reshape(shape)
            first += blocks * shape[-1]
        results.append(piece.astype(jnp.float32))
    return tuple(results)


def body(
    tokens,
    segment_ids,
    out_grad,
    ln1_gain,
    ln1_bias,
    glu_weight,
    glu_bias,
    ln2_gain,
    ln2_bias,
    left_weight,
    left_bias,
    conv_weight,
    conv_bias,
    ln3_gain,
    ln3_bias,
    depth_weight,
    point_weight,
    point_bias,
    ln4_gain,
    ln4_bias,
    qkv_weight,
    attn_out_weight,
    attn_out_bias,
    ln5_gain,
    ln5_bias,
    expand_weight,
    expand_bias,
    shrink_weight,
    shrink_bias,
):
    (
        n1_gain,
        n1_shift,
        glu_w,
        glu_b,
        n2_gain,
        n2_shift,
        left_w,
        left_b,
        conv_w,
        conv_b,
        n3_gain,
        n3_shift,
        depth_w,
        point_w,
        point_b,
        n4_gain,
        n4_shift,
        qkv_w,
        attn_w,
        attn_b,
        n5_gain,
        n5_shift,
        expand_w,
        expand_b,
        shrink_w,
        shrink_b,
    ) = (
        lax.all_gather(to_low(ln1_gain), "ws", axis=0, tiled=True),
        lax.all_gather(to_low(ln1_bias), "ws", axis=0, tiled=True),
        lax.all_gather(to_low(glu_weight), "ws", axis=0, tiled=True),
        lax.all_gather(to_low(glu_bias), "ws", axis=0, tiled=True),
        lax.all_gather(to_low(ln2_gain), "ws", axis=0, tiled=True),
        lax.all_gather(to_low(ln2_bias), "ws", axis=0, tiled=True),
        lax.all_gather(to_low(left_weight), "ws", axis=0, tiled=True),
        lax.all_gather(to_low(left_bias), "ws", axis=0, tiled=True),
        lax.all_gather(to_low(conv_weight), "ws", axis=1, tiled=True),
        lax.all_gather(to_low(conv_bias), "ws", axis=0, tiled=True),
        lax.all_gather(to_low(ln3_gain), "ws", axis=0, tiled=True),
        lax.all_gather(to_low(ln3_bias), "ws", axis=0, tiled=True),
        lax.all_gather(to_low(depth_weight), "ws", axis=1, tiled=True),
        lax.all_gather(to_low(point_weight), "ws", axis=0, tiled=True),
        lax.all_gather(to_low(point_bias), "ws", axis=0, tiled=True),
        lax.all_gather(to_low(ln4_gain), "ws", axis=0, tiled=True),
        lax.all_gather(to_low(ln4_bias), "ws", axis=0, tiled=True),
        lax.all_gather(to_low(qkv_weight), "ws", axis=0, tiled=True),
        lax.all_gather(to_low(attn_out_weight), "ws", axis=0, tiled=True),
        lax.all_gather(to_low(attn_out_bias), "ws", axis=0, tiled=True),
        lax.all_gather(to_low(ln5_gain), "ws", axis=0, tiled=True),
        lax.all_gather(to_low(ln5_bias), "ws", axis=0, tiled=True),
        lax.all_gather(to_low(expand_weight), "ws", axis=0, tiled=True),
        lax.all_gather(to_low(expand_bias), "ws", axis=0, tiled=True),
        lax.all_gather(to_low(shrink_weight), "ws", axis=0, tiled=True),
        lax.all_gather(to_low(shrink_bias), "ws", axis=0, tiled=True),
    )
    float_t = jnp.float32
    gain_one = n1_gain.astype(float_t)
    gain_two = n2_gain.astype(float_t)
    gain_three = n3_gain.astype(float_t)
    gain_four = n4_gain.astype(float_t)
    gain_five = n5_gain.astype(float_t)
    row_count = tokens.shape[1]
    state_in = tokens[0].astype(float_t)
    model_width = state_in.shape[1]
    seg_own = segment_ids[0]
    ctx_count = lax.axis_size("ctx")
    seg_all = gather_segments(segment_ids, ctx_count).reshape(-1)
    start_row = lax.axis_index("ctx") * row_count
    seg_rim = lax.dynamic_slice_in_dim(
        jnp.pad(seg_all, 4, constant_values=-1), start_row, row_count + 8
    )
    seg_near = lax.slice_in_dim(seg_rim, 3, row_count + 5)
    ln_out, normed_one, inv_one = norm_fwd(state_in, gain_one, n1_shift.astype(float_t))
    h_one = to_low(ln_out)
    glu_pre = matmul(h_one, glu_w) + glu_b.astype(float_t)
    glu_val = glu_pre[:, :model_width]
    glu_gate = jax.nn.sigmoid(glu_pre[:, model_width:])
    state_one = state_in + glu_val * glu_gate
    ln_out, normed_two, inv_two = norm_fwd(state_one, gain_two, n2_shift.astype(float_t))
    h_two = to_low(ln_out)
    left_pre = matmul(h_two, left_w) + left_b.astype(float_t)
    h_two_rim = extended(h_two, (("ctx", 0),), 1)
    conv_pre = conv_b.astype(float_t)
    for tap_no in range(3):
        conv_pre = conv_pre + matmul(
            masked_rows(h_two_rim, seg_near, seg_own, tap_no, row_count), conv_w[tap_no]
        )
    narrow = conv_pre.shape[1]
    wide_width = left_pre.shape[1]
    mixed_sum = jax.nn.silu(left_pre) + jnp.pad(
        jax.nn.silu(conv_pre), ((0, 0), (0, wide_width - narrow))
    )
    ln_out, normed_three, inv_three = norm_fwd(mixed_sum, gain_three, n3_shift.astype(float_t))
    g_three = to_low(ln_out)
    g_rim = extended(g_three, (("ctx", 0),), 4)
    depth_f = depth_w.astype(float_t)
    depth_acc = jnp.zeros((row_count, wide_width), float_t)
    for tap_no in range(9):
        depth_acc = (
            depth_acc
            + masked_rows(g_rim, seg_rim, seg_own, tap_no, row_count).astype(float_t)
            * depth_f[tap_no]
        )
    depth_out = to_low(depth_acc)
    sep_out = matmul(depth_out, point_w) + point_b.astype(float_t)
    state_two = state_one + jnp.pad(sep_out, ((0, 0), (0, model_width - narrow)))
    ln_out, normed_four, inv_four = norm_fwd(state_two, gain_four, n4_shift.astype(float_t))
    h_four = to_low(ln_out)
    qkv_all = matmul(h_four, qkv_w)
    head_count = model_width // HEAD_DIM
    parts = ctx_count // head_count
    queries_turned = to_low(qkv_all[:, :model_width]).T
    key_value = (
        to_low(qkv_all[:, model_width:])
        .reshape(row_count, 2, head_count, HEAD_DIM)
        .transpose(0, 2, 1, 3)
        .reshape(row_count, 2 * model_width)
    )
    part = lax.rem(lax.axis_index("ctx"), parts)
    seg_q = lax.dynamic_slice_in_dim(
        seg_all.reshape(head_count, parts, row_count), part, 1, axis=1
    ).reshape(head_count, row_count)
    key_first = jnp.sum(seg_all[None, :] < seg_q[:, :1], axis=1, dtype=jnp.int32)
    key_end = jnp.sum(seg_all[None, :] <= seg_q[:, -1:], axis=1, dtype=jnp.int32)
    ranges = jnp.stack([key_first // KEY_TILE, (key_end + KEY_TILE - 1) // KEY_TILE])
    seg_q = seg_q.reshape(1, head_count * row_count)
    seg_k = jnp.broadcast_to(seg_all[:, None], (seg_all.shape[0], LANES))
    q_head, kv_head = spread_heads(queries_turned, key_value, ctx_count, head_count)
    o_head, o_low, log_sum = attend(ranges, q_head, kv_head, seg_q, seg_k, row_count)
    attn_turned = swap_heads(o_low, ctx_count, head_count, False, 4)
    attn_low = attn_turned.T
    state_three = state_two + matmul(attn_low, attn_w) + attn_b.astype(float_t)
    ln_out, normed_five, inv_five = norm_fwd(state_three, gain_five, n5_shift.astype(float_t))
    h_five = to_low(ln_out)
    expand_pre = matmul(h_five, expand_w) + expand_b.astype(float_t)
    hidden = to_low(jax.nn.silu(expand_pre))
    state_four = state_three + matmul(hidden, shrink_w) + shrink_b.astype(float_t)
    output = to_low(state_four)[None]
    grad_four = out_grad[0].astype(float_t)
    z_grad = to_low(grad_four)
    g_shrink_w = outer_sum(hidden, z_grad)
    g_shrink_b = col_sum(z_grad)
    pre_grad = to_low(back_mul(z_grad, shrink_w) * smooth_slope(expand_pre))
    g_expand_w = outer_sum(h_five, pre_grad)
    g_expand_b = col_sum(pre_grad)
    in_grad, g_n5_gain, g_n5_shift = norm_back(
        back_mul(pre_grad, expand_w), normed_five, inv_five, gain_five
    )
    grad_three = grad_four + in_grad
    y_grad = to_low(grad_three)
    g_attn_w = outer_sum(attn_low, y_grad)
    g_attn_b = col_sum(y_grad)
    o_grad = to_low(back_mul(y_grad, attn_w)).T
    do_head = swap_heads(o_grad, ctx_count, head_count, True, 6)
    dq_head, dkv_head = attend_back(
        ranges, q_head, do_head, o_head, log_sum, kv_head, seg_q, seg_k, row_count
    )
    dq_turned, dkv_parts = collect_heads(dq_head, dkv_head, ctx_count, head_count)
    dkv = (
        to_low(jnp.sum(dkv_parts.astype(float_t), axis=0))
        .reshape(row_count, head_count, 2, HEAD_DIM)
        .transpose(0, 2, 1, 3)
        .reshape(row_count, 2 * model_width)
    )
    qkv_grad = jnp.concatenate([dq_turned.T, dkv], axis=1)
    g_qkv_w = outer_sum(h_four, qkv_grad)
    in_grad, g_n4_gain, g_n4_shift = norm_back(
        back_mul(qkv_grad, qkv_w), normed_four, inv_four, gain_four
    )
    grad_two = grad_three + in_grad
    sep_grad = to_low(grad_two[:, :narrow])
    g_point_w = outer_sum(depth_out, sep_grad)
    g_point_b = col_sum(sep_grad)
    depth_grad = to_low(back_mul(sep_grad, point_w))
    depth_rim = extended(depth_grad, (("ctx", 0),), 4)
    depth_grad_f = depth_grad.astype(float_t)
    g_depth = []
    g3_grad = jnp.zeros((row_count, wide_width), float_t)
    for tap_no in range(9):
        g_depth.append(
            jnp.sum(
                masked_rows(g_rim, seg_rim, seg_own, tap_no, row_count).astype(float_t)
                * depth_grad_f,
                axis=0,
            )
        )
        g3_grad = (
            g3_grad
            + masked_rows(depth_rim, seg_rim, seg_own, 8 - tap_no, row_count).astype(float_t)
            * depth_f[tap_no]
        )
    g_depth_w = jnp.stack(g_depth)
    mixed_grad, g_n3_gain, g_n3_shift = norm_back(g3_grad, normed_three, inv_three, gain_three)
    left_grad = to_low(mixed_grad * smooth_slope(left_pre))
    conv_grad = to_low(mixed_grad[:, :narrow] * smooth_slope(conv_pre))
    g_left_w = outer_sum(h_two, left_grad)
    g_left_b = col_sum(left_grad)
    h_two_grad = back_mul(left_grad, left_w)
    conv_grad_rim = extended(conv_grad, (("ctx", 0),), 1)
    g_conv = []
    for tap_no in range(3):
        g_conv.append(
            outer_sum(masked_rows(h_two_rim, seg_near, seg_own, tap_no, row_count), conv_grad)
        )
        h_two_grad = h_two_grad + back_mul(
            masked_rows(conv_grad_rim, seg_near, seg_own, 2 - tap_no, row_count), conv_w[tap_no]
        )
    g_conv_w = jnp.stack(g_conv)
    g_conv_b = col_sum(conv_grad)
    in_grad, g_n2_gain, g_n2_shift = norm_back(h_two_grad, normed_two, inv_two, gain_two)
    grad_one = grad_two + in_grad
    glu_grad = to_low(
        jnp.concatenate(
            [grad_one * glu_gate, grad_one * glu_val * glu_gate * (1.0 - glu_gate)], axis=1
        )
    )
    g_glu_w = outer_sum(h_one, glu_grad)
    g_glu_b = col_sum(glu_grad)
    in_grad, g_n1_gain, g_n1_shift = norm_back(
        back_mul(glu_grad, glu_w), normed_one, inv_one, gain_one
    )
    grad_zero = grad_one + in_grad
    local_grads = (
        g_n1_gain,
        g_n1_shift,
        g_glu_w,
        g_glu_b,
        g_n2_gain,
        g_n2_shift,
        g_left_w,
        g_left_b,
        g_conv_w,
        g_conv_b,
        g_n3_gain,
        g_n3_shift,
        g_depth_w,
        g_point_w,
        g_point_b,
        g_n4_gain,
        g_n4_shift,
        g_qkv_w,
        g_attn_w,
        g_attn_b,
        g_n5_gain,
        g_n5_shift,
        g_expand_w,
        g_expand_b,
        g_shrink_w,
        g_shrink_b,
    )
    packed = pack_grads(local_grads)
    return (output, grad_zero[None]) + unpack_grads(
        reduce_grads(packed, ctx_count), local_grads
    )


def solution(mesh):
    return jax.shard_map(
        body,
        mesh=mesh,
        in_specs=(
            P("ws", "ctx", None),
            P("ws", "ctx"),
            P("ws", "ctx", None),
            P("ws"),
            P("ws"),
            P("ws", None),
            P("ws"),
            P("ws"),
            P("ws"),
            P("ws", None),
            P("ws"),
            P(None, "ws", None),
            P("ws"),
            P("ws"),
            P("ws"),
            P(None, "ws"),
            P("ws", None),
            P("ws"),
            P("ws"),
            P("ws"),
            P("ws", None),
            P("ws", None),
            P("ws"),
            P("ws"),
            P("ws"),
            P("ws", None),
            P("ws"),
            P("ws", None),
            P("ws"),
        ),
        out_specs=(
            P("ws", "ctx", None),
            P("ws", "ctx", None),
            P("ws"),
            P("ws"),
            P("ws", None),
            P("ws"),
            P("ws"),
            P("ws"),
            P("ws", None),
            P("ws"),
            P(None, "ws", None),
            P("ws"),
            P("ws"),
            P("ws"),
            P(None, "ws"),
            P("ws", None),
            P("ws"),
            P("ws"),
            P("ws"),
            P("ws", None),
            P("ws", None),
            P("ws"),
            P("ws"),
            P("ws"),
            P("ws", None),
            P("ws"),
            P("ws", None),
            P("ws"),
        ),
        check_vma=False,
    )
```

```python
import functools
import math

import jax
import jax.numpy as jnp
from jax import lax
from jax.experimental import pallas as pl
from jax.experimental.pallas import tpu as pltpu
from jax.sharding import PartitionSpec as P

MESH_ID = pl.DeviceIdType.MESH
F32 = jnp.float32
BF16 = jnp.bfloat16
HEAD_DIM = 64
NORM_EPS = 1e-06
MASK_FILL = -1e30
LANES = 128
ROW_BLOCK = 16
EDGE = 16
KEY_TILE = 512
BLOCK = 256
VMEM_MOST = 60 * 1024 * 1024

D = 512
FF = 2048
HALF = 256
TAPS = 9
REACH = 4

QKV, POINT, LEFT, CONV, GLU, SMALL, LATE = 0, 1536, 2560, 4608, 5376, 6400, 6656
ATTN, EXPAND, SHRINK, EARLY = 0, 512, 2560, 4608
WIDTH = LATE + EARLY

SMALL_ROWS = 32
SMALL_WIDTH = 1024
(LN1G, LN1B, GLUB, LN2G, LN2B, LEFTB, CONVB, LN3G, LN3B, DEPTH) = range(10)
(POINTB, LN4G, LN4B, ATTNB, LN5G, LN5B, EXPANDB, SHRINKB) = range(DEPTH + TAPS, DEPTH + TAPS + 8)


def vmem_spec():
    return pl.BlockSpec(memory_space=pltpu.VMEM)


def any_spec():
    return pl.BlockSpec(memory_space=pl.ANY)


def smem_spec():
    return pl.BlockSpec(memory_space=pltpu.SMEM)


def shaped(shape, kind=F32):
    return jax.ShapeDtypeStruct(shape, kind)


def comm_params(number):
    return pltpu.CompilerParams(
        collective_id=number, has_side_effects=True, vmem_limit_bytes=VMEM_MOST
    )


def greet(peers):
    barrier = pltpu.get_barrier_semaphore()
    for peer in peers:
        pl.semaphore_signal(barrier, inc=1, device_id=peer, device_id_type=MESH_ID)
    pl.semaphore_wait(barrier, len(peers))


def push(src, dst, sems, at, peer):
    copy = pltpu.make_async_remote_copy(
        src_ref=src,
        dst_ref=dst,
        send_sem=sems[0].at[at],
        recv_sem=sems[1].at[at],
        device_id=peer,
        device_id_type=MESH_ID,
    )
    copy.start()
    return copy


def move(src, dst, sem):
    copy = pltpu.make_async_copy(src, dst, sem)
    copy.start()
    return copy


def sem_pair(count):
    return [pltpu.SemaphoreType.DMA((count,)), pltpu.SemaphoreType.DMA((count,))]


def bound(value, step):
    return value if isinstance(value, int) else pl.multiple_of(value, step)


def span(value, step):
    return pl.ds(bound(value * step, step), step)


def matmul(left_op, right_op):
    return jnp.dot(left_op, right_op, preferred_element_type=F32)


def back_mul(grad_in, weight):
    return lax.dot_general(grad_in, weight, (((1,), (1,)), ((), ())), preferred_element_type=F32)


def turn(block):
    return block.astype(F32).T.astype(BF16)


def col_sum(block):
    return jnp.sum(block.astype(F32), axis=0, keepdims=True)


def lane_mean(block):
    return jnp.mean(block, axis=-1, keepdims=True)


def smooth_slope(block):
    sigma = jax.nn.sigmoid(block)
    return sigma * (1.0 + block * (1.0 - sigma))


def norm_fwd(block):
    centred = block - lane_mean(block)
    inv_std = lax.rsqrt(lane_mean(centred * centred) + NORM_EPS)
    return centred * inv_std, inv_std


def norm_back(grad_in, normed, inv_std, gain):
    scaled = grad_in * gain
    inner, cross = lane_mean(scaled), lane_mean(scaled * normed)
    return inv_std * (scaled - inner - normed * cross)


def vector(small_ref, row, size):
    half = size // 2
    return jnp.concatenate(
        [small_ref[core, row : row + 1, :half] for core in range(2)], axis=1
    )


def put_vector(small_ref, row, value):
    half = value.shape[1] // 2
    for core in range(2):
        small_ref[core, row : row + 1, :half] = value[:, core * half : (core + 1) * half]


def place():
    own, core = lax.axis_index("ctx"), lax.axis_index("ws")
    return own, core


def others_of(own, core, count):
    return [(lax.rem(own + gap, count), core) for gap in range(1, count)]


def widened(dst_ref, src_ref):
    @pl.loop(0, 2)
    def _(core):
        dst_ref[core] = src_ref[core].astype(BF16).astype(F32)


WEIGHT_COLUMNS = [
    (0, GLU, 1024, 1, False),
    (1, LEFT, 2048, 1, False),
    (2, CONV, 256, 3, False),
    (3, POINT, 256, 4, False),
    (4, QKV, 1536, 1, False),
    (5, ATTN, 512, 1, True),
    (6, EXPAND, 2048, 1, True),
    (7, SHRINK, 512, 4, True),
]


def tap_masks(mask_ref, seg_ref):
    seg = seg_ref[...]
    for tap in range(TAPS):
        moved = pltpu.roll(seg, (REACH - tap) % seg.shape[0], 0)
        mask_ref[tap] = jnp.where(moved == seg, 1.0, 0.0).astype(F32)


def first_body(
    count,
    heads,
    tok_ref,
    seg_row_ref,
    seg_col_ref,
    small_in,
    *refs,
):
    weights, refs = refs[:8], refs[8:]
    outs, refs = refs[:18], refs[18:]
    (
        late_out,
        early_out,
        small_out,
        seg_all,
        plan_out,
        q_out,
        kv_out,
        n1_out,
        glu_out,
        n2_out,
        left_out,
        conv_out,
        n3_out,
        depth_out,
        n4_out,
        x2_out,
        inv_out,
        masks_out,
    ) = outs
    (
        staged,
        late,
        early,
        edges,
        seg_edges,
        x_ext,
        seg_ext,
        masks,
        small,
        low_ext,
        n1,
        glu_pre,
        x1,
        n2,
        shifted,
        left_pre,
        conv_pre,
        n3,
        g3,
        depth,
        x2,
        n4,
        inv,
        q_turned,
        kv_own,
        load_sem,
        out_sem,
        ws_send,
        ws_recv,
        edge_send,
        edge_recv,
        row_send,
        row_recv,
        q_send,
        q_recv,
        kv_send,
        kv_recv,
    ) = refs
    own, core = place()
    parts = count // heads
    head, part = own // parts, lax.rem(own, parts)
    rows = tok_ref.shape[0]
    ext = rows + 2 * EDGE
    mid = slice(EDGE, EDGE + rows)
    sibling = (own, 1 - core)
    peers = others_of(own, core, count)

    loads, column = [], 0
    stage_at = []
    for number, first, width, blocks, _ in WEIGHT_COLUMNS:
        stage_at.append(column)
        for block in range(blocks):
            source = weights[number]
            if blocks == 3:
                source = source.at[block]
            elif blocks > 1:
                source = source.at[pl.ds(block * BLOCK, BLOCK), :]
            loads.append(
                move(
                    source,
                    staged.at[:, pl.ds(column, width)],
                    load_sem.at[len(loads)],
                )
            )
            column += width
    greet([sibling] + peers)

    copies = []
    right, left = (lax.rem(own + 1, count), core), (lax.rem(own + count - 1, count), core)
    edge_copies = [
        push(tok_ref.at[pl.ds(rows - EDGE, EDGE), :], edges.at[0], (edge_send, edge_recv), 0, right),
        push(tok_ref.at[pl.ds(0, EDGE), :], edges.at[1], (edge_send, edge_recv), 1, left),
        push(seg_col_ref.at[pl.ds(rows - EDGE, EDGE), :], seg_edges.at[0], (edge_send, edge_recv), 2, right),
        push(seg_col_ref.at[pl.ds(0, EDGE), :], seg_edges.at[1], (edge_send, edge_recv), 3, left),
    ]
    small_copy = push(small_in, small_out.at[core], (ws_send, ws_recv), len(WEIGHT_COLUMNS), sibling)
    small_out[core] = small_in[...]

    at, weight_copies = 0, []
    for (number, first, width, blocks, is_early), column in zip(WEIGHT_COLUMNS, stage_at):
        target = early if is_early else late
        for _ in range(blocks):
            loads[at].wait()
            at += 1
        size = width * blocks
        mine = pl.ds(bound(core * BLOCK, BLOCK), BLOCK)

        @pl.loop(0, BLOCK // ROW_BLOCK)
        def _(step):
            source = staged[span(step, ROW_BLOCK), pl.ds(column, size)]
            goes = pl.ds(bound(core * BLOCK + step * ROW_BLOCK, ROW_BLOCK), ROW_BLOCK)
            target[goes, pl.ds(first, size)] = source.astype(BF16)

        piece = target.at[mine, pl.ds(first, size)]
        weight_copies.append(push(piece, piece, (ws_send, ws_recv), number, sibling))

    for copy in edge_copies:
        copy.wait()
    small_copy.wait()
    row_copies = [
        push(seg_row_ref, seg_all.at[own], (row_send, row_recv), gap, peer)
        for gap, peer in enumerate(peers)
    ]
    seg_all[own] = seg_row_ref[...]
    widened(small, small_out)

    x_ext[:EDGE, :] = edges[0].astype(F32)
    x_ext[mid, :] = tok_ref[...].astype(F32)
    x_ext[EDGE + rows :, :] = edges[1].astype(F32)
    seg_ext[:EDGE, :] = jnp.where(own == 0, -1, seg_edges[0])
    seg_ext[mid, :] = seg_col_ref[...]
    seg_ext[EDGE + rows :, :] = jnp.where(own == count - 1, -1, seg_edges[1])
    tap_masks(masks, seg_ext)

    normed, inv_std = norm_fwd(x_ext[...])
    n1[...] = normed[mid, :]
    inv[0] = jnp.broadcast_to(inv_std, (ext, LANES))
    low_ext[...] = (normed * vector(small, LN1G, D) + vector(small, LN1B, D)).astype(BF16)

    weight_copies[0].wait()
    glu_bias = vector(small, GLUB, 2 * D)
    for step in range(2 * D // 512):
        cols = slice(512 * step, 512 * (step + 1))
        glu_pre[:, cols] = (
            matmul(low_ext[...], late[:, GLU + 512 * step : GLU + 512 * (step + 1)])
            + glu_bias[:, cols]
        )
    state = x_ext[...] + glu_pre[:, :D] * jax.nn.sigmoid(glu_pre[:, D:])
    x1[...] = state[mid, :]
    normed, inv_std = norm_fwd(state)
    n2[...] = normed[mid, :]
    inv[1] = jnp.broadcast_to(inv_std, (ext, LANES))
    low_f = (normed * vector(small, LN2G, D) + vector(small, LN2B, D)).astype(BF16).astype(F32)
    before = pltpu.roll(low_f, 1, 0) * jnp.concatenate([masks[REACH - 1]] * (D // LANES), axis=1)
    after = pltpu.roll(low_f, ext - 1, 0) * jnp.concatenate([masks[REACH + 1]] * (D // LANES), axis=1)
    shifted[0] = before.astype(BF16)
    shifted[1] = low_f.astype(BF16)
    shifted[2] = after.astype(BF16)

    weight_copies[1].wait()

    @pl.loop(0, FF // 512)
    def _(step):
        weight = late[:, pl.ds(bound(LEFT + step * 512, 512), 512)]
        left_pre[:, span(step, 512)] = matmul(shifted[1], weight)

    weight_copies[2].wait()
    conv_sum = vector(small, CONVB, HALF)
    for tap in range(3):
        conv_sum = conv_sum + matmul(
            shifted[tap], late[:, CONV + HALF * tap : CONV + HALF * (tap + 1)]
        )
    conv_pre[...] = conv_sum

    left_bias = vector(small, LEFTB, FF)
    gain, shift = vector(small, LN3G, FF), vector(small, LN3B, FF)

    @pl.loop(0, ext // ROW_BLOCK)
    def _(step):
        here = span(step, ROW_BLOCK)
        pre = left_pre[here, :] + left_bias
        left_pre[here, :] = pre
        mixed = jax.nn.silu(pre)
        mixed = jnp.concatenate(
            [mixed[:, :HALF] + jax.nn.silu(conv_pre[here, :]), mixed[:, HALF:]], axis=1
        )
        normed, inv_std = norm_fwd(mixed)
        n3[here, :] = normed
        inv[2, here, :] = jnp.broadcast_to(inv_std, (ROW_BLOCK, LANES))
        g3[here, :] = (normed * gain + shift).astype(BF16).astype(F32)

    saves = [
        move(n1, n1_out, out_sem.at[0]),
        move(glu_pre.at[pl.ds(EDGE, rows), :], glu_out, out_sem.at[1]),
        move(n2, n2_out, out_sem.at[2]),
        move(left_pre.at[pl.ds(EDGE, rows), :], left_out, out_sem.at[3]),
        move(conv_pre, conv_out, out_sem.at[4]),
        move(n3, n3_out, out_sem.at[5]),
    ]

    @pl.loop(0, FF // LANES)
    def _(step):
        cols = span(step, LANES)
        block = g3[:, cols]
        total = jnp.zeros((rows, LANES), F32)
        for tap in range(TAPS):
            row = DEPTH + tap
            moved = pltpu.roll(block, (REACH - tap) % ext, 0)[mid, :]
            half = FF // 2 // LANES
            taps = small[step // half, row : row + 1, span(lax.rem(step, half), LANES)]
            total = total + moved * masks[tap, mid, :] * taps
        depth[:, cols] = total.astype(BF16)

    saves.append(move(depth, depth_out, out_sem.at[6]))
    weight_copies[3].wait()
    sep = vector(small, POINTB, HALF)
    for side in range(2):
        for block in range(4):
            first = side * (FF // 2) + block * BLOCK
            sep = sep + matmul(
                depth[:, first : first + BLOCK],
                late[side * BLOCK : (side + 1) * BLOCK, POINT + HALF * block : POINT + HALF * (block + 1)],
            )
    state = jnp.concatenate([x1[:, :HALF] + sep, x1[:, HALF:]], axis=1)
    x2[...] = state
    normed, inv_std = norm_fwd(state)
    n4[...] = normed
    inv[3, :rows, :] = jnp.broadcast_to(inv_std, (rows, LANES))
    low = (normed * vector(small, LN4G, D) + vector(small, LN4B, D)).astype(BF16)
    weight_copies[4].wait()
    for step in range(D // 256):
        cols = slice(256 * step, 256 * (step + 1))
        query = matmul(low, late[:, QKV + 256 * step : QKV + 256 * (step + 1)])
        q_turned[cols, :] = turn(query)
    near = lax.broadcasted_iota(jnp.int32, (rows, LANES), 1) < HEAD_DIM
    for step in range(D // LANES):
        first = QKV + D + LANES * step
        keys = matmul(low, late[:, first : first + LANES])
        values = matmul(low, late[:, first + D : first + D + LANES])
        kv_own[:, 2 * step * LANES : (2 * step + 1) * LANES] = jnp.where(
            near, keys, pltpu.roll(values, HEAD_DIM, 1)
        ).astype(BF16)
        kv_own[:, (2 * step + 1) * LANES : (2 * step + 2) * LANES] = jnp.where(
            near, pltpu.roll(keys, HEAD_DIM, 1), values
        ).astype(BF16)

    q_slot = q_out.at[:, span(head, rows)]
    kv_slot = kv_out.at[span(own, rows), :]
    for gap, (peer, _) in enumerate(peers):
        copies.append(
            push(kv_own.at[:, span(peer // parts, LANES)], kv_slot, (kv_send, kv_recv), gap, (peer, core))
        )
    for gap in range(1, heads):
        other = lax.rem(head + gap, heads)
        copies.append(
            push(q_turned.at[span(other, HEAD_DIM), :], q_slot, (q_send, q_recv), gap - 1, (other * parts + part, core))
        )
    saves.append(move(q_turned.at[span(head, HEAD_DIM), :], q_slot, out_sem.at[7]))
    saves.append(move(kv_own.at[:, span(head, LANES)], kv_slot, out_sem.at[8]))
    saves.append(move(n4, n4_out, out_sem.at[9]))
    saves.append(move(x2, x2_out, out_sem.at[10]))
    saves.append(move(inv, inv_out, out_sem.at[11]))
    saves.append(move(masks, masks_out, out_sem.at[14]))
    for copy in weight_copies[5:]:
        copy.wait()
    saves.append(move(late, late_out, out_sem.at[12]))
    saves.append(move(early, early_out, out_sem.at[13]))

    for copy in row_copies:
        copy.wait()
    lane = lax.broadcasted_iota(jnp.int32, (1, LANES), 1)
    every = seg_all[:, 0, :]
    for tile in range(heads):
        source = tile * parts + part
        mine = seg_all[source]
        first = jnp.min(mine, axis=1, keepdims=True)
        last = jnp.max(mine, axis=1, keepdims=True)
        below = jnp.sum(jnp.sum((every < first).astype(F32), axis=0, keepdims=True), axis=1, keepdims=True).astype(jnp.int32)
        upto = jnp.sum(jnp.sum((every <= last).astype(F32), axis=0, keepdims=True), axis=1, keepdims=True).astype(jnp.int32)
        plan_out[tile : tile + 1, :] = jnp.where(
            lane == 0, below, jnp.where(lane == 1, upto, source)
        )
    for copy in copies + saves:
        copy.wait()


def first_kernel(tokens, seg_row, seg_col, small, weights, count, heads):
    rows = tokens.shape[0]
    ext = rows + 2 * EDGE
    late = (2 * BLOCK, SMALL)
    early = (2 * BLOCK, EARLY)
    out_shape = (
        shaped(late, BF16),
        shaped(early, BF16),
        shaped((2, SMALL_ROWS, SMALL_WIDTH)),
        shaped((count, 1, rows), jnp.int32),
        shaped((heads, LANES), jnp.int32),
        shaped((HEAD_DIM, heads * rows), BF16),
        shaped((count * rows, LANES), BF16),
        shaped((rows, D)),
        shaped((rows, 2 * D)),
        shaped((rows, D)),
        shaped((rows, FF)),
        shaped((ext, HALF)),
        shaped((ext, FF)),
        shaped((rows, FF), BF16),
        shaped((rows, D)),
        shaped((rows, D)),
        shaped((4, ext, LANES)),
        shaped((TAPS, ext, LANES)),
    )
    out_specs = (
        [any_spec()] * 2 + [vmem_spec()] * 3 + [any_spec()] * 13
    )
    scratch = [
        pltpu.VMEM((BLOCK, SMALL + EARLY), F32),
        pltpu.VMEM(late, BF16),
        pltpu.VMEM(early, BF16),
        pltpu.VMEM((2, EDGE, D), BF16),
        pltpu.VMEM((2, EDGE, LANES), jnp.int32),
        pltpu.VMEM((ext, D), F32),
        pltpu.VMEM((ext, LANES), jnp.int32),
        pltpu.VMEM((TAPS, ext, LANES), F32),
        pltpu.VMEM((2, SMALL_ROWS, SMALL_WIDTH), F32),
        pltpu.VMEM((ext, D), BF16),
        pltpu.VMEM((rows, D), F32),
        pltpu.VMEM((ext, 2 * D), F32),
        pltpu.VMEM((rows, D), F32),
        pltpu.VMEM((rows, D), F32),
        pltpu.VMEM((3, ext, D), BF16),
        pltpu.VMEM((ext, FF), F32),
        pltpu.VMEM((ext, HALF), F32),
        pltpu.VMEM((ext, FF), F32),
        pltpu.VMEM((ext, FF), F32),
        pltpu.VMEM((rows, FF), BF16),
        pltpu.VMEM((rows, D), F32),
        pltpu.VMEM((rows, D), F32),
        pltpu.VMEM((4, ext, LANES), F32),
        pltpu.VMEM((D, rows), BF16),
        pltpu.VMEM((rows, 2 * D), BF16),
        pltpu.SemaphoreType.DMA((sum(item[3] for item in WEIGHT_COLUMNS),)),
        pltpu.SemaphoreType.DMA((15,)),
    ]
    scratch += sem_pair(len(WEIGHT_COLUMNS) + 1) + sem_pair(4) + sem_pair(count - 1)
    scratch += sem_pair(heads - 1) + sem_pair(count - 1)
    return pl.pallas_call(
        functools.partial(first_body, count, heads),
        out_shape=out_shape,
        in_specs=[vmem_spec()] * 4 + [any_spec()] * 8,
        out_specs=out_specs,
        scratch_shapes=scratch,
        compiler_params=comm_params(1),
        name="first_layers",
    )(tokens, seg_row, seg_col, small, *weights)


def turn_keys(kv_ref, turned):
    @pl.loop(0, kv_ref.shape[0] // KEY_TILE)
    def _(tile):
        here = span(tile, KEY_TILE)
        turned[:, here] = turn(kv_ref[here, :])


def key_segments(seg_ref, segk):
    count, _, rows = seg_ref.shape

    @pl.loop(0, count)
    def _(source):
        for step in range(rows // LANES):
            row = seg_ref[source, :, step * LANES : (step + 1) * LANES].astype(F32)
            column = jnp.broadcast_to(row, (LANES, LANES)).T
            segk[pl.ds(bound(source * rows + step * LANES, LANES), LANES), :] = column


def masked(scores, segk, here, seg_q):
    seg_k = jnp.concatenate([segk[here, :]] * (scores.shape[1] // LANES), axis=1)
    return jnp.where(seg_k == seg_q, scores, MASK_FILL)


def key_tiles(plan_ref, tile):
    return plan_ref[tile, 0] // KEY_TILE, (plan_ref[tile, 1] + KEY_TILE - 1) // KEY_TILE


def attend_body(rows, plan_ref, q_ref, kv_ref, seg_ref, o_ref, low_ref, lse_ref, turned, segk):
    turn_keys(kv_ref, turned)
    key_segments(seg_ref, segk)

    @pl.loop(0, q_ref.shape[1] // rows)
    def _(tile):
        at = span(tile, rows)
        q = q_ref[:, at] * jnp.bfloat16(HEAD_DIM**-0.5)
        q_pad = jnp.concatenate([q, jnp.zeros_like(q)], axis=0)
        seg_q = seg_ref[plan_ref[tile, 2]].astype(F32)

        def block(key_tile, carry):
            top, total, acc = carry
            here = span(key_tile, KEY_TILE)
            scores = masked(matmul(kv_ref[here, :], q_pad), segk, here, seg_q)
            new_top = jnp.maximum(top, jnp.max(scores, axis=0, keepdims=True))
            probs = jnp.exp(scores - new_top)
            shrink = jnp.exp(top - new_top)
            total = total * shrink + jnp.sum(probs, axis=0, keepdims=True)
            acc = acc * shrink + matmul(turned[HEAD_DIM:, here], probs.astype(BF16))
            return (new_top, total, acc)

        first, end = key_tiles(plan_ref, tile)
        top, total, acc = lax.fori_loop(
            first,
            end,
            block,
            (
                jnp.full((1, rows), MASK_FILL, F32),
                jnp.zeros((1, rows), F32),
                jnp.zeros((HEAD_DIM, rows), F32),
            ),
        )
        out = acc / total
        o_ref[:, at] = out
        low_ref[:, at] = out.astype(BF16)
        lse_ref[:, at] = top + jnp.log(total)


def attend(plan, q_t, kv, seg, rows):
    return pl.pallas_call(
        functools.partial(attend_body, rows),
        out_shape=(shaped(q_t.shape), shaped(q_t.shape, BF16), shaped((1, q_t.shape[1]))),
        in_specs=[smem_spec()] + [vmem_spec()] * 3,
        out_specs=(vmem_spec(),) * 3,
        scratch_shapes=[pltpu.VMEM(kv.shape[::-1], BF16), pltpu.VMEM(kv.shape, F32)],
        compiler_params=pltpu.CompilerParams(vmem_limit_bytes=VMEM_MOST),
        name="attend",
    )(plan, q_t, kv, seg)


def attend_back_body(
    rows, plan_ref, q_ref, do_ref, o_ref, lse_ref, kv_ref, seg_ref, dq_ref, dkv_ref, turned, segk, dkv_acc
):
    turn_keys(kv_ref, turned)
    key_segments(seg_ref, segk)
    dkv_acc[...] = jnp.zeros_like(dkv_acc)
    scale = HEAD_DIM**-0.5

    @pl.loop(0, q_ref.shape[1] // rows)
    def _(tile):
        at = span(tile, rows)
        q = q_ref[:, at] * jnp.bfloat16(scale)
        do = do_ref[:, at]
        none = jnp.zeros_like(q)
        both = jnp.concatenate(
            [jnp.concatenate([q, none], axis=1), jnp.concatenate([none, do], axis=1)], axis=0
        )
        delta = jnp.sum(o_ref[:, at] * do.astype(F32), axis=0, keepdims=True)
        lse = lse_ref[:, at]
        seg_q = seg_ref[plan_ref[tile, 2]].astype(F32)

        def block(key_tile, dq):
            here = span(key_tile, KEY_TILE)
            pair = matmul(kv_ref[here, :], both)
            probs = jnp.exp(masked(pair[:, :rows], segk, here, seg_q) - lse)
            score_grad = (probs * (pair[:, rows:] - delta)).astype(BF16)
            joined = jnp.concatenate([score_grad, probs.astype(BF16)], axis=1)
            dkv_acc[here, :] += back_mul(joined, both)
            return dq + matmul(turned[:HEAD_DIM, here], score_grad)

        first, end = key_tiles(plan_ref, tile)
        dq = lax.fori_loop(first, end, block, jnp.zeros((HEAD_DIM, rows), F32))
        dq_ref[:, at] = (dq * scale).astype(BF16)

    dkv_ref[...] = dkv_acc[...].astype(BF16)


def attend_back(plan, q_t, do_t, o_t, lse, kv, seg, rows):
    return pl.pallas_call(
        functools.partial(attend_back_body, rows),
        out_shape=(shaped(q_t.shape, BF16), shaped(kv.shape, BF16)),
        in_specs=[smem_spec()] + [vmem_spec()] * 6,
        out_specs=(vmem_spec(),) * 2,
        scratch_shapes=[
            pltpu.VMEM(kv.shape[::-1], BF16),
            pltpu.VMEM(kv.shape, F32),
            pltpu.VMEM(kv.shape, F32),
        ],
        compiler_params=pltpu.CompilerParams(vmem_limit_bytes=VMEM_MOST),
        name="attend_back",
    )(plan, q_t, do_t, o_t, lse, kv, seg)


def middle_body(
    count,
    heads,
    o_in,
    out_grad,
    small_in,
    x2_in,
    early_in,
    out_ref,
    small_grads,
    dx3_out,
    grads_out,
    do_out,
    weights,
    x2,
    small,
    o_t,
    x3,
    expand_pre,
    hidden,
    dpre,
    do_t,
    grads,
    dx3,
    load_sem,
    o_send,
    o_recv,
    do_send,
    do_recv,
):
    own, core = place()
    parts = count // heads
    head, part = own // parts, lax.rem(own, parts)
    rows = out_grad.shape[0]
    loads = [move(early_in, weights, load_sem.at[0]), move(x2_in, x2, load_sem.at[1])]
    near = [lax.rem(head + gap, heads) for gap in range(1, heads)]
    peers = [(other * parts + part, core) for other in near]
    greet(peers)
    copies = [
        push(o_in.at[:, span(other, rows)], o_t.at[span(head, HEAD_DIM), :], (o_send, o_recv), gap, peer)
        for gap, (other, peer) in enumerate(zip(near, peers))
    ]
    copies.append(move(o_in.at[:, span(head, rows)], o_t.at[span(head, HEAD_DIM), :], load_sem.at[2]))
    widened(small, small_in)
    small_grads[...] = jnp.zeros_like(small_grads)
    for copy in copies + loads:
        copy.wait()

    state = (
        x2[...]
        + matmul(turn(o_t[...]), weights[:, ATTN : ATTN + D])
        + vector(small, ATTNB, D)
    )
    x3[...] = state
    normed, inv_std = norm_fwd(state)
    gain = vector(small, LN5G, D)
    low = (normed * gain + vector(small, LN5B, D)).astype(BF16)
    expand_bias = vector(small, EXPANDB, FF)
    for step in range(FF // 512):
        cols = slice(512 * step, 512 * (step + 1))
        pre = matmul(low, weights[:, EXPAND + 512 * step : EXPAND + 512 * (step + 1)]) + expand_bias[:, cols]
        expand_pre[:, cols] = pre
        hidden[:, cols] = jax.nn.silu(pre).astype(BF16)
    state = x3[...] + vector(small, SHRINKB, D)
    for block in range(FF // BLOCK):
        side, column = block // 4, SHRINK + D * (block % 4)
        state = state + matmul(
            hidden[:, block * BLOCK : (block + 1) * BLOCK],
            weights[side * BLOCK : (side + 1) * BLOCK, column : column + D],
        )
    out_ref[...] = state.astype(BF16)

    dz = out_grad[...]
    for block in range(FF // BLOCK):
        side, column = block // 4, SHRINK + D * (block % 4)
        cols = slice(block * BLOCK, (block + 1) * BLOCK)
        grad = back_mul(dz, weights[side * BLOCK : (side + 1) * BLOCK, column : column + D])
        dpre[:, cols] = (grad * smooth_slope(expand_pre[:, cols])).astype(BF16)
    grad = jnp.concatenate(
        [
            back_mul(dpre[...], weights[side * BLOCK : (side + 1) * BLOCK, EXPAND : EXPAND + FF])
            for side in range(2)
        ],
        axis=1,
    )
    state = dz.astype(F32) + norm_back(grad, normed, inv_std, gain)
    dx3[...] = state
    dy3 = state.astype(BF16)
    do_t[...] = back_mul(weights[:, ATTN : ATTN + D], dy3).astype(BF16)
    slot = do_out.at[:, span(head, rows)]
    copies = [
        push(do_t.at[span(other, HEAD_DIM), :], slot, (do_send, do_recv), gap, peer)
        for gap, (other, peer) in enumerate(zip(near, peers))
    ]
    copies.append(move(do_t.at[span(head, HEAD_DIM), :], slot, load_sem.at[0]))
    copies.append(move(dx3, dx3_out, load_sem.at[1]))

    put_vector(small_grads, LN5G, col_sum(grad * normed))
    put_vector(small_grads, LN5B, col_sum(grad))
    put_vector(small_grads, ATTNB, col_sum(dy3))
    put_vector(small_grads, EXPANDB, col_sum(dpre[...]))
    put_vector(small_grads, SHRINKB, col_sum(dz))
    grads[:, ATTN : ATTN + D] = matmul(o_t[...], dy3).astype(BF16)
    low_t = turn(low)
    for step in range(FF // 512):
        grads[:, EXPAND + 512 * step : EXPAND + 512 * (step + 1)] = matmul(
            low_t, dpre[:, 512 * step : 512 * (step + 1)]
        ).astype(BF16)
    for block in range(FF // BLOCK):
        side, column = block // 4, SHRINK + D * (block % 4)
        grads[side * BLOCK : (side + 1) * BLOCK, column : column + D] = matmul(
            turn(hidden[:, block * BLOCK : (block + 1) * BLOCK]), dz
        ).astype(BF16)
    copies.append(move(grads, grads_out, load_sem.at[2]))
    for copy in copies:
        copy.wait()


def middle_kernel(o_low, out_grad, small, x2, early, count, heads):
    rows = out_grad.shape[0]
    return pl.pallas_call(
        functools.partial(middle_body, count, heads),
        out_shape=(
            shaped((rows, D), BF16),
            shaped((2, SMALL_ROWS, SMALL_WIDTH)),
            shaped((rows, D)),
            shaped(early.shape, BF16),
            shaped((HEAD_DIM, heads * rows), BF16),
        ),
        in_specs=[vmem_spec()] * 3 + [any_spec()] * 2,
        out_specs=[vmem_spec()] * 2 + [any_spec()] * 3,
        scratch_shapes=[
            pltpu.VMEM(early.shape, BF16),
            pltpu.VMEM((rows, D), F32),
            pltpu.VMEM((2, SMALL_ROWS, SMALL_WIDTH), F32),
            pltpu.VMEM((D, rows), BF16),
            pltpu.VMEM((rows, D), F32),
            pltpu.VMEM((rows, FF), F32),
            pltpu.VMEM((rows, FF), BF16),
            pltpu.VMEM((rows, FF), BF16),
            pltpu.VMEM((D, rows), BF16),
            pltpu.VMEM(early.shape, BF16),
            pltpu.VMEM((rows, D), F32),
            pltpu.SemaphoreType.DMA((3,)),
        ]
        + sem_pair(heads - 1)
        + sem_pair(heads - 1),
        compiler_params=comm_params(2),
        name="middle_layers",
    )(o_low, out_grad, small, x2, early)


def column_groups(first, width, bits):
    tiles = width // LANES
    unit = 2 ** max(0, bits - 4)
    long = max(1, round(tiles * 0.36 / unit)) * unit
    orders = [
        list(range(bits)),
        [1, 0] + list(range(2, bits)),
        list(range(2, bits)) + [0, 1],
    ]
    groups = []
    for size, order in zip([long, long, tiles - 2 * long], orders):
        groups.append((first, size * LANES, order))
        first += size * LANES
    return groups


def grad_sets(bits):
    bounds = [LATE, QKV, LEFT, CONV]
    widths = [EARLY, LEFT - QKV, CONV - LEFT, LATE - CONV]
    return [column_groups(first, width, bits) for first, width in zip(bounds, widths)]


class Piece:
    def __init__(self, at, group, links, sums, got, total, sems):
        self.at, (self.first, self.width, self.order) = at, group
        self.core, self.sibling, self.bit_of, self.partner = links
        self.view, self.got, self.total, self.sems = sums, got, total, sems
        self.bits, self.phase, self.trail = len(self.order), 0, []
        self.copy = None

    def whole(self):
        return (0, BLOCK, self.first, self.width)

    def out(self, where):
        row, tall, col, wide = where
        return self.total.at[pl.ds(bound(row, ROW_BLOCK), tall), pl.ds(bound(col, LANES), wide)]

    def start(self, other_half):
        self.copy = push(other_half, self.out(self.whole()), self.sems[0], self.at, self.sibling)

    def add(self, where, source, spot, last):
        row, tall, col, wide = where

        @pl.loop(0, tall // ROW_BLOCK)
        def _(step):
            gap = step * ROW_BLOCK
            here = (row + gap, ROW_BLOCK, col, wide)
            there = source.at[pl.ds(bound(spot + gap, ROW_BLOCK), ROW_BLOCK), pl.ds(self.first, wide)]
            mine = self.view(here)[...].astype(F32)
            added = (mine + there[...].astype(F32)).astype(BF16)
            if last:
                self.out(here)[...] = added
            else:
                self.view(here)[...] = added

    def halve(self, step):
        row, tall, col, wide = self.where
        bit = self.order[step]
        mine = self.bit_of[bit]
        if tall > ROW_BLOCK:
            half = tall // 2
            kept = (row + half * mine, half, col, wide)
            sent = (row + half * (1 - mine), half, col, wide)
        else:
            half = wide // 2
            kept = (row, tall, col + half * mine, half)
            sent = (row, tall, col + half * (1 - mine), half)
        self.copy = push(
            self.view(sent),
            self.got.at[pl.ds(self.spot, sent[1]), pl.ds(self.first, sent[3])],
            self.sems[1],
            self.at * self.bits + step,
            self.partner[bit],
        )
        self.where = kept

    def double(self, step):
        place_out = self.out(self.trail[step])
        self.copy = push(
            place_out,
            place_out,
            self.sems[2],
            self.at * self.bits + step,
            self.partner[self.order[step]],
        )

    def done(self):
        return self.phase > 2 * self.bits

    def advance(self):
        if self.done():
            return
        self.copy.wait()
        if self.phase == 0:
            self.where, self.spot = self.whole(), 0
            self.add(self.where, self.total, 0, False)
            self.halve(0)
        elif self.phase <= self.bits:
            last = self.phase == self.bits
            self.add(self.where, self.got, self.spot, last)
            self.trail.append(self.where)
            self.spot += self.where[1]
            if last:
                self.double(self.bits - 1)
            else:
                self.halve(self.phase)
        elif self.phase < 2 * self.bits:
            self.double(2 * self.bits - 1 - self.phase)
        self.phase += 1


def last_body(count, heads, dq_in, dkv_in, small_in, small_grads_in, *refs):
    (
        early_grads,
        dx3_in,
        late_in,
        n1_in,
        glu_in,
        n2_in,
        left_in,
        conv_in,
        n3_in,
        depth_in,
        n4_in,
        inv_in,
        masks_in,
        total,
        grad_out,
        weights,
        dx3,
        n1,
        glu_pre,
        n2,
        left_pre,
        conv_pre,
        n3,
        depth,
        n4,
        inv,
        masks,
        small,
        small_grads,
        dq_t,
        dkv_parts,
        dqkv,
        sep_own,
        sep_edges,
        sep_ext,
        depth_grad,
        g3_grad,
        row_sums,
        dleft,
        conv_grad,
        conv_taps,
        grads,
        early_own,
        got,
        result,
        load_sem,
        keep_sem,
        dq_send,
        dq_recv,
        dkv_send,
        dkv_recv,
        edge_send,
        edge_recv,
        ws_send,
        ws_recv,
        rs_send,
        rs_recv,
        ag_send,
        ag_recv,
    ) = refs
    own, core = place()
    parts = count // heads
    head, part = own // parts, lax.rem(own, parts)
    rows = dx3.shape[0]
    ext = rows + 2 * EDGE
    mid = slice(EDGE, EDGE + rows)
    sibling = (own, 1 - core)
    peers = others_of(own, core, count)
    bits = count.bit_length() - 1

    sources = (dx3_in, late_in, n4_in, inv_in, depth_in, masks_in, n3_in, left_in, conv_in, n2_in, glu_in, n1_in)
    targets = (dx3, weights, n4, inv, depth, masks, n3, left_pre, conv_pre, n2, glu_pre, n1)
    loads = [move(a, b, load_sem.at[at]) for at, (a, b) in enumerate(zip(sources, targets))]
    greet([sibling] + peers)

    slot = dq_t.at[span(head, HEAD_DIM), :]
    kv_slot = dkv_parts.at[part, :, span(head, LANES)]
    collect = []
    for gap, (peer, _) in enumerate(peers):
        collect.append(push(dkv_in.at[span(peer, rows), :], kv_slot, (dkv_send, dkv_recv), gap, (peer, core)))
    for gap in range(1, heads):
        other = lax.rem(head + gap, heads)
        collect.append(
            push(dq_in.at[:, span(other, rows)], slot, (dq_send, dq_recv), gap - 1, (other * parts + part, core))
        )
    collect.append(move(dq_in.at[:, span(head, rows)], slot, keep_sem.at[0]))
    collect.append(move(dkv_in.at[span(own, rows), :], kv_slot, keep_sem.at[1]))

    bit_of = [lax.rem(own // 2**bit, 2) for bit in range(bits)]
    partner = [(own + 2**bit - 2 * 2**bit * bit_of[bit], core) for bit in range(bits)]
    links = (core, sibling, bit_of, partner)
    sems = ((ws_send, ws_recv), (rs_send, rs_recv), (ag_send, ag_recv))

    def early_view(where):
        row, tall, col, wide = where
        return early_own.at[pl.ds(bound(row, ROW_BLOCK), tall), pl.ds(bound(col - LATE, LANES), wide)]

    def late_view(where):
        row, tall, col, wide = where
        return grads.at[pl.ds(bound(core * BLOCK + row, ROW_BLOCK), tall), pl.ds(bound(col, LANES), wide)]

    sets, at = [], 0
    for number, groups in enumerate(grad_sets(bits)):
        members = []
        for group in groups:
            view = late_view if number else early_view
            members.append(Piece(at, group, links, view, got, total, sems))
            at += 1
        sets.append(members)
    other_rows = pl.ds(bound((1 - core) * BLOCK, BLOCK), BLOCK)
    own_rows = pl.ds(bound(core * BLOCK, BLOCK), BLOCK)

    def start(members, source, shift):
        for piece in members:
            piece.start(source.at[other_rows, pl.ds(piece.first - shift, piece.width)])

    def advance(members):
        for piece in members:
            piece.advance()

    keep = move(early_grads.at[own_rows, :], early_own, keep_sem.at[2])
    start(sets[0], early_grads, LATE)
    widened(small, small_in)
    small_grads[...] = small_grads_in[...]
    keep.wait()
    for copy in loads:
        copy.wait()
    for copy in collect:
        copy.wait()
    advance(sets[0])

    dqkv[:, :D] = turn(dq_t[...])
    lane = lax.broadcasted_iota(jnp.int32, (rows, LANES), 1) < HEAD_DIM
    for step in range(D // LANES):
        pair = []
        for side in range(2):
            first = (2 * step + side) * LANES
            share = dkv_parts[0, :, first : first + LANES].astype(F32)
            for number in range(1, parts):
                share = share + dkv_parts[number, :, first : first + LANES].astype(F32)
            pair.append(share)
        cols = slice(D + step * LANES, D + (step + 1) * LANES)
        dqkv[:, cols] = jnp.where(lane, pair[0], pltpu.roll(pair[1], HEAD_DIM, 1)).astype(BF16)
        cols = slice(2 * D + step * LANES, 2 * D + (step + 1) * LANES)
        dqkv[:, cols] = jnp.where(lane, pltpu.roll(pair[0], HEAD_DIM, 1), pair[1]).astype(BF16)

    def through(grad, column, width):
        return jnp.concatenate(
            [
                back_mul(grad, weights[side * BLOCK : (side + 1) * BLOCK, column : column + width])
                for side in range(2)
            ],
            axis=1,
        )

    def norm_step(grad, normed, inv_std, row):
        put_vector(small_grads, row, col_sum(grad * normed))
        put_vector(small_grads, row + 1, col_sum(grad))
        return norm_back(grad, normed, inv_std, vector(small, row, D))

    grad = through(dqkv[...], QKV, 3 * D)
    dx2 = dx3[...] + norm_step(grad, n4[...], inv[3, :rows, :1], LN4G)
    dx3[...] = dx2
    sep_own[...] = dx2[:, :HALF].astype(BF16)
    right, left = (lax.rem(own + 1, count), core), (lax.rem(own + count - 1, count), core)
    edge_copies = [
        push(sep_own.at[pl.ds(rows - EDGE, EDGE), :], sep_edges.at[0], (edge_send, edge_recv), 0, right),
        push(sep_own.at[pl.ds(0, EDGE), :], sep_edges.at[1], (edge_send, edge_recv), 1, left),
    ]
    low_t = turn(n4[...] * vector(small, LN4G, D) + vector(small, LN4B, D))
    for step in range(3):
        grads[:, QKV + D * step : QKV + D * (step + 1)] = matmul(
            low_t, dqkv[:, D * step : D * (step + 1)]
        ).astype(BF16)
    for block in range(FF // BLOCK):
        side, column = block // 4, POINT + HALF * (block % 4)
        grads[side * BLOCK : (side + 1) * BLOCK, column : column + HALF] = matmul(
            turn(depth[:, block * BLOCK : (block + 1) * BLOCK]), sep_own[...]
        ).astype(BF16)
    put_vector(small_grads, POINTB, col_sum(sep_own[...]))
    start(sets[1], grads, 0)

    for copy in edge_copies:
        copy.wait()
    sep_ext[:EDGE, :] = sep_edges[0]
    sep_ext[mid, :] = sep_own[...]
    sep_ext[EDGE + rows :, :] = sep_edges[1]
    for block in range(FF // BLOCK):
        side, column = block // 4, POINT + HALF * (block % 4)
        depth_grad[:, block * BLOCK : (block + 1) * BLOCK] = (
            back_mul(sep_ext[...], weights[side * BLOCK : (side + 1) * BLOCK, column : column + HALF])
            .astype(BF16)
            .astype(F32)
        )
    advance(sets[0])
    advance(sets[1])

    row_sums[...] = jnp.zeros_like(row_sums)
    half = FF // 2 // LANES

    @pl.loop(0, FF // LANES)
    def _(step):
        cols = span(step, LANES)
        side, lanes = step // half, span(lax.rem(step, half), LANES)
        block = depth_grad[:, cols]
        normed = n3[:, cols]
        gain = small[side, LN3G : LN3G + 1, lanes]
        low = (normed[mid, :] * gain + small[side, LN3B : LN3B + 1, lanes]).astype(BF16).astype(F32)
        summed = jnp.zeros((ext, LANES), F32)
        for tap in range(TAPS):
            row = DEPTH + tap
            moved = pltpu.roll(block, (tap - REACH) % ext, 0) * masks[TAPS - 1 - tap]
            summed = summed + moved * small[side, row : row + 1, lanes]
            small_grads[side, row : row + 1, lanes] = col_sum(low * moved[mid, :])
        g3_grad[:, cols] = summed
        small_grads[side, LN3G : LN3G + 1, lanes] = col_sum(summed[mid, :] * normed[mid, :])
        small_grads[side, LN3B : LN3B + 1, lanes] = col_sum(summed[mid, :])
        scaled = summed * gain
        row_sums[0] = row_sums[0] + scaled
        row_sums[1] = row_sums[1] + scaled * normed

    advance(sets[0])
    inner = jnp.sum(row_sums[0], axis=1, keepdims=True) * (1.0 / FF)
    cross = jnp.sum(row_sums[1], axis=1, keepdims=True) * (1.0 / FF)
    row_sums[0] = jnp.broadcast_to(inner, (ext, LANES))
    row_sums[1] = jnp.broadcast_to(cross, (ext, LANES))

    @pl.loop(0, FF // LANES)
    def _(step):
        cols = span(step, LANES)
        side, lanes = step // half, span(lax.rem(step, half), LANES)
        scaled = g3_grad[mid, cols] * small[side, LN3G : LN3G + 1, lanes]
        mixed_grad = inv[2, mid, :] * (scaled - row_sums[0, mid, :] - n3[mid, cols] * row_sums[1, mid, :])
        low = (mixed_grad * smooth_slope(left_pre[:, cols])).astype(BF16)
        dleft[:, cols] = low
        small_grads[side, LEFTB : LEFTB + 1, lanes] = col_sum(low)

    for step in range(HALF // LANES):
        cols = slice(step * LANES, (step + 1) * LANES)
        scaled = g3_grad[:, cols] * small[0, LN3G : LN3G + 1, cols]
        mixed_grad = inv[2] * (scaled - row_sums[0] - n3[:, cols] * row_sums[1])
        low = (mixed_grad * smooth_slope(conv_pre[:, cols])).astype(BF16).astype(F32)
        conv_grad[:, cols] = low
        for tap in range(3):
            moved = pltpu.roll(low, (tap - 1) % ext, 0) * masks[REACH + 1 - tap]
            conv_taps[:, HALF * tap + step * LANES : HALF * tap + (step + 1) * LANES] = moved[mid, :].astype(BF16)
    put_vector(small_grads, CONVB, col_sum(conv_grad[mid, :]))

    low_t = turn(n2[...] * vector(small, LN2G, D) + vector(small, LN2B, D))
    for step in range(FF // 512):
        grads[:, LEFT + 512 * step : LEFT + 512 * (step + 1)] = matmul(
            low_t, dleft[:, 512 * step : 512 * (step + 1)]
        ).astype(BF16)
    start(sets[2], grads, 0)
    advance(sets[0])
    advance(sets[1])
    for tap in range(3):
        grads[:, CONV + HALF * tap : CONV + HALF * (tap + 1)] = matmul(
            low_t, conv_taps[:, HALF * tap : HALF * (tap + 1)]
        ).astype(BF16)
    grad = through(dleft[...], LEFT, FF) + through(conv_taps[...], CONV, 3 * HALF)
    dx1 = dx3[...] + norm_step(grad, n2[...], inv[1, mid, :1], LN2G)
    gate = jax.nn.sigmoid(glu_pre[:, D:])
    value_grad = dx1 * gate
    dglu = jnp.concatenate([value_grad, value_grad * glu_pre[:, :D] * (1.0 - gate)], axis=1).astype(BF16)
    put_vector(small_grads, GLUB, col_sum(dglu))
    advance(sets[2])
    low_t = turn(n1[...] * vector(small, LN1G, D) + vector(small, LN1B, D))
    for step in range(2):
        grads[:, GLU + D * step : GLU + D * (step + 1)] = matmul(
            low_t, dglu[:, D * step : D * (step + 1)]
        ).astype(BF16)
    grad = through(dglu, GLU, 2 * D)
    result[...] = dx1 + norm_step(grad, n1[...], inv[0, mid, :1], LN1G)
    keep = move(result, grad_out, keep_sem.at[0])
    for side in range(2):
        for block in range(SMALL_WIDTH // BLOCK):
            first = side * BLOCK + block * SMALL_ROWS
            grads[first : first + SMALL_ROWS, SMALL : SMALL + BLOCK] = small_grads[
                side, :, block * BLOCK : (block + 1) * BLOCK
            ].astype(BF16)
        first = side * BLOCK + SMALL_WIDTH // BLOCK * SMALL_ROWS
        grads[first : (side + 1) * BLOCK, SMALL : SMALL + BLOCK] = jnp.zeros(
            ((side + 1) * BLOCK - first, BLOCK), BF16
        )
    start(sets[3], grads, 0)
    while not all(piece.done() for members in sets for piece in members):
        for members in sets:
            advance(members)
    keep.wait()


def last_kernel(dq, dkv, small, small_grads, tensors, count, heads):
    rows = dkv.shape[0] // count
    ext = rows + 2 * EDGE
    bits = count.bit_length() - 1
    pieces = sum(len(groups) for groups in grad_sets(bits))
    early = tensors[0].shape
    scratch = [
        pltpu.VMEM(tensors[2].shape, BF16),
        pltpu.VMEM((rows, D), F32),
        pltpu.VMEM((rows, D), F32),
        pltpu.VMEM((rows, 2 * D), F32),
        pltpu.VMEM((rows, D), F32),
        pltpu.VMEM((rows, FF), F32),
        pltpu.VMEM((ext, HALF), F32),
        pltpu.VMEM((ext, FF), F32),
        pltpu.VMEM((rows, FF), BF16),
        pltpu.VMEM((rows, D), F32),
        pltpu.VMEM((4, ext, LANES), F32),
        pltpu.VMEM((TAPS, ext, LANES), F32),
        pltpu.VMEM((2, SMALL_ROWS, SMALL_WIDTH), F32),
        pltpu.VMEM((2, SMALL_ROWS, SMALL_WIDTH), F32),
        pltpu.VMEM((D, rows), BF16),
        pltpu.VMEM((count // heads, rows, 2 * D), BF16),
        pltpu.VMEM((rows, 3 * D), BF16),
        pltpu.VMEM((rows, HALF), BF16),
        pltpu.VMEM((2, EDGE, HALF), BF16),
        pltpu.VMEM((ext, HALF), BF16),
        pltpu.VMEM((ext, FF), F32),
        pltpu.VMEM((ext, FF), F32),
        pltpu.VMEM((2, ext, LANES), F32),
        pltpu.VMEM((rows, FF), BF16),
        pltpu.VMEM((ext, HALF), F32),
        pltpu.VMEM((rows, 3 * HALF), BF16),
        pltpu.VMEM((2 * BLOCK, LATE), BF16),
        pltpu.VMEM((BLOCK, EARLY), BF16),
        pltpu.VMEM((BLOCK + ROW_BLOCK * max(0, bits - 4), WIDTH), BF16),
        pltpu.VMEM((rows, D), F32),
        pltpu.SemaphoreType.DMA((12,)),
        pltpu.SemaphoreType.DMA((3,)),
    ]
    scratch += sem_pair(heads - 1) + sem_pair(count - 1) + sem_pair(2) + sem_pair(pieces)
    scratch += sem_pair(pieces * bits) + sem_pair(pieces * bits)
    return pl.pallas_call(
        functools.partial(last_body, count, heads),
        out_shape=(shaped((BLOCK, WIDTH), BF16), shaped((rows, D))),
        in_specs=[vmem_spec()] * 4 + [any_spec()] * len(tensors),
        out_specs=[vmem_spec(), any_spec()],
        scratch_shapes=scratch,
        compiler_params=comm_params(3),
        name="last_layers",
    )(dq, dkv, small, small_grads, *tensors)


VECTORS = [
    (LN1G, 1, 256),
    (LN1B, 1, 256),
    (GLUB, 1, 512),
    (LN2G, 1, 256),
    (LN2B, 1, 256),
    (LEFTB, 1, 1024),
    (CONVB, 1, 128),
    (LN3G, 1, 1024),
    (LN3B, 1, 1024),
    (DEPTH, TAPS, 1024),
    (POINTB, 1, 128),
    (LN4G, 1, 256),
    (LN4B, 1, 256),
    (ATTNB, 1, 256),
    (LN5G, 1, 256),
    (LN5B, 1, 256),
    (EXPANDB, 1, 1024),
    (SHRINKB, 1, 256),
]
MATRICES = [
    (GLU, 1024, 1),
    (LEFT, 2048, 1),
    (CONV, 256, 3),
    (POINT, 256, 4),
    (QKV, 1536, 1),
    (LATE + ATTN, 512, 1),
    (LATE + EXPAND, 2048, 1),
    (LATE + SHRINK, 512, 4),
]


def unpack_body(packed, *outs):
    for (first, width, blocks), out in zip(MATRICES, outs):
        for block in range(blocks):

            @pl.loop(0, BLOCK // ROW_BLOCK)
            def _(step):
                value = packed[span(step, ROW_BLOCK), first + block * width : first + (block + 1) * width].astype(F32)
                if blocks == 3:
                    out[block, span(step, ROW_BLOCK), :] = value
                else:
                    out[pl.ds(bound(block * BLOCK + step * ROW_BLOCK, ROW_BLOCK), ROW_BLOCK), :] = value

    small = jnp.concatenate(
        [
            packed[block * SMALL_ROWS : (block + 1) * SMALL_ROWS, SMALL : SMALL + BLOCK].astype(F32)
            for block in range(SMALL_WIDTH // BLOCK)
        ],
        axis=1,
    )
    for (row, tall, size), out in zip(VECTORS, outs[len(MATRICES) :]):
        out[...] = small[row : row + tall, :size]


def unpack(packed):
    shapes = []
    for _, width, blocks in MATRICES:
        shapes.append((3, BLOCK, width) if blocks == 3 else (blocks * BLOCK, width))
    shapes += [(tall, size) for _, tall, size in VECTORS]
    return pl.pallas_call(
        unpack_body,
        out_shape=tuple(shaped(shape) for shape in shapes),
        in_specs=[vmem_spec()],
        out_specs=(vmem_spec(),) * len(shapes),
        compiler_params=pltpu.CompilerParams(vmem_limit_bytes=VMEM_MOST),
        name="unpack",
    )(packed)


def body(tokens, segment_ids, out_grad, *params):
    (
        ln1g, ln1b, glu_w, glu_b, ln2g, ln2b, left_w, left_b, conv_w, conv_b, ln3g, ln3b, depth_w,
        point_w, point_b, ln4g, ln4b, qkv_w, attn_w, attn_b, ln5g, ln5b, expand_w, expand_b,
        shrink_w, shrink_b,
    ) = params
    count = lax.axis_size("ctx")
    heads = D // HEAD_DIM
    rows = tokens.shape[1]
    vectors = [
        ln1g, ln1b, glu_b, ln2g, ln2b, left_b, conv_b, ln3g, ln3b, depth_w,
        point_b, ln4g, ln4b, attn_b, ln5g, ln5b, expand_b, shrink_b,
    ]
    lines = []
    for value in vectors:
        value = value.reshape(-1, value.shape[-1])
        lines.append(jnp.pad(value, ((0, 0), (0, SMALL_WIDTH - value.shape[1]))))
    small = jnp.concatenate(lines, axis=0)
    small = jnp.pad(small, ((0, SMALL_ROWS - small.shape[0]), (0, 0)))
    seg_col = jnp.broadcast_to(segment_ids[0][:, None], (rows, LANES))
    weights = (glu_w, left_w, conv_w, point_w, qkv_w, attn_w, expand_w, shrink_w)
    (
        late, early, small, seg, plan, q_head, kv_head, n1, glu_pre, n2, left_pre, conv_pre, n3,
        depth, n4, x2, inv, masks,
    ) = first_kernel(tokens[0], segment_ids, seg_col, small, weights, count, heads)
    o_head, o_low, log_sum = attend(plan, q_head, kv_head, seg, rows)
    output, small_grads, dx3, early_grads, do_head = middle_kernel(
        o_low, out_grad[0], small, x2, early, count, heads
    )
    dq_head, dkv_head = attend_back(plan, q_head, do_head, o_head, log_sum, kv_head, seg, rows)
    tensors = (
        early_grads, dx3, late, n1, glu_pre, n2, left_pre, conv_pre, n3, depth, n4, inv, masks,
    )
    total, input_grad = last_kernel(dq_head, dkv_head, small, small_grads, tensors, count, heads)
    pieces = unpack(total)
    matrices, lines = pieces[: len(MATRICES)], pieces[len(MATRICES) :]
    lines = [line if line.shape[0] > 1 else line.reshape(-1) for line in lines]
    g_glu, g_left, g_conv, g_point, g_qkv, g_attn, g_expand, g_shrink = matrices
    (
        g_ln1g, g_ln1b, g_glu_b, g_ln2g, g_ln2b, g_left_b, g_conv_b, g_ln3g, g_ln3b, g_depth,
        g_point_b, g_ln4g, g_ln4b, g_attn_b, g_ln5g, g_ln5b, g_expand_b, g_shrink_b,
    ) = lines
    return (
        output[None], input_grad[None], g_ln1g, g_ln1b, g_glu, g_glu_b, g_ln2g, g_ln2b, g_left,
        g_left_b, g_conv, g_conv_b, g_ln3g, g_ln3b, g_depth, g_point, g_point_b, g_ln4g, g_ln4b,
        g_qkv, g_attn, g_attn_b, g_ln5g, g_ln5b, g_expand, g_expand_b, g_shrink, g_shrink_b,
    )


def solution(mesh):
    return jax.shard_map(
        body,
        mesh=mesh,
        in_specs=(
            P("ws", "ctx", None),
            P("ws", "ctx"),
            P("ws", "ctx", None),
            P("ws"),
            P("ws"),
            P("ws", None),
            P("ws"),
            P("ws"),
            P("ws"),
            P("ws", None),
            P("ws"),
            P(None, "ws", None),
            P("ws"),
            P("ws"),
            P("ws"),
            P(None, "ws"),
            P("ws", None),
            P("ws"),
            P("ws"),
            P("ws"),
            P("ws", None),
            P("ws", None),
            P("ws"),
            P("ws"),
            P("ws"),
            P("ws", None),
            P("ws"),
            P("ws", None),
            P("ws"),
        ),
        out_specs=(
            P("ws", "ctx", None),
            P("ws", "ctx", None),
            P("ws"),
            P("ws"),
            P("ws", None),
            P("ws"),
            P("ws"),
            P("ws"),
            P("ws", None),
            P("ws"),
            P(None, "ws", None),
            P("ws"),
            P("ws"),
            P("ws"),
            P(None, "ws"),
            P("ws", None),
            P("ws"),
            P("ws"),
            P("ws"),
            P("ws", None),
            P("ws", None),
            P("ws"),
            P("ws"),
            P("ws"),
            P("ws", None),
            P("ws"),
            P("ws", None),
            P("ws"),
        ),
        check_vma=False,
    )
```

```python
import functools
import math

import jax
import jax.numpy as jnp
from jax import lax
from jax.experimental import pallas as pl
from jax.experimental.pallas import tpu as pltpu
from jax.sharding import PartitionSpec as P

MESH_ID = pl.DeviceIdType.MESH
F32 = jnp.float32
BF16 = jnp.bfloat16
HEAD_DIM = 64
NORM_EPS = 1e-06
MASK_FILL = -1e30
LANES = 128
ROW_BLOCK = 16
EDGE = 16
KEY_TILE = 512
BLOCK = 256
VMEM_MOST = 60 * 1024 * 1024

D = 512
FF = 2048
HALF = 256
TAPS = 9
REACH = 4

QKV, POINT, LEFT, CONV, GLU, SMALL, LATE = 0, 1536, 2560, 4608, 5376, 6400, 6656
ATTN, EXPAND, SHRINK, EARLY = 0, 512, 2560, 4608
WIDTH = LATE + EARLY

SMALL_ROWS = 32
SMALL_WIDTH = 1024
(LN1G, LN1B, GLUB, LN2G, LN2B, LEFTB, CONVB, LN3G, LN3B, DEPTH) = range(10)
(POINTB, LN4G, LN4B, ATTNB, LN5G, LN5B, EXPANDB, SHRINKB) = range(DEPTH + TAPS, DEPTH + TAPS + 8)


VECTORS = [
    (LN1G, 1, 256),
    (LN1B, 1, 256),
    (GLUB, 1, 512),
    (LN2G, 1, 256),
    (LN2B, 1, 256),
    (LEFTB, 1, 1024),
    (CONVB, 1, 128),
    (LN3G, 1, 1024),
    (LN3B, 1, 1024),
    (DEPTH, TAPS, 1024),
    (POINTB, 1, 128),
    (LN4G, 1, 256),
    (LN4B, 1, 256),
    (ATTNB, 1, 256),
    (LN5G, 1, 256),
    (LN5B, 1, 256),
    (EXPANDB, 1, 1024),
    (SHRINKB, 1, 256),
]
MATRICES = [
    (GLU, 1024, 1),
    (LEFT, 2048, 1),
    (CONV, 256, 3),
    (POINT, 256, 4),
    (QKV, 1536, 1),
    (LATE + ATTN, 512, 1),
    (LATE + EXPAND, 2048, 1),
    (LATE + SHRINK, 512, 4),
]


def vmem_spec():
    return pl.BlockSpec(memory_space=pltpu.VMEM)


def any_spec():
    return pl.BlockSpec(memory_space=pl.ANY)


def smem_spec():
    return pl.BlockSpec(memory_space=pltpu.SMEM)


def shaped(shape, kind=F32):
    return jax.ShapeDtypeStruct(shape, kind)


def comm_params(number):
    return pltpu.CompilerParams(
        collective_id=number, has_side_effects=True, vmem_limit_bytes=VMEM_MOST
    )


def greet(peers):
    barrier = pltpu.get_barrier_semaphore()
    for peer in peers:
        pl.semaphore_signal(barrier, inc=1, device_id=peer, device_id_type=MESH_ID)
    pl.semaphore_wait(barrier, len(peers))


def push(src, dst, sems, at, peer):
    copy = pltpu.make_async_remote_copy(
        src_ref=src,
        dst_ref=dst,
        send_sem=sems[0].at[at],
        recv_sem=sems[1].at[at],
        device_id=peer,
        device_id_type=MESH_ID,
    )
    copy.start()
    return copy


def move(src, dst, sem):
    copy = pltpu.make_async_copy(src, dst, sem)
    copy.start()
    return copy


def sem_pair(count):
    return [pltpu.SemaphoreType.DMA((count,)), pltpu.SemaphoreType.DMA((count,))]


def bound(value, step):
    return value if isinstance(value, int) else pl.multiple_of(value, step)


def span(value, step):
    return pl.ds(bound(value * step, step), step)


def matmul(left_op, right_op):
    return jnp.dot(left_op, right_op, preferred_element_type=F32)


def back_mul(grad_in, weight):
    return lax.dot_general(grad_in, weight, (((1,), (1,)), ((), ())), preferred_element_type=F32)


def turn(block):
    return block.astype(F32).T.astype(BF16)


def col_sum(block):
    return jnp.sum(block.astype(F32), axis=0, keepdims=True)


def lane_mean(block):
    return jnp.mean(block, axis=-1, keepdims=True)


def smooth_slope(block):
    sigma = jax.nn.sigmoid(block)
    return sigma * (1.0 + block * (1.0 - sigma))


def norm_fwd(block):
    centred = block - lane_mean(block)
    inv_std = lax.rsqrt(lane_mean(centred * centred) + NORM_EPS)
    return centred * inv_std, inv_std


def norm_back(grad_in, normed, inv_std, gain):
    scaled = grad_in * gain
    inner, cross = lane_mean(scaled), lane_mean(scaled * normed)
    return inv_std * (scaled - inner - normed * cross)


def vector(small_ref, row, size):
    half = size // 2
    return jnp.concatenate(
        [small_ref[core, row : row + 1, :half] for core in range(2)], axis=1
    )


def put_vector(small_ref, row, value):
    half = value.shape[1] // 2
    for core in range(2):
        small_ref[core, row : row + 1, :half] = value[:, core * half : (core + 1) * half]


def place():
    own, core = lax.axis_index("ctx"), lax.axis_index("ws")
    return own, core


def others_of(own, core, count):
    return [(lax.rem(own + gap, count), core) for gap in range(1, count)]


def widened(dst_ref, src_ref):
    @pl.loop(0, 2)
    def _(core):
        dst_ref[core] = src_ref[core].astype(BF16).astype(F32)


def turned_segments(out_ref, first, row):
    for step in range(row.shape[1] // LANES):
        part = row[:, step * LANES : (step + 1) * LANES].astype(F32)
        here = pl.ds(bound(first + step * LANES, LANES), LANES)
        out_ref[here, :] = jnp.broadcast_to(part, (LANES, LANES)).T


WEIGHT_COLUMNS = [
    (0, GLU, 1024, 1, False),
    (1, LEFT, 2048, 1, False),
    (2, CONV, 256, 3, False),
    (3, POINT, 256, 4, False),
    (4, QKV, 1536, 1, False),
    (5, ATTN, 512, 1, True),
    (6, EXPAND, 2048, 1, True),
    (7, SHRINK, 512, 4, True),
]


def tap_masks(mask_ref, seg_ref):
    seg = seg_ref[...]
    for tap in range(TAPS):
        moved = pltpu.roll(seg, (REACH - tap) % seg.shape[0], 0)
        mask_ref[tap] = jnp.where(moved == seg, 1.0, 0.0).astype(F32)


def first_body(
    count,
    heads,
    tok_ref,
    seg_row_ref,
    *refs,
):
    vectors, refs = refs[: len(VECTORS)], refs[len(VECTORS) :]
    weights, refs = refs[:8], refs[8:]
    outs, refs = refs[:18], refs[18:]
    (
        late_out,
        early_out,
        small_out,
        seg_all,
        plan_out,
        q_out,
        kv_out,
        n1_out,
        glu_out,
        n2_out,
        left_out,
        conv_out,
        n3_out,
        depth_out,
        n4_out,
        x2_out,
        inv_out,
        masks_out,
    ) = outs
    (
        staged,
        late,
        early,
        edges,
        seg_edges,
        seg_col,
        small_own,
        x_ext,
        seg_ext,
        masks,
        small,
        low_ext,
        n1,
        glu_pre,
        x1,
        n2,
        shifted,
        left_pre,
        conv_pre,
        n3,
        g3,
        depth,
        x2,
        n4,
        inv,
        q_turned,
        kv_own,
        load_sem,
        out_sem,
        ws_send,
        ws_recv,
        edge_send,
        edge_recv,
        row_send,
        row_recv,
        q_send,
        q_recv,
        kv_send,
        kv_recv,
    ) = refs
    own, core = place()
    parts = count // heads
    head, part = own // parts, lax.rem(own, parts)
    rows = tok_ref.shape[0]
    ext = rows + 2 * EDGE
    mid = slice(EDGE, EDGE + rows)
    sibling = (own, 1 - core)
    peers = others_of(own, core, count)

    loads, column = [], 0
    stage_at = []
    for number, first, width, blocks, _ in WEIGHT_COLUMNS:
        stage_at.append(column)
        for block in range(blocks):
            source = weights[number]
            if blocks == 3:
                source = source.at[block]
            elif blocks > 1:
                source = source.at[pl.ds(block * BLOCK, BLOCK), :]
            loads.append(
                move(
                    source,
                    staged.at[:, pl.ds(column, width)],
                    load_sem.at[len(loads)],
                )
            )
            column += width
    small_own[...] = jnp.zeros_like(small_own)
    for (row, tall, size), vector_ref in zip(VECTORS, vectors):
        small_own[row : row + tall, :size] = vector_ref[...]
    turned_segments(seg_col, 0, seg_row_ref[...])
    greet([sibling] + peers)

    copies = []
    right, left = (lax.rem(own + 1, count), core), (lax.rem(own + count - 1, count), core)
    edge_copies = [
        push(tok_ref.at[pl.ds(rows - EDGE, EDGE), :], edges.at[0], (edge_send, edge_recv), 0, right),
        push(tok_ref.at[pl.ds(0, EDGE), :], edges.at[1], (edge_send, edge_recv), 1, left),
        push(seg_col.at[pl.ds(rows - EDGE, EDGE), :], seg_edges.at[0], (edge_send, edge_recv), 2, right),
        push(seg_col.at[pl.ds(0, EDGE), :], seg_edges.at[1], (edge_send, edge_recv), 3, left),
    ]
    small_copy = push(small_own, small_out.at[core], (ws_send, ws_recv), len(WEIGHT_COLUMNS), sibling)
    small_out[core] = small_own[...]

    at, weight_copies = 0, []
    for (number, first, width, blocks, is_early), column in zip(WEIGHT_COLUMNS, stage_at):
        target = early if is_early else late
        for _ in range(blocks):
            loads[at].wait()
            at += 1
        size = width * blocks
        mine = pl.ds(bound(core * BLOCK, BLOCK), BLOCK)

        @pl.loop(0, BLOCK // ROW_BLOCK)
        def _(step):
            source = staged[span(step, ROW_BLOCK), pl.ds(column, size)]
            goes = pl.ds(bound(core * BLOCK + step * ROW_BLOCK, ROW_BLOCK), ROW_BLOCK)
            target[goes, pl.ds(first, size)] = source.astype(BF16)

        piece = target.at[mine, pl.ds(first, size)]
        weight_copies.append(push(piece, piece, (ws_send, ws_recv), number, sibling))

    for copy in edge_copies:
        copy.wait()
    small_copy.wait()
    row_copies = [
        push(seg_row_ref, seg_all.at[own], (row_send, row_recv), gap, peer)
        for gap, peer in enumerate(peers)
    ]
    seg_all[own] = seg_row_ref[...]
    widened(small, small_out)

    x_ext[:EDGE, :] = edges[0].astype(F32)
    x_ext[mid, :] = tok_ref[...].astype(F32)
    x_ext[EDGE + rows :, :] = edges[1].astype(F32)
    seg_ext[:EDGE, :] = jnp.where(own == 0, -1.0, seg_edges[0])
    seg_ext[mid, :] = seg_col[...]
    seg_ext[EDGE + rows :, :] = jnp.where(own == count - 1, -1.0, seg_edges[1])
    tap_masks(masks, seg_ext)

    normed, inv_std = norm_fwd(x_ext[...])
    n1[...] = normed[mid, :]
    inv[0] = jnp.broadcast_to(inv_std, (ext, LANES))
    low_ext[...] = (normed * vector(small, LN1G, D) + vector(small, LN1B, D)).astype(BF16)

    weight_copies[0].wait()
    glu_bias = vector(small, GLUB, 2 * D)
    for step in range(2 * D // 512):
        cols = slice(512 * step, 512 * (step + 1))
        glu_pre[:, cols] = (
            matmul(low_ext[...], late[:, GLU + 512 * step : GLU + 512 * (step + 1)])
            + glu_bias[:, cols]
        )
    state = x_ext[...] + glu_pre[:, :D] * jax.nn.sigmoid(glu_pre[:, D:])
    x1[...] = state[mid, :]
    normed, inv_std = norm_fwd(state)
    n2[...] = normed[mid, :]
    inv[1] = jnp.broadcast_to(inv_std, (ext, LANES))
    low_f = (normed * vector(small, LN2G, D) + vector(small, LN2B, D)).astype(BF16).astype(F32)
    before = pltpu.roll(low_f, 1, 0) * jnp.concatenate([masks[REACH - 1]] * (D // LANES), axis=1)
    after = pltpu.roll(low_f, ext - 1, 0) * jnp.concatenate([masks[REACH + 1]] * (D // LANES), axis=1)
    shifted[0] = before.astype(BF16)
    shifted[1] = low_f.astype(BF16)
    shifted[2] = after.astype(BF16)

    weight_copies[1].wait()

    @pl.loop(0, FF // 512)
    def _(step):
        weight = late[:, pl.ds(bound(LEFT + step * 512, 512), 512)]
        left_pre[:, span(step, 512)] = matmul(shifted[1], weight)

    weight_copies[2].wait()
    conv_sum = vector(small, CONVB, HALF)
    for tap in range(3):
        conv_sum = conv_sum + matmul(
            shifted[tap], late[:, CONV + HALF * tap : CONV + HALF * (tap + 1)]
        )
    conv_pre[...] = conv_sum

    left_bias = vector(small, LEFTB, FF)
    gain, shift = vector(small, LN3G, FF), vector(small, LN3B, FF)

    @pl.loop(0, ext // ROW_BLOCK)
    def _(step):
        here = span(step, ROW_BLOCK)
        pre = left_pre[here, :] + left_bias
        left_pre[here, :] = pre
        mixed = jax.nn.silu(pre)
        mixed = jnp.concatenate(
            [mixed[:, :HALF] + jax.nn.silu(conv_pre[here, :]), mixed[:, HALF:]], axis=1
        )
        normed, inv_std = norm_fwd(mixed)
        n3[here, :] = normed
        inv[2, here, :] = jnp.broadcast_to(inv_std, (ROW_BLOCK, LANES))
        g3[here, :] = (normed * gain + shift).astype(BF16).astype(F32)

    saves = [
        move(n1, n1_out, out_sem.at[0]),
        move(glu_pre.at[pl.ds(EDGE, rows), :], glu_out, out_sem.at[1]),
        move(n2, n2_out, out_sem.at[2]),
        move(left_pre.at[pl.ds(EDGE, rows), :], left_out, out_sem.at[3]),
        move(conv_pre, conv_out, out_sem.at[4]),
        move(n3, n3_out, out_sem.at[5]),
    ]

    @pl.loop(0, FF // LANES)
    def _(step):
        cols = span(step, LANES)
        block = g3[:, cols]
        total = jnp.zeros((rows, LANES), F32)
        for tap in range(TAPS):
            row = DEPTH + tap
            moved = pltpu.roll(block, (REACH - tap) % ext, 0)[mid, :]
            half = FF // 2 // LANES
            taps = small[step // half, row : row + 1, span(lax.rem(step, half), LANES)]
            total = total + moved * masks[tap, mid, :] * taps
        depth[:, cols] = total.astype(BF16)

    saves.append(move(depth, depth_out, out_sem.at[6]))
    weight_copies[3].wait()
    sep = vector(small, POINTB, HALF)
    for side in range(2):
        for block in range(4):
            first = side * (FF // 2) + block * BLOCK
            sep = sep + matmul(
                depth[:, first : first + BLOCK],
                late[side * BLOCK : (side + 1) * BLOCK, POINT + HALF * block : POINT + HALF * (block + 1)],
            )
    state = jnp.concatenate([x1[:, :HALF] + sep, x1[:, HALF:]], axis=1)
    x2[...] = state
    normed, inv_std = norm_fwd(state)
    n4[...] = normed
    inv[3, :rows, :] = jnp.broadcast_to(inv_std, (rows, LANES))
    low = (normed * vector(small, LN4G, D) + vector(small, LN4B, D)).astype(BF16)
    weight_copies[4].wait()
    for step in range(D // 256):
        cols = slice(256 * step, 256 * (step + 1))
        query = matmul(low, late[:, QKV + 256 * step : QKV + 256 * (step + 1)])
        q_turned[cols, :] = turn(query)
    near = lax.broadcasted_iota(jnp.int32, (rows, LANES), 1) < HEAD_DIM
    for step in range(D // LANES):
        first = QKV + D + LANES * step
        keys = matmul(low, late[:, first : first + LANES])
        values = matmul(low, late[:, first + D : first + D + LANES])
        kv_own[:, 2 * step * LANES : (2 * step + 1) * LANES] = jnp.where(
            near, keys, pltpu.roll(values, HEAD_DIM, 1)
        ).astype(BF16)
        kv_own[:, (2 * step + 1) * LANES : (2 * step + 2) * LANES] = jnp.where(
            near, pltpu.roll(keys, HEAD_DIM, 1), values
        ).astype(BF16)

    q_slot = q_out.at[:, span(head, rows)]
    kv_slot = kv_out.at[span(own, rows), :]
    for gap, (peer, _) in enumerate(peers):
        copies.append(
            push(kv_own.at[:, span(peer // parts, LANES)], kv_slot, (kv_send, kv_recv), gap, (peer, core))
        )
    for gap in range(1, heads):
        other = lax.rem(head + gap, heads)
        copies.append(
            push(q_turned.at[span(other, HEAD_DIM), :], q_slot, (q_send, q_recv), gap - 1, (other * parts + part, core))
        )
    saves.append(move(q_turned.at[span(head, HEAD_DIM), :], q_slot, out_sem.at[7]))
    saves.append(move(kv_own.at[:, span(head, LANES)], kv_slot, out_sem.at[8]))
    saves.append(move(n4, n4_out, out_sem.at[9]))
    saves.append(move(x2, x2_out, out_sem.at[10]))
    saves.append(move(inv, inv_out, out_sem.at[11]))
    saves.append(move(masks, masks_out, out_sem.at[14]))
    for copy in weight_copies[5:]:
        copy.wait()
    saves.append(move(late, late_out, out_sem.at[12]))
    saves.append(move(early, early_out, out_sem.at[13]))

    for copy in row_copies:
        copy.wait()
    lane = lax.broadcasted_iota(jnp.int32, (1, LANES), 1)
    every = seg_all[:, 0, :]
    for tile in range(heads):
        source = tile * parts + part
        mine = seg_all[source]
        first = jnp.min(mine, axis=1, keepdims=True)
        last = jnp.max(mine, axis=1, keepdims=True)
        below = jnp.sum(jnp.sum((every < first).astype(F32), axis=0, keepdims=True), axis=1, keepdims=True).astype(jnp.int32)
        upto = jnp.sum(jnp.sum((every <= last).astype(F32), axis=0, keepdims=True), axis=1, keepdims=True).astype(jnp.int32)
        plan_out[tile : tile + 1, :] = jnp.where(
            lane == 0, below, jnp.where(lane == 1, upto, source)
        )
    for copy in copies + saves:
        copy.wait()


def first_kernel(tokens, seg_row, vectors, weights, count, heads):
    rows = tokens.shape[0]
    ext = rows + 2 * EDGE
    late = (2 * BLOCK, SMALL)
    early = (2 * BLOCK, EARLY)
    out_shape = (
        shaped(late, BF16),
        shaped(early, BF16),
        shaped((2, SMALL_ROWS, SMALL_WIDTH)),
        shaped((count, 1, rows), jnp.int32),
        shaped((heads, LANES), jnp.int32),
        shaped((HEAD_DIM, heads * rows), BF16),
        shaped((count * rows, LANES), BF16),
        shaped((rows, D)),
        shaped((rows, 2 * D)),
        shaped((rows, D)),
        shaped((rows, FF)),
        shaped((ext, HALF)),
        shaped((ext, FF)),
        shaped((rows, FF), BF16),
        shaped((rows, D)),
        shaped((rows, D)),
        shaped((4, ext, LANES)),
        shaped((TAPS, ext, LANES)),
    )
    out_specs = (
        [any_spec()] * 2 + [vmem_spec()] * 3 + [any_spec()] * 13
    )
    scratch = [
        pltpu.VMEM((BLOCK, SMALL + EARLY), F32),
        pltpu.VMEM(late, BF16),
        pltpu.VMEM(early, BF16),
        pltpu.VMEM((2, EDGE, D), BF16),
        pltpu.VMEM((2, EDGE, LANES), F32),
        pltpu.VMEM((rows, LANES), F32),
        pltpu.VMEM((SMALL_ROWS, SMALL_WIDTH), F32),
        pltpu.VMEM((ext, D), F32),
        pltpu.VMEM((ext, LANES), F32),
        pltpu.VMEM((TAPS, ext, LANES), F32),
        pltpu.VMEM((2, SMALL_ROWS, SMALL_WIDTH), F32),
        pltpu.VMEM((ext, D), BF16),
        pltpu.VMEM((rows, D), F32),
        pltpu.VMEM((ext, 2 * D), F32),
        pltpu.VMEM((rows, D), F32),
        pltpu.VMEM((rows, D), F32),
        pltpu.VMEM((3, ext, D), BF16),
        pltpu.VMEM((ext, FF), F32),
        pltpu.VMEM((ext, HALF), F32),
        pltpu.VMEM((ext, FF), F32),
        pltpu.VMEM((ext, FF), F32),
        pltpu.VMEM((rows, FF), BF16),
        pltpu.VMEM((rows, D), F32),
        pltpu.VMEM((rows, D), F32),
        pltpu.VMEM((4, ext, LANES), F32),
        pltpu.VMEM((D, rows), BF16),
        pltpu.VMEM((rows, 2 * D), BF16),
        pltpu.SemaphoreType.DMA((sum(item[3] for item in WEIGHT_COLUMNS),)),
        pltpu.SemaphoreType.DMA((15,)),
    ]
    scratch += sem_pair(len(WEIGHT_COLUMNS) + 1) + sem_pair(4) + sem_pair(count - 1)
    scratch += sem_pair(heads - 1) + sem_pair(count - 1)
    return pl.pallas_call(
        functools.partial(first_body, count, heads),
        out_shape=out_shape,
        in_specs=[vmem_spec()] * (2 + len(vectors)) + [any_spec()] * 8,
        out_specs=out_specs,
        scratch_shapes=scratch,
        compiler_params=comm_params(1),
        name="first_layers",
    )(tokens, seg_row, *vectors, *weights)


def turn_keys(kv_ref, turned):
    @pl.loop(0, kv_ref.shape[0] // KEY_TILE)
    def _(tile):
        here = span(tile, KEY_TILE)
        turned[:, here] = turn(kv_ref[here, :])


def key_segments(seg_ref, segk):
    count, _, rows = seg_ref.shape

    @pl.loop(0, count)
    def _(source):
        turned_segments(segk, source * rows, seg_ref[source])


def masked(scores, segk, here, seg_q):
    seg_k = jnp.concatenate([segk[here, :]] * (scores.shape[1] // LANES), axis=1)
    return jnp.where(seg_k == seg_q, scores, MASK_FILL)


def key_tiles(plan_ref, tile):
    return plan_ref[tile, 0] // KEY_TILE, (plan_ref[tile, 1] + KEY_TILE - 1) // KEY_TILE


def attend_body(rows, plan_ref, q_ref, kv_ref, seg_ref, o_ref, low_ref, lse_ref, turned, segk):
    turn_keys(kv_ref, turned)
    key_segments(seg_ref, segk)

    @pl.loop(0, q_ref.shape[1] // rows)
    def _(tile):
        at = span(tile, rows)
        q = q_ref[:, at] * jnp.bfloat16(HEAD_DIM**-0.5)
        q_pad = jnp.concatenate([q, jnp.zeros_like(q)], axis=0)
        seg_q = seg_ref[plan_ref[tile, 2]].astype(F32)

        def block(key_tile, carry):
            top, total, acc = carry
            here = span(key_tile, KEY_TILE)
            scores = masked(matmul(kv_ref[here, :], q_pad), segk, here, seg_q)
            new_top = jnp.maximum(top, jnp.max(scores, axis=0, keepdims=True))
            probs = jnp.exp(scores - new_top)
            shrink = jnp.exp(top - new_top)
            total = total * shrink + jnp.sum(probs, axis=0, keepdims=True)
            acc = acc * shrink + matmul(turned[HEAD_DIM:, here], probs.astype(BF16))
            return (new_top, total, acc)

        first, end = key_tiles(plan_ref, tile)
        top, total, acc = lax.fori_loop(
            first,
            end,
            block,
            (
                jnp.full((1, rows), MASK_FILL, F32),
                jnp.zeros((1, rows), F32),
                jnp.zeros((HEAD_DIM, rows), F32),
            ),
        )
        out = acc / total
        o_ref[:, at] = out
        low_ref[:, at] = out.astype(BF16)
        lse_ref[:, at] = top + jnp.log(total)


def attend(plan, q_t, kv, seg, rows):
    return pl.pallas_call(
        functools.partial(attend_body, rows),
        out_shape=(shaped(q_t.shape), shaped(q_t.shape, BF16), shaped((1, q_t.shape[1]))),
        in_specs=[smem_spec()] + [vmem_spec()] * 3,
        out_specs=(vmem_spec(),) * 3,
        scratch_shapes=[pltpu.VMEM(kv.shape[::-1], BF16), pltpu.VMEM(kv.shape, F32)],
        compiler_params=pltpu.CompilerParams(vmem_limit_bytes=VMEM_MOST),
        name="attend",
    )(plan, q_t, kv, seg)


def attend_back_body(
    rows, plan_ref, q_ref, do_ref, o_ref, lse_ref, kv_ref, seg_ref, dq_ref, dkv_ref, turned, segk, dkv_acc
):
    turn_keys(kv_ref, turned)
    key_segments(seg_ref, segk)
    dkv_acc[...] = jnp.zeros_like(dkv_acc)
    scale = HEAD_DIM**-0.5

    @pl.loop(0, q_ref.shape[1] // rows)
    def _(tile):
        at = span(tile, rows)
        q = q_ref[:, at] * jnp.bfloat16(scale)
        do = do_ref[:, at]
        none = jnp.zeros_like(q)
        both = jnp.concatenate(
            [jnp.concatenate([q, none], axis=1), jnp.concatenate([none, do], axis=1)], axis=0
        )
        delta = jnp.sum(o_ref[:, at] * do.astype(F32), axis=0, keepdims=True)
        lse = lse_ref[:, at]
        seg_q = seg_ref[plan_ref[tile, 2]].astype(F32)

        def block(key_tile, dq):
            here = span(key_tile, KEY_TILE)
            pair = matmul(kv_ref[here, :], both)
            probs = jnp.exp(masked(pair[:, :rows], segk, here, seg_q) - lse)
            score_grad = (probs * (pair[:, rows:] - delta)).astype(BF16)
            joined = jnp.concatenate([score_grad, probs.astype(BF16)], axis=1)
            dkv_acc[here, :] += back_mul(joined, both)
            return dq + matmul(turned[:HEAD_DIM, here], score_grad)

        first, end = key_tiles(plan_ref, tile)
        dq = lax.fori_loop(first, end, block, jnp.zeros((HEAD_DIM, rows), F32))
        dq_ref[:, at] = (dq * scale).astype(BF16)

    dkv_ref[...] = dkv_acc[...].astype(BF16)


def attend_back(plan, q_t, do_t, o_t, lse, kv, seg, rows):
    return pl.pallas_call(
        functools.partial(attend_back_body, rows),
        out_shape=(shaped(q_t.shape, BF16), shaped(kv.shape, BF16)),
        in_specs=[smem_spec()] + [vmem_spec()] * 6,
        out_specs=(vmem_spec(),) * 2,
        scratch_shapes=[
            pltpu.VMEM(kv.shape[::-1], BF16),
            pltpu.VMEM(kv.shape, F32),
            pltpu.VMEM(kv.shape, F32),
        ],
        compiler_params=pltpu.CompilerParams(vmem_limit_bytes=VMEM_MOST),
        name="attend_back",
    )(plan, q_t, do_t, o_t, lse, kv, seg)


def middle_body(
    count,
    heads,
    o_in,
    out_grad,
    small_in,
    x2_in,
    early_in,
    out_ref,
    small_grads,
    dx3_out,
    grads_out,
    do_out,
    weights,
    x2,
    small,
    o_t,
    x3,
    expand_pre,
    hidden,
    dpre,
    do_t,
    grads,
    dx3,
    load_sem,
    o_send,
    o_recv,
    do_send,
    do_recv,
):
    own, core = place()
    parts = count // heads
    head, part = own // parts, lax.rem(own, parts)
    rows = out_grad.shape[0]
    loads = [move(early_in, weights, load_sem.at[0]), move(x2_in, x2, load_sem.at[1])]
    near = [lax.rem(head + gap, heads) for gap in range(1, heads)]
    peers = [(other * parts + part, core) for other in near]
    greet(peers)
    copies = [
        push(o_in.at[:, span(other, rows)], o_t.at[span(head, HEAD_DIM), :], (o_send, o_recv), gap, peer)
        for gap, (other, peer) in enumerate(zip(near, peers))
    ]
    copies.append(move(o_in.at[:, span(head, rows)], o_t.at[span(head, HEAD_DIM), :], load_sem.at[2]))
    widened(small, small_in)
    small_grads[...] = jnp.zeros_like(small_grads)
    for copy in copies + loads:
        copy.wait()

    state = (
        x2[...]
        + matmul(turn(o_t[...]), weights[:, ATTN : ATTN + D])
        + vector(small, ATTNB, D)
    )
    x3[...] = state
    normed, inv_std = norm_fwd(state)
    gain = vector(small, LN5G, D)
    low = (normed * gain + vector(small, LN5B, D)).astype(BF16)
    expand_bias = vector(small, EXPANDB, FF)
    for step in range(FF // 512):
        cols = slice(512 * step, 512 * (step + 1))
        pre = matmul(low, weights[:, EXPAND + 512 * step : EXPAND + 512 * (step + 1)]) + expand_bias[:, cols]
        expand_pre[:, cols] = pre
        hidden[:, cols] = jax.nn.silu(pre).astype(BF16)
    state = x3[...] + vector(small, SHRINKB, D)
    for block in range(FF // BLOCK):
        side, column = block // 4, SHRINK + D * (block % 4)
        state = state + matmul(
            hidden[:, block * BLOCK : (block + 1) * BLOCK],
            weights[side * BLOCK : (side + 1) * BLOCK, column : column + D],
        )
    out_ref[...] = state.astype(BF16)

    dz = out_grad[...]
    for block in range(FF // BLOCK):
        side, column = block // 4, SHRINK + D * (block % 4)
        cols = slice(block * BLOCK, (block + 1) * BLOCK)
        grad = back_mul(dz, weights[side * BLOCK : (side + 1) * BLOCK, column : column + D])
        dpre[:, cols] = (grad * smooth_slope(expand_pre[:, cols])).astype(BF16)
    grad = jnp.concatenate(
        [
            back_mul(dpre[...], weights[side * BLOCK : (side + 1) * BLOCK, EXPAND : EXPAND + FF])
            for side in range(2)
        ],
        axis=1,
    )
    state = dz.astype(F32) + norm_back(grad, normed, inv_std, gain)
    dx3[...] = state
    dy3 = state.astype(BF16)
    do_t[...] = back_mul(weights[:, ATTN : ATTN + D], dy3).astype(BF16)
    slot = do_out.at[:, span(head, rows)]
    copies = [
        push(do_t.at[span(other, HEAD_DIM), :], slot, (do_send, do_recv), gap, peer)
        for gap, (other, peer) in enumerate(zip(near, peers))
    ]
    copies.append(move(do_t.at[span(head, HEAD_DIM), :], slot, load_sem.at[0]))
    copies.append(move(dx3, dx3_out, load_sem.at[1]))

    put_vector(small_grads, LN5G, col_sum(grad * normed))
    put_vector(small_grads, LN5B, col_sum(grad))
    put_vector(small_grads, ATTNB, col_sum(dy3))
    put_vector(small_grads, EXPANDB, col_sum(dpre[...]))
    put_vector(small_grads, SHRINKB, col_sum(dz))
    grads[:, ATTN : ATTN + D] = matmul(o_t[...], dy3).astype(BF16)
    low_t = turn(low)
    for step in range(FF // 512):
        grads[:, EXPAND + 512 * step : EXPAND + 512 * (step + 1)] = matmul(
            low_t, dpre[:, 512 * step : 512 * (step + 1)]
        ).astype(BF16)
    for block in range(FF // BLOCK):
        side, column = block // 4, SHRINK + D * (block % 4)
        grads[side * BLOCK : (side + 1) * BLOCK, column : column + D] = matmul(
            turn(hidden[:, block * BLOCK : (block + 1) * BLOCK]), dz
        ).astype(BF16)
    copies.append(move(grads, grads_out, load_sem.at[2]))
    for copy in copies:
        copy.wait()


def middle_kernel(o_low, out_grad, small, x2, early, count, heads):
    rows = out_grad.shape[0]
    return pl.pallas_call(
        functools.partial(middle_body, count, heads),
        out_shape=(
            shaped((rows, D), BF16),
            shaped((2, SMALL_ROWS, SMALL_WIDTH)),
            shaped((rows, D)),
            shaped(early.shape, BF16),
            shaped((HEAD_DIM, heads * rows), BF16),
        ),
        in_specs=[vmem_spec()] * 3 + [any_spec()] * 2,
        out_specs=[vmem_spec()] * 2 + [any_spec()] * 3,
        scratch_shapes=[
            pltpu.VMEM(early.shape, BF16),
            pltpu.VMEM((rows, D), F32),
            pltpu.VMEM((2, SMALL_ROWS, SMALL_WIDTH), F32),
            pltpu.VMEM((D, rows), BF16),
            pltpu.VMEM((rows, D), F32),
            pltpu.VMEM((rows, FF), F32),
            pltpu.VMEM((rows, FF), BF16),
            pltpu.VMEM((rows, FF), BF16),
            pltpu.VMEM((D, rows), BF16),
            pltpu.VMEM(early.shape, BF16),
            pltpu.VMEM((rows, D), F32),
            pltpu.SemaphoreType.DMA((3,)),
        ]
        + sem_pair(heads - 1)
        + sem_pair(heads - 1),
        compiler_params=comm_params(2),
        name="middle_layers",
    )(o_low, out_grad, small, x2, early)


def column_groups(first, width, bits):
    tiles = width // LANES
    unit = 2 ** max(0, bits - 4)
    long = max(1, round(tiles * 0.36 / unit)) * unit
    orders = [
        list(range(bits)),
        [1, 0] + list(range(2, bits)),
        list(range(2, bits)) + [0, 1],
    ]
    groups = []
    for size, order in zip([long, long, tiles - 2 * long], orders):
        groups.append((first, size * LANES, order))
        first += size * LANES
    return groups


def grad_sets(bits):
    bounds = [LATE, QKV, LEFT, CONV]
    widths = [EARLY, LEFT - QKV, CONV - LEFT, LATE - CONV]
    return [column_groups(first, width, bits) for first, width in zip(bounds, widths)]


class Piece:
    def __init__(self, at, group, links, sums, got, total, sems):
        self.at, (self.first, self.width, self.order) = at, group
        self.core, self.sibling, self.bit_of, self.partner = links
        self.view, self.got, self.total, self.sems = sums, got, total, sems
        self.bits, self.phase, self.trail = len(self.order), 0, []
        self.copy = None

    def whole(self):
        return (0, BLOCK, self.first, self.width)

    def out(self, where):
        row, tall, col, wide = where
        return self.total.at[pl.ds(bound(row, ROW_BLOCK), tall), pl.ds(bound(col, LANES), wide)]

    def start(self, other_half):
        self.copy = push(other_half, self.out(self.whole()), self.sems[0], self.at, self.sibling)

    def add(self, where, source, spot, last):
        row, tall, col, wide = where

        @pl.loop(0, tall // ROW_BLOCK)
        def _(step):
            gap = step * ROW_BLOCK
            here = (row + gap, ROW_BLOCK, col, wide)
            there = source.at[pl.ds(bound(spot + gap, ROW_BLOCK), ROW_BLOCK), pl.ds(self.first, wide)]
            mine = self.view(here)[...].astype(F32)
            added = (mine + there[...].astype(F32)).astype(BF16)
            if last:
                self.out(here)[...] = added
            else:
                self.view(here)[...] = added

    def halve(self, step):
        row, tall, col, wide = self.where
        bit = self.order[step]
        mine = self.bit_of[bit]
        if tall > ROW_BLOCK:
            half = tall // 2
            kept = (row + half * mine, half, col, wide)
            sent = (row + half * (1 - mine), half, col, wide)
        else:
            half = wide // 2
            kept = (row, tall, col + half * mine, half)
            sent = (row, tall, col + half * (1 - mine), half)
        self.copy = push(
            self.view(sent),
            self.got.at[pl.ds(self.spot, sent[1]), pl.ds(self.first, sent[3])],
            self.sems[1],
            self.at * self.bits + step,
            self.partner[bit],
        )
        self.where = kept

    def double(self, step):
        place_out = self.out(self.trail[step])
        self.copy = push(
            place_out,
            place_out,
            self.sems[2],
            self.at * self.bits + step,
            self.partner[self.order[step]],
        )

    def done(self):
        return self.phase > 2 * self.bits

    def advance(self):
        if self.done():
            return
        self.copy.wait()
        if self.phase == 0:
            self.where, self.spot = self.whole(), 0
            self.add(self.where, self.total, 0, False)
            self.halve(0)
        elif self.phase <= self.bits:
            last = self.phase == self.bits
            self.add(self.where, self.got, self.spot, last)
            self.trail.append(self.where)
            self.spot += self.where[1]
            if last:
                self.double(self.bits - 1)
            else:
                self.halve(self.phase)
        elif self.phase < 2 * self.bits:
            self.double(2 * self.bits - 1 - self.phase)
        self.phase += 1


def last_body(count, heads, dq_in, dkv_in, small_in, small_grads_in, *refs):
    (
        early_grads,
        dx3_in,
        late_in,
        n1_in,
        glu_in,
        n2_in,
        left_in,
        conv_in,
        n3_in,
        depth_in,
        n4_in,
        inv_in,
        masks_in,
        total,
        grad_out,
        weights,
        dx3,
        n1,
        glu_pre,
        n2,
        left_pre,
        conv_pre,
        n3,
        depth,
        n4,
        inv,
        masks,
        small,
        small_grads,
        dq_t,
        dkv_parts,
        dqkv,
        sep_own,
        sep_edges,
        sep_ext,
        depth_grad,
        g3_grad,
        row_sums,
        dleft,
        conv_grad,
        conv_taps,
        grads,
        early_own,
        got,
        result,
        load_sem,
        keep_sem,
        dq_send,
        dq_recv,
        dkv_send,
        dkv_recv,
        edge_send,
        edge_recv,
        ws_send,
        ws_recv,
        rs_send,
        rs_recv,
        ag_send,
        ag_recv,
    ) = refs
    own, core = place()
    parts = count // heads
    head, part = own // parts, lax.rem(own, parts)
    rows = dx3.shape[0]
    ext = rows + 2 * EDGE
    mid = slice(EDGE, EDGE + rows)
    sibling = (own, 1 - core)
    peers = others_of(own, core, count)
    bits = count.bit_length() - 1

    sources = (dx3_in, late_in, n4_in, inv_in, depth_in, masks_in, n3_in, left_in, conv_in, n2_in, glu_in, n1_in)
    targets = (dx3, weights, n4, inv, depth, masks, n3, left_pre, conv_pre, n2, glu_pre, n1)
    loads = [move(a, b, load_sem.at[at]) for at, (a, b) in enumerate(zip(sources, targets))]
    greet([sibling] + peers)

    bit_of = [lax.rem(own // 2**bit, 2) for bit in range(bits)]
    partner = [(own + 2**bit - 2 * 2**bit * bit_of[bit], core) for bit in range(bits)]
    links = (core, sibling, bit_of, partner)
    sems = ((ws_send, ws_recv), (rs_send, rs_recv), (ag_send, ag_recv))

    def early_view(where):
        row, tall, col, wide = where
        return early_own.at[pl.ds(bound(row, ROW_BLOCK), tall), pl.ds(bound(col - LATE, LANES), wide)]

    def late_view(where):
        row, tall, col, wide = where
        return grads.at[pl.ds(bound(core * BLOCK + row, ROW_BLOCK), tall), pl.ds(bound(col, LANES), wide)]

    sets, at = [], 0
    for number, groups in enumerate(grad_sets(bits)):
        members = []
        for group in groups:
            view = late_view if number else early_view
            members.append(Piece(at, group, links, view, got, total, sems))
            at += 1
        sets.append(members)
    other_rows = pl.ds(bound((1 - core) * BLOCK, BLOCK), BLOCK)
    own_rows = pl.ds(bound(core * BLOCK, BLOCK), BLOCK)

    def start(members, source, shift):
        for piece in members:
            piece.start(source.at[other_rows, pl.ds(piece.first - shift, piece.width)])

    def advance(members):
        for piece in members:
            piece.advance()

    keep = move(early_grads.at[own_rows, :], early_own, keep_sem.at[2])
    start(sets[0], early_grads, LATE)
    slot = dq_t.at[span(head, HEAD_DIM), :]
    kv_slot = dkv_parts.at[part, :, span(head, LANES)]
    collect = []
    for gap, (peer, _) in enumerate(peers):
        collect.append(push(dkv_in.at[span(peer, rows), :], kv_slot, (dkv_send, dkv_recv), gap, (peer, core)))
    for gap in range(1, heads):
        other = lax.rem(head + gap, heads)
        collect.append(
            push(dq_in.at[:, span(other, rows)], slot, (dq_send, dq_recv), gap - 1, (other * parts + part, core))
        )
    collect.append(move(dq_in.at[:, span(head, rows)], slot, keep_sem.at[0]))
    collect.append(move(dkv_in.at[span(own, rows), :], kv_slot, keep_sem.at[1]))

    widened(small, small_in)
    small_grads[...] = small_grads_in[...]
    keep.wait()
    advance(sets[0])
    for copy in loads:
        copy.wait()
    advance(sets[0][:2])
    for copy in collect:
        copy.wait()
    advance(sets[0])

    dqkv[:, :D] = turn(dq_t[...])
    lane = lax.broadcasted_iota(jnp.int32, (rows, LANES), 1) < HEAD_DIM
    for step in range(D // LANES):
        pair = []
        for side in range(2):
            first = (2 * step + side) * LANES
            share = dkv_parts[0, :, first : first + LANES].astype(F32)
            for number in range(1, parts):
                share = share + dkv_parts[number, :, first : first + LANES].astype(F32)
            pair.append(share)
        cols = slice(D + step * LANES, D + (step + 1) * LANES)
        dqkv[:, cols] = jnp.where(lane, pair[0], pltpu.roll(pair[1], HEAD_DIM, 1)).astype(BF16)
        cols = slice(2 * D + step * LANES, 2 * D + (step + 1) * LANES)
        dqkv[:, cols] = jnp.where(lane, pltpu.roll(pair[0], HEAD_DIM, 1), pair[1]).astype(BF16)

    def through(grad, column, width):
        return jnp.concatenate(
            [
                back_mul(grad, weights[side * BLOCK : (side + 1) * BLOCK, column : column + width])
                for side in range(2)
            ],
            axis=1,
        )

    def norm_step(grad, normed, inv_std, row):
        put_vector(small_grads, row, col_sum(grad * normed))
        put_vector(small_grads, row + 1, col_sum(grad))
        return norm_back(grad, normed, inv_std, vector(small, row, D))

    grad = through(dqkv[...], QKV, 3 * D)
    dx2 = dx3[...] + norm_step(grad, n4[...], inv[3, :rows, :1], LN4G)
    dx3[...] = dx2
    sep_own[...] = dx2[:, :HALF].astype(BF16)
    right, left = (lax.rem(own + 1, count), core), (lax.rem(own + count - 1, count), core)
    edge_copies = [
        push(sep_own.at[pl.ds(rows - EDGE, EDGE), :], sep_edges.at[0], (edge_send, edge_recv), 0, right),
        push(sep_own.at[pl.ds(0, EDGE), :], sep_edges.at[1], (edge_send, edge_recv), 1, left),
    ]
    advance(sets[0])
    low_t = turn(n4[...] * vector(small, LN4G, D) + vector(small, LN4B, D))
    for step in range(3):
        grads[:, QKV + D * step : QKV + D * (step + 1)] = matmul(
            low_t, dqkv[:, D * step : D * (step + 1)]
        ).astype(BF16)
    for block in range(FF // BLOCK):
        side, column = block // 4, POINT + HALF * (block % 4)
        grads[side * BLOCK : (side + 1) * BLOCK, column : column + HALF] = matmul(
            turn(depth[:, block * BLOCK : (block + 1) * BLOCK]), sep_own[...]
        ).astype(BF16)
    put_vector(small_grads, POINTB, col_sum(sep_own[...]))
    start(sets[1], grads, 0)

    for copy in edge_copies:
        copy.wait()
    sep_ext[:EDGE, :] = sep_edges[0]
    sep_ext[mid, :] = sep_own[...]
    sep_ext[EDGE + rows :, :] = sep_edges[1]
    for block in range(FF // BLOCK):
        side, column = block // 4, POINT + HALF * (block % 4)
        depth_grad[:, block * BLOCK : (block + 1) * BLOCK] = (
            back_mul(sep_ext[...], weights[side * BLOCK : (side + 1) * BLOCK, column : column + HALF])
            .astype(BF16)
            .astype(F32)
        )
    advance(sets[0])
    advance(sets[1])

    row_sums[...] = jnp.zeros_like(row_sums)
    half = FF // 2 // LANES

    @pl.loop(0, FF // LANES)
    def _(step):
        cols = span(step, LANES)
        side, lanes = step // half, span(lax.rem(step, half), LANES)
        block = depth_grad[:, cols]
        normed = n3[:, cols]
        gain = small[side, LN3G : LN3G + 1, lanes]
        low = (normed[mid, :] * gain + small[side, LN3B : LN3B + 1, lanes]).astype(BF16).astype(F32)
        summed = jnp.zeros((ext, LANES), F32)
        for tap in range(TAPS):
            row = DEPTH + tap
            moved = pltpu.roll(block, (tap - REACH) % ext, 0) * masks[TAPS - 1 - tap]
            summed = summed + moved * small[side, row : row + 1, lanes]
            small_grads[side, row : row + 1, lanes] = col_sum(low * moved[mid, :])
        g3_grad[:, cols] = summed
        small_grads[side, LN3G : LN3G + 1, lanes] = col_sum(summed[mid, :] * normed[mid, :])
        small_grads[side, LN3B : LN3B + 1, lanes] = col_sum(summed[mid, :])
        scaled = summed * gain
        row_sums[0] = row_sums[0] + scaled
        row_sums[1] = row_sums[1] + scaled * normed

    advance(sets[0])
    inner = jnp.sum(row_sums[0], axis=1, keepdims=True) * (1.0 / FF)
    cross = jnp.sum(row_sums[1], axis=1, keepdims=True) * (1.0 / FF)
    row_sums[0] = jnp.broadcast_to(inner, (ext, LANES))
    row_sums[1] = jnp.broadcast_to(cross, (ext, LANES))

    @pl.loop(0, FF // LANES)
    def _(step):
        cols = span(step, LANES)
        side, lanes = step // half, span(lax.rem(step, half), LANES)
        scaled = g3_grad[mid, cols] * small[side, LN3G : LN3G + 1, lanes]
        mixed_grad = inv[2, mid, :] * (scaled - row_sums[0, mid, :] - n3[mid, cols] * row_sums[1, mid, :])
        low = (mixed_grad * smooth_slope(left_pre[:, cols])).astype(BF16)
        dleft[:, cols] = low
        small_grads[side, LEFTB : LEFTB + 1, lanes] = col_sum(low)

    for step in range(HALF // LANES):
        cols = slice(step * LANES, (step + 1) * LANES)
        scaled = g3_grad[:, cols] * small[0, LN3G : LN3G + 1, cols]
        mixed_grad = inv[2] * (scaled - row_sums[0] - n3[:, cols] * row_sums[1])
        low = (mixed_grad * smooth_slope(conv_pre[:, cols])).astype(BF16).astype(F32)
        conv_grad[:, cols] = low
        for tap in range(3):
            moved = pltpu.roll(low, (tap - 1) % ext, 0) * masks[REACH + 1 - tap]
            conv_taps[:, HALF * tap + step * LANES : HALF * tap + (step + 1) * LANES] = moved[mid, :].astype(BF16)
    put_vector(small_grads, CONVB, col_sum(conv_grad[mid, :]))

    low_t = turn(n2[...] * vector(small, LN2G, D) + vector(small, LN2B, D))
    for step in range(FF // 512):
        grads[:, LEFT + 512 * step : LEFT + 512 * (step + 1)] = matmul(
            low_t, dleft[:, 512 * step : 512 * (step + 1)]
        ).astype(BF16)
    start(sets[2], grads, 0)
    advance(sets[0])
    advance(sets[1])
    for tap in range(3):
        grads[:, CONV + HALF * tap : CONV + HALF * (tap + 1)] = matmul(
            low_t, conv_taps[:, HALF * tap : HALF * (tap + 1)]
        ).astype(BF16)
    grad = through(dleft[...], LEFT, FF) + through(conv_taps[...], CONV, 3 * HALF)
    dx1 = dx3[...] + norm_step(grad, n2[...], inv[1, mid, :1], LN2G)
    gate = jax.nn.sigmoid(glu_pre[:, D:])
    value_grad = dx1 * gate
    dglu = jnp.concatenate([value_grad, value_grad * glu_pre[:, :D] * (1.0 - gate)], axis=1).astype(BF16)
    put_vector(small_grads, GLUB, col_sum(dglu))
    advance(sets[2])
    low_t = turn(n1[...] * vector(small, LN1G, D) + vector(small, LN1B, D))
    for step in range(2):
        grads[:, GLU + D * step : GLU + D * (step + 1)] = matmul(
            low_t, dglu[:, D * step : D * (step + 1)]
        ).astype(BF16)
    grad = through(dglu, GLU, 2 * D)
    result[...] = dx1 + norm_step(grad, n1[...], inv[0, mid, :1], LN1G)
    keep = move(result, grad_out, keep_sem.at[0])
    for side in range(2):
        for block in range(SMALL_WIDTH // BLOCK):
            first = side * BLOCK + block * SMALL_ROWS
            grads[first : first + SMALL_ROWS, SMALL : SMALL + BLOCK] = small_grads[
                side, :, block * BLOCK : (block + 1) * BLOCK
            ].astype(BF16)
        first = side * BLOCK + SMALL_WIDTH // BLOCK * SMALL_ROWS
        grads[first : (side + 1) * BLOCK, SMALL : SMALL + BLOCK] = jnp.zeros(
            ((side + 1) * BLOCK - first, BLOCK), BF16
        )
    start(sets[3], grads, 0)
    while not all(piece.done() for members in sets for piece in members):
        for members in sets:
            advance(members)
    keep.wait()


def last_kernel(dq, dkv, small, small_grads, tensors, count, heads):
    rows = dkv.shape[0] // count
    ext = rows + 2 * EDGE
    bits = count.bit_length() - 1
    pieces = sum(len(groups) for groups in grad_sets(bits))
    early = tensors[0].shape
    scratch = [
        pltpu.VMEM(tensors[2].shape, BF16),
        pltpu.VMEM((rows, D), F32),
        pltpu.VMEM((rows, D), F32),
        pltpu.VMEM((rows, 2 * D), F32),
        pltpu.VMEM((rows, D), F32),
        pltpu.VMEM((rows, FF), F32),
        pltpu.VMEM((ext, HALF), F32),
        pltpu.VMEM((ext, FF), F32),
        pltpu.VMEM((rows, FF), BF16),
        pltpu.VMEM((rows, D), F32),
        pltpu.VMEM((4, ext, LANES), F32),
        pltpu.VMEM((TAPS, ext, LANES), F32),
        pltpu.VMEM((2, SMALL_ROWS, SMALL_WIDTH), F32),
        pltpu.VMEM((2, SMALL_ROWS, SMALL_WIDTH), F32),
        pltpu.VMEM((D, rows), BF16),
        pltpu.VMEM((count // heads, rows, 2 * D), BF16),
        pltpu.VMEM((rows, 3 * D), BF16),
        pltpu.VMEM((rows, HALF), BF16),
        pltpu.VMEM((2, EDGE, HALF), BF16),
        pltpu.VMEM((ext, HALF), BF16),
        pltpu.VMEM((ext, FF), F32),
        pltpu.VMEM((ext, FF), F32),
        pltpu.VMEM((2, ext, LANES), F32),
        pltpu.VMEM((rows, FF), BF16),
        pltpu.VMEM((ext, HALF), F32),
        pltpu.VMEM((rows, 3 * HALF), BF16),
        pltpu.VMEM((2 * BLOCK, LATE), BF16),
        pltpu.VMEM((BLOCK, EARLY), BF16),
        pltpu.VMEM((BLOCK + ROW_BLOCK * max(0, bits - 4), WIDTH), BF16),
        pltpu.VMEM((rows, D), F32),
        pltpu.SemaphoreType.DMA((12,)),
        pltpu.SemaphoreType.DMA((3,)),
    ]
    scratch += sem_pair(heads - 1) + sem_pair(count - 1) + sem_pair(2) + sem_pair(pieces)
    scratch += sem_pair(pieces * bits) + sem_pair(pieces * bits)
    return pl.pallas_call(
        functools.partial(last_body, count, heads),
        out_shape=(shaped((BLOCK, WIDTH), BF16), shaped((rows, D))),
        in_specs=[vmem_spec()] * 4 + [any_spec()] * len(tensors),
        out_specs=[vmem_spec(), any_spec()],
        scratch_shapes=scratch,
        compiler_params=comm_params(3),
        name="last_layers",
    )(dq, dkv, small, small_grads, *tensors)


def unpack_body(output_in, grad_in, packed_in, *refs):
    size = len(MATRICES) + len(VECTORS) + 2
    outs, (packed, *stages, load_sem, out_sem) = refs[:size], refs[size:]
    output_ref, grad_ref, *outs = outs
    order = [len(MATRICES)] + list(range(len(MATRICES)))
    bounds = [(first, width * blocks) for first, width, blocks in MATRICES] + [(SMALL, BLOCK)]
    loads = {}
    for at in order:
        cols = pl.ds(*bounds[at])
        loads[at] = move(packed_in.at[:, cols], packed.at[:, cols], load_sem.at[at])
    stores = [
        move(output_in, output_ref, out_sem.at[len(MATRICES)]),
        move(grad_in, grad_ref, out_sem.at[len(MATRICES) + 1]),
    ]
    for at, (first, width, blocks) in enumerate(MATRICES):
        loads[at].wait()
        stage = stages[at]
        for block in range(blocks):

            @pl.loop(0, BLOCK // ROW_BLOCK)
            def _(step):
                value = packed[span(step, ROW_BLOCK), first + block * width : first + (block + 1) * width].astype(F32)
                if blocks == 3:
                    stage[block, span(step, ROW_BLOCK), :] = value
                else:
                    stage[pl.ds(bound(block * BLOCK + step * ROW_BLOCK, ROW_BLOCK), ROW_BLOCK), :] = value

        stores.append(move(stage, outs[at], out_sem.at[at]))

    loads[len(MATRICES)].wait()
    small = jnp.concatenate(
        [
            packed[block * SMALL_ROWS : (block + 1) * SMALL_ROWS, SMALL : SMALL + BLOCK].astype(F32)
            for block in range(SMALL_WIDTH // BLOCK)
        ],
        axis=1,
    )
    for (row, tall, size), out in zip(VECTORS, outs[len(MATRICES) :]):
        out[...] = small[row : row + tall, :size]
    for copy in stores:
        copy.wait()


def unpack(output, grad, packed):
    shapes = []
    for _, width, blocks in MATRICES:
        shapes.append((3, BLOCK, width) if blocks == 3 else (blocks * BLOCK, width))
    vectors = [(tall, size) for _, tall, size in VECTORS]
    return pl.pallas_call(
        unpack_body,
        out_shape=(shaped(output.shape, output.dtype), shaped(grad.shape))
        + tuple(shaped(shape) for shape in shapes + vectors),
        in_specs=[vmem_spec()] * 2 + [any_spec()],
        out_specs=[any_spec()] * (2 + len(shapes)) + [vmem_spec()] * len(vectors),
        scratch_shapes=[pltpu.VMEM(packed.shape, packed.dtype)]
        + [pltpu.VMEM(shape, F32) for shape in shapes]
        + [pltpu.SemaphoreType.DMA((len(shapes) + 1,)), pltpu.SemaphoreType.DMA((len(shapes) + 2,))],
        compiler_params=pltpu.CompilerParams(vmem_limit_bytes=VMEM_MOST),
        name="unpack",
    )(output, grad, packed)


def body(tokens, segment_ids, out_grad, *params):
    (
        ln1g, ln1b, glu_w, glu_b, ln2g, ln2b, left_w, left_b, conv_w, conv_b, ln3g, ln3b, depth_w,
        point_w, point_b, ln4g, ln4b, qkv_w, attn_w, attn_b, ln5g, ln5b, expand_w, expand_b,
        shrink_w, shrink_b,
    ) = params
    count = lax.axis_size("ctx")
    heads = D // HEAD_DIM
    rows = tokens.shape[1]
    vectors = [
        ln1g, ln1b, glu_b, ln2g, ln2b, left_b, conv_b, ln3g, ln3b, depth_w,
        point_b, ln4g, ln4b, attn_b, ln5g, ln5b, expand_b, shrink_b,
    ]
    vectors = [value.reshape(-1, value.shape[-1]) for value in vectors]
    weights = (glu_w, left_w, conv_w, point_w, qkv_w, attn_w, expand_w, shrink_w)
    (
        late, early, small, seg, plan, q_head, kv_head, n1, glu_pre, n2, left_pre, conv_pre, n3,
        depth, n4, x2, inv, masks,
    ) = first_kernel(tokens[0], segment_ids, vectors, weights, count, heads)
    o_head, o_low, log_sum = attend(plan, q_head, kv_head, seg, rows)
    output, small_grads, dx3, early_grads, do_head = middle_kernel(
        o_low, out_grad[0], small, x2, early, count, heads
    )
    dq_head, dkv_head = attend_back(plan, q_head, do_head, o_head, log_sum, kv_head, seg, rows)
    tensors = (
        early_grads, dx3, late, n1, glu_pre, n2, left_pre, conv_pre, n3, depth, n4, inv, masks,
    )
    total, input_grad = last_kernel(dq_head, dkv_head, small, small_grads, tensors, count, heads)
    output, input_grad, *pieces = unpack(output, input_grad, total)
    matrices, lines = pieces[: len(MATRICES)], pieces[len(MATRICES) :]
    lines = [line if line.shape[0] > 1 else line.reshape(-1) for line in lines]
    g_glu, g_left, g_conv, g_point, g_qkv, g_attn, g_expand, g_shrink = matrices
    (
        g_ln1g, g_ln1b, g_glu_b, g_ln2g, g_ln2b, g_left_b, g_conv_b, g_ln3g, g_ln3b, g_depth,
        g_point_b, g_ln4g, g_ln4b, g_attn_b, g_ln5g, g_ln5b, g_expand_b, g_shrink_b,
    ) = lines
    return (
        output[None], input_grad[None], g_ln1g, g_ln1b, g_glu, g_glu_b, g_ln2g, g_ln2b, g_left,
        g_left_b, g_conv, g_conv_b, g_ln3g, g_ln3b, g_depth, g_point, g_point_b, g_ln4g, g_ln4b,
        g_qkv, g_attn, g_attn_b, g_ln5g, g_ln5b, g_expand, g_expand_b, g_shrink, g_shrink_b,
    )


def solution(mesh):
    return jax.shard_map(
        body,
        mesh=mesh,
        in_specs=(
            P("ws", "ctx", None),
            P("ws", "ctx"),
            P("ws", "ctx", None),
            P("ws"),
            P("ws"),
            P("ws", None),
            P("ws"),
            P("ws"),
            P("ws"),
            P("ws", None),
            P("ws"),
            P(None, "ws", None),
            P("ws"),
            P("ws"),
            P("ws"),
            P(None, "ws"),
            P("ws", None),
            P("ws"),
            P("ws"),
            P("ws"),
            P("ws", None),
            P("ws", None),
            P("ws"),
            P("ws"),
            P("ws"),
            P("ws", None),
            P("ws"),
            P("ws", None),
            P("ws"),
        ),
        out_specs=(
            P("ws", "ctx", None),
            P("ws", "ctx", None),
            P("ws"),
            P("ws"),
            P("ws", None),
            P("ws"),
            P("ws"),
            P("ws"),
            P("ws", None),
            P("ws"),
            P(None, "ws", None),
            P("ws"),
            P("ws"),
            P("ws"),
            P(None, "ws"),
            P("ws", None),
            P("ws"),
            P("ws"),
            P("ws"),
            P("ws", None),
            P("ws", None),
            P("ws"),
            P("ws"),
            P("ws"),
            P("ws", None),
            P("ws"),
            P("ws", None),
            P("ws"),
        ),
        check_vma=False,
    )
```

```python
import functools
import math

import jax
import jax.numpy as jnp
from jax import lax
from jax.experimental import pallas as pl
from jax.experimental.pallas import tpu as pltpu
from jax.sharding import PartitionSpec as P

MESH_ID = pl.DeviceIdType.MESH
F32 = jnp.float32
BF16 = jnp.bfloat16
HEAD_DIM = 64
NORM_EPS = 1e-06
MASK_FILL = -1e30
LANES = 128
ROW_BLOCK = 16
EDGE = 16
KEY_TILE = 1024
BLOCK = 256
VMEM_MOST = 60 * 1024 * 1024

D = 512
FF = 2048
HALF = 256
TAPS = 9
REACH = 4

QKV, POINT, LEFT, CONV, GLU, SMALL, LATE = 0, 1536, 2560, 4608, 5376, 6400, 6656
ATTN, EXPAND, SHRINK, EARLY = 0, 512, 2560, 4608
WIDTH = LATE + EARLY

SMALL_ROWS = 32
SMALL_WIDTH = 1024
(LN1G, LN1B, GLUB, LN2G, LN2B, LEFTB, CONVB, LN3G, LN3B, DEPTH) = range(10)
(POINTB, LN4G, LN4B, ATTNB, LN5G, LN5B, EXPANDB, SHRINKB) = range(DEPTH + TAPS, DEPTH + TAPS + 8)


VECTORS = [
    (LN1G, 1, 256),
    (LN1B, 1, 256),
    (GLUB, 1, 512),
    (LN2G, 1, 256),
    (LN2B, 1, 256),
    (LEFTB, 1, 1024),
    (CONVB, 1, 128),
    (LN3G, 1, 1024),
    (LN3B, 1, 1024),
    (DEPTH, TAPS, 1024),
    (POINTB, 1, 128),
    (LN4G, 1, 256),
    (LN4B, 1, 256),
    (ATTNB, 1, 256),
    (LN5G, 1, 256),
    (LN5B, 1, 256),
    (EXPANDB, 1, 1024),
    (SHRINKB, 1, 256),
]
MATRICES = [
    (GLU, 1024, 1),
    (LEFT, 2048, 1),
    (CONV, 256, 3),
    (POINT, 256, 4),
    (QKV, 1536, 1),
    (LATE + ATTN, 512, 1),
    (LATE + EXPAND, 2048, 1),
    (LATE + SHRINK, 512, 4),
]


def vmem_spec():
    return pl.BlockSpec(memory_space=pltpu.VMEM)


def any_spec():
    return pl.BlockSpec(memory_space=pl.ANY)


def smem_spec():
    return pl.BlockSpec(memory_space=pltpu.SMEM)


def shaped(shape, kind=F32):
    return jax.ShapeDtypeStruct(shape, kind)


def comm_params(number):
    return pltpu.CompilerParams(
        collective_id=number, has_side_effects=True, vmem_limit_bytes=VMEM_MOST
    )


def greet(peers):
    barrier = pltpu.get_barrier_semaphore()
    for peer in peers:
        pl.semaphore_signal(barrier, inc=1, device_id=peer, device_id_type=MESH_ID)
    pl.semaphore_wait(barrier, len(peers))


def push(src, dst, sems, at, peer):
    copy = pltpu.make_async_remote_copy(
        src_ref=src,
        dst_ref=dst,
        send_sem=sems[0].at[at],
        recv_sem=sems[1].at[at],
        device_id=peer,
        device_id_type=MESH_ID,
    )
    copy.start()
    return copy


def move(src, dst, sem):
    copy = pltpu.make_async_copy(src, dst, sem)
    copy.start()
    return copy


def sem_pair(count):
    return [pltpu.SemaphoreType.DMA((count,)), pltpu.SemaphoreType.DMA((count,))]


def bound(value, step):
    return value if isinstance(value, int) else pl.multiple_of(value, step)


def span(value, step):
    return pl.ds(bound(value * step, step), step)


def matmul(left_op, right_op):
    return jnp.dot(left_op, right_op, preferred_element_type=F32)


def back_mul(grad_in, weight):
    return lax.dot_general(grad_in, weight, (((1,), (1,)), ((), ())), preferred_element_type=F32)


def turn(block):
    return block.astype(F32).T.astype(BF16)


def col_sum(block):
    return jnp.sum(block.astype(F32), axis=0, keepdims=True)


def lane_mean(block):
    return jnp.mean(block, axis=-1, keepdims=True)


def smooth_slope(block):
    sigma = jax.nn.sigmoid(block)
    return sigma * (1.0 + block * (1.0 - sigma))


def norm_fwd(block):
    centred = block - lane_mean(block)
    inv_std = lax.rsqrt(lane_mean(centred * centred) + NORM_EPS)
    return centred * inv_std, inv_std


def norm_back(grad_in, normed, inv_std, gain):
    scaled = grad_in * gain
    inner, cross = lane_mean(scaled), lane_mean(scaled * normed)
    return inv_std * (scaled - inner - normed * cross)


def vector(small_ref, row, size):
    half = size // 2
    return jnp.concatenate(
        [small_ref[core, row : row + 1, :half] for core in range(2)], axis=1
    )


def put_vector(small_ref, row, value):
    half = value.shape[1] // 2
    for core in range(2):
        small_ref[core, row : row + 1, :half] = value[:, core * half : (core + 1) * half]


def place():
    own, core = lax.axis_index("ctx"), lax.axis_index("ws")
    return own, core


def others_of(own, core, count):
    return [(lax.rem(own + gap, count), core) for gap in range(1, count)]


def widened(dst_ref, src_ref):
    @pl.loop(0, 2)
    def _(core):
        dst_ref[core] = src_ref[core].astype(BF16).astype(F32)


def turned_segments(out_ref, first, row):
    for step in range(row.shape[1] // LANES):
        part = row[:, step * LANES : (step + 1) * LANES].astype(F32)
        here = pl.ds(bound(first + step * LANES, LANES), LANES)
        out_ref[here, :] = jnp.broadcast_to(part, (LANES, LANES)).T


WEIGHT_COLUMNS = [
    (0, GLU, 1024, 1, False),
    (1, LEFT, 2048, 1, False),
    (2, CONV, 256, 3, False),
    (3, POINT, 256, 4, False),
    (4, QKV, 1536, 1, False),
    (5, ATTN, 512, 1, True),
    (6, EXPAND, 2048, 1, True),
    (7, SHRINK, 512, 4, True),
]


def tap_masks(mask_ref, seg_ref):
    seg = seg_ref[...]
    for tap in range(TAPS):
        moved = pltpu.roll(seg, (REACH - tap) % seg.shape[0], 0)
        mask_ref[tap] = jnp.where(moved == seg, 1.0, 0.0).astype(F32)


def first_body(
    count,
    heads,
    tok_ref,
    seg_row_ref,
    *refs,
):
    vectors, refs = refs[: len(VECTORS)], refs[len(VECTORS) :]
    weights, refs = refs[:8], refs[8:]
    outs, refs = refs[:18], refs[18:]
    (
        late_out,
        early_out,
        small_out,
        seg_all,
        plan_out,
        q_out,
        kv_out,
        n1_out,
        glu_out,
        n2_out,
        left_out,
        conv_out,
        n3_out,
        depth_out,
        n4_out,
        x2_out,
        inv_out,
        masks_out,
    ) = outs
    (
        staged,
        late,
        early,
        edges,
        seg_edges,
        seg_col,
        small_own,
        x_ext,
        seg_ext,
        masks,
        small,
        low_ext,
        n1,
        glu_pre,
        x1,
        n2,
        shifted,
        left_pre,
        conv_pre,
        n3,
        g3,
        depth,
        x2,
        n4,
        inv,
        q_turned,
        kv_own,
        load_sem,
        out_sem,
        ws_send,
        ws_recv,
        edge_send,
        edge_recv,
        row_send,
        row_recv,
        q_send,
        q_recv,
        kv_send,
        kv_recv,
        pass_send,
        pass_recv,
    ) = refs
    own, core = place()
    parts = count // heads
    head, part = own // parts, lax.rem(own, parts)
    rows = tok_ref.shape[0]
    ext = rows + 2 * EDGE
    mid = slice(EDGE, EDGE + rows)
    sibling = (own, 1 - core)
    peers = others_of(own, core, count)

    loads, column = [], 0
    stage_at = []
    for number, first, width, blocks, _ in WEIGHT_COLUMNS:
        stage_at.append(column)
        for block in range(blocks):
            source = weights[number]
            if blocks == 3:
                source = source.at[block]
            elif blocks > 1:
                source = source.at[pl.ds(block * BLOCK, BLOCK), :]
            loads.append(
                move(
                    source,
                    staged.at[:, pl.ds(column, width)],
                    load_sem.at[len(loads)],
                )
            )
            column += width
    small_own[...] = jnp.zeros_like(small_own)
    for (row, tall, size), vector_ref in zip(VECTORS, vectors):
        small_own[row : row + tall, :size] = vector_ref[...]
    turned_segments(seg_col, 0, seg_row_ref[...])
    greet([sibling] + peers)

    copies = []
    right, left = (lax.rem(own + 1, count), core), (lax.rem(own + count - 1, count), core)
    edge_copies = [
        push(tok_ref.at[pl.ds(rows - EDGE, EDGE), :], edges.at[0], (edge_send, edge_recv), 0, right),
        push(tok_ref.at[pl.ds(0, EDGE), :], edges.at[1], (edge_send, edge_recv), 1, left),
        push(seg_col.at[pl.ds(rows - EDGE, EDGE), :], seg_edges.at[0], (edge_send, edge_recv), 2, right),
        push(seg_col.at[pl.ds(0, EDGE), :], seg_edges.at[1], (edge_send, edge_recv), 3, left),
    ]
    small_copy = push(small_own, small_out.at[core], (ws_send, ws_recv), len(WEIGHT_COLUMNS), sibling)
    small_out[core] = small_own[...]

    at, weight_copies = 0, []
    for (number, first, width, blocks, is_early), column in zip(WEIGHT_COLUMNS, stage_at):
        target = early if is_early else late
        for _ in range(blocks):
            loads[at].wait()
            at += 1
        size = width * blocks
        mine = pl.ds(bound(core * BLOCK, BLOCK), BLOCK)

        @pl.loop(0, BLOCK // ROW_BLOCK)
        def _(step):
            source = staged[span(step, ROW_BLOCK), pl.ds(column, size)]
            goes = pl.ds(bound(core * BLOCK + step * ROW_BLOCK, ROW_BLOCK), ROW_BLOCK)
            target[goes, pl.ds(first, size)] = source.astype(BF16)

        piece = target.at[mine, pl.ds(first, size)]
        weight_copies.append(push(piece, piece, (ws_send, ws_recv), number, sibling))

    for copy in edge_copies:
        copy.wait()
    small_copy.wait()
    row_copies = [
        push(seg_row_ref, seg_all.at[own], (row_send, row_recv), gap, peer)
        for gap, peer in enumerate(peers)
    ]
    seg_all[own] = seg_row_ref[...]
    widened(small, small_out)

    x_ext[:EDGE, :] = edges[0].astype(F32)
    x_ext[mid, :] = tok_ref[...].astype(F32)
    x_ext[EDGE + rows :, :] = edges[1].astype(F32)
    seg_ext[:EDGE, :] = jnp.where(own == 0, -1.0, seg_edges[0])
    seg_ext[mid, :] = seg_col[...]
    seg_ext[EDGE + rows :, :] = jnp.where(own == count - 1, -1.0, seg_edges[1])
    tap_masks(masks, seg_ext)

    normed, inv_std = norm_fwd(x_ext[...])
    n1[...] = normed[mid, :]
    inv[0] = jnp.broadcast_to(inv_std, (ext, LANES))
    low_ext[...] = (normed * vector(small, LN1G, D) + vector(small, LN1B, D)).astype(BF16)

    weight_copies[0].wait()
    glu_bias = vector(small, GLUB, 2 * D)
    for step in range(2 * D // 512):
        cols = slice(512 * step, 512 * (step + 1))
        glu_pre[:, cols] = (
            matmul(low_ext[...], late[:, GLU + 512 * step : GLU + 512 * (step + 1)])
            + glu_bias[:, cols]
        )
    state = x_ext[...] + glu_pre[:, :D] * jax.nn.sigmoid(glu_pre[:, D:])
    x1[...] = state[mid, :]
    normed, inv_std = norm_fwd(state)
    n2[...] = normed[mid, :]
    inv[1] = jnp.broadcast_to(inv_std, (ext, LANES))
    low_f = (normed * vector(small, LN2G, D) + vector(small, LN2B, D)).astype(BF16).astype(F32)
    before = pltpu.roll(low_f, 1, 0) * jnp.concatenate([masks[REACH - 1]] * (D // LANES), axis=1)
    after = pltpu.roll(low_f, ext - 1, 0) * jnp.concatenate([masks[REACH + 1]] * (D // LANES), axis=1)
    shifted[0] = before.astype(BF16)
    shifted[1] = low_f.astype(BF16)
    shifted[2] = after.astype(BF16)

    weight_copies[1].wait()

    @pl.loop(0, FF // 512)
    def _(step):
        weight = late[:, pl.ds(bound(LEFT + step * 512, 512), 512)]
        left_pre[:, span(step, 512)] = matmul(shifted[1], weight)

    weight_copies[2].wait()
    conv_sum = vector(small, CONVB, HALF)
    for tap in range(3):
        conv_sum = conv_sum + matmul(
            shifted[tap], late[:, CONV + HALF * tap : CONV + HALF * (tap + 1)]
        )
    conv_pre[...] = conv_sum

    left_bias = vector(small, LEFTB, FF)
    gain, shift = vector(small, LN3G, FF), vector(small, LN3B, FF)

    @pl.loop(0, ext // ROW_BLOCK)
    def _(step):
        here = span(step, ROW_BLOCK)
        pre = left_pre[here, :] + left_bias
        left_pre[here, :] = pre
        mixed = jax.nn.silu(pre)
        mixed = jnp.concatenate(
            [mixed[:, :HALF] + jax.nn.silu(conv_pre[here, :]), mixed[:, HALF:]], axis=1
        )
        normed, inv_std = norm_fwd(mixed)
        n3[here, :] = normed
        inv[2, here, :] = jnp.broadcast_to(inv_std, (ROW_BLOCK, LANES))
        g3[here, :] = (normed * gain + shift).astype(BF16).astype(F32)

    saves = [
        move(n1, n1_out, out_sem.at[0]),
        move(glu_pre.at[pl.ds(EDGE, rows), :], glu_out, out_sem.at[1]),
        move(n2, n2_out, out_sem.at[2]),
        move(left_pre.at[pl.ds(EDGE, rows), :], left_out, out_sem.at[3]),
        move(conv_pre, conv_out, out_sem.at[4]),
        move(n3, n3_out, out_sem.at[5]),
    ]

    @pl.loop(0, FF // LANES)
    def _(step):
        cols = span(step, LANES)
        block = g3[:, cols]
        total = jnp.zeros((rows, LANES), F32)
        for tap in range(TAPS):
            row = DEPTH + tap
            moved = pltpu.roll(block, (REACH - tap) % ext, 0)[mid, :]
            half = FF // 2 // LANES
            taps = small[step // half, row : row + 1, span(lax.rem(step, half), LANES)]
            total = total + moved * masks[tap, mid, :] * taps
        depth[:, cols] = total.astype(BF16)

    saves.append(move(depth, depth_out, out_sem.at[6]))
    weight_copies[3].wait()
    sep = vector(small, POINTB, HALF)
    for side in range(2):
        for block in range(4):
            first = side * (FF // 2) + block * BLOCK
            sep = sep + matmul(
                depth[:, first : first + BLOCK],
                late[side * BLOCK : (side + 1) * BLOCK, POINT + HALF * block : POINT + HALF * (block + 1)],
            )
    state = jnp.concatenate([x1[:, :HALF] + sep, x1[:, HALF:]], axis=1)
    x2[...] = state
    normed, inv_std = norm_fwd(state)
    n4[...] = normed
    inv[3, :rows, :] = jnp.broadcast_to(inv_std, (rows, LANES))
    low = (normed * vector(small, LN4G, D) + vector(small, LN4B, D)).astype(BF16)
    weight_copies[4].wait()
    for step in range(D // 256):
        cols = slice(256 * step, 256 * (step + 1))
        query = matmul(low, late[:, QKV + 256 * step : QKV + 256 * (step + 1)])
        q_turned[cols, :] = turn(query)
    near = lax.broadcasted_iota(jnp.int32, (rows, LANES), 1) < HEAD_DIM
    for step in range(D // LANES):
        first = QKV + D + LANES * step
        keys = matmul(low, late[:, first : first + LANES])
        values = matmul(low, late[:, first + D : first + D + LANES])
        kv_own[:, 2 * step * LANES : (2 * step + 1) * LANES] = jnp.where(
            near, keys, pltpu.roll(values, HEAD_DIM, 1)
        ).astype(BF16)
        kv_own[:, (2 * step + 1) * LANES : (2 * step + 2) * LANES] = jnp.where(
            near, pltpu.roll(keys, HEAD_DIM, 1), values
        ).astype(BF16)

    q_slot = q_out.at[:, span(head, rows)]
    kv_slot = kv_out.at[span(own, rows), :]
    arriving = []
    for gap in range(1, heads):
        other = lax.rem(head + gap, heads)
        arriving.append(
            push(kv_own.at[:, span(other, LANES)], kv_slot, (kv_send, kv_recv), gap - 1, (other * parts + part, core))
        )
    twins = [(head * parts + lax.rem(part + gap, parts), core) for gap in range(1, parts)]
    for at, twin in enumerate(twins):
        copies.append(
            push(kv_own.at[:, span(head, LANES)], kv_slot, (pass_send, pass_recv), at * heads, twin)
        )
    for gap in range(1, heads):
        other = lax.rem(head + gap, heads)
        copies.append(
            push(q_turned.at[span(other, HEAD_DIM), :], q_slot, (q_send, q_recv), gap - 1, (other * parts + part, core))
        )
    saves.append(move(q_turned.at[span(head, HEAD_DIM), :], q_slot, out_sem.at[7]))
    saves.append(move(kv_own.at[:, span(head, LANES)], kv_slot, out_sem.at[8]))
    saves.append(move(n4, n4_out, out_sem.at[9]))
    saves.append(move(x2, x2_out, out_sem.at[10]))
    saves.append(move(inv, inv_out, out_sem.at[11]))
    saves.append(move(masks, masks_out, out_sem.at[14]))
    for copy in weight_copies[5:]:
        copy.wait()
    saves.append(move(late, late_out, out_sem.at[12]))
    saves.append(move(early, early_out, out_sem.at[13]))
    for gap in range(1, heads):
        arriving[gap - 1].wait()
        source = lax.rem(head + heads - gap, heads) * parts + part
        block = kv_out.at[span(source, rows), :]
        for at, twin in enumerate(twins):
            copies.append(push(block, block, (pass_send, pass_recv), at * heads + gap, twin))

    for copy in row_copies:
        copy.wait()
    lane = lax.broadcasted_iota(jnp.int32, (1, LANES), 1)
    every = seg_all[:, 0, :]
    for tile in range(heads):
        source = tile * parts + part
        mine = seg_all[source]
        first = jnp.min(mine, axis=1, keepdims=True)
        last = jnp.max(mine, axis=1, keepdims=True)
        below = jnp.sum(jnp.sum((every < first).astype(F32), axis=0, keepdims=True), axis=1, keepdims=True).astype(jnp.int32)
        upto = jnp.sum(jnp.sum((every <= last).astype(F32), axis=0, keepdims=True), axis=1, keepdims=True).astype(jnp.int32)
        plan_out[tile : tile + 1, :] = jnp.where(
            lane == 0, below, jnp.where(lane == 1, upto, source)
        )
    for copy in copies + saves:
        copy.wait()


def first_kernel(tokens, seg_row, vectors, weights, count, heads):
    rows = tokens.shape[0]
    ext = rows + 2 * EDGE
    parts = count // heads
    late = (2 * BLOCK, SMALL)
    early = (2 * BLOCK, EARLY)
    out_shape = (
        shaped(late, BF16),
        shaped(early, BF16),
        shaped((2, SMALL_ROWS, SMALL_WIDTH)),
        shaped((count, 1, rows), jnp.int32),
        shaped((heads, LANES), jnp.int32),
        shaped((HEAD_DIM, heads * rows), BF16),
        shaped((count * rows, LANES), BF16),
        shaped((rows, D)),
        shaped((rows, 2 * D)),
        shaped((rows, D)),
        shaped((rows, FF)),
        shaped((ext, HALF)),
        shaped((ext, FF)),
        shaped((rows, FF), BF16),
        shaped((rows, D)),
        shaped((rows, D)),
        shaped((4, ext, LANES)),
        shaped((TAPS, ext, LANES)),
    )
    out_specs = (
        [any_spec()] * 2 + [vmem_spec()] * 3 + [any_spec()] * 13
    )
    scratch = [
        pltpu.VMEM((BLOCK, SMALL + EARLY), F32),
        pltpu.VMEM(late, BF16),
        pltpu.VMEM(early, BF16),
        pltpu.VMEM((2, EDGE, D), BF16),
        pltpu.VMEM((2, EDGE, LANES), F32),
        pltpu.VMEM((rows, LANES), F32),
        pltpu.VMEM((SMALL_ROWS, SMALL_WIDTH), F32),
        pltpu.VMEM((ext, D), F32),
        pltpu.VMEM((ext, LANES), F32),
        pltpu.VMEM((TAPS, ext, LANES), F32),
        pltpu.VMEM((2, SMALL_ROWS, SMALL_WIDTH), F32),
        pltpu.VMEM((ext, D), BF16),
        pltpu.VMEM((rows, D), F32),
        pltpu.VMEM((ext, 2 * D), F32),
        pltpu.VMEM((rows, D), F32),
        pltpu.VMEM((rows, D), F32),
        pltpu.VMEM((3, ext, D), BF16),
        pltpu.VMEM((ext, FF), F32),
        pltpu.VMEM((ext, HALF), F32),
        pltpu.VMEM((ext, FF), F32),
        pltpu.VMEM((ext, FF), F32),
        pltpu.VMEM((rows, FF), BF16),
        pltpu.VMEM((rows, D), F32),
        pltpu.VMEM((rows, D), F32),
        pltpu.VMEM((4, ext, LANES), F32),
        pltpu.VMEM((D, rows), BF16),
        pltpu.VMEM((rows, 2 * D), BF16),
        pltpu.SemaphoreType.DMA((sum(item[3] for item in WEIGHT_COLUMNS),)),
        pltpu.SemaphoreType.DMA((15,)),
    ]
    scratch += sem_pair(len(WEIGHT_COLUMNS) + 1) + sem_pair(4) + sem_pair(count - 1)
    scratch += sem_pair(heads - 1) + sem_pair(heads - 1) + sem_pair((parts - 1) * heads)
    return pl.pallas_call(
        functools.partial(first_body, count, heads),
        out_shape=out_shape,
        in_specs=[vmem_spec()] * (2 + len(vectors)) + [any_spec()] * 8,
        out_specs=out_specs,
        scratch_shapes=scratch,
        compiler_params=comm_params(1),
        name="first_layers",
    )(tokens, seg_row, *vectors, *weights)


def turn_keys(kv_ref, turned):
    @pl.loop(0, kv_ref.shape[0] // KEY_TILE)
    def _(tile):
        here = span(tile, KEY_TILE)
        turned[:, here] = turn(kv_ref[here, :])


def key_segments(seg_ref, segk):
    count, _, rows = seg_ref.shape

    @pl.loop(0, count)
    def _(source):
        turned_segments(segk, source * rows, seg_ref[source])


def masked(scores, segk, here, seg_q):
    seg_k = jnp.concatenate([segk[here, :]] * (scores.shape[1] // LANES), axis=1)
    return jnp.where(seg_k == seg_q, scores, MASK_FILL)


def key_tiles(plan_ref, tile):
    return plan_ref[tile, 0] // KEY_TILE, (plan_ref[tile, 1] + KEY_TILE - 1) // KEY_TILE


def attend_body(rows, plan_ref, q_ref, kv_ref, seg_ref, o_ref, low_ref, lse_ref, turned, segk):
    turn_keys(kv_ref, turned)
    key_segments(seg_ref, segk)

    @pl.loop(0, q_ref.shape[1] // rows)
    def _(tile):
        at = span(tile, rows)
        q = q_ref[:, at] * jnp.bfloat16(HEAD_DIM**-0.5)
        q_pad = jnp.concatenate([q, jnp.zeros_like(q)], axis=0)
        seg_q = seg_ref[plan_ref[tile, 2]].astype(F32)

        def block(key_tile, carry):
            top, total, acc = carry
            here = span(key_tile, KEY_TILE)
            scores = masked(matmul(kv_ref[here, :], q_pad), segk, here, seg_q)
            new_top = jnp.maximum(top, jnp.max(scores, axis=0, keepdims=True))
            probs = jnp.exp(scores - new_top)
            shrink = jnp.exp(top - new_top)
            total = total * shrink + jnp.sum(probs, axis=0, keepdims=True)
            acc = acc * shrink + matmul(turned[HEAD_DIM:, here], probs.astype(BF16))
            return (new_top, total, acc)

        first, end = key_tiles(plan_ref, tile)
        top, total, acc = lax.fori_loop(
            first,
            end,
            block,
            (
                jnp.full((1, rows), MASK_FILL, F32),
                jnp.zeros((1, rows), F32),
                jnp.zeros((HEAD_DIM, rows), F32),
            ),
        )
        out = acc / total
        o_ref[:, at] = out
        low_ref[:, at] = out.astype(BF16)
        lse_ref[:, at] = top + jnp.log(total)


def attend(plan, q_t, kv, seg, rows):
    return pl.pallas_call(
        functools.partial(attend_body, rows),
        out_shape=(shaped(q_t.shape), shaped(q_t.shape, BF16), shaped((1, q_t.shape[1]))),
        in_specs=[smem_spec()] + [vmem_spec()] * 3,
        out_specs=(vmem_spec(),) * 3,
        scratch_shapes=[pltpu.VMEM(kv.shape[::-1], BF16), pltpu.VMEM(kv.shape, F32)],
        compiler_params=pltpu.CompilerParams(vmem_limit_bytes=VMEM_MOST),
        name="attend",
    )(plan, q_t, kv, seg)


def attend_back_body(
    rows, plan_ref, q_ref, do_ref, o_ref, lse_ref, kv_ref, seg_ref, dq_ref, dkv_ref, turned, segk, dkv_acc
):
    turn_keys(kv_ref, turned)
    key_segments(seg_ref, segk)
    dkv_acc[...] = jnp.zeros_like(dkv_acc)
    scale = HEAD_DIM**-0.5

    @pl.loop(0, q_ref.shape[1] // rows)
    def _(tile):
        at = span(tile, rows)
        q = q_ref[:, at] * jnp.bfloat16(scale)
        do = do_ref[:, at]
        none = jnp.zeros_like(q)
        both = jnp.concatenate(
            [jnp.concatenate([q, none], axis=1), jnp.concatenate([none, do], axis=1)], axis=0
        )
        delta = jnp.sum(o_ref[:, at] * do.astype(F32), axis=0, keepdims=True)
        lse = lse_ref[:, at]
        seg_q = seg_ref[plan_ref[tile, 2]].astype(F32)

        def block(key_tile, dq):
            here = span(key_tile, KEY_TILE)
            pair = matmul(kv_ref[here, :], both)
            probs = jnp.exp(masked(pair[:, :rows], segk, here, seg_q) - lse)
            score_grad = (probs * (pair[:, rows:] - delta)).astype(BF16)
            joined = jnp.concatenate([score_grad, probs.astype(BF16)], axis=1)
            dkv_acc[here, :] += back_mul(joined, both)
            return dq + matmul(turned[:HEAD_DIM, here], score_grad)

        first, end = key_tiles(plan_ref, tile)
        dq = lax.fori_loop(first, end, block, jnp.zeros((HEAD_DIM, rows), F32))
        dq_ref[:, at] = (dq * scale).astype(BF16)

    dkv_ref[...] = dkv_acc[...].astype(BF16)


def attend_back(plan, q_t, do_t, o_t, lse, kv, seg, rows):
    return pl.pallas_call(
        functools.partial(attend_back_body, rows),
        out_shape=(shaped(q_t.shape, BF16), shaped(kv.shape, BF16)),
        in_specs=[smem_spec()] + [vmem_spec()] * 6,
        out_specs=(vmem_spec(),) * 2,
        scratch_shapes=[
            pltpu.VMEM(kv.shape[::-1], BF16),
            pltpu.VMEM(kv.shape, F32),
            pltpu.VMEM(kv.shape, F32),
        ],
        compiler_params=pltpu.CompilerParams(vmem_limit_bytes=VMEM_MOST),
        name="attend_back",
    )(plan, q_t, do_t, o_t, lse, kv, seg)


def middle_body(
    count,
    heads,
    o_in,
    out_grad,
    small_in,
    x2_in,
    early_in,
    out_ref,
    small_grads,
    dx3_out,
    grads_out,
    do_out,
    weights,
    x2,
    small,
    o_t,
    x3,
    expand_pre,
    hidden,
    dpre,
    do_t,
    grads,
    dx3,
    load_sem,
    o_send,
    o_recv,
    do_send,
    do_recv,
):
    own, core = place()
    parts = count // heads
    head, part = own // parts, lax.rem(own, parts)
    rows = out_grad.shape[0]
    loads = [move(early_in, weights, load_sem.at[0]), move(x2_in, x2, load_sem.at[1])]
    near = [lax.rem(head + gap, heads) for gap in range(1, heads)]
    peers = [(other * parts + part, core) for other in near]
    greet(peers)
    copies = [
        push(o_in.at[:, span(other, rows)], o_t.at[span(head, HEAD_DIM), :], (o_send, o_recv), gap, peer)
        for gap, (other, peer) in enumerate(zip(near, peers))
    ]
    copies.append(move(o_in.at[:, span(head, rows)], o_t.at[span(head, HEAD_DIM), :], load_sem.at[2]))
    widened(small, small_in)
    small_grads[...] = jnp.zeros_like(small_grads)
    for copy in copies + loads:
        copy.wait()

    state = (
        x2[...]
        + matmul(turn(o_t[...]), weights[:, ATTN : ATTN + D])
        + vector(small, ATTNB, D)
    )
    x3[...] = state
    normed, inv_std = norm_fwd(state)
    gain = vector(small, LN5G, D)
    low = (normed * gain + vector(small, LN5B, D)).astype(BF16)
    expand_bias = vector(small, EXPANDB, FF)
    for step in range(FF // 512):
        cols = slice(512 * step, 512 * (step + 1))
        pre = matmul(low, weights[:, EXPAND + 512 * step : EXPAND + 512 * (step + 1)]) + expand_bias[:, cols]
        expand_pre[:, cols] = pre
        hidden[:, cols] = jax.nn.silu(pre).astype(BF16)
    state = x3[...] + vector(small, SHRINKB, D)
    for block in range(FF // BLOCK):
        side, column = block // 4, SHRINK + D * (block % 4)
        state = state + matmul(
            hidden[:, block * BLOCK : (block + 1) * BLOCK],
            weights[side * BLOCK : (side + 1) * BLOCK, column : column + D],
        )
    out_ref[...] = state.astype(BF16)

    dz = out_grad[...]
    for block in range(FF // BLOCK):
        side, column = block // 4, SHRINK + D * (block % 4)
        cols = slice(block * BLOCK, (block + 1) * BLOCK)
        grad = back_mul(dz, weights[side * BLOCK : (side + 1) * BLOCK, column : column + D])
        dpre[:, cols] = (grad * smooth_slope(expand_pre[:, cols])).astype(BF16)
    grad = jnp.concatenate(
        [
            back_mul(dpre[...], weights[side * BLOCK : (side + 1) * BLOCK, EXPAND : EXPAND + FF])
            for side in range(2)
        ],
        axis=1,
    )
    state = dz.astype(F32) + norm_back(grad, normed, inv_std, gain)
    dx3[...] = state
    dy3 = state.astype(BF16)
    do_t[...] = back_mul(weights[:, ATTN : ATTN + D], dy3).astype(BF16)
    slot = do_out.at[:, span(head, rows)]
    copies = [
        push(do_t.at[span(other, HEAD_DIM), :], slot, (do_send, do_recv), gap, peer)
        for gap, (other, peer) in enumerate(zip(near, peers))
    ]
    copies.append(move(do_t.at[span(head, HEAD_DIM), :], slot, load_sem.at[0]))
    copies.append(move(dx3, dx3_out, load_sem.at[1]))

    put_vector(small_grads, LN5G, col_sum(grad * normed))
    put_vector(small_grads, LN5B, col_sum(grad))
    put_vector(small_grads, ATTNB, col_sum(dy3))
    put_vector(small_grads, EXPANDB, col_sum(dpre[...]))
    put_vector(small_grads, SHRINKB, col_sum(dz))
    grads[:, ATTN : ATTN + D] = matmul(o_t[...], dy3).astype(BF16)
    low_t = turn(low)
    for step in range(FF // 512):
        grads[:, EXPAND + 512 * step : EXPAND + 512 * (step + 1)] = matmul(
            low_t, dpre[:, 512 * step : 512 * (step + 1)]
        ).astype(BF16)
    for block in range(FF // BLOCK):
        side, column = block // 4, SHRINK + D * (block % 4)
        grads[side * BLOCK : (side + 1) * BLOCK, column : column + D] = matmul(
            turn(hidden[:, block * BLOCK : (block + 1) * BLOCK]), dz
        ).astype(BF16)
    copies.append(move(grads, grads_out, load_sem.at[2]))
    for copy in copies:
        copy.wait()


def middle_kernel(o_low, out_grad, small, x2, early, count, heads):
    rows = out_grad.shape[0]
    return pl.pallas_call(
        functools.partial(middle_body, count, heads),
        out_shape=(
            shaped((rows, D), BF16),
            shaped((2, SMALL_ROWS, SMALL_WIDTH)),
            shaped((rows, D)),
            shaped(early.shape, BF16),
            shaped((HEAD_DIM, heads * rows), BF16),
        ),
        in_specs=[vmem_spec()] * 3 + [any_spec()] * 2,
        out_specs=[vmem_spec()] * 2 + [any_spec()] * 3,
        scratch_shapes=[
            pltpu.VMEM(early.shape, BF16),
            pltpu.VMEM((rows, D), F32),
            pltpu.VMEM((2, SMALL_ROWS, SMALL_WIDTH), F32),
            pltpu.VMEM((D, rows), BF16),
            pltpu.VMEM((rows, D), F32),
            pltpu.VMEM((rows, FF), F32),
            pltpu.VMEM((rows, FF), BF16),
            pltpu.VMEM((rows, FF), BF16),
            pltpu.VMEM((D, rows), BF16),
            pltpu.VMEM(early.shape, BF16),
            pltpu.VMEM((rows, D), F32),
            pltpu.SemaphoreType.DMA((3,)),
        ]
        + sem_pair(heads - 1)
        + sem_pair(heads - 1),
        compiler_params=comm_params(2),
        name="middle_layers",
    )(o_low, out_grad, small, x2, early)


def column_groups(first, width, bits):
    tiles = width // LANES
    unit = 2 ** max(0, bits - 4)
    long = max(1, round(tiles * 0.36 / unit)) * unit
    orders = [
        list(range(bits)),
        [1, 0] + list(range(2, bits)),
        list(range(2, bits)) + [0, 1],
    ]
    groups = []
    for size, order in zip([long, long, tiles - 2 * long], orders):
        groups.append((first, size * LANES, order))
        first += size * LANES
    return groups


def grad_sets(bits):
    bounds = [LATE, LATE + SHRINK, QKV, LEFT, CONV]
    widths = [SHRINK, EARLY - SHRINK, LEFT - QKV, CONV - LEFT, LATE - CONV]
    return [column_groups(first, width, bits) for first, width in zip(bounds, widths)]


class Piece:
    def __init__(self, at, group, links, sums, got, total, sems):
        self.at, (self.first, self.width, self.order) = at, group
        self.core, self.sibling, self.bit_of, self.partner = links
        self.view, self.got, self.total, self.sems = sums, got, total, sems
        self.bits, self.phase, self.trail = len(self.order), 0, []
        self.copy = None

    def whole(self):
        return (0, BLOCK, self.first, self.width)

    def out(self, where):
        row, tall, col, wide = where
        return self.total.at[pl.ds(bound(row, ROW_BLOCK), tall), pl.ds(bound(col, LANES), wide)]

    def start(self, other_half):
        self.copy = push(other_half, self.out(self.whole()), self.sems[0], self.at, self.sibling)

    def add(self, where, source, spot, last):
        row, tall, col, wide = where

        @pl.loop(0, tall // ROW_BLOCK)
        def _(step):
            gap = step * ROW_BLOCK
            here = (row + gap, ROW_BLOCK, col, wide)
            there = source.at[pl.ds(bound(spot + gap, ROW_BLOCK), ROW_BLOCK), pl.ds(self.first, wide)]
            mine = self.view(here)[...].astype(F32)
            added = (mine + there[...].astype(F32)).astype(BF16)
            if last:
                self.out(here)[...] = added
            else:
                self.view(here)[...] = added

    def halve(self, step):
        row, tall, col, wide = self.where
        bit = self.order[step]
        mine = self.bit_of[bit]
        if tall > ROW_BLOCK:
            half = tall // 2
            kept = (row + half * mine, half, col, wide)
            sent = (row + half * (1 - mine), half, col, wide)
        else:
            half = wide // 2
            kept = (row, tall, col + half * mine, half)
            sent = (row, tall, col + half * (1 - mine), half)
        self.copy = push(
            self.view(sent),
            self.got.at[pl.ds(self.spot, sent[1]), pl.ds(self.first, sent[3])],
            self.sems[1],
            self.at * self.bits + step,
            self.partner[bit],
        )
        self.where = kept

    def double(self, step):
        place_out = self.out(self.trail[step])
        self.copy = push(
            place_out,
            place_out,
            self.sems[2],
            self.at * self.bits + step,
            self.partner[self.order[step]],
        )

    def done(self):
        return self.phase > 2 * self.bits

    def advance(self):
        if self.done():
            return
        self.copy.wait()
        if self.phase == 0:
            self.where, self.spot = self.whole(), 0
            self.add(self.where, self.total, 0, False)
            self.halve(0)
        elif self.phase <= self.bits:
            last = self.phase == self.bits
            self.add(self.where, self.got, self.spot, last)
            self.trail.append(self.where)
            self.spot += self.where[1]
            if last:
                self.double(self.bits - 1)
            else:
                self.halve(self.phase)
        elif self.phase < 2 * self.bits:
            self.double(2 * self.bits - 1 - self.phase)
        self.phase += 1


def last_body(count, heads, dq_in, dkv_in, small_in, small_grads_in, *refs):
    (
        early_grads,
        dx3_in,
        late_in,
        n1_in,
        glu_in,
        n2_in,
        left_in,
        conv_in,
        n3_in,
        depth_in,
        n4_in,
        inv_in,
        masks_in,
        total,
        grad_out,
        weights,
        dx3,
        n1,
        glu_pre,
        n2,
        left_pre,
        conv_pre,
        n3,
        depth,
        n4,
        inv,
        masks,
        small,
        small_grads,
        dq_t,
        dkv_own,
        shared,
        summed,
        dqkv,
        sep_own,
        sep_edges,
        sep_ext,
        depth_grad,
        g3_grad,
        row_sums,
        dleft,
        conv_grad,
        conv_taps,
        grads,
        early_own,
        got,
        result,
        load_sem,
        keep_sem,
        dq_send,
        dq_recv,
        dkv_send,
        dkv_recv,
        pass_send,
        pass_recv,
        edge_send,
        edge_recv,
        ws_send,
        ws_recv,
        rs_send,
        rs_recv,
        ag_send,
        ag_recv,
    ) = refs
    own, core = place()
    parts = count // heads
    head, part = own // parts, lax.rem(own, parts)
    rows = dx3.shape[0]
    ext = rows + 2 * EDGE
    mid = slice(EDGE, EDGE + rows)
    sibling = (own, 1 - core)
    peers = others_of(own, core, count)
    bits = count.bit_length() - 1

    sources = (dx3_in, late_in, n4_in, inv_in, depth_in, masks_in, n3_in, left_in, conv_in, n2_in, glu_in, n1_in)
    targets = (dx3, weights, n4, inv, depth, masks, n3, left_pre, conv_pre, n2, glu_pre, n1)
    loads = [move(a, b, load_sem.at[at]) for at, (a, b) in enumerate(zip(sources, targets))]
    greet([sibling] + peers)

    bit_of = [lax.rem(own // 2**bit, 2) for bit in range(bits)]
    partner = [(own + 2**bit - 2 * 2**bit * bit_of[bit], core) for bit in range(bits)]
    links = (core, sibling, bit_of, partner)
    sems = ((ws_send, ws_recv), (rs_send, rs_recv), (ag_send, ag_recv))

    def early_view(where):
        row, tall, col, wide = where
        return early_own.at[pl.ds(bound(row, ROW_BLOCK), tall), pl.ds(bound(col - LATE, LANES), wide)]

    def late_view(where):
        row, tall, col, wide = where
        return grads.at[pl.ds(bound(core * BLOCK + row, ROW_BLOCK), tall), pl.ds(bound(col, LANES), wide)]

    sets, at = [], 0
    for number, groups in enumerate(grad_sets(bits)):
        members = []
        for group in groups:
            view = late_view if number > 1 else early_view
            members.append(Piece(at, group, links, view, got, total, sems))
            at += 1
        sets.append(members)
    other_rows = pl.ds(bound((1 - core) * BLOCK, BLOCK), BLOCK)
    own_rows = pl.ds(bound(core * BLOCK, BLOCK), BLOCK)

    def start(members, source, shift):
        for piece in members:
            piece.start(source.at[other_rows, pl.ds(piece.first - shift, piece.width)])

    def advance(members):
        for piece in members:
            piece.advance()

    keep = move(early_grads.at[own_rows, :], early_own, keep_sem.at[1])
    start(sets[0] + sets[1], early_grads, LATE)
    slot = dq_t.at[span(head, HEAD_DIM), :]
    heads_on = [lax.rem(head + gap, heads) for gap in range(heads)]
    sharing = []
    for gap, other in enumerate(heads_on[1:] + heads_on[:1]):
        for at in range(parts - 1):
            twin = lax.rem(part + at + 1, parts)
            sharing.append(
                push(
                    dkv_in.at[span(other * parts + twin, rows), :],
                    shared.at[at, other],
                    (pass_send, pass_recv),
                    at * heads + gap,
                    (head * parts + twin, core),
                )
            )
    collect = []
    for gap, other in enumerate(heads_on[1:]):
        collect.append(
            push(dq_in.at[:, span(other, rows)], slot, (dq_send, dq_recv), gap, (other * parts + part, core))
        )
    collect.append(move(dq_in.at[:, span(head, rows)], slot, keep_sem.at[0]))
    widened(small, small_in)
    small_grads[...] = small_grads_in[...]
    keep.wait()
    advance(sets[0])
    advance(sets[1])
    for gap, other in enumerate(heads_on[1:] + heads_on[:1]):
        for copy in sharing[gap * (parts - 1) : (gap + 1) * (parts - 1)]:
            copy.wait()
        total_kv = dkv_in[span(other * parts + part, rows), :].astype(F32)
        for at in range(parts - 1):
            total_kv = total_kv + shared[at, other].astype(F32)
        if gap < heads - 1:
            summed[other] = total_kv.astype(BF16)
            collect.append(
                push(
                    summed.at[other],
                    dkv_own.at[:, span(head, LANES)],
                    (dkv_send, dkv_recv),
                    gap,
                    (other * parts + part, core),
                )
            )
        else:
            dkv_own[:, span(head, LANES)] = total_kv.astype(BF16)
    for copy in loads:
        copy.wait()
    advance(sets[0][:2])
    for copy in collect:
        copy.wait()
    advance(sets[1][:2])

    dqkv[:, :D] = turn(dq_t[...])
    lane = lax.broadcasted_iota(jnp.int32, (rows, LANES), 1) < HEAD_DIM
    for step in range(D // LANES):
        pair = []
        for side in range(2):
            first = (2 * step + side) * LANES
            pair.append(dkv_own[:, first : first + LANES].astype(F32))
        cols = slice(D + step * LANES, D + (step + 1) * LANES)
        dqkv[:, cols] = jnp.where(lane, pair[0], pltpu.roll(pair[1], HEAD_DIM, 1)).astype(BF16)
        cols = slice(2 * D + step * LANES, 2 * D + (step + 1) * LANES)
        dqkv[:, cols] = jnp.where(lane, pltpu.roll(pair[0], HEAD_DIM, 1), pair[1]).astype(BF16)

    def through(grad, column, width):
        return jnp.concatenate(
            [
                back_mul(grad, weights[side * BLOCK : (side + 1) * BLOCK, column : column + width])
                for side in range(2)
            ],
            axis=1,
        )

    def norm_step(grad, normed, inv_std, row):
        put_vector(small_grads, row, col_sum(grad * normed))
        put_vector(small_grads, row + 1, col_sum(grad))
        return norm_back(grad, normed, inv_std, vector(small, row, D))

    grad = through(dqkv[...], QKV, 3 * D)
    dx2 = dx3[...] + norm_step(grad, n4[...], inv[3, :rows, :1], LN4G)
    dx3[...] = dx2
    sep_own[...] = dx2[:, :HALF].astype(BF16)
    right, left = (lax.rem(own + 1, count), core), (lax.rem(own + count - 1, count), core)
    edge_copies = [
        push(sep_own.at[pl.ds(rows - EDGE, EDGE), :], sep_edges.at[0], (edge_send, edge_recv), 0, right),
        push(sep_own.at[pl.ds(0, EDGE), :], sep_edges.at[1], (edge_send, edge_recv), 1, left),
    ]
    advance(sets[0])
    low_t = turn(n4[...] * vector(small, LN4G, D) + vector(small, LN4B, D))
    for step in range(3):
        grads[:, QKV + D * step : QKV + D * (step + 1)] = matmul(
            low_t, dqkv[:, D * step : D * (step + 1)]
        ).astype(BF16)
    for block in range(FF // BLOCK):
        side, column = block // 4, POINT + HALF * (block % 4)
        grads[side * BLOCK : (side + 1) * BLOCK, column : column + HALF] = matmul(
            turn(depth[:, block * BLOCK : (block + 1) * BLOCK]), sep_own[...]
        ).astype(BF16)
    put_vector(small_grads, POINTB, col_sum(sep_own[...]))
    start(sets[2], grads, 0)
    advance(sets[1])

    for copy in edge_copies:
        copy.wait()
    sep_ext[:EDGE, :] = sep_edges[0]
    sep_ext[mid, :] = sep_own[...]
    sep_ext[EDGE + rows :, :] = sep_edges[1]
    for block in range(FF // BLOCK):
        side, column = block // 4, POINT + HALF * (block % 4)
        depth_grad[:, block * BLOCK : (block + 1) * BLOCK] = (
            back_mul(sep_ext[...], weights[side * BLOCK : (side + 1) * BLOCK, column : column + HALF])
            .astype(BF16)
            .astype(F32)
        )
    advance(sets[2])
    advance(sets[0])

    row_sums[...] = jnp.zeros_like(row_sums)
    half = FF // 2 // LANES

    def tap_block(step):
        cols = span(step, LANES)
        side, lanes = step // half, span(lax.rem(step, half), LANES)
        block = depth_grad[:, cols]
        normed = n3[:, cols]
        gain = small[side, LN3G : LN3G + 1, lanes]
        low = (normed[mid, :] * gain + small[side, LN3B : LN3B + 1, lanes]).astype(BF16).astype(F32)
        summed = jnp.zeros((ext, LANES), F32)
        for tap in range(TAPS):
            row = DEPTH + tap
            moved = pltpu.roll(block, (tap - REACH) % ext, 0) * masks[TAPS - 1 - tap]
            summed = summed + moved * small[side, row : row + 1, lanes]
            small_grads[side, row : row + 1, lanes] = col_sum(low * moved[mid, :])
        g3_grad[:, cols] = summed
        small_grads[side, LN3G : LN3G + 1, lanes] = col_sum(summed[mid, :] * normed[mid, :])
        small_grads[side, LN3B : LN3B + 1, lanes] = col_sum(summed[mid, :])
        scaled = summed * gain
        row_sums[0] = row_sums[0] + scaled
        row_sums[1] = row_sums[1] + scaled * normed

    pl.loop(0, half)(tap_block)
    advance(sets[1])
    advance(sets[2])
    pl.loop(half, 2 * half)(tap_block)
    advance(sets[0])
    inner = jnp.sum(row_sums[0], axis=1, keepdims=True) * (1.0 / FF)
    cross = jnp.sum(row_sums[1], axis=1, keepdims=True) * (1.0 / FF)
    row_sums[0] = jnp.broadcast_to(inner, (ext, LANES))
    row_sums[1] = jnp.broadcast_to(cross, (ext, LANES))

    @pl.loop(0, FF // LANES)
    def _(step):
        cols = span(step, LANES)
        side, lanes = step // half, span(lax.rem(step, half), LANES)
        scaled = g3_grad[mid, cols] * small[side, LN3G : LN3G + 1, lanes]
        mixed_grad = inv[2, mid, :] * (scaled - row_sums[0, mid, :] - n3[mid, cols] * row_sums[1, mid, :])
        low = (mixed_grad * smooth_slope(left_pre[:, cols])).astype(BF16)
        dleft[:, cols] = low
        small_grads[side, LEFTB : LEFTB + 1, lanes] = col_sum(low)

    advance(sets[1])
    for step in range(HALF // LANES):
        cols = slice(step * LANES, (step + 1) * LANES)
        scaled = g3_grad[:, cols] * small[0, LN3G : LN3G + 1, cols]
        mixed_grad = inv[2] * (scaled - row_sums[0] - n3[:, cols] * row_sums[1])
        low = (mixed_grad * smooth_slope(conv_pre[:, cols])).astype(BF16).astype(F32)
        conv_grad[:, cols] = low
        for tap in range(3):
            moved = pltpu.roll(low, (tap - 1) % ext, 0) * masks[REACH + 1 - tap]
            conv_taps[:, HALF * tap + step * LANES : HALF * tap + (step + 1) * LANES] = moved[mid, :].astype(BF16)
    put_vector(small_grads, CONVB, col_sum(conv_grad[mid, :]))

    low_t = turn(n2[...] * vector(small, LN2G, D) + vector(small, LN2B, D))
    for step in range(FF // 512):
        grads[:, LEFT + 512 * step : LEFT + 512 * (step + 1)] = matmul(
            low_t, dleft[:, 512 * step : 512 * (step + 1)]
        ).astype(BF16)
    start(sets[3], grads, 0)
    advance(sets[2])
    advance(sets[0])
    for tap in range(3):
        grads[:, CONV + HALF * tap : CONV + HALF * (tap + 1)] = matmul(
            low_t, conv_taps[:, HALF * tap : HALF * (tap + 1)]
        ).astype(BF16)
    advance(sets[3])
    advance(sets[1])
    grad = through(dleft[...], LEFT, FF) + through(conv_taps[...], CONV, 3 * HALF)
    dx1 = dx3[...] + norm_step(grad, n2[...], inv[1, mid, :1], LN2G)
    gate = jax.nn.sigmoid(glu_pre[:, D:])
    value_grad = dx1 * gate
    dglu = jnp.concatenate([value_grad, value_grad * glu_pre[:, :D] * (1.0 - gate)], axis=1).astype(BF16)
    put_vector(small_grads, GLUB, col_sum(dglu))
    advance(sets[0])
    advance(sets[2])
    low_t = turn(n1[...] * vector(small, LN1G, D) + vector(small, LN1B, D))
    for step in range(2):
        grads[:, GLU + D * step : GLU + D * (step + 1)] = matmul(
            low_t, dglu[:, D * step : D * (step + 1)]
        ).astype(BF16)
    advance(sets[1])
    advance(sets[3])
    grad = through(dglu, GLU, 2 * D)
    result[...] = dx1 + norm_step(grad, n1[...], inv[0, mid, :1], LN1G)
    keep = move(result, grad_out, keep_sem.at[0])
    for side in range(2):
        for block in range(SMALL_WIDTH // BLOCK):
            first = side * BLOCK + block * SMALL_ROWS
            grads[first : first + SMALL_ROWS, SMALL : SMALL + BLOCK] = small_grads[
                side, :, block * BLOCK : (block + 1) * BLOCK
            ].astype(BF16)
        first = side * BLOCK + SMALL_WIDTH // BLOCK * SMALL_ROWS
        grads[first : (side + 1) * BLOCK, SMALL : SMALL + BLOCK] = jnp.zeros(
            ((side + 1) * BLOCK - first, BLOCK), BF16
        )
    start(sets[4], grads, 0)
    while not all(piece.done() for members in sets for piece in members):
        for members in sets:
            advance(members)
    keep.wait()


def last_kernel(dq, dkv, small, small_grads, tensors, count, heads):
    rows = dkv.shape[0] // count
    ext = rows + 2 * EDGE
    parts = count // heads
    bits = count.bit_length() - 1
    pieces = sum(len(groups) for groups in grad_sets(bits))
    early = tensors[0].shape
    scratch = [
        pltpu.VMEM(tensors[2].shape, BF16),
        pltpu.VMEM((rows, D), F32),
        pltpu.VMEM((rows, D), F32),
        pltpu.VMEM((rows, 2 * D), F32),
        pltpu.VMEM((rows, D), F32),
        pltpu.VMEM((rows, FF), F32),
        pltpu.VMEM((ext, HALF), F32),
        pltpu.VMEM((ext, FF), F32),
        pltpu.VMEM((rows, FF), BF16),
        pltpu.VMEM((rows, D), F32),
        pltpu.VMEM((4, ext, LANES), F32),
        pltpu.VMEM((TAPS, ext, LANES), F32),
        pltpu.VMEM((2, SMALL_ROWS, SMALL_WIDTH), F32),
        pltpu.VMEM((2, SMALL_ROWS, SMALL_WIDTH), F32),
        pltpu.VMEM((D, rows), BF16),
        pltpu.VMEM((rows, 2 * D), BF16),
        pltpu.VMEM((parts - 1, heads, rows, LANES), BF16),
        pltpu.VMEM((heads, rows, LANES), BF16),
        pltpu.VMEM((rows, 3 * D), BF16),
        pltpu.VMEM((rows, HALF), BF16),
        pltpu.VMEM((2, EDGE, HALF), BF16),
        pltpu.VMEM((ext, HALF), BF16),
        pltpu.VMEM((ext, FF), F32),
        pltpu.VMEM((ext, FF), F32),
        pltpu.VMEM((2, ext, LANES), F32),
        pltpu.VMEM((rows, FF), BF16),
        pltpu.VMEM((ext, HALF), F32),
        pltpu.VMEM((rows, 3 * HALF), BF16),
        pltpu.VMEM((2 * BLOCK, LATE), BF16),
        pltpu.VMEM((BLOCK, EARLY), BF16),
        pltpu.VMEM((BLOCK + ROW_BLOCK * max(0, bits - 4), WIDTH), BF16),
        pltpu.VMEM((rows, D), F32),
        pltpu.SemaphoreType.DMA((12,)),
        pltpu.SemaphoreType.DMA((3,)),
    ]
    scratch += sem_pair(heads - 1) + sem_pair(heads - 1) + sem_pair((parts - 1) * heads)
    scratch += sem_pair(2) + sem_pair(pieces)
    scratch += sem_pair(pieces * bits) + sem_pair(pieces * bits)
    return pl.pallas_call(
        functools.partial(last_body, count, heads),
        out_shape=(shaped((BLOCK, WIDTH), BF16), shaped((rows, D))),
        in_specs=[vmem_spec()] * 4 + [any_spec()] * len(tensors),
        out_specs=[vmem_spec(), any_spec()],
        scratch_shapes=scratch,
        compiler_params=comm_params(3),
        name="last_layers",
    )(dq, dkv, small, small_grads, *tensors)


def unpack_body(output_in, grad_in, packed_in, *refs):
    size = len(MATRICES) + len(VECTORS) + 2
    outs, (packed, *stages, load_sem, out_sem) = refs[:size], refs[size:]
    output_ref, grad_ref, *outs = outs
    order = [len(MATRICES)] + list(range(len(MATRICES)))
    bounds = [(first, width * blocks) for first, width, blocks in MATRICES] + [(SMALL, BLOCK)]
    loads = {}
    for at in order:
        cols = pl.ds(*bounds[at])
        loads[at] = move(packed_in.at[:, cols], packed.at[:, cols], load_sem.at[at])
    stores = [
        move(output_in, output_ref, out_sem.at[len(MATRICES)]),
        move(grad_in, grad_ref, out_sem.at[len(MATRICES) + 1]),
    ]
    for at, (first, width, blocks) in enumerate(MATRICES):
        loads[at].wait()
        stage = stages[at]
        for block in range(blocks):

            @pl.loop(0, BLOCK // ROW_BLOCK)
            def _(step):
                value = packed[span(step, ROW_BLOCK), first + block * width : first + (block + 1) * width].astype(F32)
                if blocks == 3:
                    stage[block, span(step, ROW_BLOCK), :] = value
                else:
                    stage[pl.ds(bound(block * BLOCK + step * ROW_BLOCK, ROW_BLOCK), ROW_BLOCK), :] = value

        stores.append(move(stage, outs[at], out_sem.at[at]))

    loads[len(MATRICES)].wait()
    small = jnp.concatenate(
        [
            packed[block * SMALL_ROWS : (block + 1) * SMALL_ROWS, SMALL : SMALL + BLOCK].astype(F32)
            for block in range(SMALL_WIDTH // BLOCK)
        ],
        axis=1,
    )
    for (row, tall, size), out in zip(VECTORS, outs[len(MATRICES) :]):
        out[...] = small[row : row + tall, :size]
    for copy in stores:
        copy.wait()


def unpack(output, grad, packed):
    shapes = []
    for _, width, blocks in MATRICES:
        shapes.append((3, BLOCK, width) if blocks == 3 else (blocks * BLOCK, width))
    vectors = [(tall, size) for _, tall, size in VECTORS]
    return pl.pallas_call(
        unpack_body,
        out_shape=(shaped(output.shape, output.dtype), shaped(grad.shape))
        + tuple(shaped(shape) for shape in shapes + vectors),
        in_specs=[vmem_spec()] * 2 + [any_spec()],
        out_specs=[any_spec()] * (2 + len(shapes)) + [vmem_spec()] * len(vectors),
        scratch_shapes=[pltpu.VMEM(packed.shape, packed.dtype)]
        + [pltpu.VMEM(shape, F32) for shape in shapes]
        + [pltpu.SemaphoreType.DMA((len(shapes) + 1,)), pltpu.SemaphoreType.DMA((len(shapes) + 2,))],
        compiler_params=pltpu.CompilerParams(vmem_limit_bytes=VMEM_MOST),
        name="unpack",
    )(output, grad, packed)


def body(tokens, segment_ids, out_grad, *params):
    (
        ln1g, ln1b, glu_w, glu_b, ln2g, ln2b, left_w, left_b, conv_w, conv_b, ln3g, ln3b, depth_w,
        point_w, point_b, ln4g, ln4b, qkv_w, attn_w, attn_b, ln5g, ln5b, expand_w, expand_b,
        shrink_w, shrink_b,
    ) = params
    count = lax.axis_size("ctx")
    heads = D // HEAD_DIM
    rows = tokens.shape[1]
    vectors = [
        ln1g, ln1b, glu_b, ln2g, ln2b, left_b, conv_b, ln3g, ln3b, depth_w,
        point_b, ln4g, ln4b, attn_b, ln5g, ln5b, expand_b, shrink_b,
    ]
    vectors = [value.reshape(-1, value.shape[-1]) for value in vectors]
    weights = (glu_w, left_w, conv_w, point_w, qkv_w, attn_w, expand_w, shrink_w)
    (
        late, early, small, seg, plan, q_head, kv_head, n1, glu_pre, n2, left_pre, conv_pre, n3,
        depth, n4, x2, inv, masks,
    ) = first_kernel(tokens[0], segment_ids, vectors, weights, count, heads)
    o_head, o_low, log_sum = attend(plan, q_head, kv_head, seg, rows)
    output, small_grads, dx3, early_grads, do_head = middle_kernel(
        o_low, out_grad[0], small, x2, early, count, heads
    )
    dq_head, dkv_head = attend_back(plan, q_head, do_head, o_head, log_sum, kv_head, seg, rows)
    tensors = (
        early_grads, dx3, late, n1, glu_pre, n2, left_pre, conv_pre, n3, depth, n4, inv, masks,
    )
    total, input_grad = last_kernel(dq_head, dkv_head, small, small_grads, tensors, count, heads)
    output, input_grad, *pieces = unpack(output, input_grad, total)
    matrices, lines = pieces[: len(MATRICES)], pieces[len(MATRICES) :]
    lines = [line if line.shape[0] > 1 else line.reshape(-1) for line in lines]
    g_glu, g_left, g_conv, g_point, g_qkv, g_attn, g_expand, g_shrink = matrices
    (
        g_ln1g, g_ln1b, g_glu_b, g_ln2g, g_ln2b, g_left_b, g_conv_b, g_ln3g, g_ln3b, g_depth,
        g_point_b, g_ln4g, g_ln4b, g_attn_b, g_ln5g, g_ln5b, g_expand_b, g_shrink_b,
    ) = lines
    return (
        output[None], input_grad[None], g_ln1g, g_ln1b, g_glu, g_glu_b, g_ln2g, g_ln2b, g_left,
        g_left_b, g_conv, g_conv_b, g_ln3g, g_ln3b, g_depth, g_point, g_point_b, g_ln4g, g_ln4b,
        g_qkv, g_attn, g_attn_b, g_ln5g, g_ln5b, g_expand, g_expand_b, g_shrink, g_shrink_b,
    )


def solution(mesh):
    return jax.shard_map(
        body,
        mesh=mesh,
        in_specs=(
            P("ws", "ctx", None),
            P("ws", "ctx"),
            P("ws", "ctx", None),
            P("ws"),
            P("ws"),
            P("ws", None),
            P("ws"),
            P("ws"),
            P("ws"),
            P("ws", None),
            P("ws"),
            P(None, "ws", None),
            P("ws"),
            P("ws"),
            P("ws"),
            P(None, "ws"),
            P("ws", None),
            P("ws"),
            P("ws"),
            P("ws"),
            P("ws", None),
            P("ws", None),
            P("ws"),
            P("ws"),
            P("ws"),
            P("ws", None),
            P("ws"),
            P("ws", None),
            P("ws"),
        ),
        out_specs=(
            P("ws", "ctx", None),
            P("ws", "ctx", None),
            P("ws"),
            P("ws"),
            P("ws", None),
            P("ws"),
            P("ws"),
            P("ws"),
            P("ws", None),
            P("ws"),
            P(None, "ws", None),
            P("ws"),
            P("ws"),
            P("ws"),
            P(None, "ws"),
            P("ws", None),
            P("ws"),
            P("ws"),
            P("ws"),
            P("ws", None),
            P("ws", None),
            P("ws"),
            P("ws"),
            P("ws"),
            P("ws", None),
            P("ws"),
            P("ws", None),
            P("ws"),
        ),
        check_vma=False,
    )
```

```python
import functools
import math

import jax
import jax.numpy as jnp
from jax import lax
from jax.experimental import pallas as pl
from jax.experimental.pallas import tpu as pltpu
from jax.sharding import PartitionSpec as P

MESH_ID = pl.DeviceIdType.MESH
F32 = jnp.float32
BF16 = jnp.bfloat16
HEAD_DIM = 64
NORM_EPS = 1e-06
MASK_FILL = -1e30
LANES = 128
ROW_BLOCK = 16
EDGE = 16
KEY_TILE = 1024
BLOCK = 256
VMEM_MOST = 60 * 1024 * 1024

D = 512
FF = 2048
HALF = 256
TAPS = 9
REACH = 4

QKV, POINT, LEFT, CONV, GLU, SMALL, LATE = 0, 1536, 2560, 4608, 5376, 6400, 6656
ATTN, EXPAND, SHRINK, EARLY = 0, 512, 2560, 4608
WIDTH = LATE + EARLY

SMALL_ROWS = 32
SMALL_WIDTH = 1024
(LN1G, LN1B, GLUB, LN2G, LN2B, LEFTB, CONVB, LN3G, LN3B, DEPTH) = range(10)
(POINTB, LN4G, LN4B, ATTNB, LN5G, LN5B, EXPANDB, SHRINKB) = range(DEPTH + TAPS, DEPTH + TAPS + 8)


VECTORS = [
    (LN1G, 1, 256),
    (LN1B, 1, 256),
    (GLUB, 1, 512),
    (LN2G, 1, 256),
    (LN2B, 1, 256),
    (LEFTB, 1, 1024),
    (CONVB, 1, 128),
    (LN3G, 1, 1024),
    (LN3B, 1, 1024),
    (DEPTH, TAPS, 1024),
    (POINTB, 1, 128),
    (LN4G, 1, 256),
    (LN4B, 1, 256),
    (ATTNB, 1, 256),
    (LN5G, 1, 256),
    (LN5B, 1, 256),
    (EXPANDB, 1, 1024),
    (SHRINKB, 1, 256),
]
MATRICES = [
    (GLU, 1024, 1),
    (LEFT, 2048, 1),
    (CONV, 256, 3),
    (POINT, 256, 4),
    (QKV, 1536, 1),
    (LATE + ATTN, 512, 1),
    (LATE + EXPAND, 2048, 1),
    (LATE + SHRINK, 512, 4),
]


def vmem_spec():
    return pl.BlockSpec(memory_space=pltpu.VMEM)


def any_spec():
    return pl.BlockSpec(memory_space=pl.ANY)


def smem_spec():
    return pl.BlockSpec(memory_space=pltpu.SMEM)


def shaped(shape, kind=F32):
    return jax.ShapeDtypeStruct(shape, kind)


def comm_params(number):
    return pltpu.CompilerParams(
        collective_id=number, has_side_effects=True, vmem_limit_bytes=VMEM_MOST
    )


def greet(peers):
    barrier = pltpu.get_barrier_semaphore()
    for peer in peers:
        pl.semaphore_signal(barrier, inc=1, device_id=peer, device_id_type=MESH_ID)
    pl.semaphore_wait(barrier, len(peers))


def push(src, dst, sems, at, peer):
    copy = pltpu.make_async_remote_copy(
        src_ref=src,
        dst_ref=dst,
        send_sem=sems[0].at[at],
        recv_sem=sems[1].at[at],
        device_id=peer,
        device_id_type=MESH_ID,
    )
    copy.start()
    return copy


def move(src, dst, sem):
    copy = pltpu.make_async_copy(src, dst, sem)
    copy.start()
    return copy


def sem_pair(count):
    return [pltpu.SemaphoreType.DMA((count,)), pltpu.SemaphoreType.DMA((count,))]


def bound(value, step):
    return value if isinstance(value, int) else pl.multiple_of(value, step)


def span(value, step):
    return pl.ds(bound(value * step, step), step)


def matmul(left_op, right_op):
    return jnp.dot(left_op, right_op, preferred_element_type=F32)


def back_mul(grad_in, weight):
    return lax.dot_general(grad_in, weight, (((1,), (1,)), ((), ())), preferred_element_type=F32)


def turn(block):
    return block.astype(F32).T.astype(BF16)


def col_sum(block):
    return jnp.sum(block.astype(F32), axis=0, keepdims=True)


def lane_mean(block):
    return jnp.mean(block, axis=-1, keepdims=True)


def smooth_slope(block):
    sigma = jax.nn.sigmoid(block)
    return sigma * (1.0 + block * (1.0 - sigma))


def norm_fwd(block):
    centred = block - lane_mean(block)
    inv_std = lax.rsqrt(lane_mean(centred * centred) + NORM_EPS)
    return centred * inv_std, inv_std


def norm_back(grad_in, normed, inv_std, gain):
    scaled = grad_in * gain
    inner, cross = lane_mean(scaled), lane_mean(scaled * normed)
    return inv_std * (scaled - inner - normed * cross)


def vector(small_ref, row, size):
    half = size // 2
    return jnp.concatenate(
        [small_ref[core, row : row + 1, :half] for core in range(2)], axis=1
    )


def put_vector(small_ref, row, value):
    half = value.shape[1] // 2
    for core in range(2):
        small_ref[core, row : row + 1, :half] = value[:, core * half : (core + 1) * half]


def place():
    own, core = lax.axis_index("ctx"), lax.axis_index("ws")
    return own, core


def others_of(own, core, count):
    return [(lax.rem(own + gap, count), core) for gap in range(1, count)]


def widened(dst_ref, src_ref):
    @pl.loop(0, 2)
    def _(core):
        dst_ref[core] = src_ref[core].astype(BF16).astype(F32)


def turned_segments(out_ref, first, row):
    for step in range(row.shape[1] // LANES):
        part = row[:, step * LANES : (step + 1) * LANES].astype(F32)
        here = pl.ds(bound(first + step * LANES, LANES), LANES)
        out_ref[here, :] = jnp.broadcast_to(part, (LANES, LANES)).T


def mark_segments(marks, columns, seg_ref):
    count, _, rows = seg_ref.shape

    @pl.loop(0, count)
    def _(source):
        row = seg_ref[source].astype(F32)
        for step in range(rows // LANES):
            part = jnp.broadcast_to(row[:, step * LANES : (step + 1) * LANES], (LANES, LANES)).T
            number = lax.broadcasted_iota(jnp.int32, (LANES, LANES), 1).astype(F32)
            here = pl.ds(bound(source * rows + step * LANES, LANES), LANES)
            columns[here, :] = part
            marks[here, :] = jnp.where(part == number, 1.0, 0.0).astype(BF16)


WEIGHT_COLUMNS = [
    (0, GLU, 1024, 1, False),
    (1, LEFT, 2048, 1, False),
    (2, CONV, 256, 3, False),
    (3, POINT, 256, 4, False),
    (4, QKV, 1536, 1, False),
    (5, ATTN, 512, 1, True),
    (6, EXPAND, 2048, 1, True),
    (7, SHRINK, 512, 4, True),
]


def tap_masks(mask_ref, seg_ref):
    seg = seg_ref[...]
    for tap in range(TAPS):
        moved = pltpu.roll(seg, (REACH - tap) % seg.shape[0], 0)
        mask_ref[tap] = jnp.where(moved == seg, 1.0, 0.0).astype(F32)


def first_body(
    count,
    heads,
    tok_ref,
    seg_row_ref,
    *refs,
):
    vectors, refs = refs[: len(VECTORS)], refs[len(VECTORS) :]
    weights, refs = refs[:8], refs[8:]
    outs, refs = refs[:19], refs[19:]
    (
        late_out,
        early_out,
        small_out,
        seg_all,
        plan_out,
        q_out,
        kv_out,
        n1_out,
        glu_out,
        n2_out,
        left_out,
        conv_out,
        n3_out,
        depth_out,
        n4_out,
        x2_out,
        inv_out,
        masks_out,
        seg_out,
    ) = outs
    (
        staged,
        late,
        early,
        edges,
        seg_edges,
        seg_col,
        small_own,
        x_ext,
        seg_ext,
        masks,
        small,
        low_ext,
        n1,
        glu_pre,
        x1,
        n2,
        shifted,
        left_pre,
        conv_pre,
        n3,
        g3,
        depth,
        x2,
        n4,
        inv,
        q_turned,
        kv_own,
        marks,
        columns,
        load_sem,
        out_sem,
        ws_send,
        ws_recv,
        edge_send,
        edge_recv,
        row_send,
        row_recv,
        q_send,
        q_recv,
        kv_send,
        kv_recv,
        pass_send,
        pass_recv,
    ) = refs
    own, core = place()
    parts = count // heads
    head, part = own // parts, lax.rem(own, parts)
    rows = tok_ref.shape[0]
    ext = rows + 2 * EDGE
    mid = slice(EDGE, EDGE + rows)
    sibling = (own, 1 - core)
    peers = others_of(own, core, count)

    loads, column = [], 0
    stage_at = []
    for number, first, width, blocks, _ in WEIGHT_COLUMNS:
        stage_at.append(column)
        for block in range(blocks):
            source = weights[number]
            if blocks == 3:
                source = source.at[block]
            elif blocks > 1:
                source = source.at[pl.ds(block * BLOCK, BLOCK), :]
            loads.append(
                pltpu.make_async_copy(
                    source,
                    staged.at[:, pl.ds(column, width)],
                    load_sem.at[len(loads)],
                )
            )
            if number < 3:
                loads[-1].start()
            column += width
    small_own[...] = jnp.zeros_like(small_own)
    for (row, tall, size), vector_ref in zip(VECTORS, vectors):
        small_own[row : row + tall, :size] = vector_ref[...]
    turned_segments(seg_col, 0, seg_row_ref[...])
    greet([sibling] + peers)
    for load in loads[5:]:
        load.start()

    copies = []
    right, left = (lax.rem(own + 1, count), core), (lax.rem(own + count - 1, count), core)
    edge_copies = [
        push(tok_ref.at[pl.ds(rows - EDGE, EDGE), :], edges.at[0], (edge_send, edge_recv), 0, right),
        push(tok_ref.at[pl.ds(0, EDGE), :], edges.at[1], (edge_send, edge_recv), 1, left),
        push(seg_col.at[pl.ds(rows - EDGE, EDGE), :], seg_edges.at[0], (edge_send, edge_recv), 2, right),
        push(seg_col.at[pl.ds(0, EDGE), :], seg_edges.at[1], (edge_send, edge_recv), 3, left),
    ]
    small_copy = push(small_own, small_out.at[core], (ws_send, ws_recv), len(WEIGHT_COLUMNS), sibling)
    small_out[core] = small_own[...]

    at, weight_copies = 0, []
    for (number, first, width, blocks, is_early), column in zip(WEIGHT_COLUMNS, stage_at):
        target = early if is_early else late
        for _ in range(blocks):
            loads[at].wait()
            at += 1
        size = width * blocks
        mine = pl.ds(bound(core * BLOCK, BLOCK), BLOCK)

        @pl.loop(0, BLOCK // ROW_BLOCK)
        def _(step):
            source = staged[span(step, ROW_BLOCK), pl.ds(column, size)]
            goes = pl.ds(bound(core * BLOCK + step * ROW_BLOCK, ROW_BLOCK), ROW_BLOCK)
            target[goes, pl.ds(first, size)] = source.astype(BF16)

        piece = target.at[mine, pl.ds(first, size)]
        weight_copies.append(push(piece, piece, (ws_send, ws_recv), number, sibling))

    for copy in edge_copies:
        copy.wait()
    small_copy.wait()
    row_copies = [
        push(seg_row_ref, seg_all.at[own], (row_send, row_recv), gap, peer)
        for gap, peer in enumerate(peers)
    ]
    seg_all[own] = seg_row_ref[...]
    widened(small, small_out)

    x_ext[:EDGE, :] = edges[0].astype(F32)
    x_ext[mid, :] = tok_ref[...].astype(F32)
    x_ext[EDGE + rows :, :] = edges[1].astype(F32)
    seg_ext[:EDGE, :] = jnp.where(own == 0, -1.0, seg_edges[0])
    seg_ext[mid, :] = seg_col[...]
    seg_ext[EDGE + rows :, :] = jnp.where(own == count - 1, -1.0, seg_edges[1])
    tap_masks(masks, seg_ext)

    normed, inv_std = norm_fwd(x_ext[...])
    n1[...] = normed[mid, :]
    inv[0] = jnp.broadcast_to(inv_std, (ext, LANES))
    low_ext[...] = (normed * vector(small, LN1G, D) + vector(small, LN1B, D)).astype(BF16)

    weight_copies[0].wait()
    glu_bias = vector(small, GLUB, 2 * D)
    for step in range(2 * D // 512):
        cols = slice(512 * step, 512 * (step + 1))
        glu_pre[:, cols] = (
            matmul(low_ext[...], late[:, GLU + 512 * step : GLU + 512 * (step + 1)])
            + glu_bias[:, cols]
        )
    state = x_ext[...] + glu_pre[:, :D] * jax.nn.sigmoid(glu_pre[:, D:])
    x1[...] = state[mid, :]
    normed, inv_std = norm_fwd(state)
    n2[...] = normed[mid, :]
    inv[1] = jnp.broadcast_to(inv_std, (ext, LANES))
    low_f = (normed * vector(small, LN2G, D) + vector(small, LN2B, D)).astype(BF16).astype(F32)
    before = pltpu.roll(low_f, 1, 0) * jnp.concatenate([masks[REACH - 1]] * (D // LANES), axis=1)
    after = pltpu.roll(low_f, ext - 1, 0) * jnp.concatenate([masks[REACH + 1]] * (D // LANES), axis=1)
    shifted[0] = before.astype(BF16)
    shifted[1] = low_f.astype(BF16)
    shifted[2] = after.astype(BF16)

    weight_copies[1].wait()

    @pl.loop(0, FF // 512)
    def _(step):
        weight = late[:, pl.ds(bound(LEFT + step * 512, 512), 512)]
        left_pre[:, span(step, 512)] = matmul(shifted[1], weight)

    weight_copies[2].wait()
    conv_sum = vector(small, CONVB, HALF)
    for tap in range(3):
        conv_sum = conv_sum + matmul(
            shifted[tap], late[:, CONV + HALF * tap : CONV + HALF * (tap + 1)]
        )
    conv_pre[...] = conv_sum

    left_bias = vector(small, LEFTB, FF)
    gain, shift = vector(small, LN3G, FF), vector(small, LN3B, FF)

    @pl.loop(0, ext // ROW_BLOCK)
    def _(step):
        here = span(step, ROW_BLOCK)
        pre = left_pre[here, :] + left_bias
        left_pre[here, :] = pre
        mixed = jax.nn.silu(pre)
        mixed = jnp.concatenate(
            [mixed[:, :HALF] + jax.nn.silu(conv_pre[here, :]), mixed[:, HALF:]], axis=1
        )
        normed, inv_std = norm_fwd(mixed)
        n3[here, :] = normed
        inv[2, here, :] = jnp.broadcast_to(inv_std, (ROW_BLOCK, LANES))
        g3[here, :] = (normed * gain + shift).astype(BF16).astype(F32)

    saves = [
        move(n1, n1_out, out_sem.at[0]),
        move(glu_pre.at[pl.ds(EDGE, rows), :], glu_out, out_sem.at[1]),
        move(n2, n2_out, out_sem.at[2]),
        move(left_pre.at[pl.ds(EDGE, rows), :], left_out, out_sem.at[3]),
        move(conv_pre, conv_out, out_sem.at[4]),
        move(n3, n3_out, out_sem.at[5]),
    ]

    @pl.loop(0, FF // LANES)
    def _(step):
        cols = span(step, LANES)
        block = g3[:, cols]
        total = jnp.zeros((rows, LANES), F32)
        for tap in range(TAPS):
            row = DEPTH + tap
            moved = pltpu.roll(block, (REACH - tap) % ext, 0)[mid, :]
            half = FF // 2 // LANES
            taps = small[step // half, row : row + 1, span(lax.rem(step, half), LANES)]
            total = total + moved * masks[tap, mid, :] * taps
        depth[:, cols] = total.astype(BF16)

    saves.append(move(depth, depth_out, out_sem.at[6]))
    weight_copies[3].wait()
    sep = vector(small, POINTB, HALF)
    for side in range(2):
        for block in range(4):
            first = side * (FF // 2) + block * BLOCK
            sep = sep + matmul(
                depth[:, first : first + BLOCK],
                late[side * BLOCK : (side + 1) * BLOCK, POINT + HALF * block : POINT + HALF * (block + 1)],
            )
    state = jnp.concatenate([x1[:, :HALF] + sep, x1[:, HALF:]], axis=1)
    x2[...] = state
    normed, inv_std = norm_fwd(state)
    n4[...] = normed
    inv[3, :rows, :] = jnp.broadcast_to(inv_std, (rows, LANES))
    low = (normed * vector(small, LN4G, D) + vector(small, LN4B, D)).astype(BF16)
    weight_copies[4].wait()
    for step in range(D // 256):
        cols = slice(256 * step, 256 * (step + 1))
        query = matmul(low, late[:, QKV + 256 * step : QKV + 256 * (step + 1)])
        q_turned[cols, :] = turn(query)
    near = lax.broadcasted_iota(jnp.int32, (rows, LANES), 1) < HEAD_DIM
    for step in range(D // LANES):
        first = QKV + D + LANES * step
        keys = matmul(low, late[:, first : first + LANES])
        values = matmul(low, late[:, first + D : first + D + LANES])
        kv_own[:, 2 * step * LANES : (2 * step + 1) * LANES] = jnp.where(
            near, keys, pltpu.roll(values, HEAD_DIM, 1)
        ).astype(BF16)
        kv_own[:, (2 * step + 1) * LANES : (2 * step + 2) * LANES] = jnp.where(
            near, pltpu.roll(keys, HEAD_DIM, 1), values
        ).astype(BF16)

    q_slot = q_out.at[:, span(head, rows)]
    kv_slot = kv_out.at[span(own, rows), pl.ds(0, LANES)]
    arriving = []
    for gap in range(1, heads):
        other = lax.rem(head + gap, heads)
        arriving.append(
            push(kv_own.at[:, span(other, LANES)], kv_slot, (kv_send, kv_recv), gap - 1, (other * parts + part, core))
        )
    twins = [(head * parts + lax.rem(part + gap, parts), core) for gap in range(1, parts)]
    for at, twin in enumerate(twins):
        copies.append(
            push(kv_own.at[:, span(head, LANES)], kv_slot, (pass_send, pass_recv), at * heads, twin)
        )
    for gap in range(1, heads):
        other = lax.rem(head + gap, heads)
        copies.append(
            push(q_turned.at[span(other, HEAD_DIM), :], q_slot, (q_send, q_recv), gap - 1, (other * parts + part, core))
        )
    saves.append(move(q_turned.at[span(head, HEAD_DIM), :], q_slot, out_sem.at[7]))
    saves.append(move(kv_own.at[:, span(head, LANES)], kv_slot, out_sem.at[8]))
    saves.append(move(n4, n4_out, out_sem.at[9]))
    saves.append(move(x2, x2_out, out_sem.at[10]))
    saves.append(move(inv, inv_out, out_sem.at[11]))
    saves.append(move(masks, masks_out, out_sem.at[14]))
    for copy in row_copies:
        copy.wait()
    lane = lax.broadcasted_iota(jnp.int32, (1, LANES), 1)
    every = seg_all[:, 0, :]
    for tile in range(heads):
        source = tile * parts + part
        mine = seg_all[source]
        first = jnp.min(mine, axis=1, keepdims=True)
        last = jnp.max(mine, axis=1, keepdims=True)
        below = jnp.sum(jnp.sum((every < first).astype(F32), axis=0, keepdims=True), axis=1, keepdims=True).astype(jnp.int32)
        upto = jnp.sum(jnp.sum((every <= last).astype(F32), axis=0, keepdims=True), axis=1, keepdims=True).astype(jnp.int32)
        plan_out[tile : tile + 1, :] = jnp.where(
            lane == 0, below, jnp.where(lane == 1, upto, source)
        )
    mark_segments(marks, columns, seg_all)
    saves.append(move(columns, seg_out, out_sem.at[16]))
    saves.append(move(marks, kv_out.at[:, pl.ds(LANES, LANES)], out_sem.at[15]))
    for copy in weight_copies[5:]:
        copy.wait()
    saves.append(move(late, late_out, out_sem.at[12]))
    saves.append(move(early, early_out, out_sem.at[13]))
    for gap in range(1, heads):
        arriving[gap - 1].wait()
        source = lax.rem(head + heads - gap, heads) * parts + part
        block = kv_out.at[span(source, rows), pl.ds(0, LANES)]
        for at, twin in enumerate(twins):
            copies.append(push(block, block, (pass_send, pass_recv), at * heads + gap, twin))

    for copy in copies + saves:
        copy.wait()


def first_kernel(tokens, seg_row, vectors, weights, count, heads):
    rows = tokens.shape[0]
    ext = rows + 2 * EDGE
    parts = count // heads
    late = (2 * BLOCK, SMALL)
    early = (2 * BLOCK, EARLY)
    out_shape = (
        shaped(late, BF16),
        shaped(early, BF16),
        shaped((2, SMALL_ROWS, SMALL_WIDTH)),
        shaped((count, 1, rows), jnp.int32),
        shaped((heads, LANES), jnp.int32),
        shaped((HEAD_DIM, heads * rows), BF16),
        shaped((count * rows, 2 * LANES), BF16),
        shaped((rows, D)),
        shaped((rows, 2 * D)),
        shaped((rows, D)),
        shaped((rows, FF)),
        shaped((ext, HALF)),
        shaped((ext, FF)),
        shaped((rows, FF), BF16),
        shaped((rows, D)),
        shaped((rows, D)),
        shaped((4, ext, LANES)),
        shaped((TAPS, ext, LANES)),
        shaped((count * rows, LANES)),
    )
    out_specs = (
        [any_spec()] * 2 + [vmem_spec()] * 3 + [any_spec()] * 14
    )
    scratch = [
        pltpu.VMEM((BLOCK, SMALL + EARLY), F32),
        pltpu.VMEM(late, BF16),
        pltpu.VMEM(early, BF16),
        pltpu.VMEM((2, EDGE, D), BF16),
        pltpu.VMEM((2, EDGE, LANES), F32),
        pltpu.VMEM((rows, LANES), F32),
        pltpu.VMEM((SMALL_ROWS, SMALL_WIDTH), F32),
        pltpu.VMEM((ext, D), F32),
        pltpu.VMEM((ext, LANES), F32),
        pltpu.VMEM((TAPS, ext, LANES), F32),
        pltpu.VMEM((2, SMALL_ROWS, SMALL_WIDTH), F32),
        pltpu.VMEM((ext, D), BF16),
        pltpu.VMEM((rows, D), F32),
        pltpu.VMEM((ext, 2 * D), F32),
        pltpu.VMEM((rows, D), F32),
        pltpu.VMEM((rows, D), F32),
        pltpu.VMEM((3, ext, D), BF16),
        pltpu.VMEM((ext, FF), F32),
        pltpu.VMEM((ext, HALF), F32),
        pltpu.VMEM((ext, FF), F32),
        pltpu.VMEM((ext, FF), F32),
        pltpu.VMEM((rows, FF), BF16),
        pltpu.VMEM((rows, D), F32),
        pltpu.VMEM((rows, D), F32),
        pltpu.VMEM((4, ext, LANES), F32),
        pltpu.VMEM((D, rows), BF16),
        pltpu.VMEM((rows, 2 * D), BF16),
        pltpu.VMEM((count * rows, LANES), BF16),
        pltpu.VMEM((count * rows, LANES), F32),
        pltpu.SemaphoreType.DMA((sum(item[3] for item in WEIGHT_COLUMNS),)),
        pltpu.SemaphoreType.DMA((17,)),
    ]
    scratch += sem_pair(len(WEIGHT_COLUMNS) + 1) + sem_pair(4) + sem_pair(count - 1)
    scratch += sem_pair(heads - 1) + sem_pair(heads - 1) + sem_pair((parts - 1) * heads)
    return pl.pallas_call(
        functools.partial(first_body, count, heads),
        out_shape=out_shape,
        in_specs=[vmem_spec()] * (2 + len(vectors)) + [any_spec()] * 8,
        out_specs=out_specs,
        scratch_shapes=scratch,
        compiler_params=comm_params(1),
        name="first_layers",
    )(tokens, seg_row, *vectors, *weights)


def turn_keys(kv_ref, turned):
    @pl.loop(0, kv_ref.shape[0] // KEY_TILE)
    def _(tile):
        here = span(tile, KEY_TILE)
        turned[:, here] = turn(kv_ref[here, :LANES])


def other_segments(seg_q):
    number = lax.broadcasted_iota(jnp.int32, (LANES, seg_q.shape[1]), 0)
    return jnp.where(number == seg_q, 0.0, MASK_FILL).astype(BF16)


def key_tiles(plan_ref, tile):
    return plan_ref[tile, 0] // KEY_TILE, (plan_ref[tile, 1] + KEY_TILE - 1) // KEY_TILE


def attend_body(rows, plan_ref, q_ref, kv_ref, seg_ref, o_ref, low_ref, lse_ref, turned):
    turn_keys(kv_ref, turned)

    @pl.loop(0, q_ref.shape[1] // rows)
    def _(tile):
        at = span(tile, rows)
        q = q_ref[:, at] * jnp.bfloat16(HEAD_DIM**-0.5)
        others = other_segments(seg_ref[plan_ref[tile, 2]])
        q_pad = jnp.concatenate([q, jnp.zeros_like(q), others], axis=0)

        def block(key_tile, carry):
            top, total, acc = carry
            here = span(key_tile, KEY_TILE)
            scores = matmul(kv_ref[here, :], q_pad)
            new_top = jnp.maximum(top, jnp.max(scores, axis=0, keepdims=True))
            probs = jnp.exp(scores - new_top)
            shrink = jnp.exp(top - new_top)
            total = total * shrink + jnp.sum(probs, axis=0, keepdims=True)
            acc = acc * shrink + matmul(turned[HEAD_DIM:, here], probs.astype(BF16))
            return (new_top, total, acc)

        first, end = key_tiles(plan_ref, tile)
        top, total, acc = lax.fori_loop(
            first,
            end,
            block,
            (
                jnp.full((1, rows), MASK_FILL, F32),
                jnp.zeros((1, rows), F32),
                jnp.zeros((HEAD_DIM, rows), F32),
            ),
        )
        out = acc / total
        o_ref[:, at] = out
        low_ref[:, at] = out.astype(BF16)
        lse_ref[:, at] = top + jnp.log(total)


def attend(plan, q_t, kv, seg, rows):
    return pl.pallas_call(
        functools.partial(attend_body, rows),
        out_shape=(shaped(q_t.shape), shaped(q_t.shape, BF16), shaped((1, q_t.shape[1]))),
        in_specs=[smem_spec()] + [vmem_spec()] * 3,
        out_specs=(vmem_spec(),) * 3,
        scratch_shapes=[pltpu.VMEM((LANES, kv.shape[0]), BF16)],
        compiler_params=pltpu.CompilerParams(vmem_limit_bytes=VMEM_MOST),
        name="attend",
    )(plan, q_t, kv, seg)


def attend_back_body(
    rows, plan_ref, q_ref, do_ref, o_ref, lse_ref, seg_ref, kv_in, seg_in, dq_ref, dkv_ref, kv_ref, segk, turned, dkv_acc, sems
):
    loads = [
        move(kv_in.at[:, pl.ds(0, LANES)], kv_ref, sems.at[0]),
        move(seg_in, segk, sems.at[1]),
    ]
    dkv_acc[...] = jnp.zeros_like(dkv_acc)
    loads[0].wait()
    turn_keys(kv_ref, turned)
    loads[1].wait()
    scale = HEAD_DIM**-0.5

    @pl.loop(0, q_ref.shape[1] // rows)
    def _(tile):
        at = span(tile, rows)
        q = q_ref[:, at] * jnp.bfloat16(scale)
        do = do_ref[:, at]
        none = jnp.zeros_like(q)
        both = jnp.concatenate(
            [jnp.concatenate([q, none], axis=1), jnp.concatenate([none, do], axis=1)], axis=0
        )
        delta = jnp.sum(o_ref[:, at] * do.astype(F32), axis=0, keepdims=True)
        lse = lse_ref[:, at]
        seg_q = seg_ref[plan_ref[tile, 2]].astype(F32)

        def block(key_tile, dq):
            here = span(key_tile, KEY_TILE)
            pair = matmul(kv_ref[here, :], both)
            seg_k = jnp.concatenate([segk[here, :]] * (rows // LANES), axis=1)
            scores = jnp.where(seg_k == seg_q, pair[:, :rows], MASK_FILL)
            probs = jnp.exp(scores - lse)
            score_grad = (probs * (pair[:, rows:] - delta)).astype(BF16)
            joined = jnp.concatenate([score_grad, probs.astype(BF16)], axis=1)
            dkv_acc[here, :] += back_mul(joined, both)
            return dq + matmul(turned[:HEAD_DIM, here], score_grad)

        first, end = key_tiles(plan_ref, tile)
        dq = lax.fori_loop(first, end, block, jnp.zeros((HEAD_DIM, rows), F32))
        dq_ref[:, at] = (dq * scale).astype(BF16)

    dkv_ref[...] = dkv_acc[...].astype(BF16)


def attend_back(plan, q_t, do_t, o_t, lse, seg, kv, seg_cols, rows):
    return pl.pallas_call(
        functools.partial(attend_back_body, rows),
        out_shape=(shaped(q_t.shape, BF16), shaped((kv.shape[0], LANES), BF16)),
        in_specs=[smem_spec()] + [vmem_spec()] * 5 + [any_spec()] * 2,
        out_specs=(vmem_spec(),) * 2,
        scratch_shapes=[
            pltpu.VMEM((kv.shape[0], LANES), BF16),
            pltpu.VMEM((kv.shape[0], LANES), F32),
            pltpu.VMEM((LANES, kv.shape[0]), BF16),
            pltpu.VMEM((kv.shape[0], LANES), F32),
            pltpu.SemaphoreType.DMA((2,)),
        ],
        compiler_params=pltpu.CompilerParams(vmem_limit_bytes=VMEM_MOST),
        name="attend_back",
    )(plan, q_t, do_t, o_t, lse, seg, kv, seg_cols)


def middle_body(
    count,
    heads,
    o_in,
    out_grad_in,
    small_in,
    x2_in,
    early_in,
    out_ref,
    small_grads,
    dx3_out,
    grads_out,
    do_out,
    out_grad,
    small_raw,
    weights,
    x2,
    small,
    o_t,
    x3,
    expand_pre,
    hidden,
    dpre,
    do_t,
    grads,
    dx3,
    load_sem,
    o_send,
    o_recv,
    do_send,
    do_recv,
):
    own, core = place()
    parts = count // heads
    head, part = own // parts, lax.rem(own, parts)
    rows = out_grad.shape[0]
    slot = o_t.at[span(head, HEAD_DIM), :]
    loads = [
        move(o_in.at[:, span(head, rows)], slot, load_sem.at[2]),
        move(small_in, small_raw, load_sem.at[3]),
        move(x2_in, x2, load_sem.at[1]),
        move(early_in, weights, load_sem.at[0]),
        move(out_grad_in, out_grad, load_sem.at[4]),
    ]
    near = [lax.rem(head + gap, heads) for gap in range(1, heads)]
    peers = [(other * parts + part, core) for other in near]
    greet(peers)
    copies = [
        push(o_in.at[:, span(other, rows)], slot, (o_send, o_recv), gap, peer)
        for gap, (other, peer) in enumerate(zip(near, peers))
    ]
    small_grads[...] = jnp.zeros_like(small_grads)
    for copy in loads:
        copy.wait()
    widened(small, small_raw)
    for copy in copies:
        copy.wait()

    state = (
        x2[...]
        + matmul(turn(o_t[...]), weights[:, ATTN : ATTN + D])
        + vector(small, ATTNB, D)
    )
    x3[...] = state
    normed, inv_std = norm_fwd(state)
    gain = vector(small, LN5G, D)
    low = (normed * gain + vector(small, LN5B, D)).astype(BF16)
    expand_bias = vector(small, EXPANDB, FF)
    for step in range(FF // 512):
        cols = slice(512 * step, 512 * (step + 1))
        pre = matmul(low, weights[:, EXPAND + 512 * step : EXPAND + 512 * (step + 1)]) + expand_bias[:, cols]
        expand_pre[:, cols] = pre
        hidden[:, cols] = jax.nn.silu(pre).astype(BF16)
    state = x3[...] + vector(small, SHRINKB, D)
    for block in range(FF // BLOCK):
        side, column = block // 4, SHRINK + D * (block % 4)
        state = state + matmul(
            hidden[:, block * BLOCK : (block + 1) * BLOCK],
            weights[side * BLOCK : (side + 1) * BLOCK, column : column + D],
        )
    out_ref[...] = state.astype(BF16)

    dz = out_grad[...]
    for block in range(FF // BLOCK):
        side, column = block // 4, SHRINK + D * (block % 4)
        cols = slice(block * BLOCK, (block + 1) * BLOCK)
        grad = back_mul(dz, weights[side * BLOCK : (side + 1) * BLOCK, column : column + D])
        dpre[:, cols] = (grad * smooth_slope(expand_pre[:, cols])).astype(BF16)
    grad = jnp.concatenate(
        [
            back_mul(dpre[...], weights[side * BLOCK : (side + 1) * BLOCK, EXPAND : EXPAND + FF])
            for side in range(2)
        ],
        axis=1,
    )
    state = dz.astype(F32) + norm_back(grad, normed, inv_std, gain)
    dx3[...] = state
    dy3 = state.astype(BF16)
    do_t[...] = back_mul(weights[:, ATTN : ATTN + D], dy3).astype(BF16)
    slot = do_out.at[:, span(head, rows)]
    copies = [
        push(do_t.at[span(other, HEAD_DIM), :], slot, (do_send, do_recv), gap, peer)
        for gap, (other, peer) in enumerate(zip(near, peers))
    ]
    copies.append(move(do_t.at[span(head, HEAD_DIM), :], slot, load_sem.at[0]))
    copies.append(move(dx3, dx3_out, load_sem.at[1]))

    put_vector(small_grads, LN5G, col_sum(grad * normed))
    put_vector(small_grads, LN5B, col_sum(grad))
    put_vector(small_grads, ATTNB, col_sum(dy3))
    put_vector(small_grads, EXPANDB, col_sum(dpre[...]))
    put_vector(small_grads, SHRINKB, col_sum(dz))
    for block in range(FF // BLOCK):
        side, column = block // 4, SHRINK + D * (block % 4)
        grads[side * BLOCK : (side + 1) * BLOCK, column : column + D] = matmul(
            turn(hidden[:, block * BLOCK : (block + 1) * BLOCK]), dz
        ).astype(BF16)
    grads[:, ATTN : ATTN + D] = matmul(o_t[...], dy3).astype(BF16)
    low_t = turn(low)
    for step in range(FF // 512):
        grads[:, EXPAND + 512 * step : EXPAND + 512 * (step + 1)] = matmul(
            low_t, dpre[:, 512 * step : 512 * (step + 1)]
        ).astype(BF16)
    copies.append(move(grads, grads_out, load_sem.at[2]))
    for copy in copies:
        copy.wait()


def middle_kernel(o_low, out_grad, small, x2, early, count, heads):
    rows = out_grad.shape[0]
    return pl.pallas_call(
        functools.partial(middle_body, count, heads),
        out_shape=(
            shaped((rows, D), BF16),
            shaped((2, SMALL_ROWS, SMALL_WIDTH)),
            shaped((rows, D)),
            shaped(early.shape, BF16),
            shaped((HEAD_DIM, heads * rows), BF16),
        ),
        in_specs=[any_spec()] * 5,
        out_specs=[vmem_spec()] * 2 + [any_spec()] * 3,
        scratch_shapes=[
            pltpu.VMEM((rows, D), BF16),
            pltpu.VMEM((2, SMALL_ROWS, SMALL_WIDTH), F32),
            pltpu.VMEM(early.shape, BF16),
            pltpu.VMEM((rows, D), F32),
            pltpu.VMEM((2, SMALL_ROWS, SMALL_WIDTH), F32),
            pltpu.VMEM((D, rows), BF16),
            pltpu.VMEM((rows, D), F32),
            pltpu.VMEM((rows, FF), F32),
            pltpu.VMEM((rows, FF), BF16),
            pltpu.VMEM((rows, FF), BF16),
            pltpu.VMEM((D, rows), BF16),
            pltpu.VMEM(early.shape, BF16),
            pltpu.VMEM((rows, D), F32),
            pltpu.SemaphoreType.DMA((5,)),
        ]
        + sem_pair(heads - 1)
        + sem_pair(heads - 1),
        compiler_params=comm_params(2),
        name="middle_layers",
    )(o_low, out_grad, small, x2, early)


def column_groups(first, width, bits):
    tiles = width // LANES
    unit = 2 ** max(0, bits - 4)
    long = max(1, round(tiles * 0.36 / unit)) * unit
    orders = [
        list(range(bits)),
        [1, 0] + list(range(2, bits)),
        list(range(2, bits)) + [0, 1],
    ]
    groups = []
    for size, order in zip([long, long, tiles - 2 * long], orders):
        if size == 0:
            continue
        groups.append((first, size * LANES, order))
        first += size * LANES
    return groups


def grad_sets(bits):
    bounds = [LATE, LATE + SHRINK, QKV, POINT, LEFT, LEFT + FF // 2, CONV, CONV + FF // 2]
    widths = [SHRINK, EARLY - SHRINK, POINT - QKV, LEFT - POINT] + [FF // 2] * 4
    return [column_groups(first, width, bits) for first, width in zip(bounds, widths)]


class Piece:
    def __init__(self, at, group, links, sums, got, total, sems):
        self.at, (self.first, self.width, self.order) = at, group
        self.core, self.sibling, self.bit_of, self.partner = links
        self.view, self.got, self.total, self.sems = sums, got, total, sems
        self.bits, self.phase, self.trail = len(self.order), 0, []
        self.since = -1
        self.copy = None

    def whole(self):
        return (0, BLOCK, self.first, self.width)

    def out(self, where):
        row, tall, col, wide = where
        return self.total.at[pl.ds(bound(row, ROW_BLOCK), tall), pl.ds(bound(col, LANES), wide)]

    def start(self, other_half):
        self.copy = push(other_half, self.out(self.whole()), self.sems[0], self.at, self.sibling)

    def add(self, where, source, spot, last):
        row, tall, col, wide = where

        @pl.loop(0, tall // ROW_BLOCK)
        def _(step):
            gap = step * ROW_BLOCK
            here = (row + gap, ROW_BLOCK, col, wide)
            there = source.at[pl.ds(bound(spot + gap, ROW_BLOCK), ROW_BLOCK), pl.ds(self.first, wide)]
            mine = self.view(here)[...].astype(F32)
            added = (mine + there[...].astype(F32)).astype(BF16)
            if last:
                self.out(here)[...] = added
            else:
                self.view(here)[...] = added

    def halve(self, step):
        row, tall, col, wide = self.where
        bit = self.order[step]
        mine = self.bit_of[bit]
        if tall > ROW_BLOCK:
            half = tall // 2
            kept = (row + half * mine, half, col, wide)
            sent = (row + half * (1 - mine), half, col, wide)
        else:
            half = wide // 2
            kept = (row, tall, col + half * mine, half)
            sent = (row, tall, col + half * (1 - mine), half)
        self.copy = push(
            self.view(sent),
            self.got.at[pl.ds(self.spot, sent[1]), pl.ds(self.first, sent[3])],
            self.sems[1],
            self.at * self.bits + step,
            self.partner[bit],
        )
        self.where = kept

    def double(self, step):
        place_out = self.out(self.trail[step])
        self.copy = push(
            place_out,
            place_out,
            self.sems[2],
            self.at * self.bits + step,
            self.partner[self.order[step]],
        )

    def done(self):
        return self.phase > 2 * self.bits

    def sent_all(self):
        return self.phase >= 2 * self.bits

    def advance(self):
        if self.done():
            return
        self.copy.wait()
        if self.phase == 0:
            self.where, self.spot = self.whole(), 0
            self.add(self.where, self.total, 0, False)
            self.halve(0)
        elif self.phase <= self.bits:
            last = self.phase == self.bits
            self.add(self.where, self.got, self.spot, last)
            self.trail.append(self.where)
            self.spot += self.where[1]
            if last:
                self.double(self.bits - 1)
            else:
                self.halve(self.phase)
        elif self.phase < 2 * self.bits:
            self.double(2 * self.bits - 1 - self.phase)
        self.phase += 1


def last_body(count, heads, *refs):
    (
        dq_in,
        dkv_in,
        small_in,
        small_grads_in,
        early_grads,
        dx3_in,
        late_in,
        n1_in,
        glu_in,
        n2_in,
        left_in,
        conv_in,
        n3_in,
        depth_in,
        n4_in,
        inv_in,
        masks_in,
        total_out,
        grad_out,
        total,
        weights,
        dx3,
        n1,
        glu_pre,
        n2,
        left_pre,
        conv_pre,
        n3,
        depth,
        n4,
        inv,
        masks,
        small,
        small_grads,
        dq_t,
        dkv_own,
        dkv_mine,
        small_raw,
        shared,
        summed,
        dqkv,
        sep_own,
        sep_edges,
        sep_ext,
        depth_grad,
        g3_grad,
        row_sums,
        dleft,
        conv_grad,
        conv_taps,
        grads,
        early_own,
        got,
        result,
        load_sem,
        keep_sem,
        store_sem,
        dq_send,
        dq_recv,
        dkv_send,
        dkv_recv,
        pass_send,
        pass_recv,
        edge_send,
        edge_recv,
        ws_send,
        ws_recv,
        rs_send,
        rs_recv,
        ag_send,
        ag_recv,
    ) = refs
    own, core = place()
    parts = count // heads
    head, part = own // parts, lax.rem(own, parts)
    rows = dx3.shape[0]
    ext = rows + 2 * EDGE
    mid = slice(EDGE, EDGE + rows)
    sibling = (own, 1 - core)
    peers = others_of(own, core, count)
    bits = count.bit_length() - 1

    sources = (dx3_in, late_in, n4_in, inv_in, depth_in, masks_in, n3_in, left_in, conv_in, n2_in, glu_in, n1_in)
    targets = (dx3, weights, n4, inv, depth, masks, n3, left_pre, conv_pre, n2, glu_pre, n1)
    slot = dq_t.at[span(head, HEAD_DIM), :]
    own_rows = pl.ds(bound(core * BLOCK, BLOCK), BLOCK)
    keeps = [
        move(dkv_in.at[:, part], dkv_mine, keep_sem.at[2]),
        move(early_grads.at[own_rows, :], early_own, keep_sem.at[1]),
        move(dq_in.at[:, span(head, rows)], slot, keep_sem.at[0]),
        move(small_in, small_raw, keep_sem.at[3]),
        move(small_grads_in, small_grads, keep_sem.at[4]),
    ]
    greet([sibling] + peers)
    loads = [move(a, b, load_sem.at[at]) for at, (a, b) in enumerate(zip(sources, targets))]

    bit_of = [lax.rem(own // 2**bit, 2) for bit in range(bits)]
    partner = [(own + 2**bit - 2 * 2**bit * bit_of[bit], core) for bit in range(bits)]
    links = (core, sibling, bit_of, partner)
    sems = ((ws_send, ws_recv), (rs_send, rs_recv), (ag_send, ag_recv))

    def early_view(where):
        row, tall, col, wide = where
        return early_own.at[pl.ds(bound(row, ROW_BLOCK), tall), pl.ds(bound(col - LATE, LANES), wide)]

    def late_view(where):
        row, tall, col, wide = where
        return grads.at[pl.ds(bound(core * BLOCK + row, ROW_BLOCK), tall), pl.ds(bound(col, LANES), wide)]

    sets, at = [], 0
    for number, groups in enumerate(grad_sets(bits)):
        members = []
        for group in groups:
            view = late_view if number > 1 else early_view
            members.append(Piece(at, group, links, view, got, total, sems))
            at += 1
        sets.append(members)
    other_rows = pl.ds(bound((1 - core) * BLOCK, BLOCK), BLOCK)

    def start(members, source, shift):
        for piece in members:
            piece.start(source.at[other_rows, pl.ds(piece.first - shift, piece.width)])

    def advance(members):
        for piece in members:
            piece.advance()

    start(sets[0] + sets[1], early_grads, LATE)
    heads_on = [lax.rem(head + gap, heads) for gap in range(heads)]
    sharing = []
    for gap, other in enumerate(heads_on[1:] + heads_on[:1]):
        for at in range(parts - 1):
            twin = lax.rem(part + at + 1, parts)
            sharing.append(
                push(
                    dkv_in.at[other, twin],
                    shared.at[at, other],
                    (pass_send, pass_recv),
                    at * heads + gap,
                    (head * parts + twin, core),
                )
            )
    collect = []
    for gap, other in enumerate(heads_on[1:]):
        collect.append(
            push(dq_in.at[:, span(other, rows)], slot, (dq_send, dq_recv), gap, (other * parts + part, core))
        )
    for copy in keeps:
        copy.wait()
    widened(small, small_raw)
    advance(sets[0] + sets[1])
    for gap, other in enumerate(heads_on[1:] + heads_on[:1]):
        for copy in sharing[gap * (parts - 1) : (gap + 1) * (parts - 1)]:
            copy.wait()
        total_kv = dkv_mine[other].astype(F32)
        for at in range(parts - 1):
            total_kv = total_kv + shared[at, other].astype(F32)
        if gap < heads - 1:
            summed[other] = total_kv.astype(BF16)
            collect.append(
                push(
                    summed.at[other],
                    dkv_own.at[:, span(head, LANES)],
                    (dkv_send, dkv_recv),
                    gap,
                    (other * parts + part, core),
                )
            )
        else:
            dkv_own[:, span(head, LANES)] = total_kv.astype(BF16)
        if gap == heads // 2:
            advance(sets[0][1:])
    advance(sets[1][1:])
    for copy in loads:
        copy.wait()
    advance(sets[0][:1])
    for copy in collect:
        copy.wait()
    advance(sets[1][:1])

    dqkv[:, :D] = turn(dq_t[...])
    lane = lax.broadcasted_iota(jnp.int32, (rows, LANES), 1) < HEAD_DIM
    for step in range(D // LANES):
        pair = []
        for side in range(2):
            first = (2 * step + side) * LANES
            pair.append(dkv_own[:, first : first + LANES].astype(F32))
        cols = slice(D + step * LANES, D + (step + 1) * LANES)
        dqkv[:, cols] = jnp.where(lane, pair[0], pltpu.roll(pair[1], HEAD_DIM, 1)).astype(BF16)
        cols = slice(2 * D + step * LANES, 2 * D + (step + 1) * LANES)
        dqkv[:, cols] = jnp.where(lane, pltpu.roll(pair[0], HEAD_DIM, 1), pair[1]).astype(BF16)

    def through(grad, column, width):
        return jnp.concatenate(
            [
                back_mul(grad, weights[side * BLOCK : (side + 1) * BLOCK, column : column + width])
                for side in range(2)
            ],
            axis=1,
        )

    def norm_step(grad, normed, inv_std, row):
        put_vector(small_grads, row, col_sum(grad * normed))
        put_vector(small_grads, row + 1, col_sum(grad))
        return norm_back(grad, normed, inv_std, vector(small, row, D))

    grad = through(dqkv[...], QKV, 3 * D)
    dx2 = dx3[...] + norm_step(grad, n4[...], inv[3, :rows, :1], LN4G)
    dx3[...] = dx2
    sep_own[...] = dx2[:, :HALF].astype(BF16)
    right, left = (lax.rem(own + 1, count), core), (lax.rem(own + count - 1, count), core)
    edge_copies = [
        push(sep_own.at[pl.ds(rows - EDGE, EDGE), :], sep_edges.at[0], (edge_send, edge_recv), 0, right),
        push(sep_own.at[pl.ds(0, EDGE), :], sep_edges.at[1], (edge_send, edge_recv), 1, left),
    ]
    advance(sets[0])
    low_t = turn(n4[...] * vector(small, LN4G, D) + vector(small, LN4B, D))
    for step in range(3):
        grads[:, QKV + D * step : QKV + D * (step + 1)] = matmul(
            low_t, dqkv[:, D * step : D * (step + 1)]
        ).astype(BF16)
    start(sets[2], grads, 0)
    for block in range(FF // BLOCK):
        side, column = block // 4, POINT + HALF * (block % 4)
        grads[side * BLOCK : (side + 1) * BLOCK, column : column + HALF] = matmul(
            turn(depth[:, block * BLOCK : (block + 1) * BLOCK]), sep_own[...]
        ).astype(BF16)
    start(sets[3], grads, 0)
    advance(sets[1])
    put_vector(small_grads, POINTB, col_sum(sep_own[...]))

    for copy in edge_copies:
        copy.wait()
    sep_ext[:EDGE, :] = sep_edges[0]
    sep_ext[mid, :] = sep_own[...]
    sep_ext[EDGE + rows :, :] = sep_edges[1]
    for block in range(FF // BLOCK):
        side, column = block // 4, POINT + HALF * (block % 4)
        depth_grad[:, block * BLOCK : (block + 1) * BLOCK] = (
            back_mul(sep_ext[...], weights[side * BLOCK : (side + 1) * BLOCK, column : column + HALF])
            .astype(BF16)
            .astype(F32)
        )

    advance(sets[2])
    advance(sets[0])
    row_sums[...] = jnp.zeros_like(row_sums)
    half = FF // 2 // LANES

    def tap_block(step):
        cols = span(step, LANES)
        side, lanes = step // half, span(lax.rem(step, half), LANES)
        block = depth_grad[:, cols]
        normed = n3[:, cols]
        gain = small[side, LN3G : LN3G + 1, lanes]
        low = (normed[mid, :] * gain + small[side, LN3B : LN3B + 1, lanes]).astype(BF16).astype(F32)
        summed = jnp.zeros((ext, LANES), F32)
        for tap in range(TAPS):
            row = DEPTH + tap
            moved = pltpu.roll(block, (tap - REACH) % ext, 0) * masks[TAPS - 1 - tap]
            summed = summed + moved * small[side, row : row + 1, lanes]
            small_grads[side, row : row + 1, lanes] = col_sum(low * moved[mid, :])
        g3_grad[:, cols] = summed
        small_grads[side, LN3G : LN3G + 1, lanes] = col_sum(summed[mid, :] * normed[mid, :])
        small_grads[side, LN3B : LN3B + 1, lanes] = col_sum(summed[mid, :])
        scaled = summed * gain
        row_sums[0] = row_sums[0] + scaled
        row_sums[1] = row_sums[1] + scaled * normed

    for quarter, turns in enumerate(
        (sets[1] + sets[3], sets[0] + sets[2], sets[1] + sets[3], sets[0] + sets[2])
    ):
        pl.loop(quarter * half // 2, (quarter + 1) * half // 2)(tap_block)
        advance(turns)
    inner = jnp.sum(row_sums[0], axis=1, keepdims=True) * (1.0 / FF)
    cross = jnp.sum(row_sums[1], axis=1, keepdims=True) * (1.0 / FF)
    row_sums[0] = jnp.broadcast_to(inner, (ext, LANES))
    row_sums[1] = jnp.broadcast_to(cross, (ext, LANES))

    def left_block(step):
        cols = span(step, LANES)
        side, lanes = step // half, span(lax.rem(step, half), LANES)
        scaled = g3_grad[mid, cols] * small[side, LN3G : LN3G + 1, lanes]
        mixed_grad = inv[2, mid, :] * (scaled - row_sums[0, mid, :] - n3[mid, cols] * row_sums[1, mid, :])
        low = (mixed_grad * smooth_slope(left_pre[:, cols])).astype(BF16)
        dleft[:, cols] = low
        small_grads[side, LEFTB : LEFTB + 1, lanes] = col_sum(low)

    pl.loop(0, half)(left_block)
    advance(sets[1])
    pl.loop(half, 2 * half)(left_block)
    advance(sets[3] + sets[0])
    for step in range(HALF // LANES):
        cols = slice(step * LANES, (step + 1) * LANES)
        scaled = g3_grad[:, cols] * small[0, LN3G : LN3G + 1, cols]
        mixed_grad = inv[2] * (scaled - row_sums[0] - n3[:, cols] * row_sums[1])
        low = (mixed_grad * smooth_slope(conv_pre[:, cols])).astype(BF16).astype(F32)
        conv_grad[:, cols] = low
        for tap in range(3):
            moved = pltpu.roll(low, (tap - 1) % ext, 0) * masks[REACH + 1 - tap]
            conv_taps[:, HALF * tap + step * LANES : HALF * tap + (step + 1) * LANES] = moved[mid, :].astype(BF16)
    put_vector(small_grads, CONVB, col_sum(conv_grad[mid, :]))

    low_t = turn(n2[...] * vector(small, LN2G, D) + vector(small, LN2B, D))
    for step in range(FF // 512):
        grads[:, LEFT + 512 * step : LEFT + 512 * (step + 1)] = matmul(
            low_t, dleft[:, 512 * step : 512 * (step + 1)]
        ).astype(BF16)
        if step % 2:
            start(sets[4 + step // 2], grads, 0)
    advance(sets[2])
    advance(sets[1])
    for tap in range(3):
        grads[:, CONV + HALF * tap : CONV + HALF * (tap + 1)] = matmul(
            low_t, conv_taps[:, HALF * tap : HALF * (tap + 1)]
        ).astype(BF16)
    advance(sets[4] + sets[5])
    grad = through(dleft[...], LEFT, FF) + through(conv_taps[...], CONV, 3 * HALF)
    dx1 = dx3[...] + norm_step(grad, n2[...], inv[1, mid, :1], LN2G)
    gate = jax.nn.sigmoid(glu_pre[:, D:])
    value_grad = dx1 * gate
    dglu = jnp.concatenate([value_grad, value_grad * glu_pre[:, :D] * (1.0 - gate)], axis=1).astype(BF16)
    put_vector(small_grads, GLUB, col_sum(dglu))
    advance(sets[3])
    advance(sets[0])
    low_t = turn(n1[...] * vector(small, LN1G, D) + vector(small, LN1B, D))
    for step in range(2):
        grads[:, GLU + D * step : GLU + D * (step + 1)] = matmul(
            low_t, dglu[:, D * step : D * (step + 1)]
        ).astype(BF16)
    start(sets[6], grads, 0)
    advance(sets[1] + sets[2])
    grad = through(dglu, GLU, 2 * D)
    result[...] = dx1 + norm_step(grad, n1[...], inv[0, mid, :1], LN1G)
    keep = move(result, grad_out, keep_sem.at[0])
    for side in range(2):
        for block in range(SMALL_WIDTH // BLOCK):
            first = side * BLOCK + block * SMALL_ROWS
            grads[first : first + SMALL_ROWS, SMALL : SMALL + BLOCK] = small_grads[
                side, :, block * BLOCK : (block + 1) * BLOCK
            ].astype(BF16)
        first = side * BLOCK + SMALL_WIDTH // BLOCK * SMALL_ROWS
        grads[first : (side + 1) * BLOCK, SMALL : SMALL + BLOCK] = jnp.zeros(
            ((side + 1) * BLOCK - first, BLOCK), BF16
        )
    start(sets[7], grads, 0)
    advance(sets[4] + sets[5])
    pieces = [piece for number in (0, 3, 1, 2, 6, 7, 4, 5) for piece in sets[number]]
    stores, rounds = [], 0
    while not all(piece.done() for piece in pieces):
        last = all(piece.sent_all() for piece in pieces)
        for piece in pieces:
            if not piece.sent_all():
                piece.advance()
                piece.since = rounds
            elif not piece.done() and (last or piece.since < rounds - 1):
                piece.advance()
                cols = pl.ds(piece.first, piece.width)
                stores.append(move(total.at[:, cols], total_out.at[:, cols], store_sem.at[piece.at]))
        rounds += 1
    for copy in stores:
        copy.wait()
    keep.wait()


def last_kernel(dq, dkv, small, small_grads, tensors, count, heads):
    rows = dkv.shape[0] // count
    ext = rows + 2 * EDGE
    parts = count // heads
    bits = count.bit_length() - 1
    pieces = sum(len(groups) for groups in grad_sets(bits))
    scratch = [
        pltpu.VMEM((BLOCK, WIDTH), BF16),
        pltpu.VMEM(tensors[2].shape, BF16),
        pltpu.VMEM((rows, D), F32),
        pltpu.VMEM((rows, D), F32),
        pltpu.VMEM((rows, 2 * D), F32),
        pltpu.VMEM((rows, D), F32),
        pltpu.VMEM((rows, FF), F32),
        pltpu.VMEM((ext, HALF), F32),
        pltpu.VMEM((ext, FF), F32),
        pltpu.VMEM((rows, FF), BF16),
        pltpu.VMEM((rows, D), F32),
        pltpu.VMEM((4, ext, LANES), F32),
        pltpu.VMEM((TAPS, ext, LANES), F32),
        pltpu.VMEM((2, SMALL_ROWS, SMALL_WIDTH), F32),
        pltpu.VMEM((2, SMALL_ROWS, SMALL_WIDTH), F32),
        pltpu.VMEM((D, rows), BF16),
        pltpu.VMEM((rows, 2 * D), BF16),
        pltpu.VMEM((heads, rows, LANES), BF16),
        pltpu.VMEM((2, SMALL_ROWS, SMALL_WIDTH), F32),
        pltpu.VMEM((parts - 1, heads, rows, LANES), BF16),
        pltpu.VMEM((heads, rows, LANES), BF16),
        pltpu.VMEM((rows, 3 * D), BF16),
        pltpu.VMEM((rows, HALF), BF16),
        pltpu.VMEM((2, EDGE, HALF), BF16),
        pltpu.VMEM((ext, HALF), BF16),
        pltpu.VMEM((ext, FF), F32),
        pltpu.VMEM((ext, FF), F32),
        pltpu.VMEM((2, ext, LANES), F32),
        pltpu.VMEM((rows, FF), BF16),
        pltpu.VMEM((ext, HALF), F32),
        pltpu.VMEM((rows, 3 * HALF), BF16),
        pltpu.VMEM((2 * BLOCK, LATE), BF16),
        pltpu.VMEM((BLOCK, EARLY), BF16),
        pltpu.VMEM((BLOCK + ROW_BLOCK * max(0, bits - 4), WIDTH), BF16),
        pltpu.VMEM((rows, D), F32),
        pltpu.SemaphoreType.DMA((12,)),
        pltpu.SemaphoreType.DMA((5,)),
        pltpu.SemaphoreType.DMA((pieces,)),
    ]
    scratch += sem_pair(heads - 1) + sem_pair(heads - 1) + sem_pair((parts - 1) * heads)
    scratch += sem_pair(2) + sem_pair(pieces)
    scratch += sem_pair(pieces * bits) + sem_pair(pieces * bits)
    return pl.pallas_call(
        functools.partial(last_body, count, heads),
        out_shape=(shaped((BLOCK, WIDTH), BF16), shaped((rows, D))),
        in_specs=[any_spec()] * (4 + len(tensors)),
        out_specs=[any_spec(), any_spec()],
        scratch_shapes=scratch,
        compiler_params=comm_params(3),
        name="last_layers",
    )(dq, dkv.reshape(heads, parts, rows, LANES), small, small_grads, *tensors)


def unpack_body(output_in, grad_in, packed_in, *refs):
    size = len(MATRICES) + len(VECTORS) + 2
    outs, (packed, output, grad, *stages, load_sem, out_sem) = refs[:size], refs[size:]
    output_ref, grad_ref, *outs = outs
    order = [len(MATRICES)] + list(range(len(MATRICES)))
    bounds = [(first, width * blocks) for first, width, blocks in MATRICES] + [(SMALL, BLOCK)]
    loads = {}
    for at in order:
        cols = pl.ds(*bounds[at])
        loads[at] = move(packed_in.at[:, cols], packed.at[:, cols], load_sem.at[at])
    passed = [
        move(output_in, output, load_sem.at[len(MATRICES) + 1]),
        move(grad_in, grad, load_sem.at[len(MATRICES) + 2]),
    ]
    stores = []
    for at, (first, width, blocks) in enumerate(MATRICES):
        loads[at].wait()
        stage = stages[at]
        tall = 2 * ROW_BLOCK

        @pl.loop(0, BLOCK // tall, unroll=2)
        def _(step):
            for block in range(blocks):
                value = packed[span(step, tall), first + block * width : first + (block + 1) * width].astype(F32)
                if blocks == 3:
                    stage[block, span(step, tall), :] = value
                else:
                    stage[pl.ds(bound(block * BLOCK + step * tall, tall), tall), :] = value

        stores.append(move(stage, outs[at], out_sem.at[at]))

    for copy in passed:
        copy.wait()
    stores.append(move(output, output_ref, out_sem.at[len(MATRICES)]))
    stores.append(move(grad, grad_ref, out_sem.at[len(MATRICES) + 1]))
    loads[len(MATRICES)].wait()
    small = jnp.concatenate(
        [
            packed[block * SMALL_ROWS : (block + 1) * SMALL_ROWS, SMALL : SMALL + BLOCK].astype(F32)
            for block in range(SMALL_WIDTH // BLOCK)
        ],
        axis=1,
    )
    for (row, tall, size), out in zip(VECTORS, outs[len(MATRICES) :]):
        out[...] = small[row : row + tall, :size]
    for copy in stores:
        copy.wait()


def unpack(output, grad, packed):
    shapes = []
    for _, width, blocks in MATRICES:
        shapes.append((3, BLOCK, width) if blocks == 3 else (blocks * BLOCK, width))
    vectors = [(tall, size) for _, tall, size in VECTORS]
    return pl.pallas_call(
        unpack_body,
        out_shape=(shaped(output.shape, output.dtype), shaped(grad.shape))
        + tuple(shaped(shape) for shape in shapes + vectors),
        in_specs=[any_spec()] * 3,
        out_specs=[any_spec()] * (2 + len(shapes)) + [vmem_spec()] * len(vectors),
        scratch_shapes=[
            pltpu.VMEM(packed.shape, packed.dtype),
            pltpu.VMEM(output.shape, output.dtype),
            pltpu.VMEM(grad.shape, F32),
        ]
        + [pltpu.VMEM(shape, F32) for shape in shapes]
        + [pltpu.SemaphoreType.DMA((len(shapes) + 3,)), pltpu.SemaphoreType.DMA((len(shapes) + 2,))],
        compiler_params=pltpu.CompilerParams(vmem_limit_bytes=VMEM_MOST),
        name="unpack",
    )(output, grad, packed)


def body(tokens, segment_ids, out_grad, *params):
    (
        ln1g, ln1b, glu_w, glu_b, ln2g, ln2b, left_w, left_b, conv_w, conv_b, ln3g, ln3b, depth_w,
        point_w, point_b, ln4g, ln4b, qkv_w, attn_w, attn_b, ln5g, ln5b, expand_w, expand_b,
        shrink_w, shrink_b,
    ) = params
    count = lax.axis_size("ctx")
    heads = D // HEAD_DIM
    rows = tokens.shape[1]
    vectors = [
        ln1g, ln1b, glu_b, ln2g, ln2b, left_b, conv_b, ln3g, ln3b, depth_w,
        point_b, ln4g, ln4b, attn_b, ln5g, ln5b, expand_b, shrink_b,
    ]
    vectors = [value.reshape(-1, value.shape[-1]) for value in vectors]
    weights = (glu_w, left_w, conv_w, point_w, qkv_w, attn_w, expand_w, shrink_w)
    (
        late, early, small, seg, plan, q_head, kv_head, n1, glu_pre, n2, left_pre, conv_pre, n3,
        depth, n4, x2, inv, masks, seg_cols,
    ) = first_kernel(tokens[0], segment_ids, vectors, weights, count, heads)
    o_head, o_low, log_sum = attend(plan, q_head, kv_head, seg, rows)
    output, small_grads, dx3, early_grads, do_head = middle_kernel(
        o_low, out_grad[0], small, x2, early, count, heads
    )
    dq_head, dkv_head = attend_back(
        plan, q_head, do_head, o_head, log_sum, seg, kv_head, seg_cols, rows
    )
    tensors = (
        early_grads, dx3, late, n1, glu_pre, n2, left_pre, conv_pre, n3, depth, n4, inv, masks,
    )
    total, input_grad = last_kernel(dq_head, dkv_head, small, small_grads, tensors, count, heads)
    output, input_grad, *pieces = unpack(output, input_grad, total)
    matrices, lines = pieces[: len(MATRICES)], pieces[len(MATRICES) :]
    lines = [line if line.shape[0] > 1 else line.reshape(-1) for line in lines]
    g_glu, g_left, g_conv, g_point, g_qkv, g_attn, g_expand, g_shrink = matrices
    (
        g_ln1g, g_ln1b, g_glu_b, g_ln2g, g_ln2b, g_left_b, g_conv_b, g_ln3g, g_ln3b, g_depth,
        g_point_b, g_ln4g, g_ln4b, g_attn_b, g_ln5g, g_ln5b, g_expand_b, g_shrink_b,
    ) = lines
    return (
        output[None], input_grad[None], g_ln1g, g_ln1b, g_glu, g_glu_b, g_ln2g, g_ln2b, g_left,
        g_left_b, g_conv, g_conv_b, g_ln3g, g_ln3b, g_depth, g_point, g_point_b, g_ln4g, g_ln4b,
        g_qkv, g_attn, g_attn_b, g_ln5g, g_ln5b, g_expand, g_expand_b, g_shrink, g_shrink_b,
    )


def solution(mesh):
    return jax.shard_map(
        body,
        mesh=mesh,
        in_specs=(
            P("ws", "ctx", None),
            P("ws", "ctx"),
            P("ws", "ctx", None),
            P("ws"),
            P("ws"),
            P("ws", None),
            P("ws"),
            P("ws"),
            P("ws"),
            P("ws", None),
            P("ws"),
            P(None, "ws", None),
            P("ws"),
            P("ws"),
            P("ws"),
            P(None, "ws"),
            P("ws", None),
            P("ws"),
            P("ws"),
            P("ws"),
            P("ws", None),
            P("ws", None),
            P("ws"),
            P("ws"),
            P("ws"),
            P("ws", None),
            P("ws"),
            P("ws", None),
            P("ws"),
        ),
        out_specs=(
            P("ws", "ctx", None),
            P("ws", "ctx", None),
            P("ws"),
            P("ws"),
            P("ws", None),
            P("ws"),
            P("ws"),
            P("ws"),
            P("ws", None),
            P("ws"),
            P(None, "ws", None),
            P("ws"),
            P("ws"),
            P("ws"),
            P(None, "ws"),
            P("ws", None),
            P("ws"),
            P("ws"),
            P("ws"),
            P("ws", None),
            P("ws", None),
            P("ws"),
            P("ws"),
            P("ws"),
            P("ws", None),
            P("ws"),
            P("ws", None),
            P("ws"),
        ),
        check_vma=False,
    )
```

```python
import functools
import math

import jax
import jax.numpy as jnp
from jax import lax
from jax.experimental import pallas as pl
from jax.experimental.pallas import tpu as pltpu
from jax.sharding import PartitionSpec as P

MESH_ID = pl.DeviceIdType.MESH
F32 = jnp.float32
BF16 = jnp.bfloat16
HEAD_DIM = 64
NORM_EPS = 1e-06
MASK_FILL = -1e30
LANES = 128
ROW_BLOCK = 16
EDGE = 16
KEY_TILE = 1024
BLOCK = 256
VMEM_MOST = 62 * 1024 * 1024

D = 512
FF = 2048
HALF = 256
TAPS = 9
REACH = 4

QKV, POINT, LEFT, CONV, GLU, SMALL, LATE = 0, 1536, 2560, 4608, 5376, 6400, 6656
ATTN, EXPAND, SHRINK, EARLY = 0, 512, 2560, 4608
WIDTH = LATE + EARLY

SMALL_ROWS = 32
SMALL_WIDTH = 1024
(LN1G, LN1B, GLUB, LN2G, LN2B, LEFTB, CONVB, LN3G, LN3B, DEPTH) = range(10)
(POINTB, LN4G, LN4B, ATTNB, LN5G, LN5B, EXPANDB, SHRINKB) = range(DEPTH + TAPS, DEPTH + TAPS + 8)


VECTORS = [
    (LN1G, 1, 256),
    (LN1B, 1, 256),
    (GLUB, 1, 512),
    (LN2G, 1, 256),
    (LN2B, 1, 256),
    (LEFTB, 1, 1024),
    (CONVB, 1, 128),
    (LN3G, 1, 1024),
    (LN3B, 1, 1024),
    (DEPTH, TAPS, 1024),
    (POINTB, 1, 128),
    (LN4G, 1, 256),
    (LN4B, 1, 256),
    (ATTNB, 1, 256),
    (LN5G, 1, 256),
    (LN5B, 1, 256),
    (EXPANDB, 1, 1024),
    (SHRINKB, 1, 256),
]
MATRICES = [
    (GLU, 1024, 1),
    (LEFT, 2048, 1),
    (CONV, 256, 3),
    (POINT, 256, 4),
    (QKV, 1536, 1),
    (LATE + ATTN, 512, 1),
    (LATE + EXPAND, 2048, 1),
    (LATE + SHRINK, 512, 4),
]


def vmem_spec():
    return pl.BlockSpec(memory_space=pltpu.VMEM)


def any_spec():
    return pl.BlockSpec(memory_space=pl.ANY)


def smem_spec():
    return pl.BlockSpec(memory_space=pltpu.SMEM)


def shaped(shape, kind=F32):
    return jax.ShapeDtypeStruct(shape, kind)


def comm_params(number):
    return pltpu.CompilerParams(
        collective_id=number, has_side_effects=True, vmem_limit_bytes=VMEM_MOST
    )


def announce(peers):
    barrier = pltpu.get_barrier_semaphore()
    for peer in peers:
        pl.semaphore_signal(barrier, inc=1, device_id=peer, device_id_type=MESH_ID)


def all_here(peers):
    pl.semaphore_wait(pltpu.get_barrier_semaphore(), len(peers))


def greet(peers):
    announce(peers)
    all_here(peers)


def push(src, dst, sems, at, peer):
    copy = pltpu.make_async_remote_copy(
        src_ref=src,
        dst_ref=dst,
        send_sem=sems[0].at[at],
        recv_sem=sems[1].at[at],
        device_id=peer,
        device_id_type=MESH_ID,
    )
    copy.start()
    return copy


def move(src, dst, sem):
    copy = pltpu.make_async_copy(src, dst, sem)
    copy.start()
    return copy


def sem_pair(count):
    return [pltpu.SemaphoreType.DMA((count,)), pltpu.SemaphoreType.DMA((count,))]


def bound(value, step):
    return value if isinstance(value, int) else pl.multiple_of(value, step)


def span(value, step):
    return pl.ds(bound(value * step, step), step)


def matmul(left_op, right_op):
    return jnp.dot(left_op, right_op, preferred_element_type=F32)


def back_mul(grad_in, weight):
    return lax.dot_general(grad_in, weight, (((1,), (1,)), ((), ())), preferred_element_type=F32)


def turn(block):
    return block.astype(F32).T.astype(BF16)


def col_sum(block):
    return jnp.sum(block.astype(F32), axis=0, keepdims=True)


def lane_mean(block):
    return jnp.mean(block, axis=-1, keepdims=True)


def smooth_slope(block):
    sigma = jax.nn.sigmoid(block)
    return sigma * (1.0 + block * (1.0 - sigma))


def norm_fwd(block):
    centred = block - lane_mean(block)
    inv_std = lax.rsqrt(lane_mean(centred * centred) + NORM_EPS)
    return centred * inv_std, inv_std


def norm_back(grad_in, normed, inv_std, gain):
    scaled = grad_in * gain
    inner, cross = lane_mean(scaled), lane_mean(scaled * normed)
    return inv_std * (scaled - inner - normed * cross)


def vector(small_ref, row, size):
    half = size // 2
    return jnp.concatenate(
        [small_ref[core, row : row + 1, :half] for core in range(2)], axis=1
    )


def put_vector(small_ref, row, value):
    half = value.shape[1] // 2
    for core in range(2):
        small_ref[core, row : row + 1, :half] = value[:, core * half : (core + 1) * half]


def place():
    own, core = lax.axis_index("ctx"), lax.axis_index("ws")
    return own, core


def others_of(own, core, count):
    return [(lax.rem(own + gap, count), core) for gap in range(1, count)]


def widened(dst_ref, src_ref):
    @pl.loop(0, 2)
    def _(core):
        dst_ref[core] = src_ref[core].astype(BF16).astype(F32)


def turned_segments(out_ref, first, row):
    for step in range(row.shape[1] // LANES):
        part = row[:, step * LANES : (step + 1) * LANES].astype(F32)
        here = pl.ds(bound(first + step * LANES, LANES), LANES)
        out_ref[here, :] = jnp.broadcast_to(part, (LANES, LANES)).T


def mark_segments(marks, columns, seg_ref):
    count, _, rows = seg_ref.shape

    @pl.loop(0, count)
    def _(source):
        row = seg_ref[source].astype(F32)
        for step in range(rows // LANES):
            part = jnp.broadcast_to(row[:, step * LANES : (step + 1) * LANES], (LANES, LANES)).T
            number = lax.broadcasted_iota(jnp.int32, (LANES, LANES), 1).astype(F32)
            here = pl.ds(bound(source * rows + step * LANES, LANES), LANES)
            columns[here, :] = part
            marks[here, :] = jnp.where(part == number, 1.0, 0.0).astype(BF16)


WEIGHT_COLUMNS = [
    (0, GLU, 1024, 1, False),
    (1, LEFT, 2048, 1, False),
    (2, CONV, 256, 3, False),
    (3, POINT, 256, 4, False),
    (4, QKV, 1536, 1, False),
    (5, ATTN, 512, 1, True),
    (6, EXPAND, 2048, 1, True),
    (7, SHRINK, 512, 4, True),
]


def tap_masks(mask_ref, seg_ref):
    seg = seg_ref[...]
    for tap in range(TAPS):
        moved = pltpu.roll(seg, (REACH - tap) % seg.shape[0], 0)
        mask_ref[tap] = jnp.where(moved == seg, 1.0, 0.0).astype(F32)


def first_body(
    count,
    heads,
    tok_ref,
    seg_row_ref,
    *refs,
):
    vectors, refs = refs[: len(VECTORS)], refs[len(VECTORS) :]
    weights, refs = refs[:8], refs[8:]
    outs, refs = refs[:19], refs[19:]
    (
        late_out,
        early_out,
        small_out,
        seg_all,
        plan_out,
        q_out,
        kv_out,
        n1_out,
        glu_out,
        n2_out,
        left_out,
        conv_out,
        n3_out,
        depth_out,
        n4_out,
        x2_out,
        inv_out,
        masks_out,
        seg_out,
    ) = outs
    (
        staged,
        late,
        early,
        edges,
        seg_edges,
        seg_col,
        small_own,
        x_ext,
        seg_ext,
        masks,
        small,
        low_ext,
        n1,
        glu_pre,
        x1,
        n2,
        shifted,
        left_pre,
        conv_pre,
        n3,
        g3,
        depth,
        x2,
        n4,
        inv,
        q_turned,
        kv_own,
        marks,
        columns,
        load_sem,
        out_sem,
        ws_send,
        ws_recv,
        edge_send,
        edge_recv,
        row_send,
        row_recv,
        q_send,
        q_recv,
        kv_send,
        kv_recv,
        pass_send,
        pass_recv,
    ) = refs
    own, core = place()
    parts = count // heads
    head, part = own // parts, lax.rem(own, parts)
    rows = tok_ref.shape[0]
    ext = rows + 2 * EDGE
    mid = slice(EDGE, EDGE + rows)
    sibling = (own, 1 - core)
    peers = others_of(own, core, count)

    loads, column = [], 0
    stage_at = []
    for number, first, width, blocks, _ in WEIGHT_COLUMNS:
        stage_at.append(column)
        for block in range(blocks):
            source = weights[number]
            if blocks == 3:
                source = source.at[block]
            elif blocks > 1:
                source = source.at[pl.ds(block * BLOCK, BLOCK), :]
            loads.append(
                pltpu.make_async_copy(
                    source,
                    staged.at[:, pl.ds(column, width)],
                    load_sem.at[len(loads)],
                )
            )
            if number < 3:
                loads[-1].start()
            column += width
    small_own[...] = jnp.zeros_like(small_own)
    for (row, tall, size), vector_ref in zip(VECTORS, vectors):
        small_own[row : row + tall, :size] = vector_ref[...]
    turned_segments(seg_col, 0, seg_row_ref[...])
    greet([sibling] + peers)
    for load in loads[5:]:
        load.start()

    copies = []
    right, left = (lax.rem(own + 1, count), core), (lax.rem(own + count - 1, count), core)
    edge_copies = [
        push(tok_ref.at[pl.ds(rows - EDGE, EDGE), :], edges.at[0], (edge_send, edge_recv), 0, right),
        push(tok_ref.at[pl.ds(0, EDGE), :], edges.at[1], (edge_send, edge_recv), 1, left),
        push(seg_col.at[pl.ds(rows - EDGE, EDGE), :], seg_edges.at[0], (edge_send, edge_recv), 2, right),
        push(seg_col.at[pl.ds(0, EDGE), :], seg_edges.at[1], (edge_send, edge_recv), 3, left),
    ]
    small_copy = push(small_own, small_out.at[core], (ws_send, ws_recv), len(WEIGHT_COLUMNS), sibling)
    small_out[core] = small_own[...]

    at, weight_copies = 0, []
    for (number, first, width, blocks, is_early), column in zip(WEIGHT_COLUMNS, stage_at):
        target = early if is_early else late
        for _ in range(blocks):
            loads[at].wait()
            at += 1
        size = width * blocks
        mine = pl.ds(bound(core * BLOCK, BLOCK), BLOCK)

        @pl.loop(0, BLOCK // ROW_BLOCK)
        def _(step):
            source = staged[span(step, ROW_BLOCK), pl.ds(column, size)]
            goes = pl.ds(bound(core * BLOCK + step * ROW_BLOCK, ROW_BLOCK), ROW_BLOCK)
            target[goes, pl.ds(first, size)] = source.astype(BF16)

        piece = target.at[mine, pl.ds(first, size)]
        weight_copies.append(push(piece, piece, (ws_send, ws_recv), number, sibling))

    for copy in edge_copies:
        copy.wait()
    small_copy.wait()
    row_copies = [
        push(seg_row_ref, seg_all.at[own], (row_send, row_recv), gap, peer)
        for gap, peer in enumerate(peers)
    ]
    seg_all[own] = seg_row_ref[...]
    widened(small, small_out)

    x_ext[:EDGE, :] = edges[0].astype(F32)
    x_ext[mid, :] = tok_ref[...].astype(F32)
    x_ext[EDGE + rows :, :] = edges[1].astype(F32)
    seg_ext[:EDGE, :] = jnp.where(own == 0, -1.0, seg_edges[0])
    seg_ext[mid, :] = seg_col[...]
    seg_ext[EDGE + rows :, :] = jnp.where(own == count - 1, -1.0, seg_edges[1])
    tap_masks(masks, seg_ext)

    normed, inv_std = norm_fwd(x_ext[...])
    n1[...] = normed[mid, :]
    inv[0] = jnp.broadcast_to(inv_std, (ext, LANES))
    low_ext[...] = (normed * vector(small, LN1G, D) + vector(small, LN1B, D)).astype(BF16)

    weight_copies[0].wait()
    glu_bias = vector(small, GLUB, 2 * D)
    for step in range(2 * D // 512):
        cols = slice(512 * step, 512 * (step + 1))
        glu_pre[:, cols] = (
            matmul(low_ext[...], late[:, GLU + 512 * step : GLU + 512 * (step + 1)])
            + glu_bias[:, cols]
        )
    state = x_ext[...] + glu_pre[:, :D] * jax.nn.sigmoid(glu_pre[:, D:])
    x1[...] = state[mid, :]
    normed, inv_std = norm_fwd(state)
    n2[...] = normed[mid, :]
    inv[1] = jnp.broadcast_to(inv_std, (ext, LANES))
    low_f = (normed * vector(small, LN2G, D) + vector(small, LN2B, D)).astype(BF16).astype(F32)
    before = pltpu.roll(low_f, 1, 0) * jnp.concatenate([masks[REACH - 1]] * (D // LANES), axis=1)
    after = pltpu.roll(low_f, ext - 1, 0) * jnp.concatenate([masks[REACH + 1]] * (D // LANES), axis=1)
    shifted[0] = before.astype(BF16)
    shifted[1] = low_f.astype(BF16)
    shifted[2] = after.astype(BF16)

    weight_copies[1].wait()

    @pl.loop(0, FF // 512)
    def _(step):
        weight = late[:, pl.ds(bound(LEFT + step * 512, 512), 512)]
        left_pre[:, span(step, 512)] = matmul(shifted[1], weight)

    weight_copies[2].wait()
    conv_sum = vector(small, CONVB, HALF)
    for tap in range(3):
        conv_sum = conv_sum + matmul(
            shifted[tap], late[:, CONV + HALF * tap : CONV + HALF * (tap + 1)]
        )
    conv_pre[...] = conv_sum

    left_bias = vector(small, LEFTB, FF)
    gain, shift = vector(small, LN3G, FF), vector(small, LN3B, FF)

    @pl.loop(0, ext // ROW_BLOCK)
    def _(step):
        here = span(step, ROW_BLOCK)
        pre = left_pre[here, :] + left_bias
        left_pre[here, :] = pre
        mixed = jax.nn.silu(pre)
        mixed = jnp.concatenate(
            [mixed[:, :HALF] + jax.nn.silu(conv_pre[here, :]), mixed[:, HALF:]], axis=1
        )
        normed, inv_std = norm_fwd(mixed)
        n3[here, :] = normed
        inv[2, here, :] = jnp.broadcast_to(inv_std, (ROW_BLOCK, LANES))
        g3[here, :] = (normed * gain + shift).astype(BF16).astype(F32)

    saves = [
        move(n1, n1_out, out_sem.at[0]),
        move(glu_pre.at[pl.ds(EDGE, rows), :], glu_out, out_sem.at[1]),
        move(n2, n2_out, out_sem.at[2]),
        move(left_pre.at[pl.ds(EDGE, rows), :], left_out, out_sem.at[3]),
        move(conv_pre, conv_out, out_sem.at[4]),
        move(n3, n3_out, out_sem.at[5]),
    ]

    @pl.loop(0, FF // LANES)
    def _(step):
        cols = span(step, LANES)
        block = g3[:, cols]
        total = jnp.zeros((rows, LANES), F32)
        for tap in range(TAPS):
            row = DEPTH + tap
            moved = pltpu.roll(block, (REACH - tap) % ext, 0)[mid, :]
            half = FF // 2 // LANES
            taps = small[step // half, row : row + 1, span(lax.rem(step, half), LANES)]
            total = total + moved * masks[tap, mid, :] * taps
        depth[:, cols] = total.astype(BF16)

    saves.append(move(depth, depth_out, out_sem.at[6]))
    weight_copies[3].wait()
    sep = vector(small, POINTB, HALF)
    for side in range(2):
        for block in range(4):
            first = side * (FF // 2) + block * BLOCK
            sep = sep + matmul(
                depth[:, first : first + BLOCK],
                late[side * BLOCK : (side + 1) * BLOCK, POINT + HALF * block : POINT + HALF * (block + 1)],
            )
    state = jnp.concatenate([x1[:, :HALF] + sep, x1[:, HALF:]], axis=1)
    x2[...] = state
    normed, inv_std = norm_fwd(state)
    n4[...] = normed
    inv[3, :rows, :] = jnp.broadcast_to(inv_std, (rows, LANES))
    low = (normed * vector(small, LN4G, D) + vector(small, LN4B, D)).astype(BF16)
    weight_copies[4].wait()
    for step in range(D // 256):
        cols = slice(256 * step, 256 * (step + 1))
        query = matmul(low, late[:, QKV + 256 * step : QKV + 256 * (step + 1)])
        q_turned[cols, :] = turn(query)
    near = lax.broadcasted_iota(jnp.int32, (rows, LANES), 1) < HEAD_DIM
    for step in range(D // LANES):
        first = QKV + D + LANES * step
        keys = matmul(low, late[:, first : first + LANES])
        values = matmul(low, late[:, first + D : first + D + LANES])
        kv_own[:, 2 * step * LANES : (2 * step + 1) * LANES] = jnp.where(
            near, keys, pltpu.roll(values, HEAD_DIM, 1)
        ).astype(BF16)
        kv_own[:, (2 * step + 1) * LANES : (2 * step + 2) * LANES] = jnp.where(
            near, pltpu.roll(keys, HEAD_DIM, 1), values
        ).astype(BF16)

    q_slot = q_out.at[:, span(head, rows)]
    kv_slot = kv_out.at[span(own, rows), pl.ds(0, LANES)]
    arriving = []
    for gap in range(1, heads):
        other = lax.rem(head + gap, heads)
        arriving.append(
            push(kv_own.at[:, span(other, LANES)], kv_slot, (kv_send, kv_recv), gap - 1, (other * parts + part, core))
        )
    twins = [(head * parts + lax.rem(part + gap, parts), core) for gap in range(1, parts)]
    for at, twin in enumerate(twins):
        copies.append(
            push(kv_own.at[:, span(head, LANES)], kv_slot, (pass_send, pass_recv), at * heads, twin)
        )
    for gap in range(1, heads):
        other = lax.rem(head + gap, heads)
        copies.append(
            push(q_turned.at[span(other, HEAD_DIM), :], q_slot, (q_send, q_recv), gap - 1, (other * parts + part, core))
        )
    saves.append(move(q_turned.at[span(head, HEAD_DIM), :], q_slot, out_sem.at[7]))
    saves.append(move(kv_own.at[:, span(head, LANES)], kv_slot, out_sem.at[8]))
    saves.append(move(n4, n4_out, out_sem.at[9]))
    saves.append(move(x2, x2_out, out_sem.at[10]))
    saves.append(move(inv, inv_out, out_sem.at[11]))
    saves.append(move(masks, masks_out, out_sem.at[14]))
    for copy in row_copies:
        copy.wait()
    lane = lax.broadcasted_iota(jnp.int32, (1, LANES), 1)
    every = seg_all[:, 0, :]
    for tile in range(heads):
        source = tile * parts + part
        mine = seg_all[source]
        first = jnp.min(mine, axis=1, keepdims=True)
        last = jnp.max(mine, axis=1, keepdims=True)
        below = jnp.sum(jnp.sum((every < first).astype(F32), axis=0, keepdims=True), axis=1, keepdims=True).astype(jnp.int32)
        upto = jnp.sum(jnp.sum((every <= last).astype(F32), axis=0, keepdims=True), axis=1, keepdims=True).astype(jnp.int32)
        plan_out[tile : tile + 1, :] = jnp.where(
            lane == 0, below, jnp.where(lane == 1, upto, source)
        )
    mark_segments(marks, columns, seg_all)
    saves.append(move(columns, seg_out, out_sem.at[16]))
    saves.append(move(marks, kv_out.at[:, pl.ds(LANES, LANES)], out_sem.at[15]))
    for copy in weight_copies[5:]:
        copy.wait()
    saves.append(move(late, late_out, out_sem.at[12]))
    saves.append(move(early, early_out, out_sem.at[13]))
    for gap in range(1, heads):
        arriving[gap - 1].wait()
        source = lax.rem(head + heads - gap, heads) * parts + part
        block = kv_out.at[span(source, rows), pl.ds(0, LANES)]
        for at, twin in enumerate(twins):
            copies.append(push(block, block, (pass_send, pass_recv), at * heads + gap, twin))

    for copy in copies + saves:
        copy.wait()


def first_kernel(tokens, seg_row, vectors, weights, count, heads):
    rows = tokens.shape[0]
    ext = rows + 2 * EDGE
    parts = count // heads
    late = (2 * BLOCK, SMALL)
    early = (2 * BLOCK, EARLY)
    out_shape = (
        shaped(late, BF16),
        shaped(early, BF16),
        shaped((2, SMALL_ROWS, SMALL_WIDTH)),
        shaped((count, 1, rows), jnp.int32),
        shaped((heads, LANES), jnp.int32),
        shaped((HEAD_DIM, heads * rows), BF16),
        shaped((count * rows, 2 * LANES), BF16),
        shaped((rows, D)),
        shaped((rows, 2 * D)),
        shaped((rows, D)),
        shaped((rows, FF)),
        shaped((ext, HALF)),
        shaped((ext, FF)),
        shaped((rows, FF), BF16),
        shaped((rows, D)),
        shaped((rows, D)),
        shaped((4, ext, LANES)),
        shaped((TAPS, ext, LANES)),
        shaped((count * rows, LANES)),
    )
    out_specs = (
        [any_spec()] * 2 + [vmem_spec()] * 3 + [any_spec()] * 14
    )
    scratch = [
        pltpu.VMEM((BLOCK, SMALL + EARLY), F32),
        pltpu.VMEM(late, BF16),
        pltpu.VMEM(early, BF16),
        pltpu.VMEM((2, EDGE, D), BF16),
        pltpu.VMEM((2, EDGE, LANES), F32),
        pltpu.VMEM((rows, LANES), F32),
        pltpu.VMEM((SMALL_ROWS, SMALL_WIDTH), F32),
        pltpu.VMEM((ext, D), F32),
        pltpu.VMEM((ext, LANES), F32),
        pltpu.VMEM((TAPS, ext, LANES), F32),
        pltpu.VMEM((2, SMALL_ROWS, SMALL_WIDTH), F32),
        pltpu.VMEM((ext, D), BF16),
        pltpu.VMEM((rows, D), F32),
        pltpu.VMEM((ext, 2 * D), F32),
        pltpu.VMEM((rows, D), F32),
        pltpu.VMEM((rows, D), F32),
        pltpu.VMEM((3, ext, D), BF16),
        pltpu.VMEM((ext, FF), F32),
        pltpu.VMEM((ext, HALF), F32),
        pltpu.VMEM((ext, FF), F32),
        pltpu.VMEM((ext, FF), F32),
        pltpu.VMEM((rows, FF), BF16),
        pltpu.VMEM((rows, D), F32),
        pltpu.VMEM((rows, D), F32),
        pltpu.VMEM((4, ext, LANES), F32),
        pltpu.VMEM((D, rows), BF16),
        pltpu.VMEM((rows, 2 * D), BF16),
        pltpu.VMEM((count * rows, LANES), BF16),
        pltpu.VMEM((count * rows, LANES), F32),
        pltpu.SemaphoreType.DMA((sum(item[3] for item in WEIGHT_COLUMNS),)),
        pltpu.SemaphoreType.DMA((17,)),
    ]
    scratch += sem_pair(len(WEIGHT_COLUMNS) + 1) + sem_pair(4) + sem_pair(count - 1)
    scratch += sem_pair(heads - 1) + sem_pair(heads - 1) + sem_pair((parts - 1) * heads)
    return pl.pallas_call(
        functools.partial(first_body, count, heads),
        out_shape=out_shape,
        in_specs=[vmem_spec()] * (2 + len(vectors)) + [any_spec()] * 8,
        out_specs=out_specs,
        scratch_shapes=scratch,
        compiler_params=comm_params(1),
        name="first_layers",
    )(tokens, seg_row, *vectors, *weights)


def turn_keys(kv_ref, turned):
    @pl.loop(0, kv_ref.shape[0] // KEY_TILE)
    def _(tile):
        here = span(tile, KEY_TILE)
        turned[:, here] = turn(kv_ref[here, :LANES])


def other_segments(seg_q):
    number = lax.broadcasted_iota(jnp.int32, (LANES, seg_q.shape[1]), 0)
    return jnp.where(number == seg_q, 0.0, MASK_FILL).astype(BF16)


def key_tiles(plan_ref, tile):
    return plan_ref[tile, 0] // KEY_TILE, (plan_ref[tile, 1] + KEY_TILE - 1) // KEY_TILE


def attend_body(rows, plan_ref, q_ref, kv_ref, seg_ref, o_ref, low_ref, lse_ref, turned):
    turn_keys(kv_ref, turned)

    @pl.loop(0, q_ref.shape[1] // rows)
    def _(tile):
        at = span(tile, rows)
        q = q_ref[:, at] * jnp.bfloat16(HEAD_DIM**-0.5)
        others = other_segments(seg_ref[plan_ref[tile, 2]])
        q_pad = jnp.concatenate([q, jnp.zeros_like(q), others], axis=0)

        def block(key_tile, carry):
            top, total, acc = carry
            here = span(key_tile, KEY_TILE)
            scores = matmul(kv_ref[here, :], q_pad)
            new_top = jnp.maximum(top, jnp.max(scores, axis=0, keepdims=True))
            probs = jnp.exp(scores - new_top)
            shrink = jnp.exp(top - new_top)
            total = total * shrink + jnp.sum(probs, axis=0, keepdims=True)
            acc = acc * shrink + matmul(turned[HEAD_DIM:, here], probs.astype(BF16))
            return (new_top, total, acc)

        first, end = key_tiles(plan_ref, tile)
        top, total, acc = lax.fori_loop(
            first,
            end,
            block,
            (
                jnp.full((1, rows), MASK_FILL, F32),
                jnp.zeros((1, rows), F32),
                jnp.zeros((HEAD_DIM, rows), F32),
            ),
        )
        out = acc / total
        o_ref[:, at] = out
        low_ref[:, at] = out.astype(BF16)
        lse_ref[:, at] = top + jnp.log(total)


def attend(plan, q_t, kv, seg, rows):
    return pl.pallas_call(
        functools.partial(attend_body, rows),
        out_shape=(shaped(q_t.shape), shaped(q_t.shape, BF16), shaped((1, q_t.shape[1]))),
        in_specs=[smem_spec()] + [vmem_spec()] * 3,
        out_specs=(vmem_spec(),) * 3,
        scratch_shapes=[pltpu.VMEM((LANES, kv.shape[0]), BF16)],
        compiler_params=pltpu.CompilerParams(vmem_limit_bytes=VMEM_MOST),
        name="attend",
    )(plan, q_t, kv, seg)


def middle_body(
    count,
    heads,
    o_in,
    out_grad_in,
    small_in,
    x2_in,
    early_in,
    out_ref,
    small_grads,
    dx3_out,
    grads_out,
    do_out,
    out_grad,
    small_raw,
    weights,
    x2,
    small,
    o_t,
    x3,
    expand_pre,
    hidden,
    dpre,
    do_t,
    grads,
    dx3,
    load_sem,
    o_send,
    o_recv,
    do_send,
    do_recv,
):
    own, core = place()
    parts = count // heads
    head, part = own // parts, lax.rem(own, parts)
    rows = out_grad.shape[0]
    slot = o_t.at[span(head, HEAD_DIM), :]
    loads = [
        move(o_in.at[:, span(head, rows)], slot, load_sem.at[2]),
        move(small_in, small_raw, load_sem.at[3]),
        move(x2_in, x2, load_sem.at[1]),
        move(early_in, weights, load_sem.at[0]),
        move(out_grad_in, out_grad, load_sem.at[4]),
    ]
    near = [lax.rem(head + gap, heads) for gap in range(1, heads)]
    peers = [(other * parts + part, core) for other in near]
    greet(peers)
    copies = [
        push(o_in.at[:, span(other, rows)], slot, (o_send, o_recv), gap, peer)
        for gap, (other, peer) in enumerate(zip(near, peers))
    ]
    small_grads[...] = jnp.zeros_like(small_grads)
    for copy in loads:
        copy.wait()
    widened(small, small_raw)
    for copy in copies:
        copy.wait()

    state = (
        x2[...]
        + matmul(turn(o_t[...]), weights[:, ATTN : ATTN + D])
        + vector(small, ATTNB, D)
    )
    x3[...] = state
    normed, inv_std = norm_fwd(state)
    gain = vector(small, LN5G, D)
    low = (normed * gain + vector(small, LN5B, D)).astype(BF16)
    expand_bias = vector(small, EXPANDB, FF)
    for step in range(FF // 512):
        cols = slice(512 * step, 512 * (step + 1))
        pre = matmul(low, weights[:, EXPAND + 512 * step : EXPAND + 512 * (step + 1)]) + expand_bias[:, cols]
        expand_pre[:, cols] = pre
        hidden[:, cols] = jax.nn.silu(pre).astype(BF16)
    state = x3[...] + vector(small, SHRINKB, D)
    for block in range(FF // BLOCK):
        side, column = block // 4, SHRINK + D * (block % 4)
        state = state + matmul(
            hidden[:, block * BLOCK : (block + 1) * BLOCK],
            weights[side * BLOCK : (side + 1) * BLOCK, column : column + D],
        )
    out_ref[...] = state.astype(BF16)

    dz = out_grad[...]
    for block in range(FF // BLOCK):
        side, column = block // 4, SHRINK + D * (block % 4)
        cols = slice(block * BLOCK, (block + 1) * BLOCK)
        grad = back_mul(dz, weights[side * BLOCK : (side + 1) * BLOCK, column : column + D])
        dpre[:, cols] = (grad * smooth_slope(expand_pre[:, cols])).astype(BF16)
    grad = jnp.concatenate(
        [
            back_mul(dpre[...], weights[side * BLOCK : (side + 1) * BLOCK, EXPAND : EXPAND + FF])
            for side in range(2)
        ],
        axis=1,
    )
    state = dz.astype(F32) + norm_back(grad, normed, inv_std, gain)
    dx3[...] = state
    dy3 = state.astype(BF16)
    do_t[...] = back_mul(weights[:, ATTN : ATTN + D], dy3).astype(BF16)
    slot = do_out.at[:, span(head, rows)]
    copies = [
        push(do_t.at[span(other, HEAD_DIM), :], slot, (do_send, do_recv), gap, peer)
        for gap, (other, peer) in enumerate(zip(near, peers))
    ]
    copies.append(move(do_t.at[span(head, HEAD_DIM), :], slot, load_sem.at[0]))
    copies.append(move(dx3, dx3_out, load_sem.at[1]))

    put_vector(small_grads, LN5G, col_sum(grad * normed))
    put_vector(small_grads, LN5B, col_sum(grad))
    put_vector(small_grads, ATTNB, col_sum(dy3))
    put_vector(small_grads, EXPANDB, col_sum(dpre[...]))
    put_vector(small_grads, SHRINKB, col_sum(dz))
    for block in range(FF // BLOCK):
        side, column = block // 4, SHRINK + D * (block % 4)
        grads[side * BLOCK : (side + 1) * BLOCK, column : column + D] = matmul(
            turn(hidden[:, block * BLOCK : (block + 1) * BLOCK]), dz
        ).astype(BF16)
    grads[:, ATTN : ATTN + D] = matmul(o_t[...], dy3).astype(BF16)
    low_t = turn(low)
    for step in range(FF // 512):
        grads[:, EXPAND + 512 * step : EXPAND + 512 * (step + 1)] = matmul(
            low_t, dpre[:, 512 * step : 512 * (step + 1)]
        ).astype(BF16)
    copies.append(move(grads, grads_out, load_sem.at[2]))
    for copy in copies:
        copy.wait()


def middle_kernel(o_low, out_grad, small, x2, early, count, heads):
    rows = out_grad.shape[0]
    return pl.pallas_call(
        functools.partial(middle_body, count, heads),
        out_shape=(
            shaped((rows, D), BF16),
            shaped((2, SMALL_ROWS, SMALL_WIDTH)),
            shaped((rows, D)),
            shaped(early.shape, BF16),
            shaped((HEAD_DIM, heads * rows), BF16),
        ),
        in_specs=[any_spec()] * 5,
        out_specs=[vmem_spec()] * 2 + [any_spec()] * 3,
        scratch_shapes=[
            pltpu.VMEM((rows, D), BF16),
            pltpu.VMEM((2, SMALL_ROWS, SMALL_WIDTH), F32),
            pltpu.VMEM(early.shape, BF16),
            pltpu.VMEM((rows, D), F32),
            pltpu.VMEM((2, SMALL_ROWS, SMALL_WIDTH), F32),
            pltpu.VMEM((D, rows), BF16),
            pltpu.VMEM((rows, D), F32),
            pltpu.VMEM((rows, FF), F32),
            pltpu.VMEM((rows, FF), BF16),
            pltpu.VMEM((rows, FF), BF16),
            pltpu.VMEM((D, rows), BF16),
            pltpu.VMEM(early.shape, BF16),
            pltpu.VMEM((rows, D), F32),
            pltpu.SemaphoreType.DMA((5,)),
        ]
        + sem_pair(heads - 1)
        + sem_pair(heads - 1),
        compiler_params=comm_params(2),
        name="middle_layers",
    )(o_low, out_grad, small, x2, early)


def column_groups(first, width, bits):
    tiles = width // LANES
    unit = 2 ** max(0, bits - 4)
    long = max(1, round(tiles * 0.36 / unit)) * unit
    orders = [
        list(range(bits)),
        [1, 0] + list(range(2, bits)),
        list(range(2, bits)) + [0, 1],
    ]
    groups = []
    for size, order in zip([long, long, tiles - 2 * long], orders):
        if size == 0:
            continue
        groups.append((first, size * LANES, order))
        first += size * LANES
    return groups


def grad_sets(bits):
    bounds = [LATE, LATE + SHRINK, QKV, POINT, LEFT, LEFT + FF // 2, CONV, CONV + FF // 2]
    widths = [SHRINK, EARLY - SHRINK, POINT - QKV, LEFT - POINT] + [FF // 2] * 4
    return [column_groups(first, width, bits) for first, width in zip(bounds, widths)]


class Piece:
    def __init__(self, at, group, links, sums, got, total, sems):
        self.at, (self.first, self.width, self.order) = at, group
        self.core, self.sibling, self.bit_of, self.partner = links
        self.view, self.got, self.total, self.sems = sums, got, total, sems
        self.bits, self.phase, self.trail = len(self.order), 0, []
        self.since = -1
        self.copy = None

    def whole(self):
        return (0, BLOCK, self.first, self.width)

    def out(self, where):
        row, tall, col, wide = where
        return self.total.at[pl.ds(bound(row, ROW_BLOCK), tall), pl.ds(bound(col, LANES), wide)]

    def start(self, other_half):
        self.copy = push(other_half, self.out(self.whole()), self.sems[0], self.at, self.sibling)

    def add(self, where, source, spot, last):
        row, tall, col, wide = where

        @pl.loop(0, tall // ROW_BLOCK)
        def _(step):
            gap = step * ROW_BLOCK
            here = (row + gap, ROW_BLOCK, col, wide)
            there = source.at[pl.ds(bound(spot + gap, ROW_BLOCK), ROW_BLOCK), pl.ds(self.first, wide)]
            mine = self.view(here)[...].astype(F32)
            added = (mine + there[...].astype(F32)).astype(BF16)
            if last:
                self.out(here)[...] = added
            else:
                self.view(here)[...] = added

    def halve(self, step):
        row, tall, col, wide = self.where
        bit = self.order[step]
        mine = self.bit_of[bit]
        if tall > ROW_BLOCK:
            half = tall // 2
            kept = (row + half * mine, half, col, wide)
            sent = (row + half * (1 - mine), half, col, wide)
        else:
            half = wide // 2
            kept = (row, tall, col + half * mine, half)
            sent = (row, tall, col + half * (1 - mine), half)
        self.copy = push(
            self.view(sent),
            self.got.at[pl.ds(self.spot, sent[1]), pl.ds(self.first, sent[3])],
            self.sems[1],
            self.at * self.bits + step,
            self.partner[bit],
        )
        self.where = kept

    def double(self, step):
        place_out = self.out(self.trail[step])
        self.copy = push(
            place_out,
            place_out,
            self.sems[2],
            self.at * self.bits + step,
            self.partner[self.order[step]],
        )

    def done(self):
        return self.phase > 2 * self.bits

    def sent_all(self):
        return self.phase >= 2 * self.bits

    def advance(self):
        if self.done():
            return
        self.copy.wait()
        if self.phase == 0:
            self.where, self.spot = self.whole(), 0
            self.add(self.where, self.total, 0, False)
            self.halve(0)
        elif self.phase <= self.bits:
            last = self.phase == self.bits
            self.add(self.where, self.got, self.spot, last)
            self.trail.append(self.where)
            self.spot += self.where[1]
            if last:
                self.double(self.bits - 1)
            else:
                self.halve(self.phase)
        elif self.phase < 2 * self.bits:
            self.double(2 * self.bits - 1 - self.phase)
        self.phase += 1


def last_body(count, heads, *refs):
    (
        q_in,
        do_in,
        o_in,
        lse_in,
        kv_in,
        seg_in,
        small_in,
        small_grads_in,
        seg_ref,
        early_grads,
        dx3_in,
        late_in,
        n1_in,
        glu_in,
        n2_in,
        left_in,
        conv_in,
        n3_in,
        depth_in,
        n4_in,
        inv_in,
        masks_in,
        total_out,
        grad_out,
        total,
        weights,
        dx3,
        n1,
        glu_pre,
        n2,
        left_pre,
        conv_pre,
        n3,
        depth,
        n4,
        inv,
        masks,
        small,
        small_grads,
        dq_t,
        dkv_own,
        q_all,
        do_all,
        o_all,
        lse,
        both,
        delta,
        kv_slots,
        seg_slots,
        turned,
        dkv_acc,
        dq_acc,
        dq_low,
        dkv_all,
        small_raw,
        shared,
        summed,
        dqkv,
        sep_own,
        sep_edges,
        sep_ext,
        depth_grad,
        g3_grad,
        row_sums,
        dleft,
        conv_grad,
        conv_taps,
        grads,
        early_own,
        got,
        load_sem,
        keep_sem,
        store_sem,
        tile_sem,
        dq_send,
        dq_recv,
        dkv_send,
        dkv_recv,
        pass_send,
        pass_recv,
        edge_send,
        edge_recv,
        ws_send,
        ws_recv,
        rs_send,
        rs_recv,
        ag_send,
        ag_recv,
    ) = refs
    own, core = place()
    parts = count // heads
    head, part = own // parts, lax.rem(own, parts)
    rows = dx3.shape[0]
    ext = rows + 2 * EDGE
    mid = slice(EDGE, EDGE + rows)
    sibling = (own, 1 - core)
    peers = others_of(own, core, count)
    bits = count.bit_length() - 1

    sources = (dx3_in, late_in, n4_in, inv_in, depth_in, masks_in, n3_in, left_in, conv_in, n2_in, glu_in, n1_in)
    targets = (dx3, weights, n4, inv, depth, masks, n3, left_pre, conv_pre, n2, glu_pre, n1)
    announce([sibling] + peers)
    own_rows = pl.ds(bound(core * BLOCK, BLOCK), BLOCK)
    attention_loads = [
        move(q_in, q_all, keep_sem.at[2]),
        move(do_in, do_all, keep_sem.at[5]),
        move(o_in, o_all, keep_sem.at[6]),
        move(lse_in, lse, keep_sem.at[7]),
    ]

    near_heads = max(1, KEY_TILE // (parts * rows))
    tiles_each = max(1, parts * rows // KEY_TILE)
    group_count = heads // near_heads
    key_count = count * rows
    longest = key_count // 2

    def group_first(group):
        return lax.rem(head // near_heads + group, group_count) * near_heads

    def group_head(group, at):
        mixed = lax.rem(head, near_heads)
        bit = sum(
            (lax.rem(mixed // 2**k, 2) + (at >> k & 1) - 2 * lax.rem(mixed // 2**k, 2) * (at >> k & 1)) * 2**k
            for k in range(near_heads.bit_length() - 1)
        )
        return group_first(group) + bit

    def tile_first(number):
        group, tile = number // tiles_each, number % tiles_each
        return group_first(group) * parts * rows + tile * KEY_TILE

    def fetch(number):
        here = pl.ds(bound(tile_first(number), KEY_TILE), KEY_TILE)
        return [
            move(kv_in.at[here, pl.ds(0, LANES)], kv_slots.at[number % 2], tile_sem.at[number % 2]),
            move(seg_in.at[here, :], seg_slots.at[number % 2], tile_sem.at[2 + number % 2]),
        ]

    fetched = fetch(0)

    bit_of = [lax.rem(own // 2**bit, 2) for bit in range(bits)]
    partner = [(own + 2**bit - 2 * 2**bit * bit_of[bit], core) for bit in range(bits)]
    links = (core, sibling, bit_of, partner)
    sems = ((ws_send, ws_recv), (rs_send, rs_recv), (ag_send, ag_recv))

    def early_view(where):
        row, tall, col, wide = where
        return early_own.at[pl.ds(bound(row, ROW_BLOCK), tall), pl.ds(bound(col - LATE, LANES), wide)]

    def late_view(where):
        row, tall, col, wide = where
        return grads.at[pl.ds(bound(core * BLOCK + row, ROW_BLOCK), tall), pl.ds(bound(col, LANES), wide)]

    sets, at = [], 0
    for number, groups in enumerate(grad_sets(bits)):
        members = []
        for group in groups:
            view = late_view if number > 1 else early_view
            members.append(Piece(at, group, links, view, got, total, sems))
            at += 1
        sets.append(members)
    other_rows = pl.ds(bound((1 - core) * BLOCK, BLOCK), BLOCK)

    def start(members, source, shift):
        for piece in members:
            piece.start(source.at[other_rows, pl.ds(piece.first - shift, piece.width)])

    def advance(members):
        for piece in members:
            if not piece.sent_all():
                piece.advance()

    scale = HEAD_DIM**-0.5
    for copy in attention_loads:
        copy.wait()
    dq_acc[...] = jnp.zeros_like(dq_acc)

    @pl.loop(0, heads)
    def _(tile):
        at = span(tile, rows)
        q = q_all[:, at] * jnp.bfloat16(scale)
        do = do_all[:, at]
        none = jnp.zeros_like(q)
        both[tile] = jnp.concatenate(
            [jnp.concatenate([q, none], axis=1), jnp.concatenate([none, do], axis=1)], axis=0
        )
        delta[:, at] = jnp.sum(o_all[:, at] * do.astype(F32), axis=0, keepdims=True)

    def attention_tile(number):
        first, slot = tile_first(number), number % 2

        def one(tile):
            source = tile * parts + part
            apart = jnp.maximum(
                first - (source * rows + rows - 1), source * rows - (first + KEY_TILE - 1)
            )

            @pl.when(apart < longest)
            def _():
                at = span(tile, rows)
                operand = both[tile]
                pair = matmul(kv_slots[slot], operand)
                seg_k = jnp.concatenate([seg_slots[slot]] * (rows // LANES), axis=1)
                seg_q = seg_ref[source].astype(F32)
                scores = jnp.where(seg_k == seg_q, pair[:, :rows], MASK_FILL)
                probs = jnp.exp(scores - lse[:, at])
                score_grad = (probs * (pair[:, rows:] - delta[:, at])).astype(BF16)
                joined = jnp.concatenate([score_grad, probs.astype(BF16)], axis=1)
                dkv_acc[...] += back_mul(joined, operand)
                dq_acc[:, at] += matmul(turned[...], score_grad)

        return one

    collect, sharing, arrived = [], [], []

    def share_group(group):
        for at in range(near_heads):
            other = group_head(group, at)
            for gap in range(parts - 1):
                twin = lax.rem(part + gap + 1, parts)
                sharing.append(
                    push(
                        dkv_all.at[span(other * parts + twin, rows), :],
                        shared.at[gap, group * near_heads + at],
                        (pass_send, pass_recv),
                        gap * heads + group * near_heads + at,
                        (head * parts + twin, core),
                    )
                )

    def send_group(group):
        for at in range(near_heads):
            other, index = group_head(group, at), group * near_heads + at
            for copy in sharing[index * (parts - 1) : (index + 1) * (parts - 1)]:
                copy.wait()
            total_kv = dkv_all[span(other * parts + part, rows), :].astype(F32)
            for gap in range(parts - 1):
                total_kv = total_kv + shared[gap, index].astype(F32)
            if index:
                summed[index] = total_kv.astype(BF16)
                collect.append(
                    push(
                        summed.at[index],
                        dkv_own.at[:, span(head, LANES)],
                        (dkv_send, dkv_recv),
                        index - 1,
                        (other * parts + part, core),
                    )
                )
            else:
                dkv_own[:, span(head, LANES)] = total_kv.astype(BF16)

    slot = dq_t.at[span(head, HEAD_DIM), :]

    def send_dq(gap, other):
        here = span(other, rows)
        dq_low[:, here] = (dq_acc[:, here] * scale).astype(BF16)
        if gap < heads:
            collect.append(
                push(dq_low.at[:, here], slot, (dq_send, dq_recv), gap - 1, (other * parts + part, core))
            )
        else:
            collect.append(move(dq_low.at[:, here], slot, keep_sem.at[0]))

    points, keeps, loads = [], [], []

    def pump():
        at = len(points)
        points.append(at)
        if at == 0:
            all_here([sibling] + peers)
            start(sets[0] + sets[1], early_grads, LATE)
            keeps.append(move(early_grads.at[own_rows, :], early_own, keep_sem.at[1]))
            keeps.append(move(small_in, small_raw, keep_sem.at[3]))
            keeps.append(move(small_grads_in, small_grads, keep_sem.at[4]))
        elif at == 1:
            for copy in keeps:
                copy.wait()
            widened(small, small_raw)
            advance(sets[0])
            loads.extend(move(a, b, load_sem.at[k]) for k, (a, b) in enumerate(zip(sources, targets)))
        elif at in (5, 9, 12, 15):
            advance(sets[0])
        elif at in (2, 7, 11, 14):
            advance(sets[1])

    tiles = group_count * tiles_each
    for number in range(tiles):
        for copy in fetched:
            copy.wait()
        if number + 1 < tiles:
            fetched = fetch(number + 1)
        turned[...] = turn(kv_slots[number % 2, :, :HEAD_DIM])
        dkv_acc[...] = jnp.zeros_like(dkv_acc)
        group = number // tiles_each
        one = attention_tile(number)
        for turn_no in range(4):
            reach = (turn_no * heads // 4 + 1, (turn_no + 1) * heads // 4 + 1)
            pl.loop(*reach)(lambda gap: one(lax.rem(head + gap, heads)))
            if number == tiles - 1:
                for gap in range(*reach):
                    send_dq(gap, lax.rem(head + gap, heads))
            if turn_no == 2 and group and number % tiles_each == 0:
                send_group(group - 1)
            if turn_no < 3:
                pump()
        here = pl.ds(bound(tile_first(number), KEY_TILE), KEY_TILE)
        dkv_all[here, :] = dkv_acc[...].astype(BF16)
        if number % tiles_each == tiles_each - 1:
            share_group(group)
        pump()
    for copy in loads:
        copy.wait()
    send_group(group_count - 1)
    for copy in collect:
        copy.wait()

    dqkv[:, :D] = turn(dq_t[...])
    lane = lax.broadcasted_iota(jnp.int32, (rows, LANES), 1) < HEAD_DIM
    for step in range(D // LANES):
        pair = []
        for side in range(2):
            first = (2 * step + side) * LANES
            pair.append(dkv_own[:, first : first + LANES].astype(F32))
        cols = slice(D + step * LANES, D + (step + 1) * LANES)
        dqkv[:, cols] = jnp.where(lane, pair[0], pltpu.roll(pair[1], HEAD_DIM, 1)).astype(BF16)
        cols = slice(2 * D + step * LANES, 2 * D + (step + 1) * LANES)
        dqkv[:, cols] = jnp.where(lane, pltpu.roll(pair[0], HEAD_DIM, 1), pair[1]).astype(BF16)

    def through(grad, column, width):
        return jnp.concatenate(
            [
                back_mul(grad, weights[side * BLOCK : (side + 1) * BLOCK, column : column + width])
                for side in range(2)
            ],
            axis=1,
        )

    def norm_step(grad, normed, inv_std, row):
        put_vector(small_grads, row, col_sum(grad * normed))
        put_vector(small_grads, row + 1, col_sum(grad))
        return norm_back(grad, normed, inv_std, vector(small, row, D))

    grad = through(dqkv[...], QKV, 3 * D)
    dx2 = dx3[...] + norm_step(grad, n4[...], inv[3, :rows, :1], LN4G)
    dx3[...] = dx2
    sep_own[...] = dx2[:, :HALF].astype(BF16)
    right, left = (lax.rem(own + 1, count), core), (lax.rem(own + count - 1, count), core)
    edge_copies = [
        push(sep_own.at[pl.ds(rows - EDGE, EDGE), :], sep_edges.at[0], (edge_send, edge_recv), 0, right),
        push(sep_own.at[pl.ds(0, EDGE), :], sep_edges.at[1], (edge_send, edge_recv), 1, left),
    ]
    low_t = turn(n4[...] * vector(small, LN4G, D) + vector(small, LN4B, D))
    for step in range(3):
        grads[:, QKV + D * step : QKV + D * (step + 1)] = matmul(
            low_t, dqkv[:, D * step : D * (step + 1)]
        ).astype(BF16)
    start(sets[2], grads, 0)
    advance(sets[0])
    for block in range(FF // BLOCK):
        side, column = block // 4, POINT + HALF * (block % 4)
        grads[side * BLOCK : (side + 1) * BLOCK, column : column + HALF] = matmul(
            turn(depth[:, block * BLOCK : (block + 1) * BLOCK]), sep_own[...]
        ).astype(BF16)
    start(sets[3], grads, 0)
    put_vector(small_grads, POINTB, col_sum(sep_own[...]))

    for copy in edge_copies:
        copy.wait()
    sep_ext[:EDGE, :] = sep_edges[0]
    sep_ext[mid, :] = sep_own[...]
    sep_ext[EDGE + rows :, :] = sep_edges[1]
    for block in range(FF // BLOCK):
        side, column = block // 4, POINT + HALF * (block % 4)
        depth_grad[:, block * BLOCK : (block + 1) * BLOCK] = (
            back_mul(sep_ext[...], weights[side * BLOCK : (side + 1) * BLOCK, column : column + HALF])
            .astype(BF16)
            .astype(F32)
        )

    advance(sets[2])
    row_sums[...] = jnp.zeros_like(row_sums)
    half = FF // 2 // LANES

    def tap_block(step):
        cols = span(step, LANES)
        side, lanes = step // half, span(lax.rem(step, half), LANES)
        block = depth_grad[:, cols]
        normed = n3[:, cols]
        gain = small[side, LN3G : LN3G + 1, lanes]
        low = (normed[mid, :] * gain + small[side, LN3B : LN3B + 1, lanes]).astype(BF16).astype(F32)
        summed = jnp.zeros((ext, LANES), F32)
        for tap in range(TAPS):
            row = DEPTH + tap
            moved = pltpu.roll(block, (tap - REACH) % ext, 0) * masks[TAPS - 1 - tap]
            summed = summed + moved * small[side, row : row + 1, lanes]
            small_grads[side, row : row + 1, lanes] = col_sum(low * moved[mid, :])
        g3_grad[:, cols] = summed
        small_grads[side, LN3G : LN3G + 1, lanes] = col_sum(summed[mid, :] * normed[mid, :])
        small_grads[side, LN3B : LN3B + 1, lanes] = col_sum(summed[mid, :])
        scaled = summed * gain
        row_sums[0] = row_sums[0] + scaled
        row_sums[1] = row_sums[1] + scaled * normed

    for quarter, turns in enumerate((sets[1], sets[3], sets[2], sets[1])):
        pl.loop(quarter * half // 2, (quarter + 1) * half // 2)(tap_block)
        advance(turns)
    inner = jnp.sum(row_sums[0], axis=1, keepdims=True) * (1.0 / FF)
    cross = jnp.sum(row_sums[1], axis=1, keepdims=True) * (1.0 / FF)
    row_sums[0] = jnp.broadcast_to(inner, (ext, LANES))
    row_sums[1] = jnp.broadcast_to(cross, (ext, LANES))

    def left_block(step):
        cols = span(step, LANES)
        side, lanes = step // half, span(lax.rem(step, half), LANES)
        scaled = g3_grad[mid, cols] * small[side, LN3G : LN3G + 1, lanes]
        mixed_grad = inv[2, mid, :] * (scaled - row_sums[0, mid, :] - n3[mid, cols] * row_sums[1, mid, :])
        low = (mixed_grad * smooth_slope(left_pre[:, cols])).astype(BF16)
        dleft[:, cols] = low
        small_grads[side, LEFTB : LEFTB + 1, lanes] = col_sum(low)

    pl.loop(0, half)(left_block)
    advance(sets[3])
    pl.loop(half, 2 * half)(left_block)
    advance(sets[0])
    for step in range(HALF // LANES):
        cols = slice(step * LANES, (step + 1) * LANES)
        scaled = g3_grad[:, cols] * small[0, LN3G : LN3G + 1, cols]
        mixed_grad = inv[2] * (scaled - row_sums[0] - n3[:, cols] * row_sums[1])
        low = (mixed_grad * smooth_slope(conv_pre[:, cols])).astype(BF16).astype(F32)
        conv_grad[:, cols] = low
        for tap in range(3):
            moved = pltpu.roll(low, (tap - 1) % ext, 0) * masks[REACH + 1 - tap]
            conv_taps[:, HALF * tap + step * LANES : HALF * tap + (step + 1) * LANES] = moved[mid, :].astype(BF16)
    put_vector(small_grads, CONVB, col_sum(conv_grad[mid, :]))

    low_t = turn(n2[...] * vector(small, LN2G, D) + vector(small, LN2B, D))
    for step in range(FF // 512):
        grads[:, LEFT + 512 * step : LEFT + 512 * (step + 1)] = matmul(
            low_t, dleft[:, 512 * step : 512 * (step + 1)]
        ).astype(BF16)
        if step % 2:
            start(sets[4 + step // 2], grads, 0)
    advance(sets[2])
    for tap in range(3):
        grads[:, CONV + HALF * tap : CONV + HALF * (tap + 1)] = matmul(
            low_t, conv_taps[:, HALF * tap : HALF * (tap + 1)]
        ).astype(BF16)
    advance(sets[4])
    advance(sets[5])
    grad = through(dleft[...], LEFT, FF) + through(conv_taps[...], CONV, 3 * HALF)
    dx1 = dx3[...] + norm_step(grad, n2[...], inv[1, mid, :1], LN2G)
    gate = jax.nn.sigmoid(glu_pre[:, D:])
    value_grad = dx1 * gate
    dglu = jnp.concatenate([value_grad, value_grad * glu_pre[:, :D] * (1.0 - gate)], axis=1).astype(BF16)
    put_vector(small_grads, GLUB, col_sum(dglu))
    advance(sets[1])
    advance(sets[3])
    low_t = turn(n1[...] * vector(small, LN1G, D) + vector(small, LN1B, D))
    for step in range(2):
        grads[:, GLU + D * step : GLU + D * (step + 1)] = matmul(
            low_t, dglu[:, D * step : D * (step + 1)]
        ).astype(BF16)
    start(sets[6], grads, 0)
    advance(sets[2])
    grad = through(dglu, GLU, 2 * D)
    dx3[...] = dx1 + norm_step(grad, n1[...], inv[0, mid, :1], LN1G)
    keep = move(dx3, grad_out, keep_sem.at[0])
    for side in range(2):
        for block in range(SMALL_WIDTH // BLOCK):
            first = side * BLOCK + block * SMALL_ROWS
            grads[first : first + SMALL_ROWS, SMALL : SMALL + BLOCK] = small_grads[
                side, :, block * BLOCK : (block + 1) * BLOCK
            ].astype(BF16)
        first = side * BLOCK + SMALL_WIDTH // BLOCK * SMALL_ROWS
        grads[first : (side + 1) * BLOCK, SMALL : SMALL + BLOCK] = jnp.zeros(
            ((side + 1) * BLOCK - first, BLOCK), BF16
        )
    start(sets[7], grads, 0)
    advance(sets[4] + sets[5])
    pieces = [piece for number in (0, 3, 1, 2, 6, 7, 4, 5) for piece in sets[number]]
    stores, rounds = [], 0
    while not all(piece.done() for piece in pieces):
        last = all(piece.sent_all() for piece in pieces)
        for piece in pieces:
            if not piece.sent_all():
                piece.advance()
                piece.since = rounds
            elif not piece.done() and (last or piece.since < rounds - 1):
                piece.advance()
                cols = pl.ds(piece.first, piece.width)
                stores.append(move(total.at[:, cols], total_out.at[:, cols], store_sem.at[piece.at]))
        rounds += 1
    for copy in stores:
        copy.wait()
    keep.wait()


def last_kernel(attention, small, small_grads, seg, tensors, count, heads):
    rows = seg.shape[2]
    ext = rows + 2 * EDGE
    parts = count // heads
    bits = count.bit_length() - 1
    pieces = sum(len(groups) for groups in grad_sets(bits))
    scratch = [
        pltpu.VMEM((BLOCK, WIDTH), BF16),
        pltpu.VMEM(tensors[2].shape, BF16),
        pltpu.VMEM((rows, D), F32),
        pltpu.VMEM((rows, D), F32),
        pltpu.VMEM((rows, 2 * D), F32),
        pltpu.VMEM((rows, D), F32),
        pltpu.VMEM((rows, FF), F32),
        pltpu.VMEM((ext, HALF), F32),
        pltpu.VMEM((ext, FF), F32),
        pltpu.VMEM((rows, FF), BF16),
        pltpu.VMEM((rows, D), F32),
        pltpu.VMEM((4, ext, LANES), F32),
        pltpu.VMEM((TAPS, ext, LANES), F32),
        pltpu.VMEM((2, SMALL_ROWS, SMALL_WIDTH), F32),
        pltpu.VMEM((2, SMALL_ROWS, SMALL_WIDTH), F32),
        pltpu.VMEM((D, rows), BF16),
        pltpu.VMEM((rows, 2 * D), BF16),
        pltpu.VMEM((HEAD_DIM, heads * rows), BF16),
        pltpu.VMEM((HEAD_DIM, heads * rows), BF16),
        pltpu.VMEM((HEAD_DIM, heads * rows), F32),
        pltpu.VMEM((1, heads * rows), F32),
        pltpu.VMEM((heads, LANES, 2 * rows), BF16),
        pltpu.VMEM((1, heads * rows), F32),
        pltpu.VMEM((2, KEY_TILE, LANES), BF16),
        pltpu.VMEM((2, KEY_TILE, LANES), F32),
        pltpu.VMEM((HEAD_DIM, KEY_TILE), BF16),
        pltpu.VMEM((KEY_TILE, LANES), F32),
        pltpu.VMEM((HEAD_DIM, heads * rows), F32),
        pltpu.VMEM((HEAD_DIM, heads * rows), BF16),
        pltpu.VMEM((count * rows, LANES), BF16),
        pltpu.VMEM((2, SMALL_ROWS, SMALL_WIDTH), F32),
        pltpu.VMEM((parts - 1, heads, rows, LANES), BF16),
        pltpu.VMEM((heads, rows, LANES), BF16),
        pltpu.VMEM((rows, 3 * D), BF16),
        pltpu.VMEM((rows, HALF), BF16),
        pltpu.VMEM((2, EDGE, HALF), BF16),
        pltpu.VMEM((ext, HALF), BF16),
        pltpu.VMEM((ext, FF), F32),
        pltpu.VMEM((ext, FF), F32),
        pltpu.VMEM((2, ext, LANES), F32),
        pltpu.VMEM((rows, FF), BF16),
        pltpu.VMEM((ext, HALF), F32),
        pltpu.VMEM((rows, 3 * HALF), BF16),
        pltpu.VMEM((2 * BLOCK, LATE), BF16),
        pltpu.VMEM((BLOCK, EARLY), BF16),
        pltpu.VMEM((BLOCK + ROW_BLOCK * max(0, bits - 4), WIDTH), BF16),
        pltpu.SemaphoreType.DMA((12,)),
        pltpu.SemaphoreType.DMA((8,)),
        pltpu.SemaphoreType.DMA((pieces,)),
        pltpu.SemaphoreType.DMA((4,)),
    ]
    scratch += sem_pair(heads - 1) + sem_pair(heads - 1) + sem_pair((parts - 1) * heads)
    scratch += sem_pair(2) + sem_pair(pieces)
    scratch += sem_pair(pieces * bits) + sem_pair(pieces * bits)
    return pl.pallas_call(
        functools.partial(last_body, count, heads),
        out_shape=(shaped((BLOCK, WIDTH), BF16), shaped((rows, D))),
        in_specs=[any_spec()] * (len(attention) + 2) + [vmem_spec()] + [any_spec()] * len(tensors),
        out_specs=[any_spec(), any_spec()],
        scratch_shapes=scratch,
        compiler_params=comm_params(3),
        name="last_layers",
    )(*attention, small, small_grads, seg, *tensors)


def unpack_body(output_in, grad_in, packed_in, *refs):
    size = len(MATRICES) + len(VECTORS) + 2
    outs, (packed, output, grad, *stages, load_sem, out_sem) = refs[:size], refs[size:]
    output_ref, grad_ref, *outs = outs
    order = [len(MATRICES)] + list(range(len(MATRICES)))
    bounds = [(first, width * blocks) for first, width, blocks in MATRICES] + [(SMALL, BLOCK)]
    loads = {}
    for at in order:
        cols = pl.ds(*bounds[at])
        loads[at] = move(packed_in.at[:, cols], packed.at[:, cols], load_sem.at[at])
    passed = [
        move(output_in, output, load_sem.at[len(MATRICES) + 1]),
        move(grad_in, grad, load_sem.at[len(MATRICES) + 2]),
    ]
    stores = []
    for at, (first, width, blocks) in enumerate(MATRICES):
        loads[at].wait()
        stage = stages[at]
        tall = 2 * ROW_BLOCK

        @pl.loop(0, BLOCK // tall, unroll=2)
        def _(step):
            for block in range(blocks):
                value = packed[span(step, tall), first + block * width : first + (block + 1) * width].astype(F32)
                if blocks == 3:
                    stage[block, span(step, tall), :] = value
                else:
                    stage[pl.ds(bound(block * BLOCK + step * tall, tall), tall), :] = value

        stores.append(move(stage, outs[at], out_sem.at[at]))

    for copy in passed:
        copy.wait()
    stores.append(move(output, output_ref, out_sem.at[len(MATRICES)]))
    stores.append(move(grad, grad_ref, out_sem.at[len(MATRICES) + 1]))
    loads[len(MATRICES)].wait()
    small = jnp.concatenate(
        [
            packed[block * SMALL_ROWS : (block + 1) * SMALL_ROWS, SMALL : SMALL + BLOCK].astype(F32)
            for block in range(SMALL_WIDTH // BLOCK)
        ],
        axis=1,
    )
    for (row, tall, size), out in zip(VECTORS, outs[len(MATRICES) :]):
        out[...] = small[row : row + tall, :size]
    for copy in stores:
        copy.wait()


def unpack(output, grad, packed):
    shapes = []
    for _, width, blocks in MATRICES:
        shapes.append((3, BLOCK, width) if blocks == 3 else (blocks * BLOCK, width))
    vectors = [(tall, size) for _, tall, size in VECTORS]
    return pl.pallas_call(
        unpack_body,
        out_shape=(shaped(output.shape, output.dtype), shaped(grad.shape))
        + tuple(shaped(shape) for shape in shapes + vectors),
        in_specs=[any_spec()] * 3,
        out_specs=[any_spec()] * (2 + len(shapes)) + [vmem_spec()] * len(vectors),
        scratch_shapes=[
            pltpu.VMEM(packed.shape, packed.dtype),
            pltpu.VMEM(output.shape, output.dtype),
            pltpu.VMEM(grad.shape, F32),
        ]
        + [pltpu.VMEM(shape, F32) for shape in shapes]
        + [pltpu.SemaphoreType.DMA((len(shapes) + 3,)), pltpu.SemaphoreType.DMA((len(shapes) + 2,))],
        compiler_params=pltpu.CompilerParams(vmem_limit_bytes=VMEM_MOST),
        name="unpack",
    )(output, grad, packed)


def body(tokens, segment_ids, out_grad, *params):
    (
        ln1g, ln1b, glu_w, glu_b, ln2g, ln2b, left_w, left_b, conv_w, conv_b, ln3g, ln3b, depth_w,
        point_w, point_b, ln4g, ln4b, qkv_w, attn_w, attn_b, ln5g, ln5b, expand_w, expand_b,
        shrink_w, shrink_b,
    ) = params
    count = lax.axis_size("ctx")
    heads = D // HEAD_DIM
    rows = tokens.shape[1]
    vectors = [
        ln1g, ln1b, glu_b, ln2g, ln2b, left_b, conv_b, ln3g, ln3b, depth_w,
        point_b, ln4g, ln4b, attn_b, ln5g, ln5b, expand_b, shrink_b,
    ]
    vectors = [value.reshape(-1, value.shape[-1]) for value in vectors]
    weights = (glu_w, left_w, conv_w, point_w, qkv_w, attn_w, expand_w, shrink_w)
    (
        late, early, small, seg, plan, q_head, kv_head, n1, glu_pre, n2, left_pre, conv_pre, n3,
        depth, n4, x2, inv, masks, seg_cols,
    ) = first_kernel(tokens[0], segment_ids, vectors, weights, count, heads)
    o_head, o_low, log_sum = attend(plan, q_head, kv_head, seg, rows)
    output, small_grads, dx3, early_grads, do_head = middle_kernel(
        o_low, out_grad[0], small, x2, early, count, heads
    )
    tensors = (
        early_grads, dx3, late, n1, glu_pre, n2, left_pre, conv_pre, n3, depth, n4, inv, masks,
    )
    attention = (q_head, do_head, o_head, log_sum, kv_head, seg_cols)
    total, input_grad = last_kernel(attention, small, small_grads, seg, tensors, count, heads)
    output, input_grad, *pieces = unpack(output, input_grad, total)
    matrices, lines = pieces[: len(MATRICES)], pieces[len(MATRICES) :]
    lines = [line if line.shape[0] > 1 else line.reshape(-1) for line in lines]
    g_glu, g_left, g_conv, g_point, g_qkv, g_attn, g_expand, g_shrink = matrices
    (
        g_ln1g, g_ln1b, g_glu_b, g_ln2g, g_ln2b, g_left_b, g_conv_b, g_ln3g, g_ln3b, g_depth,
        g_point_b, g_ln4g, g_ln4b, g_attn_b, g_ln5g, g_ln5b, g_expand_b, g_shrink_b,
    ) = lines
    return (
        output[None], input_grad[None], g_ln1g, g_ln1b, g_glu, g_glu_b, g_ln2g, g_ln2b, g_left,
        g_left_b, g_conv, g_conv_b, g_ln3g, g_ln3b, g_depth, g_point, g_point_b, g_ln4g, g_ln4b,
        g_qkv, g_attn, g_attn_b, g_ln5g, g_ln5b, g_expand, g_expand_b, g_shrink, g_shrink_b,
    )


def solution(mesh):
    return jax.shard_map(
        body,
        mesh=mesh,
        in_specs=(
            P("ws", "ctx", None),
            P("ws", "ctx"),
            P("ws", "ctx", None),
            P("ws"),
            P("ws"),
            P("ws", None),
            P("ws"),
            P("ws"),
            P("ws"),
            P("ws", None),
            P("ws"),
            P(None, "ws", None),
            P("ws"),
            P("ws"),
            P("ws"),
            P(None, "ws"),
            P("ws", None),
            P("ws"),
            P("ws"),
            P("ws"),
            P("ws", None),
            P("ws", None),
            P("ws"),
            P("ws"),
            P("ws"),
            P("ws", None),
            P("ws"),
            P("ws", None),
            P("ws"),
        ),
        out_specs=(
            P("ws", "ctx", None),
            P("ws", "ctx", None),
            P("ws"),
            P("ws"),
            P("ws", None),
            P("ws"),
            P("ws"),
            P("ws"),
            P("ws", None),
            P("ws"),
            P(None, "ws", None),
            P("ws"),
            P("ws"),
            P("ws"),
            P(None, "ws"),
            P("ws", None),
            P("ws"),
            P("ws"),
            P("ws"),
            P("ws", None),
            P("ws", None),
            P("ws"),
            P("ws"),
            P("ws"),
            P("ws", None),
            P("ws"),
            P("ws", None),
            P("ws"),
        ),
        check_vma=False,
    )
```

```python
import functools
import math

import jax
import jax.numpy as jnp
from jax import lax
from jax.experimental import pallas as pl
from jax.experimental.pallas import tpu as pltpu
from jax.sharding import PartitionSpec as P

MESH_ID = pl.DeviceIdType.MESH
F32 = jnp.float32
BF16 = jnp.bfloat16
HEAD_DIM = 64
NORM_EPS = 1e-06
MASK_FILL = -1e30
LANES = 128
ROW_BLOCK = 16
EDGE = 16
KEY_TILE = 1024
BLOCK = 256
VMEM_MOST = 62 * 1024 * 1024

D = 512
FF = 2048
HALF = 256
TAPS = 9
REACH = 4

QKV, POINT, LEFT, CONV, GLU, SMALL, LATE = 0, 1536, 2560, 4608, 5376, 6400, 6656
ATTN, EXPAND, SHRINK, EARLY = 0, 512, 2560, 4608
WIDTH = LATE + EARLY

SMALL_ROWS = 32
SMALL_WIDTH = 1024
(LN1G, LN1B, GLUB, LN2G, LN2B, LEFTB, CONVB, LN3G, LN3B, DEPTH) = range(10)
(POINTB, LN4G, LN4B, ATTNB, LN5G, LN5B, EXPANDB, SHRINKB) = range(DEPTH + TAPS, DEPTH + TAPS + 8)


VECTORS = [
    (LN1G, 1, 256),
    (LN1B, 1, 256),
    (GLUB, 1, 512),
    (LN2G, 1, 256),
    (LN2B, 1, 256),
    (LEFTB, 1, 1024),
    (CONVB, 1, 128),
    (LN3G, 1, 1024),
    (LN3B, 1, 1024),
    (DEPTH, TAPS, 1024),
    (POINTB, 1, 128),
    (LN4G, 1, 256),
    (LN4B, 1, 256),
    (ATTNB, 1, 256),
    (LN5G, 1, 256),
    (LN5B, 1, 256),
    (EXPANDB, 1, 1024),
    (SHRINKB, 1, 256),
]
MATRICES = [
    (GLU, 1024, 1),
    (LEFT, 2048, 1),
    (CONV, 256, 3),
    (POINT, 256, 4),
    (QKV, 1536, 1),
    (LATE + ATTN, 512, 1),
    (LATE + EXPAND, 2048, 1),
    (LATE + SHRINK, 512, 4),
]


def vmem_spec():
    return pl.BlockSpec(memory_space=pltpu.VMEM)


def any_spec():
    return pl.BlockSpec(memory_space=pl.ANY)


def smem_spec():
    return pl.BlockSpec(memory_space=pltpu.SMEM)


def shaped(shape, kind=F32):
    return jax.ShapeDtypeStruct(shape, kind)


def comm_params(number):
    return pltpu.CompilerParams(
        collective_id=number, has_side_effects=True, vmem_limit_bytes=VMEM_MOST
    )


def announce(peers):
    barrier = pltpu.get_barrier_semaphore()
    for peer in peers:
        pl.semaphore_signal(barrier, inc=1, device_id=peer, device_id_type=MESH_ID)


def all_here(peers):
    pl.semaphore_wait(pltpu.get_barrier_semaphore(), len(peers))


def greet(peers):
    announce(peers)
    all_here(peers)


def push(src, dst, sems, at, peer):
    copy = pltpu.make_async_remote_copy(
        src_ref=src,
        dst_ref=dst,
        send_sem=sems[0].at[at],
        recv_sem=sems[1].at[at],
        device_id=peer,
        device_id_type=MESH_ID,
    )
    copy.start()
    return copy


def push_by(src, dst, send_sem, recv_sem, peer):
    copy = pltpu.make_async_remote_copy(
        src_ref=src,
        dst_ref=dst,
        send_sem=send_sem,
        recv_sem=recv_sem,
        device_id=peer,
        device_id_type=MESH_ID,
    )
    copy.start()
    return copy


def move(src, dst, sem):
    copy = pltpu.make_async_copy(src, dst, sem)
    copy.start()
    return copy


def sem_pair(count):
    return [pltpu.SemaphoreType.DMA((count,)), pltpu.SemaphoreType.DMA((count,))]


def bound(value, step):
    return value if isinstance(value, int) else pl.multiple_of(value, step)


def span(value, step):
    return pl.ds(bound(value * step, step), step)


def matmul(left_op, right_op):
    return jnp.dot(left_op, right_op, preferred_element_type=F32)


def back_mul(grad_in, weight):
    return lax.dot_general(grad_in, weight, (((1,), (1,)), ((), ())), preferred_element_type=F32)


def turn(block):
    return block.astype(F32).T.astype(BF16)


def col_sum(block):
    return jnp.sum(block.astype(F32), axis=0, keepdims=True)


def lane_mean(block):
    return jnp.mean(block, axis=-1, keepdims=True)


def smooth_slope(block):
    sigma = jax.nn.sigmoid(block)
    return sigma * (1.0 + block * (1.0 - sigma))


def norm_fwd(block):
    centred = block - lane_mean(block)
    inv_std = lax.rsqrt(lane_mean(centred * centred) + NORM_EPS)
    return centred * inv_std, inv_std


def norm_back(grad_in, normed, inv_std, gain):
    scaled = grad_in * gain
    inner, cross = lane_mean(scaled), lane_mean(scaled * normed)
    return inv_std * (scaled - inner - normed * cross)


def vector(small_ref, row, size):
    half = size // 2
    return jnp.concatenate(
        [small_ref[core, row : row + 1, :half] for core in range(2)], axis=1
    )


def put_vector(small_ref, row, value):
    half = value.shape[1] // 2
    for core in range(2):
        small_ref[core, row : row + 1, :half] = value[:, core * half : (core + 1) * half]


def place():
    own, core = lax.axis_index("ctx"), lax.axis_index("ws")
    return own, core


def others_of(own, core, count):
    return [(lax.rem(own + gap, count), core) for gap in range(1, count)]


def widened(dst_ref, src_ref):
    @pl.loop(0, 2)
    def _(core):
        dst_ref[core] = src_ref[core].astype(BF16).astype(F32)


def turned_segments(out_ref, first, row):
    for step in range(row.shape[1] // LANES):
        part = row[:, step * LANES : (step + 1) * LANES].astype(F32)
        here = pl.ds(bound(first + step * LANES, LANES), LANES)
        out_ref[here, :] = jnp.broadcast_to(part, (LANES, LANES)).T


def mark_segments(marks, columns, seg_ref):
    count, _, rows = seg_ref.shape

    @pl.loop(0, count)
    def _(source):
        row = seg_ref[source].astype(F32)
        for step in range(rows // LANES):
            part = jnp.broadcast_to(row[:, step * LANES : (step + 1) * LANES], (LANES, LANES)).T
            number = lax.broadcasted_iota(jnp.int32, (LANES, LANES), 1).astype(F32)
            here = pl.ds(bound(source * rows + step * LANES, LANES), LANES)
            columns[here, :] = part
            marks[here, :] = jnp.where(part == number, 1.0, 0.0).astype(BF16)


WEIGHT_COLUMNS = [
    (0, GLU, 1024, 1, False),
    (1, LEFT, 2048, 1, False),
    (2, CONV, 256, 3, False),
    (3, POINT, 256, 4, False),
    (4, QKV, 1536, 1, False),
    (5, ATTN, 512, 1, True),
    (6, EXPAND, 2048, 1, True),
    (7, SHRINK, 512, 4, True),
]


def tap_masks(mask_ref, seg_ref):
    seg = seg_ref[...]
    for tap in range(TAPS):
        moved = pltpu.roll(seg, (REACH - tap) % seg.shape[0], 0)
        mask_ref[tap] = jnp.where(moved == seg, 1.0, 0.0).astype(F32)


def first_body(
    count,
    heads,
    tok_ref,
    seg_row_ref,
    *refs,
):
    vectors, refs = refs[: len(VECTORS)], refs[len(VECTORS) :]
    weights, refs = refs[:8], refs[8:]
    outs, refs = refs[:19], refs[19:]
    (
        late_out,
        early_out,
        small_out,
        seg_all,
        plan_out,
        q_out,
        kv_out,
        n1_out,
        glu_out,
        n2_out,
        left_out,
        conv_out,
        n3_out,
        depth_out,
        n4_out,
        x2_out,
        inv_out,
        masks_out,
        seg_out,
    ) = outs
    (
        staged,
        late,
        early,
        edges,
        seg_edges,
        seg_col,
        small_own,
        x_ext,
        seg_ext,
        masks,
        small,
        low_ext,
        n1,
        glu_pre,
        x1,
        n2,
        shifted,
        left_pre,
        conv_pre,
        n3,
        g3,
        depth,
        x2,
        n4,
        inv,
        q_turned,
        kv_own,
        marks,
        columns,
        load_sem,
        out_sem,
        ws_send,
        ws_recv,
        edge_send,
        edge_recv,
        row_send,
        row_recv,
        q_send,
        q_recv,
        kv_send,
        kv_recv,
        pass_send,
        pass_recv,
    ) = refs
    own, core = place()
    parts = count // heads
    head, part = own // parts, lax.rem(own, parts)
    rows = tok_ref.shape[0]
    ext = rows + 2 * EDGE
    mid = slice(EDGE, EDGE + rows)
    sibling = (own, 1 - core)
    peers = others_of(own, core, count)

    loads, column = [], 0
    stage_at = []
    for number, first, width, blocks, _ in WEIGHT_COLUMNS:
        stage_at.append(column)
        for block in range(blocks):
            source = weights[number]
            if blocks == 3:
                source = source.at[block]
            elif blocks > 1:
                source = source.at[pl.ds(block * BLOCK, BLOCK), :]
            loads.append(
                pltpu.make_async_copy(
                    source,
                    staged.at[:, pl.ds(column, width)],
                    load_sem.at[len(loads)],
                )
            )
            if number < 3:
                loads[-1].start()
            column += width
    small_own[...] = jnp.zeros_like(small_own)
    for (row, tall, size), vector_ref in zip(VECTORS, vectors):
        small_own[row : row + tall, :size] = vector_ref[...]
    turned_segments(seg_col, 0, seg_row_ref[...])
    greet([sibling] + peers)
    for load in loads[5:]:
        load.start()

    copies = []
    right, left = (lax.rem(own + 1, count), core), (lax.rem(own + count - 1, count), core)
    edge_copies = [
        push(tok_ref.at[pl.ds(rows - EDGE, EDGE), :], edges.at[0], (edge_send, edge_recv), 0, right),
        push(tok_ref.at[pl.ds(0, EDGE), :], edges.at[1], (edge_send, edge_recv), 1, left),
        push(seg_col.at[pl.ds(rows - EDGE, EDGE), :], seg_edges.at[0], (edge_send, edge_recv), 2, right),
        push(seg_col.at[pl.ds(0, EDGE), :], seg_edges.at[1], (edge_send, edge_recv), 3, left),
    ]
    small_copy = push(small_own, small_out.at[core], (ws_send, ws_recv), len(WEIGHT_COLUMNS), sibling)
    small_out[core] = small_own[...]

    at, weight_copies = 0, []
    for (number, first, width, blocks, is_early), column in zip(WEIGHT_COLUMNS, stage_at):
        target = early if is_early else late
        for _ in range(blocks):
            loads[at].wait()
            at += 1
        size = width * blocks
        mine = pl.ds(bound(core * BLOCK, BLOCK), BLOCK)

        @pl.loop(0, BLOCK // ROW_BLOCK)
        def _(step):
            source = staged[span(step, ROW_BLOCK), pl.ds(column, size)]
            goes = pl.ds(bound(core * BLOCK + step * ROW_BLOCK, ROW_BLOCK), ROW_BLOCK)
            target[goes, pl.ds(first, size)] = source.astype(BF16)

        piece = target.at[mine, pl.ds(first, size)]
        weight_copies.append(push(piece, piece, (ws_send, ws_recv), number, sibling))

    for copy in edge_copies:
        copy.wait()
    small_copy.wait()
    row_copies = [
        push(seg_row_ref, seg_all.at[own], (row_send, row_recv), gap, peer)
        for gap, peer in enumerate(peers)
    ]
    seg_all[own] = seg_row_ref[...]
    widened(small, small_out)

    x_ext[:EDGE, :] = edges[0].astype(F32)
    x_ext[mid, :] = tok_ref[...].astype(F32)
    x_ext[EDGE + rows :, :] = edges[1].astype(F32)
    seg_ext[:EDGE, :] = jnp.where(own == 0, -1.0, seg_edges[0])
    seg_ext[mid, :] = seg_col[...]
    seg_ext[EDGE + rows :, :] = jnp.where(own == count - 1, -1.0, seg_edges[1])
    tap_masks(masks, seg_ext)

    normed, inv_std = norm_fwd(x_ext[...])
    n1[...] = normed[mid, :]
    inv[0] = jnp.broadcast_to(inv_std, (ext, LANES))
    low_ext[...] = (normed * vector(small, LN1G, D) + vector(small, LN1B, D)).astype(BF16)

    weight_copies[0].wait()
    glu_bias = vector(small, GLUB, 2 * D)
    for step in range(2 * D // 512):
        cols = slice(512 * step, 512 * (step + 1))
        glu_pre[:, cols] = (
            matmul(low_ext[...], late[:, GLU + 512 * step : GLU + 512 * (step + 1)])
            + glu_bias[:, cols]
        )
    state = x_ext[...] + glu_pre[:, :D] * jax.nn.sigmoid(glu_pre[:, D:])
    x1[...] = state[mid, :]
    normed, inv_std = norm_fwd(state)
    n2[...] = normed[mid, :]
    inv[1] = jnp.broadcast_to(inv_std, (ext, LANES))
    low_f = (normed * vector(small, LN2G, D) + vector(small, LN2B, D)).astype(BF16).astype(F32)
    before = pltpu.roll(low_f, 1, 0) * jnp.concatenate([masks[REACH - 1]] * (D // LANES), axis=1)
    after = pltpu.roll(low_f, ext - 1, 0) * jnp.concatenate([masks[REACH + 1]] * (D // LANES), axis=1)
    shifted[0] = before.astype(BF16)
    shifted[1] = low_f.astype(BF16)
    shifted[2] = after.astype(BF16)

    weight_copies[1].wait()

    @pl.loop(0, FF // 512)
    def _(step):
        weight = late[:, pl.ds(bound(LEFT + step * 512, 512), 512)]
        left_pre[:, span(step, 512)] = matmul(shifted[1], weight)

    weight_copies[2].wait()
    conv_sum = vector(small, CONVB, HALF)
    for tap in range(3):
        conv_sum = conv_sum + matmul(
            shifted[tap], late[:, CONV + HALF * tap : CONV + HALF * (tap + 1)]
        )
    conv_pre[...] = conv_sum

    left_bias = vector(small, LEFTB, FF)
    gain, shift = vector(small, LN3G, FF), vector(small, LN3B, FF)

    @pl.loop(0, ext // ROW_BLOCK)
    def _(step):
        here = span(step, ROW_BLOCK)
        pre = left_pre[here, :] + left_bias
        left_pre[here, :] = pre
        mixed = jax.nn.silu(pre)
        mixed = jnp.concatenate(
            [mixed[:, :HALF] + jax.nn.silu(conv_pre[here, :]), mixed[:, HALF:]], axis=1
        )
        normed, inv_std = norm_fwd(mixed)
        n3[here, :] = normed
        inv[2, here, :] = jnp.broadcast_to(inv_std, (ROW_BLOCK, LANES))
        g3[here, :] = (normed * gain + shift).astype(BF16).astype(F32)

    saves = [
        move(n1, n1_out, out_sem.at[0]),
        move(glu_pre.at[pl.ds(EDGE, rows), :], glu_out, out_sem.at[1]),
        move(n2, n2_out, out_sem.at[2]),
        move(left_pre.at[pl.ds(EDGE, rows), :], left_out, out_sem.at[3]),
        move(conv_pre, conv_out, out_sem.at[4]),
        move(n3, n3_out, out_sem.at[5]),
    ]

    @pl.loop(0, FF // LANES)
    def _(step):
        cols = span(step, LANES)
        block = g3[:, cols]
        total = jnp.zeros((rows, LANES), F32)
        for tap in range(TAPS):
            row = DEPTH + tap
            moved = pltpu.roll(block, (REACH - tap) % ext, 0)[mid, :]
            half = FF // 2 // LANES
            taps = small[step // half, row : row + 1, span(lax.rem(step, half), LANES)]
            total = total + moved * masks[tap, mid, :] * taps
        depth[:, cols] = total.astype(BF16)

    saves.append(move(depth, depth_out, out_sem.at[6]))
    weight_copies[3].wait()
    sep = vector(small, POINTB, HALF)
    for side in range(2):
        for block in range(4):
            first = side * (FF // 2) + block * BLOCK
            sep = sep + matmul(
                depth[:, first : first + BLOCK],
                late[side * BLOCK : (side + 1) * BLOCK, POINT + HALF * block : POINT + HALF * (block + 1)],
            )
    state = jnp.concatenate([x1[:, :HALF] + sep, x1[:, HALF:]], axis=1)
    x2[...] = state
    normed, inv_std = norm_fwd(state)
    n4[...] = normed
    inv[3, :rows, :] = jnp.broadcast_to(inv_std, (rows, LANES))
    low = (normed * vector(small, LN4G, D) + vector(small, LN4B, D)).astype(BF16)
    weight_copies[4].wait()
    for step in range(D // 256):
        cols = slice(256 * step, 256 * (step + 1))
        query = matmul(low, late[:, QKV + 256 * step : QKV + 256 * (step + 1)])
        q_turned[cols, :] = turn(query)
    near = lax.broadcasted_iota(jnp.int32, (rows, LANES), 1) < HEAD_DIM
    for step in range(D // LANES):
        first = QKV + D + LANES * step
        keys = matmul(low, late[:, first : first + LANES])
        values = matmul(low, late[:, first + D : first + D + LANES])
        kv_own[:, 2 * step * LANES : (2 * step + 1) * LANES] = jnp.where(
            near, keys, pltpu.roll(values, HEAD_DIM, 1)
        ).astype(BF16)
        kv_own[:, (2 * step + 1) * LANES : (2 * step + 2) * LANES] = jnp.where(
            near, pltpu.roll(keys, HEAD_DIM, 1), values
        ).astype(BF16)

    q_slot = q_out.at[:, span(head, rows)]
    kv_slot = kv_out.at[span(own, rows), pl.ds(0, LANES)]
    arriving = []
    for gap in range(1, heads):
        other = lax.rem(head + gap, heads)
        arriving.append(
            push(kv_own.at[:, span(other, LANES)], kv_slot, (kv_send, kv_recv), gap - 1, (other * parts + part, core))
        )
    twins = [(head * parts + lax.rem(part + gap, parts), core) for gap in range(1, parts)]
    for at, twin in enumerate(twins):
        copies.append(
            push(kv_own.at[:, span(head, LANES)], kv_slot, (pass_send, pass_recv), at * heads, twin)
        )
    for gap in range(1, heads):
        other = lax.rem(head + gap, heads)
        copies.append(
            push(q_turned.at[span(other, HEAD_DIM), :], q_slot, (q_send, q_recv), gap - 1, (other * parts + part, core))
        )
    saves.append(move(q_turned.at[span(head, HEAD_DIM), :], q_slot, out_sem.at[7]))
    saves.append(move(kv_own.at[:, span(head, LANES)], kv_slot, out_sem.at[8]))
    saves.append(move(n4, n4_out, out_sem.at[9]))
    saves.append(move(x2, x2_out, out_sem.at[10]))
    saves.append(move(inv, inv_out, out_sem.at[11]))
    saves.append(move(masks, masks_out, out_sem.at[14]))
    for copy in row_copies:
        copy.wait()
    lane = lax.broadcasted_iota(jnp.int32, (1, LANES), 1)
    every = seg_all[:, 0, :]
    for tile in range(heads):
        source = tile * parts + part
        mine = seg_all[source]
        first = jnp.min(mine, axis=1, keepdims=True)
        last = jnp.max(mine, axis=1, keepdims=True)
        below = jnp.sum(jnp.sum((every < first).astype(F32), axis=0, keepdims=True), axis=1, keepdims=True).astype(jnp.int32)
        upto = jnp.sum(jnp.sum((every <= last).astype(F32), axis=0, keepdims=True), axis=1, keepdims=True).astype(jnp.int32)
        plan_out[tile : tile + 1, :] = jnp.where(
            lane == 0, below, jnp.where(lane == 1, upto, source)
        )
    mark_segments(marks, columns, seg_all)
    saves.append(move(columns, seg_out, out_sem.at[16]))
    saves.append(move(marks, kv_out.at[:, pl.ds(LANES, LANES)], out_sem.at[15]))
    for copy in weight_copies[5:]:
        copy.wait()
    saves.append(move(late, late_out, out_sem.at[12]))
    saves.append(move(early, early_out, out_sem.at[13]))
    for gap in range(1, heads):
        arriving[gap - 1].wait()
        source = lax.rem(head + heads - gap, heads) * parts + part
        block = kv_out.at[span(source, rows), pl.ds(0, LANES)]
        for at, twin in enumerate(twins):
            copies.append(push(block, block, (pass_send, pass_recv), at * heads + gap, twin))

    for copy in copies + saves:
        copy.wait()


def first_kernel(tokens, seg_row, vectors, weights, count, heads):
    rows = tokens.shape[0]
    ext = rows + 2 * EDGE
    parts = count // heads
    late = (2 * BLOCK, SMALL)
    early = (2 * BLOCK, EARLY)
    out_shape = (
        shaped(late, BF16),
        shaped(early, BF16),
        shaped((2, SMALL_ROWS, SMALL_WIDTH)),
        shaped((count, 1, rows), jnp.int32),
        shaped((heads, LANES), jnp.int32),
        shaped((HEAD_DIM, heads * rows), BF16),
        shaped((count * rows, 2 * LANES), BF16),
        shaped((rows, D)),
        shaped((rows, 2 * D)),
        shaped((rows, D)),
        shaped((rows, FF)),
        shaped((ext, HALF)),
        shaped((ext, FF)),
        shaped((rows, FF), BF16),
        shaped((rows, D)),
        shaped((rows, D)),
        shaped((4, ext, LANES)),
        shaped((TAPS, ext, LANES)),
        shaped((count * rows, LANES)),
    )
    out_specs = (
        [any_spec()] * 2 + [vmem_spec()] * 3 + [any_spec()] * 14
    )
    scratch = [
        pltpu.VMEM((BLOCK, SMALL + EARLY), F32),
        pltpu.VMEM(late, BF16),
        pltpu.VMEM(early, BF16),
        pltpu.VMEM((2, EDGE, D), BF16),
        pltpu.VMEM((2, EDGE, LANES), F32),
        pltpu.VMEM((rows, LANES), F32),
        pltpu.VMEM((SMALL_ROWS, SMALL_WIDTH), F32),
        pltpu.VMEM((ext, D), F32),
        pltpu.VMEM((ext, LANES), F32),
        pltpu.VMEM((TAPS, ext, LANES), F32),
        pltpu.VMEM((2, SMALL_ROWS, SMALL_WIDTH), F32),
        pltpu.VMEM((ext, D), BF16),
        pltpu.VMEM((rows, D), F32),
        pltpu.VMEM((ext, 2 * D), F32),
        pltpu.VMEM((rows, D), F32),
        pltpu.VMEM((rows, D), F32),
        pltpu.VMEM((3, ext, D), BF16),
        pltpu.VMEM((ext, FF), F32),
        pltpu.VMEM((ext, HALF), F32),
        pltpu.VMEM((ext, FF), F32),
        pltpu.VMEM((ext, FF), F32),
        pltpu.VMEM((rows, FF), BF16),
        pltpu.VMEM((rows, D), F32),
        pltpu.VMEM((rows, D), F32),
        pltpu.VMEM((4, ext, LANES), F32),
        pltpu.VMEM((D, rows), BF16),
        pltpu.VMEM((rows, 2 * D), BF16),
        pltpu.VMEM((count * rows, LANES), BF16),
        pltpu.VMEM((count * rows, LANES), F32),
        pltpu.SemaphoreType.DMA((sum(item[3] for item in WEIGHT_COLUMNS),)),
        pltpu.SemaphoreType.DMA((17,)),
    ]
    scratch += sem_pair(len(WEIGHT_COLUMNS) + 1) + sem_pair(4) + sem_pair(count - 1)
    scratch += sem_pair(heads - 1) + sem_pair(heads - 1) + sem_pair((parts - 1) * heads)
    return pl.pallas_call(
        functools.partial(first_body, count, heads),
        out_shape=out_shape,
        in_specs=[vmem_spec()] * (2 + len(vectors)) + [any_spec()] * 8,
        out_specs=out_specs,
        scratch_shapes=scratch,
        compiler_params=comm_params(1),
        name="first_layers",
    )(tokens, seg_row, *vectors, *weights)


def turn_keys(kv_ref, turned):
    @pl.loop(0, kv_ref.shape[0] // KEY_TILE)
    def _(tile):
        here = span(tile, KEY_TILE)
        turned[:, here] = turn(kv_ref[here, :LANES])


def other_segments(seg_q):
    number = lax.broadcasted_iota(jnp.int32, (LANES, seg_q.shape[1]), 0)
    return jnp.where(number == seg_q, 0.0, MASK_FILL).astype(BF16)


def key_tiles(plan_ref, tile):
    return plan_ref[tile, 0] // KEY_TILE, (plan_ref[tile, 1] + KEY_TILE - 1) // KEY_TILE


def attend_body(rows, plan_ref, q_ref, kv_ref, seg_ref, o_ref, low_ref, lse_ref, turned):
    turn_keys(kv_ref, turned)

    @pl.loop(0, q_ref.shape[1] // rows)
    def _(tile):
        at = span(tile, rows)
        q = q_ref[:, at] * jnp.bfloat16(HEAD_DIM**-0.5)
        others = other_segments(seg_ref[plan_ref[tile, 2]])
        q_pad = jnp.concatenate([q, jnp.zeros_like(q), others], axis=0)

        def block(key_tile, carry):
            top, total, acc = carry
            here = span(key_tile, KEY_TILE)
            scores = matmul(kv_ref[here, :], q_pad)
            new_top = jnp.maximum(top, jnp.max(scores, axis=0, keepdims=True))
            probs = jnp.exp(scores - new_top)
            shrink = jnp.exp(top - new_top)
            total = total * shrink + jnp.sum(probs, axis=0, keepdims=True)
            acc = acc * shrink + matmul(turned[HEAD_DIM:, here], probs.astype(BF16))
            return (new_top, total, acc)

        first, end = key_tiles(plan_ref, tile)
        top, total, acc = lax.fori_loop(
            first,
            end,
            block,
            (
                jnp.full((1, rows), MASK_FILL, F32),
                jnp.zeros((1, rows), F32),
                jnp.zeros((HEAD_DIM, rows), F32),
            ),
        )
        out = acc / total
        o_ref[:, at] = out
        low_ref[:, at] = out.astype(BF16)
        lse_ref[:, at] = top + jnp.log(total)


def attend(plan, q_t, kv, seg, rows):
    return pl.pallas_call(
        functools.partial(attend_body, rows),
        out_shape=(shaped(q_t.shape), shaped(q_t.shape, BF16), shaped((1, q_t.shape[1]))),
        in_specs=[smem_spec()] + [vmem_spec()] * 3,
        out_specs=(vmem_spec(),) * 3,
        scratch_shapes=[pltpu.VMEM((LANES, kv.shape[0]), BF16)],
        compiler_params=pltpu.CompilerParams(vmem_limit_bytes=VMEM_MOST),
        name="attend",
    )(plan, q_t, kv, seg)


def middle_body(
    count,
    heads,
    o_in,
    out_grad_in,
    small_in,
    x2_in,
    early_in,
    out_ref,
    small_grads,
    dx3_out,
    grads_out,
    do_out,
    out_grad,
    small_raw,
    weights,
    x2,
    small,
    o_t,
    x3,
    expand_pre,
    hidden,
    dpre,
    do_t,
    grads,
    dx3,
    load_sem,
    o_send,
    o_recv,
    do_send,
    do_recv,
):
    own, core = place()
    parts = count // heads
    head, part = own // parts, lax.rem(own, parts)
    rows = out_grad.shape[0]
    slot = o_t.at[span(head, HEAD_DIM), :]
    loads = [
        move(o_in.at[:, span(head, rows)], slot, load_sem.at[2]),
        move(small_in, small_raw, load_sem.at[3]),
        move(x2_in, x2, load_sem.at[1]),
        move(early_in, weights, load_sem.at[0]),
        move(out_grad_in, out_grad, load_sem.at[4]),
    ]
    near = [lax.rem(head + gap, heads) for gap in range(1, heads)]
    peers = [(other * parts + part, core) for other in near]
    greet(peers)
    copies = [
        push(o_in.at[:, span(other, rows)], slot, (o_send, o_recv), gap, peer)
        for gap, (other, peer) in enumerate(zip(near, peers))
    ]
    small_grads[...] = jnp.zeros_like(small_grads)
    for copy in loads:
        copy.wait()
    widened(small, small_raw)
    for copy in copies:
        copy.wait()

    state = (
        x2[...]
        + matmul(turn(o_t[...]), weights[:, ATTN : ATTN + D])
        + vector(small, ATTNB, D)
    )
    x3[...] = state
    normed, inv_std = norm_fwd(state)
    gain = vector(small, LN5G, D)
    low = (normed * gain + vector(small, LN5B, D)).astype(BF16)
    expand_bias = vector(small, EXPANDB, FF)
    for step in range(FF // 512):
        cols = slice(512 * step, 512 * (step + 1))
        pre = matmul(low, weights[:, EXPAND + 512 * step : EXPAND + 512 * (step + 1)]) + expand_bias[:, cols]
        expand_pre[:, cols] = pre
        hidden[:, cols] = jax.nn.silu(pre).astype(BF16)
    state = x3[...] + vector(small, SHRINKB, D)
    for block in range(FF // BLOCK):
        side, column = block // 4, SHRINK + D * (block % 4)
        state = state + matmul(
            hidden[:, block * BLOCK : (block + 1) * BLOCK],
            weights[side * BLOCK : (side + 1) * BLOCK, column : column + D],
        )
    out_ref[...] = state.astype(BF16)

    dz = out_grad[...]
    for block in range(FF // BLOCK):
        side, column = block // 4, SHRINK + D * (block % 4)
        cols = slice(block * BLOCK, (block + 1) * BLOCK)
        grad = back_mul(dz, weights[side * BLOCK : (side + 1) * BLOCK, column : column + D])
        dpre[:, cols] = (grad * smooth_slope(expand_pre[:, cols])).astype(BF16)
    grad = jnp.concatenate(
        [
            back_mul(dpre[...], weights[side * BLOCK : (side + 1) * BLOCK, EXPAND : EXPAND + FF])
            for side in range(2)
        ],
        axis=1,
    )
    state = dz.astype(F32) + norm_back(grad, normed, inv_std, gain)
    dx3[...] = state
    dy3 = state.astype(BF16)
    do_t[...] = back_mul(weights[:, ATTN : ATTN + D], dy3).astype(BF16)
    slot = do_out.at[:, span(head, rows)]
    copies = [
        push(do_t.at[span(other, HEAD_DIM), :], slot, (do_send, do_recv), gap, peer)
        for gap, (other, peer) in enumerate(zip(near, peers))
    ]
    copies.append(move(do_t.at[span(head, HEAD_DIM), :], slot, load_sem.at[0]))
    copies.append(move(dx3, dx3_out, load_sem.at[1]))

    put_vector(small_grads, LN5G, col_sum(grad * normed))
    put_vector(small_grads, LN5B, col_sum(grad))
    put_vector(small_grads, ATTNB, col_sum(dy3))
    put_vector(small_grads, EXPANDB, col_sum(dpre[...]))
    put_vector(small_grads, SHRINKB, col_sum(dz))
    for block in range(FF // BLOCK):
        side, column = block // 4, SHRINK + D * (block % 4)
        grads[side * BLOCK : (side + 1) * BLOCK, column : column + D] = matmul(
            turn(hidden[:, block * BLOCK : (block + 1) * BLOCK]), dz
        ).astype(BF16)
    grads[:, ATTN : ATTN + D] = matmul(o_t[...], dy3).astype(BF16)
    low_t = turn(low)
    for step in range(FF // 512):
        grads[:, EXPAND + 512 * step : EXPAND + 512 * (step + 1)] = matmul(
            low_t, dpre[:, 512 * step : 512 * (step + 1)]
        ).astype(BF16)
    copies.append(move(grads, grads_out, load_sem.at[2]))
    for copy in copies:
        copy.wait()


def middle_kernel(o_low, out_grad, small, x2, early, count, heads):
    rows = out_grad.shape[0]
    return pl.pallas_call(
        functools.partial(middle_body, count, heads),
        out_shape=(
            shaped((rows, D), BF16),
            shaped((2, SMALL_ROWS, SMALL_WIDTH)),
            shaped((rows, D)),
            shaped(early.shape, BF16),
            shaped((HEAD_DIM, heads * rows), BF16),
        ),
        in_specs=[any_spec()] * 5,
        out_specs=[vmem_spec()] * 2 + [any_spec()] * 3,
        scratch_shapes=[
            pltpu.VMEM((rows, D), BF16),
            pltpu.VMEM((2, SMALL_ROWS, SMALL_WIDTH), F32),
            pltpu.VMEM(early.shape, BF16),
            pltpu.VMEM((rows, D), F32),
            pltpu.VMEM((2, SMALL_ROWS, SMALL_WIDTH), F32),
            pltpu.VMEM((D, rows), BF16),
            pltpu.VMEM((rows, D), F32),
            pltpu.VMEM((rows, FF), F32),
            pltpu.VMEM((rows, FF), BF16),
            pltpu.VMEM((rows, FF), BF16),
            pltpu.VMEM((D, rows), BF16),
            pltpu.VMEM(early.shape, BF16),
            pltpu.VMEM((rows, D), F32),
            pltpu.SemaphoreType.DMA((5,)),
        ]
        + sem_pair(heads - 1)
        + sem_pair(heads - 1),
        compiler_params=comm_params(2),
        name="middle_layers",
    )(o_low, out_grad, small, x2, early)


def column_groups(first, width, bits):
    tiles = width // LANES
    unit = 2 ** max(0, bits - 4)
    long = max(1, round(tiles * 0.36 / unit)) * unit
    orders = [
        list(range(bits)),
        [1, 0] + list(range(2, bits)),
        list(range(2, bits)) + [0, 1],
    ]
    groups = []
    for size, order in zip([long, long, tiles - 2 * long], orders):
        if size == 0:
            continue
        groups.append((first, size * LANES, order))
        first += size * LANES
    return groups


def grad_sets(bits):
    bounds = [LATE, LATE + SHRINK, QKV, POINT, LEFT, LEFT + FF // 2, CONV, CONV + FF // 2]
    widths = [SHRINK, EARLY - SHRINK, POINT - QKV, LEFT - POINT] + [FF // 2] * 4
    return [column_groups(first, width, bits) for first, width in zip(bounds, widths)]


class Piece:
    def __init__(self, at, group, links, sums, got, total, sems):
        self.at, (self.first, self.width, self.order) = at, group
        self.core, self.sibling, self.bit_of, self.partner = links
        self.view, self.got, self.total, self.sems = sums, got, total, sems
        self.bits, self.phase, self.trail = len(self.order), 0, []
        self.since = -1
        self.copy = None

    def whole(self):
        return (0, BLOCK, self.first, self.width)

    def out(self, where):
        row, tall, col, wide = where
        return self.total.at[pl.ds(bound(row, ROW_BLOCK), tall), pl.ds(bound(col, LANES), wide)]

    def start(self, other_half):
        self.copy = push_by(
            other_half, self.out(self.whole()), self.sems[0].at[self.at], self.sems[1].at[self.at], self.sibling
        )

    def add(self, where, source, spot, last):
        row, tall, col, wide = where

        @pl.loop(0, tall // ROW_BLOCK)
        def _(step):
            gap = step * ROW_BLOCK
            here = (row + gap, ROW_BLOCK, col, wide)
            there = source.at[pl.ds(bound(spot + gap, ROW_BLOCK), ROW_BLOCK), pl.ds(self.first, wide)]
            mine = self.view(here)[...].astype(F32)
            added = (mine + there[...].astype(F32)).astype(BF16)
            if last:
                self.out(here)[...] = added
            else:
                self.view(here)[...] = added

    def halve(self, step):
        row, tall, col, wide = self.where
        bit = self.order[step]
        mine = self.bit_of[bit]
        if tall > ROW_BLOCK:
            half = tall // 2
            kept = (row + half * mine, half, col, wide)
            sent = (row + half * (1 - mine), half, col, wide)
        else:
            half = wide // 2
            kept = (row, tall, col + half * mine, half)
            sent = (row, tall, col + half * (1 - mine), half)
        self.copy = push_by(
            self.view(sent),
            self.got.at[pl.ds(self.spot, sent[1]), pl.ds(self.first, sent[3])],
            self.sems[0].at[self.at],
            self.sems[2].at[self.at * self.bits + step],
            self.partner[bit],
        )
        self.where = kept

    def double(self, step):
        place_out = self.out(self.trail[step])
        self.copy = push_by(
            place_out,
            place_out,
            self.sems[0].at[self.at],
            self.sems[3].at[self.at * self.bits + step],
            self.partner[self.order[step]],
        )

    def done(self):
        return self.phase > 2 * self.bits

    def sent_all(self):
        return self.phase >= 2 * self.bits

    def advance(self):
        if self.done():
            return
        self.copy.wait()
        if self.phase == 0:
            self.where, self.spot = self.whole(), 0
            self.add(self.where, self.total, 0, False)
            self.halve(0)
        elif self.phase <= self.bits:
            last = self.phase == self.bits
            self.add(self.where, self.got, self.spot, last)
            self.trail.append(self.where)
            self.spot += self.where[1]
            if last:
                self.double(self.bits - 1)
            else:
                self.halve(self.phase)
        elif self.phase < 2 * self.bits:
            self.double(2 * self.bits - 1 - self.phase)
        self.phase += 1


def last_body(count, heads, *refs):
    (
        q_in,
        do_in,
        o_in,
        lse_in,
        kv_in,
        seg_in,
        small_in,
        small_grads_in,
        seg_ref,
        early_grads,
        dx3_in,
        late_in,
        n1_in,
        glu_in,
        n2_in,
        left_in,
        conv_in,
        n3_in,
        depth_in,
        n4_in,
        inv_in,
        masks_in,
        total_out,
        grad_out,
        total,
        weights,
        dx3,
        n1,
        glu_pre,
        n2,
        left_pre,
        conv_pre,
        n3,
        depth,
        n4,
        inv,
        masks,
        small,
        small_grads,
        dq_t,
        dkv_own,
        q_all,
        do_all,
        o_all,
        lse,
        both,
        delta,
        kv_slots,
        seg_slots,
        turned,
        dkv_acc,
        dq_acc,
        dq_low,
        dkv_all,
        small_raw,
        shared,
        summed,
        dqkv,
        sep_own,
        sep_edges,
        sep_ext,
        depth_grad,
        g3_grad,
        row_sums,
        dleft,
        conv_grad,
        conv_taps,
        grads,
        early_own,
        got,
        load_sem,
        keep_sem,
        store_sem,
        tile_sem,
        dq_send,
        dq_recv,
        dkv_send,
        dkv_recv,
        pass_send,
        pass_recv,
        edge_send,
        edge_recv,
        piece_send,
        ws_recv,
        rs_recv,
        ag_recv,
    ) = refs
    own, core = place()
    parts = count // heads
    head, part = own // parts, lax.rem(own, parts)
    rows = dx3.shape[0]
    ext = rows + 2 * EDGE
    mid = slice(EDGE, EDGE + rows)
    sibling = (own, 1 - core)
    peers = others_of(own, core, count)
    bits = count.bit_length() - 1

    sources = (dx3_in, late_in, n4_in, inv_in, depth_in, masks_in, n3_in, left_in, conv_in, n2_in, glu_in, n1_in)
    targets = (dx3, weights, n4, inv, depth, masks, n3, left_pre, conv_pre, n2, glu_pre, n1)
    announce([sibling] + peers)
    own_rows = pl.ds(bound(core * BLOCK, BLOCK), BLOCK)
    attention_loads = [
        move(q_in, q_all, keep_sem.at[2]),
        move(do_in, do_all, keep_sem.at[5]),
        move(o_in, o_all, keep_sem.at[6]),
        move(lse_in, lse, keep_sem.at[7]),
    ]

    near_heads = max(1, KEY_TILE // (parts * rows))
    tiles_each = max(1, parts * rows // KEY_TILE)
    group_count = heads // near_heads
    key_count = count * rows
    longest = key_count // 2

    def group_first(group):
        return lax.rem(head // near_heads + group, group_count) * near_heads

    def group_head(group, at):
        mixed = lax.rem(head, near_heads)
        bit = sum(
            (lax.rem(mixed // 2**k, 2) + (at >> k & 1) - 2 * lax.rem(mixed // 2**k, 2) * (at >> k & 1)) * 2**k
            for k in range(near_heads.bit_length() - 1)
        )
        return group_first(group) + bit

    def tile_first(number):
        group, tile = number // tiles_each, number % tiles_each
        return group_first(group) * parts * rows + tile * KEY_TILE

    def fetch(number):
        here = pl.ds(bound(tile_first(number), KEY_TILE), KEY_TILE)
        return [
            move(kv_in.at[here, pl.ds(0, LANES)], kv_slots.at[number % 2], tile_sem.at[number % 2]),
            move(seg_in.at[here, :], seg_slots.at[number % 2], tile_sem.at[2 + number % 2]),
        ]

    fetched = fetch(0)

    bit_of = [lax.rem(own // 2**bit, 2) for bit in range(bits)]
    partner = [(own + 2**bit - 2 * 2**bit * bit_of[bit], core) for bit in range(bits)]
    links = (core, sibling, bit_of, partner)
    sems = (piece_send, ws_recv, rs_recv, ag_recv)

    def early_view(where):
        row, tall, col, wide = where
        return early_own.at[pl.ds(bound(row, ROW_BLOCK), tall), pl.ds(bound(col - LATE, LANES), wide)]

    def late_view(where):
        row, tall, col, wide = where
        return grads.at[pl.ds(bound(core * BLOCK + row, ROW_BLOCK), tall), pl.ds(bound(col, LANES), wide)]

    sets, at = [], 0
    for number, groups in enumerate(grad_sets(bits)):
        members = []
        for group in groups:
            view = late_view if number > 1 else early_view
            members.append(Piece(at, group, links, view, got, total, sems))
            at += 1
        sets.append(members)
    other_rows = pl.ds(bound((1 - core) * BLOCK, BLOCK), BLOCK)

    def start(members, source, shift):
        for piece in members:
            piece.start(source.at[other_rows, pl.ds(piece.first - shift, piece.width)])

    def advance(members):
        for piece in members:
            if not piece.sent_all():
                piece.advance()

    scale = HEAD_DIM**-0.5
    for copy in attention_loads:
        copy.wait()
    dq_acc[...] = jnp.zeros_like(dq_acc)

    @pl.loop(0, heads)
    def _(tile):
        at = span(tile, rows)
        q = q_all[:, at] * jnp.bfloat16(scale)
        do = do_all[:, at]
        none = jnp.zeros_like(q)
        both[tile] = jnp.concatenate(
            [jnp.concatenate([q, none], axis=1), jnp.concatenate([none, do], axis=1)], axis=0
        )
        delta[:, at] = jnp.sum(o_all[:, at] * do.astype(F32), axis=0, keepdims=True)

    def attention_tile(number):
        first, slot = tile_first(number), number % 2

        def one(tile):
            source = tile * parts + part
            apart = jnp.maximum(
                first - (source * rows + rows - 1), source * rows - (first + KEY_TILE - 1)
            )

            @pl.when(apart < longest)
            def _():
                at = span(tile, rows)
                operand = both[tile]
                pair = matmul(kv_slots[slot], operand)
                seg_k = jnp.concatenate([seg_slots[slot]] * (rows // LANES), axis=1)
                seg_q = seg_ref[source].astype(F32)
                scores = jnp.where(seg_k == seg_q, pair[:, :rows], MASK_FILL)
                probs = jnp.exp(scores - lse[:, at])
                score_grad = (probs * (pair[:, rows:] - delta[:, at])).astype(BF16)
                joined = jnp.concatenate([score_grad, probs.astype(BF16)], axis=1)
                dkv_acc[...] += back_mul(joined, operand)
                dq_acc[:, at] += matmul(turned[...], score_grad)

        return one

    collect, sharing, arrived = [], [], []

    def share_group(group):
        for at in range(near_heads):
            other = group_head(group, at)
            for gap in range(parts - 1):
                twin = lax.rem(part + gap + 1, parts)
                sharing.append(
                    push(
                        dkv_all.at[span(other * parts + twin, rows), :],
                        shared.at[gap, group * near_heads + at],
                        (pass_send, pass_recv),
                        gap * heads + group * near_heads + at,
                        (head * parts + twin, core),
                    )
                )

    def send_group(group):
        for at in range(near_heads):
            other, index = group_head(group, at), group * near_heads + at
            for copy in sharing[index * (parts - 1) : (index + 1) * (parts - 1)]:
                copy.wait()
            total_kv = dkv_all[span(other * parts + part, rows), :].astype(F32)
            for gap in range(parts - 1):
                total_kv = total_kv + shared[gap, index].astype(F32)
            if index:
                summed[index] = total_kv.astype(BF16)
                collect.append(
                    push(
                        summed.at[index],
                        dkv_own.at[:, span(head, LANES)],
                        (dkv_send, dkv_recv),
                        index - 1,
                        (other * parts + part, core),
                    )
                )
            else:
                dkv_own[:, span(head, LANES)] = total_kv.astype(BF16)

    slot = dq_t.at[span(head, HEAD_DIM), :]

    def send_dq(gap, other):
        here = span(other, rows)
        dq_low[:, here] = (dq_acc[:, here] * scale).astype(BF16)
        if gap < heads:
            collect.append(
                push(dq_low.at[:, here], slot, (dq_send, dq_recv), gap - 1, (other * parts + part, core))
            )
        else:
            collect.append(move(dq_low.at[:, here], slot, keep_sem.at[0]))

    points, keeps, loads = [], [], []

    def pump():
        at = len(points)
        points.append(at)
        if at == 0:
            all_here([sibling] + peers)
            start(sets[0] + sets[1], early_grads, LATE)
            keeps.append(move(early_grads.at[own_rows, :], early_own, keep_sem.at[1]))
            keeps.append(move(small_in, small_raw, keep_sem.at[3]))
            keeps.append(move(small_grads_in, small_grads, keep_sem.at[4]))
        elif at == 1:
            for copy in keeps:
                copy.wait()
            widened(small, small_raw)
            advance(sets[0])
            loads.extend(move(a, b, load_sem.at[k]) for k, (a, b) in enumerate(zip(sources, targets)))
        elif at in (4, 7, 9, 11, 13, 15):
            advance(sets[0])
        elif at in (2, 6, 8, 10, 12, 14):
            advance(sets[1])

    tiles = group_count * tiles_each
    for number in range(tiles):
        for copy in fetched:
            copy.wait()
        if number + 1 < tiles:
            fetched = fetch(number + 1)
        turned[...] = turn(kv_slots[number % 2, :, :HEAD_DIM])
        dkv_acc[...] = jnp.zeros_like(dkv_acc)
        group = number // tiles_each
        one = attention_tile(number)
        for turn_no in range(4):
            reach = (turn_no * heads // 4 + 1, (turn_no + 1) * heads // 4 + 1)
            pl.loop(*reach)(lambda gap: one(lax.rem(head + gap, heads)))
            if number == tiles - 1:
                for gap in range(*reach):
                    send_dq(gap, lax.rem(head + gap, heads))
            if turn_no == 2 and group and number % tiles_each == 0:
                send_group(group - 1)
            if turn_no < 3:
                pump()
        here = pl.ds(bound(tile_first(number), KEY_TILE), KEY_TILE)
        dkv_all[here, :] = dkv_acc[...].astype(BF16)
        if number % tiles_each == tiles_each - 1:
            share_group(group)
        pump()
    for copy in loads:
        copy.wait()
    send_group(group_count - 1)
    for copy in collect:
        copy.wait()

    dqkv[:, :D] = turn(dq_t[...])
    lane = lax.broadcasted_iota(jnp.int32, (rows, LANES), 1) < HEAD_DIM
    for step in range(D // LANES):
        pair = []
        for side in range(2):
            first = (2 * step + side) * LANES
            pair.append(dkv_own[:, first : first + LANES].astype(F32))
        cols = slice(D + step * LANES, D + (step + 1) * LANES)
        dqkv[:, cols] = jnp.where(lane, pair[0], pltpu.roll(pair[1], HEAD_DIM, 1)).astype(BF16)
        cols = slice(2 * D + step * LANES, 2 * D + (step + 1) * LANES)
        dqkv[:, cols] = jnp.where(lane, pltpu.roll(pair[0], HEAD_DIM, 1), pair[1]).astype(BF16)

    def through(grad, column, width):
        return jnp.concatenate(
            [
                back_mul(grad, weights[side * BLOCK : (side + 1) * BLOCK, column : column + width])
                for side in range(2)
            ],
            axis=1,
        )

    def norm_step(grad, normed, inv_std, row):
        put_vector(small_grads, row, col_sum(grad * normed))
        put_vector(small_grads, row + 1, col_sum(grad))
        return norm_back(grad, normed, inv_std, vector(small, row, D))

    grad = through(dqkv[...], QKV, 3 * D)
    dx2 = dx3[...] + norm_step(grad, n4[...], inv[3, :rows, :1], LN4G)
    dx3[...] = dx2
    sep_own[...] = dx2[:, :HALF].astype(BF16)
    right, left = (lax.rem(own + 1, count), core), (lax.rem(own + count - 1, count), core)
    edge_copies = [
        push(sep_own.at[pl.ds(rows - EDGE, EDGE), :], sep_edges.at[0], (edge_send, edge_recv), 0, right),
        push(sep_own.at[pl.ds(0, EDGE), :], sep_edges.at[1], (edge_send, edge_recv), 1, left),
    ]
    low_t = turn(n4[...] * vector(small, LN4G, D) + vector(small, LN4B, D))
    for step in range(3):
        grads[:, QKV + D * step : QKV + D * (step + 1)] = matmul(
            low_t, dqkv[:, D * step : D * (step + 1)]
        ).astype(BF16)
    start(sets[2], grads, 0)
    advance(sets[0])
    for block in range(FF // BLOCK):
        side, column = block // 4, POINT + HALF * (block % 4)
        grads[side * BLOCK : (side + 1) * BLOCK, column : column + HALF] = matmul(
            turn(depth[:, block * BLOCK : (block + 1) * BLOCK]), sep_own[...]
        ).astype(BF16)
    start(sets[3], grads, 0)
    put_vector(small_grads, POINTB, col_sum(sep_own[...]))

    for copy in edge_copies:
        copy.wait()
    sep_ext[:EDGE, :] = sep_edges[0]
    sep_ext[mid, :] = sep_own[...]
    sep_ext[EDGE + rows :, :] = sep_edges[1]
    for block in range(FF // BLOCK):
        side, column = block // 4, POINT + HALF * (block % 4)
        depth_grad[:, block * BLOCK : (block + 1) * BLOCK] = (
            back_mul(sep_ext[...], weights[side * BLOCK : (side + 1) * BLOCK, column : column + HALF])
            .astype(BF16)
            .astype(F32)
        )

    advance(sets[2])
    row_sums[...] = jnp.zeros_like(row_sums)
    half = FF // 2 // LANES

    def tap_block(step):
        cols = span(step, LANES)
        side, lanes = step // half, span(lax.rem(step, half), LANES)
        block = depth_grad[:, cols]
        normed = n3[:, cols]
        gain = small[side, LN3G : LN3G + 1, lanes]
        low = (normed[mid, :] * gain + small[side, LN3B : LN3B + 1, lanes]).astype(BF16).astype(F32)
        summed = jnp.zeros((ext, LANES), F32)
        for tap in range(TAPS):
            row = DEPTH + tap
            moved = pltpu.roll(block, (tap - REACH) % ext, 0) * masks[TAPS - 1 - tap]
            summed = summed + moved * small[side, row : row + 1, lanes]
            small_grads[side, row : row + 1, lanes] = col_sum(low * moved[mid, :])
        g3_grad[:, cols] = summed
        small_grads[side, LN3G : LN3G + 1, lanes] = col_sum(summed[mid, :] * normed[mid, :])
        small_grads[side, LN3B : LN3B + 1, lanes] = col_sum(summed[mid, :])
        scaled = summed * gain
        row_sums[0] = row_sums[0] + scaled
        row_sums[1] = row_sums[1] + scaled * normed

    for quarter, turns in enumerate((sets[1], sets[3], sets[2], sets[1])):
        pl.loop(quarter * half // 2, (quarter + 1) * half // 2)(tap_block)
        advance(turns)
    inner = jnp.sum(row_sums[0], axis=1, keepdims=True) * (1.0 / FF)
    cross = jnp.sum(row_sums[1], axis=1, keepdims=True) * (1.0 / FF)
    row_sums[0] = jnp.broadcast_to(inner, (ext, LANES))
    row_sums[1] = jnp.broadcast_to(cross, (ext, LANES))

    def left_block(step):
        cols = span(step, LANES)
        side, lanes = step // half, span(lax.rem(step, half), LANES)
        scaled = g3_grad[mid, cols] * small[side, LN3G : LN3G + 1, lanes]
        mixed_grad = inv[2, mid, :] * (scaled - row_sums[0, mid, :] - n3[mid, cols] * row_sums[1, mid, :])
        low = (mixed_grad * smooth_slope(left_pre[:, cols])).astype(BF16)
        dleft[:, cols] = low
        small_grads[side, LEFTB : LEFTB + 1, lanes] = col_sum(low)

    pl.loop(0, half)(left_block)
    advance(sets[3])
    pl.loop(half, 2 * half)(left_block)
    advance(sets[0])
    for step in range(HALF // LANES):
        cols = slice(step * LANES, (step + 1) * LANES)
        scaled = g3_grad[:, cols] * small[0, LN3G : LN3G + 1, cols]
        mixed_grad = inv[2] * (scaled - row_sums[0] - n3[:, cols] * row_sums[1])
        low = (mixed_grad * smooth_slope(conv_pre[:, cols])).astype(BF16).astype(F32)
        conv_grad[:, cols] = low
        for tap in range(3):
            moved = pltpu.roll(low, (tap - 1) % ext, 0) * masks[REACH + 1 - tap]
            conv_taps[:, HALF * tap + step * LANES : HALF * tap + (step + 1) * LANES] = moved[mid, :].astype(BF16)
    put_vector(small_grads, CONVB, col_sum(conv_grad[mid, :]))

    low_t = turn(n2[...] * vector(small, LN2G, D) + vector(small, LN2B, D))
    for step in range(FF // 512):
        grads[:, LEFT + 512 * step : LEFT + 512 * (step + 1)] = matmul(
            low_t, dleft[:, 512 * step : 512 * (step + 1)]
        ).astype(BF16)
        if step % 2:
            start(sets[4 + step // 2], grads, 0)
    advance(sets[2])
    for tap in range(3):
        grads[:, CONV + HALF * tap : CONV + HALF * (tap + 1)] = matmul(
            low_t, conv_taps[:, HALF * tap : HALF * (tap + 1)]
        ).astype(BF16)
    advance(sets[4])
    advance(sets[5])
    grad = through(dleft[...], LEFT, FF) + through(conv_taps[...], CONV, 3 * HALF)
    dx1 = dx3[...] + norm_step(grad, n2[...], inv[1, mid, :1], LN2G)
    gate = jax.nn.sigmoid(glu_pre[:, D:])
    value_grad = dx1 * gate
    dglu = jnp.concatenate([value_grad, value_grad * glu_pre[:, :D] * (1.0 - gate)], axis=1).astype(BF16)
    put_vector(small_grads, GLUB, col_sum(dglu))
    advance(sets[1])
    advance(sets[3])
    low_t = turn(n1[...] * vector(small, LN1G, D) + vector(small, LN1B, D))
    for step in range(2):
        grads[:, GLU + D * step : GLU + D * (step + 1)] = matmul(
            low_t, dglu[:, D * step : D * (step + 1)]
        ).astype(BF16)
    start(sets[6], grads, 0)
    advance(sets[2])
    grad = through(dglu, GLU, 2 * D)
    dx3[...] = dx1 + norm_step(grad, n1[...], inv[0, mid, :1], LN1G)
    keep = move(dx3, grad_out, keep_sem.at[0])
    for side in range(2):
        for block in range(SMALL_WIDTH // BLOCK):
            first = side * BLOCK + block * SMALL_ROWS
            grads[first : first + SMALL_ROWS, SMALL : SMALL + BLOCK] = small_grads[
                side, :, block * BLOCK : (block + 1) * BLOCK
            ].astype(BF16)
        first = side * BLOCK + SMALL_WIDTH // BLOCK * SMALL_ROWS
        grads[first : (side + 1) * BLOCK, SMALL : SMALL + BLOCK] = jnp.zeros(
            ((side + 1) * BLOCK - first, BLOCK), BF16
        )
    start(sets[7], grads, 0)
    advance(sets[4] + sets[5])
    pieces = [piece for number in (6, 7, 4, 5, 2, 3, 0, 1) for piece in sets[number]]
    stores, rounds = [], 0
    while not all(piece.done() for piece in pieces):
        last = all(piece.sent_all() for piece in pieces)
        for piece in pieces:
            if not piece.sent_all():
                piece.advance()
                piece.since = rounds
            elif not piece.done() and (last or piece.since < rounds - 1):
                piece.advance()
                cols = pl.ds(piece.first, piece.width)
                stores.append(move(total.at[:, cols], total_out.at[:, cols], store_sem.at[piece.at]))
        rounds += 1
    for copy in stores:
        copy.wait()
    keep.wait()


def last_kernel(attention, small, small_grads, seg, tensors, count, heads):
    rows = seg.shape[2]
    ext = rows + 2 * EDGE
    parts = count // heads
    bits = count.bit_length() - 1
    pieces = sum(len(groups) for groups in grad_sets(bits))
    scratch = [
        pltpu.VMEM((BLOCK, WIDTH), BF16),
        pltpu.VMEM(tensors[2].shape, BF16),
        pltpu.VMEM((rows, D), F32),
        pltpu.VMEM((rows, D), F32),
        pltpu.VMEM((rows, 2 * D), F32),
        pltpu.VMEM((rows, D), F32),
        pltpu.VMEM((rows, FF), F32),
        pltpu.VMEM((ext, HALF), F32),
        pltpu.VMEM((ext, FF), F32),
        pltpu.VMEM((rows, FF), BF16),
        pltpu.VMEM((rows, D), F32),
        pltpu.VMEM((4, ext, LANES), F32),
        pltpu.VMEM((TAPS, ext, LANES), F32),
        pltpu.VMEM((2, SMALL_ROWS, SMALL_WIDTH), F32),
        pltpu.VMEM((2, SMALL_ROWS, SMALL_WIDTH), F32),
        pltpu.VMEM((D, rows), BF16),
        pltpu.VMEM((rows, 2 * D), BF16),
        pltpu.VMEM((HEAD_DIM, heads * rows), BF16),
        pltpu.VMEM((HEAD_DIM, heads * rows), BF16),
        pltpu.VMEM((HEAD_DIM, heads * rows), F32),
        pltpu.VMEM((1, heads * rows), F32),
        pltpu.VMEM((heads, LANES, 2 * rows), BF16),
        pltpu.VMEM((1, heads * rows), F32),
        pltpu.VMEM((2, KEY_TILE, LANES), BF16),
        pltpu.VMEM((2, KEY_TILE, LANES), F32),
        pltpu.VMEM((HEAD_DIM, KEY_TILE), BF16),
        pltpu.VMEM((KEY_TILE, LANES), F32),
        pltpu.VMEM((HEAD_DIM, heads * rows), F32),
        pltpu.VMEM((HEAD_DIM, heads * rows), BF16),
        pltpu.VMEM((count * rows, LANES), BF16),
        pltpu.VMEM((2, SMALL_ROWS, SMALL_WIDTH), F32),
        pltpu.VMEM((parts - 1, heads, rows, LANES), BF16),
        pltpu.VMEM((heads, rows, LANES), BF16),
        pltpu.VMEM((rows, 3 * D), BF16),
        pltpu.VMEM((rows, HALF), BF16),
        pltpu.VMEM((2, EDGE, HALF), BF16),
        pltpu.VMEM((ext, HALF), BF16),
        pltpu.VMEM((ext, FF), F32),
        pltpu.VMEM((ext, FF), F32),
        pltpu.VMEM((2, ext, LANES), F32),
        pltpu.VMEM((rows, FF), BF16),
        pltpu.VMEM((ext, HALF), F32),
        pltpu.VMEM((rows, 3 * HALF), BF16),
        pltpu.VMEM((2 * BLOCK, LATE), BF16),
        pltpu.VMEM((BLOCK, EARLY), BF16),
        pltpu.VMEM((BLOCK + ROW_BLOCK * max(0, bits - 4), WIDTH), BF16),
        pltpu.SemaphoreType.DMA((12,)),
        pltpu.SemaphoreType.DMA((8,)),
        pltpu.SemaphoreType.DMA((pieces,)),
        pltpu.SemaphoreType.DMA((4,)),
    ]
    scratch += sem_pair(heads - 1) + sem_pair(heads - 1) + sem_pair((parts - 1) * heads)
    scratch += sem_pair(2) + sem_pair(pieces)
    scratch += [pltpu.SemaphoreType.DMA((pieces * bits,))] * 2
    return pl.pallas_call(
        functools.partial(last_body, count, heads),
        out_shape=(shaped((BLOCK, WIDTH), BF16), shaped((rows, D))),
        in_specs=[any_spec()] * (len(attention) + 2) + [vmem_spec()] + [any_spec()] * len(tensors),
        out_specs=[any_spec(), any_spec()],
        scratch_shapes=scratch,
        compiler_params=comm_params(3),
        name="last_layers",
    )(*attention, small, small_grads, seg, *tensors)


def unpack_body(output_in, grad_in, packed_in, *refs):
    size = len(MATRICES) + len(VECTORS) + 2
    outs, (packed, output, grad, *stages, load_sem, out_sem) = refs[:size], refs[size:]
    output_ref, grad_ref, *outs = outs
    order = [len(MATRICES)] + list(range(len(MATRICES)))
    bounds = [(first, width * blocks) for first, width, blocks in MATRICES] + [(SMALL, BLOCK)]
    loads = {}
    for at in order:
        cols = pl.ds(*bounds[at])
        loads[at] = move(packed_in.at[:, cols], packed.at[:, cols], load_sem.at[at])
    passed = [
        move(output_in, output, load_sem.at[len(MATRICES) + 1]),
        move(grad_in, grad, load_sem.at[len(MATRICES) + 2]),
    ]
    stores = []
    for at, (first, width, blocks) in enumerate(MATRICES):
        loads[at].wait()
        stage = stages[at]
        tall = 2 * ROW_BLOCK

        @pl.loop(0, BLOCK // tall, unroll=2)
        def _(step):
            for block in range(blocks):
                value = packed[span(step, tall), first + block * width : first + (block + 1) * width].astype(F32)
                if blocks == 3:
                    stage[block, span(step, tall), :] = value
                else:
                    stage[pl.ds(bound(block * BLOCK + step * tall, tall), tall), :] = value

        stores.append(move(stage, outs[at], out_sem.at[at]))

    for copy in passed:
        copy.wait()
    stores.append(move(output, output_ref, out_sem.at[len(MATRICES)]))
    stores.append(move(grad, grad_ref, out_sem.at[len(MATRICES) + 1]))
    loads[len(MATRICES)].wait()
    small = jnp.concatenate(
        [
            packed[block * SMALL_ROWS : (block + 1) * SMALL_ROWS, SMALL : SMALL + BLOCK].astype(F32)
            for block in range(SMALL_WIDTH // BLOCK)
        ],
        axis=1,
    )
    for (row, tall, size), out in zip(VECTORS, outs[len(MATRICES) :]):
        out[...] = small[row : row + tall, :size]
    for copy in stores:
        copy.wait()


def unpack(output, grad, packed):
    shapes = []
    for _, width, blocks in MATRICES:
        shapes.append((3, BLOCK, width) if blocks == 3 else (blocks * BLOCK, width))
    vectors = [(tall, size) for _, tall, size in VECTORS]
    return pl.pallas_call(
        unpack_body,
        out_shape=(shaped(output.shape, output.dtype), shaped(grad.shape))
        + tuple(shaped(shape) for shape in shapes + vectors),
        in_specs=[any_spec()] * 3,
        out_specs=[any_spec()] * (2 + len(shapes)) + [vmem_spec()] * len(vectors),
        scratch_shapes=[
            pltpu.VMEM(packed.shape, packed.dtype),
            pltpu.VMEM(output.shape, output.dtype),
            pltpu.VMEM(grad.shape, F32),
        ]
        + [pltpu.VMEM(shape, F32) for shape in shapes]
        + [pltpu.SemaphoreType.DMA((len(shapes) + 3,)), pltpu.SemaphoreType.DMA((len(shapes) + 2,))],
        compiler_params=pltpu.CompilerParams(vmem_limit_bytes=VMEM_MOST),
        name="unpack",
    )(output, grad, packed)


def body(tokens, segment_ids, out_grad, *params):
    (
        ln1g, ln1b, glu_w, glu_b, ln2g, ln2b, left_w, left_b, conv_w, conv_b, ln3g, ln3b, depth_w,
        point_w, point_b, ln4g, ln4b, qkv_w, attn_w, attn_b, ln5g, ln5b, expand_w, expand_b,
        shrink_w, shrink_b,
    ) = params
    count = lax.axis_size("ctx")
    heads = D // HEAD_DIM
    rows = tokens.shape[1]
    vectors = [
        ln1g, ln1b, glu_b, ln2g, ln2b, left_b, conv_b, ln3g, ln3b, depth_w,
        point_b, ln4g, ln4b, attn_b, ln5g, ln5b, expand_b, shrink_b,
    ]
    vectors = [value.reshape(-1, value.shape[-1]) for value in vectors]
    weights = (glu_w, left_w, conv_w, point_w, qkv_w, attn_w, expand_w, shrink_w)
    (
        late, early, small, seg, plan, q_head, kv_head, n1, glu_pre, n2, left_pre, conv_pre, n3,
        depth, n4, x2, inv, masks, seg_cols,
    ) = first_kernel(tokens[0], segment_ids, vectors, weights, count, heads)
    o_head, o_low, log_sum = attend(plan, q_head, kv_head, seg, rows)
    output, small_grads, dx3, early_grads, do_head = middle_kernel(
        o_low, out_grad[0], small, x2, early, count, heads
    )
    tensors = (
        early_grads, dx3, late, n1, glu_pre, n2, left_pre, conv_pre, n3, depth, n4, inv, masks,
    )
    attention = (q_head, do_head, o_head, log_sum, kv_head, seg_cols)
    total, input_grad = last_kernel(attention, small, small_grads, seg, tensors, count, heads)
    output, input_grad, *pieces = unpack(output, input_grad, total)
    matrices, lines = pieces[: len(MATRICES)], pieces[len(MATRICES) :]
    lines = [line if line.shape[0] > 1 else line.reshape(-1) for line in lines]
    g_glu, g_left, g_conv, g_point, g_qkv, g_attn, g_expand, g_shrink = matrices
    (
        g_ln1g, g_ln1b, g_glu_b, g_ln2g, g_ln2b, g_left_b, g_conv_b, g_ln3g, g_ln3b, g_depth,
        g_point_b, g_ln4g, g_ln4b, g_attn_b, g_ln5g, g_ln5b, g_expand_b, g_shrink_b,
    ) = lines
    return (
        output[None], input_grad[None], g_ln1g, g_ln1b, g_glu, g_glu_b, g_ln2g, g_ln2b, g_left,
        g_left_b, g_conv, g_conv_b, g_ln3g, g_ln3b, g_depth, g_point, g_point_b, g_ln4g, g_ln4b,
        g_qkv, g_attn, g_attn_b, g_ln5g, g_ln5b, g_expand, g_expand_b, g_shrink, g_shrink_b,
    )


def solution(mesh):
    return jax.shard_map(
        body,
        mesh=mesh,
        in_specs=(
            P("ws", "ctx", None),
            P("ws", "ctx"),
            P("ws", "ctx", None),
            P("ws"),
            P("ws"),
            P("ws", None),
            P("ws"),
            P("ws"),
            P("ws"),
            P("ws", None),
            P("ws"),
            P(None, "ws", None),
            P("ws"),
            P("ws"),
            P("ws"),
            P(None, "ws"),
            P("ws", None),
            P("ws"),
            P("ws"),
            P("ws"),
            P("ws", None),
            P("ws", None),
            P("ws"),
            P("ws"),
            P("ws"),
            P("ws", None),
            P("ws"),
            P("ws", None),
            P("ws"),
        ),
        out_specs=(
            P("ws", "ctx", None),
            P("ws", "ctx", None),
            P("ws"),
            P("ws"),
            P("ws", None),
            P("ws"),
            P("ws"),
            P("ws"),
            P("ws", None),
            P("ws"),
            P(None, "ws", None),
            P("ws"),
            P("ws"),
            P("ws"),
            P(None, "ws"),
            P("ws", None),
            P("ws"),
            P("ws"),
            P("ws"),
            P("ws", None),
            P("ws", None),
            P("ws"),
            P("ws"),
            P("ws"),
            P("ws", None),
            P("ws"),
            P("ws", None),
            P("ws"),
        ),
        check_vma=False,
    )
```

```python
import functools
import math

import jax
import jax.numpy as jnp
from jax import lax
from jax.experimental import pallas as pl
from jax.experimental.pallas import tpu as pltpu
from jax.sharding import PartitionSpec as P

MESH_ID = pl.DeviceIdType.MESH
F32 = jnp.float32
BF16 = jnp.bfloat16
HEAD_DIM = 64
NORM_EPS = 1e-06
MASK_FILL = -1e30
LANES = 128
ROW_BLOCK = 16
EDGE = 16
KEY_TILE = 1024
BLOCK = 256
VMEM_MOST = 62 * 1024 * 1024

D = 512
FF = 2048
HALF = 256
TAPS = 9
REACH = 4

QKV, POINT, LEFT, CONV, GLU, SMALL, LATE = 0, 1536, 2560, 4608, 5376, 6400, 6656
ATTN, EXPAND, SHRINK, EARLY = 0, 512, 2560, 4608
WIDTH = LATE + EARLY

SMALL_ROWS = 32
SMALL_WIDTH = 1024
(LN1G, LN1B, GLUB, LN2G, LN2B, LEFTB, CONVB, LN3G, LN3B, DEPTH) = range(10)
(POINTB, LN4G, LN4B, ATTNB, LN5G, LN5B, EXPANDB, SHRINKB) = range(DEPTH + TAPS, DEPTH + TAPS + 8)


VECTORS = [
    (LN1G, 1, 256),
    (LN1B, 1, 256),
    (GLUB, 1, 512),
    (LN2G, 1, 256),
    (LN2B, 1, 256),
    (LEFTB, 1, 1024),
    (CONVB, 1, 128),
    (LN3G, 1, 1024),
    (LN3B, 1, 1024),
    (DEPTH, TAPS, 1024),
    (POINTB, 1, 128),
    (LN4G, 1, 256),
    (LN4B, 1, 256),
    (ATTNB, 1, 256),
    (LN5G, 1, 256),
    (LN5B, 1, 256),
    (EXPANDB, 1, 1024),
    (SHRINKB, 1, 256),
]
MATRICES = [
    (GLU, 1024, 1),
    (LEFT, 2048, 1),
    (CONV, 256, 3),
    (POINT, 256, 4),
    (QKV, 1536, 1),
    (LATE + ATTN, 512, 1),
    (LATE + EXPAND, 2048, 1),
    (LATE + SHRINK, 512, 4),
]


def vmem_spec():
    return pl.BlockSpec(memory_space=pltpu.VMEM)


def any_spec():
    return pl.BlockSpec(memory_space=pl.ANY)


def smem_spec():
    return pl.BlockSpec(memory_space=pltpu.SMEM)


def shaped(shape, kind=F32):
    return jax.ShapeDtypeStruct(shape, kind)


def comm_params(number):
    return pltpu.CompilerParams(
        collective_id=number, has_side_effects=True, vmem_limit_bytes=VMEM_MOST
    )


def announce(peers):
    barrier = pltpu.get_barrier_semaphore()
    for peer in peers:
        pl.semaphore_signal(barrier, inc=1, device_id=peer, device_id_type=MESH_ID)


def all_here(peers):
    pl.semaphore_wait(pltpu.get_barrier_semaphore(), len(peers))


def greet(peers):
    announce(peers)
    all_here(peers)


def push(src, dst, sems, at, peer):
    copy = pltpu.make_async_remote_copy(
        src_ref=src,
        dst_ref=dst,
        send_sem=sems[0].at[at],
        recv_sem=sems[1].at[at],
        device_id=peer,
        device_id_type=MESH_ID,
    )
    copy.start()
    return copy


def push_by(src, dst, send_sem, recv_sem, peer):
    copy = pltpu.make_async_remote_copy(
        src_ref=src,
        dst_ref=dst,
        send_sem=send_sem,
        recv_sem=recv_sem,
        device_id=peer,
        device_id_type=MESH_ID,
    )
    copy.start()
    return copy


def move(src, dst, sem):
    copy = pltpu.make_async_copy(src, dst, sem)
    copy.start()
    return copy


def sem_pair(count):
    return [pltpu.SemaphoreType.DMA((count,)), pltpu.SemaphoreType.DMA((count,))]


def bound(value, step):
    return value if isinstance(value, int) else pl.multiple_of(value, step)


def span(value, step):
    return pl.ds(bound(value * step, step), step)


def matmul(left_op, right_op):
    return jnp.dot(left_op, right_op, preferred_element_type=F32)


def back_mul(grad_in, weight):
    return lax.dot_general(grad_in, weight, (((1,), (1,)), ((), ())), preferred_element_type=F32)


def turn(block):
    return block.astype(F32).T.astype(BF16)


def col_sum(block):
    return jnp.sum(block.astype(F32), axis=0, keepdims=True)


def lane_mean(block):
    return jnp.mean(block, axis=-1, keepdims=True)


def smooth_slope(block):
    sigma = jax.nn.sigmoid(block)
    return sigma * (1.0 + block * (1.0 - sigma))


def norm_fwd(block):
    centred = block - lane_mean(block)
    inv_std = lax.rsqrt(lane_mean(centred * centred) + NORM_EPS)
    return centred * inv_std, inv_std


def norm_back(grad_in, normed, inv_std, gain):
    scaled = grad_in * gain
    inner, cross = lane_mean(scaled), lane_mean(scaled * normed)
    return inv_std * (scaled - inner - normed * cross)


def vector(small_ref, row, size):
    half = size // 2
    return jnp.concatenate(
        [small_ref[core, row : row + 1, :half] for core in range(2)], axis=1
    )


def put_vector(small_ref, row, value):
    half = value.shape[1] // 2
    for core in range(2):
        small_ref[core, row : row + 1, :half] = value[:, core * half : (core + 1) * half]


def place():
    own, core = lax.axis_index("ctx"), lax.axis_index("ws")
    return own, core


def others_of(own, core, count):
    return [(lax.rem(own + gap, count), core) for gap in range(1, count)]


def widened(dst_ref, src_ref):
    @pl.loop(0, 2)
    def _(core):
        dst_ref[core] = src_ref[core].astype(BF16).astype(F32)


def turned_segments(out_ref, first, row):
    for step in range(row.shape[1] // LANES):
        part = row[:, step * LANES : (step + 1) * LANES].astype(F32)
        here = pl.ds(bound(first + step * LANES, LANES), LANES)
        out_ref[here, :] = jnp.broadcast_to(part, (LANES, LANES)).T


def mark_segments(marks, columns, seg_ref):
    count, _, rows = seg_ref.shape

    @pl.loop(0, count)
    def _(source):
        row = seg_ref[source].astype(F32)
        for step in range(rows // LANES):
            part = jnp.broadcast_to(row[:, step * LANES : (step + 1) * LANES], (LANES, LANES)).T
            number = lax.broadcasted_iota(jnp.int32, (LANES, LANES), 1).astype(F32)
            here = pl.ds(bound(source * rows + step * LANES, LANES), LANES)
            columns[here, :] = part
            marks[here, :] = jnp.where(part == number, 1.0, 0.0).astype(BF16)


WEIGHT_COLUMNS = [
    (0, GLU, 1024, 1, False),
    (1, LEFT, 2048, 1, False),
    (2, CONV, 256, 3, False),
    (3, POINT, 256, 4, False),
    (4, QKV, 1536, 1, False),
    (5, ATTN, 512, 1, True),
    (6, EXPAND, 2048, 1, True),
    (7, SHRINK, 512, 4, True),
]


def tap_masks(mask_ref, seg_ref):
    seg = seg_ref[...]
    for tap in range(TAPS):
        moved = pltpu.roll(seg, (REACH - tap) % seg.shape[0], 0)
        mask_ref[tap] = jnp.where(moved == seg, 1.0, 0.0).astype(F32)


def first_body(
    count,
    heads,
    tok_ref,
    seg_row_ref,
    *refs,
):
    vectors, refs = refs[: len(VECTORS)], refs[len(VECTORS) :]
    weights, refs = refs[:8], refs[8:]
    outs, refs = refs[:19], refs[19:]
    (
        late_out,
        early_out,
        small_out,
        seg_all,
        plan_out,
        q_out,
        kv_out,
        n1_out,
        glu_out,
        n2_out,
        left_out,
        conv_out,
        n3_out,
        depth_out,
        n4_out,
        x2_out,
        inv_out,
        masks_out,
        seg_out,
    ) = outs
    (
        staged,
        late,
        early,
        edges,
        seg_edges,
        seg_col,
        small_own,
        x_ext,
        seg_ext,
        masks,
        small,
        low_ext,
        n1,
        glu_pre,
        x1,
        n2,
        shifted,
        left_pre,
        conv_pre,
        n3,
        g3,
        depth,
        x2,
        n4,
        inv,
        q_turned,
        kv_own,
        marks,
        columns,
        load_sem,
        out_sem,
        ws_send,
        ws_recv,
        edge_send,
        edge_recv,
        row_send,
        row_recv,
        q_send,
        q_recv,
        kv_send,
        kv_recv,
        pass_send,
        pass_recv,
    ) = refs
    own, core = place()
    parts = count // heads
    head, part = own // parts, lax.rem(own, parts)
    rows = tok_ref.shape[0]
    ext = rows + 2 * EDGE
    mid = slice(EDGE, EDGE + rows)
    sibling = (own, 1 - core)
    peers = others_of(own, core, count)

    loads, column = [], 0
    stage_at = []
    for number, first, width, blocks, _ in WEIGHT_COLUMNS:
        stage_at.append(column)
        for block in range(blocks):
            source = weights[number]
            if blocks == 3:
                source = source.at[block]
            elif blocks > 1:
                source = source.at[pl.ds(block * BLOCK, BLOCK), :]
            loads.append(
                pltpu.make_async_copy(
                    source,
                    staged.at[:, pl.ds(column, width)],
                    load_sem.at[len(loads)],
                )
            )
            if number < 3:
                loads[-1].start()
            column += width
    small_own[...] = jnp.zeros_like(small_own)
    for (row, tall, size), vector_ref in zip(VECTORS, vectors):
        small_own[row : row + tall, :size] = vector_ref[...]
    turned_segments(seg_col, 0, seg_row_ref[...])
    greet([sibling] + peers)
    for load in loads[5:]:
        load.start()

    copies = []
    right, left = (lax.rem(own + 1, count), core), (lax.rem(own + count - 1, count), core)
    edge_copies = [
        push(tok_ref.at[pl.ds(rows - EDGE, EDGE), :], edges.at[0], (edge_send, edge_recv), 0, right),
        push(tok_ref.at[pl.ds(0, EDGE), :], edges.at[1], (edge_send, edge_recv), 1, left),
        push(seg_col.at[pl.ds(rows - EDGE, EDGE), :], seg_edges.at[0], (edge_send, edge_recv), 2, right),
        push(seg_col.at[pl.ds(0, EDGE), :], seg_edges.at[1], (edge_send, edge_recv), 3, left),
    ]
    small_copy = push(small_own, small_out.at[core], (ws_send, ws_recv), len(WEIGHT_COLUMNS), sibling)
    small_out[core] = small_own[...]

    at, weight_copies = 0, []
    for (number, first, width, blocks, is_early), column in zip(WEIGHT_COLUMNS, stage_at):
        target = early if is_early else late
        for _ in range(blocks):
            loads[at].wait()
            at += 1
        size = width * blocks
        mine = pl.ds(bound(core * BLOCK, BLOCK), BLOCK)

        @pl.loop(0, BLOCK // ROW_BLOCK)
        def _(step):
            source = staged[span(step, ROW_BLOCK), pl.ds(column, size)]
            goes = pl.ds(bound(core * BLOCK + step * ROW_BLOCK, ROW_BLOCK), ROW_BLOCK)
            target[goes, pl.ds(first, size)] = source.astype(BF16)

        piece = target.at[mine, pl.ds(first, size)]
        weight_copies.append(push(piece, piece, (ws_send, ws_recv), number, sibling))

    for copy in edge_copies:
        copy.wait()
    small_copy.wait()
    row_copies = [
        push(seg_row_ref, seg_all.at[own], (row_send, row_recv), gap, peer)
        for gap, peer in enumerate(peers)
    ]
    seg_all[own] = seg_row_ref[...]
    widened(small, small_out)

    x_ext[:EDGE, :] = edges[0].astype(F32)
    x_ext[mid, :] = tok_ref[...].astype(F32)
    x_ext[EDGE + rows :, :] = edges[1].astype(F32)
    seg_ext[:EDGE, :] = jnp.where(own == 0, -1.0, seg_edges[0])
    seg_ext[mid, :] = seg_col[...]
    seg_ext[EDGE + rows :, :] = jnp.where(own == count - 1, -1.0, seg_edges[1])
    tap_masks(masks, seg_ext)

    normed, inv_std = norm_fwd(x_ext[...])
    n1[...] = normed[mid, :]
    inv[0] = jnp.broadcast_to(inv_std, (ext, LANES))
    low_ext[...] = (normed * vector(small, LN1G, D) + vector(small, LN1B, D)).astype(BF16)

    weight_copies[0].wait()
    glu_bias = vector(small, GLUB, 2 * D)
    for step in range(2 * D // 512):
        cols = slice(512 * step, 512 * (step + 1))
        glu_pre[:, cols] = (
            matmul(low_ext[...], late[:, GLU + 512 * step : GLU + 512 * (step + 1)])
            + glu_bias[:, cols]
        )
    state = x_ext[...] + glu_pre[:, :D] * jax.nn.sigmoid(glu_pre[:, D:])
    x1[...] = state[mid, :]
    normed, inv_std = norm_fwd(state)
    n2[...] = normed[mid, :]
    inv[1] = jnp.broadcast_to(inv_std, (ext, LANES))
    low_f = (normed * vector(small, LN2G, D) + vector(small, LN2B, D)).astype(BF16).astype(F32)
    before = pltpu.roll(low_f, 1, 0) * jnp.concatenate([masks[REACH - 1]] * (D // LANES), axis=1)
    after = pltpu.roll(low_f, ext - 1, 0) * jnp.concatenate([masks[REACH + 1]] * (D // LANES), axis=1)
    shifted[0] = before.astype(BF16)
    shifted[1] = low_f.astype(BF16)
    shifted[2] = after.astype(BF16)

    weight_copies[1].wait()

    @pl.loop(0, FF // 512)
    def _(step):
        weight = late[:, pl.ds(bound(LEFT + step * 512, 512), 512)]
        left_pre[:, span(step, 512)] = matmul(shifted[1], weight)

    weight_copies[2].wait()
    conv_sum = vector(small, CONVB, HALF)
    for tap in range(3):
        conv_sum = conv_sum + matmul(
            shifted[tap], late[:, CONV + HALF * tap : CONV + HALF * (tap + 1)]
        )
    conv_pre[...] = conv_sum

    left_bias = vector(small, LEFTB, FF)
    gain, shift = vector(small, LN3G, FF), vector(small, LN3B, FF)

    @pl.loop(0, ext // ROW_BLOCK)
    def _(step):
        here = span(step, ROW_BLOCK)
        pre = left_pre[here, :] + left_bias
        left_pre[here, :] = pre
        mixed = jax.nn.silu(pre)
        mixed = jnp.concatenate(
            [mixed[:, :HALF] + jax.nn.silu(conv_pre[here, :]), mixed[:, HALF:]], axis=1
        )
        normed, inv_std = norm_fwd(mixed)
        n3[here, :] = normed
        inv[2, here, :] = jnp.broadcast_to(inv_std, (ROW_BLOCK, LANES))
        g3[here, :] = (normed * gain + shift).astype(BF16).astype(F32)

    saves = [
        move(n1, n1_out, out_sem.at[0]),
        move(glu_pre.at[pl.ds(EDGE, rows), :], glu_out, out_sem.at[1]),
        move(n2, n2_out, out_sem.at[2]),
        move(left_pre.at[pl.ds(EDGE, rows), :], left_out, out_sem.at[3]),
        move(conv_pre, conv_out, out_sem.at[4]),
        move(n3, n3_out, out_sem.at[5]),
    ]

    @pl.loop(0, FF // LANES)
    def _(step):
        cols = span(step, LANES)
        block = g3[:, cols]
        total = jnp.zeros((rows, LANES), F32)
        for tap in range(TAPS):
            row = DEPTH + tap
            moved = pltpu.roll(block, (REACH - tap) % ext, 0)[mid, :]
            half = FF // 2 // LANES
            taps = small[step // half, row : row + 1, span(lax.rem(step, half), LANES)]
            total = total + moved * masks[tap, mid, :] * taps
        depth[:, cols] = total.astype(BF16)

    saves.append(move(depth, depth_out, out_sem.at[6]))
    weight_copies[3].wait()
    sep = vector(small, POINTB, HALF)
    for side in range(2):
        for block in range(4):
            first = side * (FF // 2) + block * BLOCK
            sep = sep + matmul(
                depth[:, first : first + BLOCK],
                late[side * BLOCK : (side + 1) * BLOCK, POINT + HALF * block : POINT + HALF * (block + 1)],
            )
    state = jnp.concatenate([x1[:, :HALF] + sep, x1[:, HALF:]], axis=1)
    x2[...] = state
    normed, inv_std = norm_fwd(state)
    n4[...] = normed
    inv[3, :rows, :] = jnp.broadcast_to(inv_std, (rows, LANES))
    low = (normed * vector(small, LN4G, D) + vector(small, LN4B, D)).astype(BF16)
    weight_copies[4].wait()
    for step in range(D // 256):
        cols = slice(256 * step, 256 * (step + 1))
        query = matmul(low, late[:, QKV + 256 * step : QKV + 256 * (step + 1)])
        q_turned[cols, :] = turn(query)
    near = lax.broadcasted_iota(jnp.int32, (rows, LANES), 1) < HEAD_DIM
    for step in range(D // LANES):
        first = QKV + D + LANES * step
        keys = matmul(low, late[:, first : first + LANES])
        values = matmul(low, late[:, first + D : first + D + LANES])
        kv_own[:, 2 * step * LANES : (2 * step + 1) * LANES] = jnp.where(
            near, keys, pltpu.roll(values, HEAD_DIM, 1)
        ).astype(BF16)
        kv_own[:, (2 * step + 1) * LANES : (2 * step + 2) * LANES] = jnp.where(
            near, pltpu.roll(keys, HEAD_DIM, 1), values
        ).astype(BF16)

    q_slot = q_out.at[:, span(head, rows)]
    kv_slot = kv_out.at[span(own, rows), pl.ds(0, LANES)]
    arriving = []
    for gap in range(1, heads):
        other = lax.rem(head + gap, heads)
        arriving.append(
            push(kv_own.at[:, span(other, LANES)], kv_slot, (kv_send, kv_recv), gap - 1, (other * parts + part, core))
        )
    twins = [(head * parts + lax.rem(part + gap, parts), core) for gap in range(1, parts)]
    for at, twin in enumerate(twins):
        copies.append(
            push(kv_own.at[:, span(head, LANES)], kv_slot, (pass_send, pass_recv), at * heads, twin)
        )
    for gap in range(1, heads):
        other = lax.rem(head + gap, heads)
        copies.append(
            push(q_turned.at[span(other, HEAD_DIM), :], q_slot, (q_send, q_recv), gap - 1, (other * parts + part, core))
        )
    saves.append(move(q_turned.at[span(head, HEAD_DIM), :], q_slot, out_sem.at[7]))
    saves.append(move(kv_own.at[:, span(head, LANES)], kv_slot, out_sem.at[8]))
    saves.append(move(n4, n4_out, out_sem.at[9]))
    saves.append(move(x2, x2_out, out_sem.at[10]))
    saves.append(move(inv, inv_out, out_sem.at[11]))
    saves.append(move(masks, masks_out, out_sem.at[14]))
    for copy in row_copies:
        copy.wait()
    lane = lax.broadcasted_iota(jnp.int32, (1, LANES), 1)
    every = seg_all[:, 0, :]
    for tile in range(heads):
        source = tile * parts + part
        mine = seg_all[source]
        first = jnp.min(mine, axis=1, keepdims=True)
        last = jnp.max(mine, axis=1, keepdims=True)
        below = jnp.sum(jnp.sum((every < first).astype(F32), axis=0, keepdims=True), axis=1, keepdims=True).astype(jnp.int32)
        upto = jnp.sum(jnp.sum((every <= last).astype(F32), axis=0, keepdims=True), axis=1, keepdims=True).astype(jnp.int32)
        plan_out[tile : tile + 1, :] = jnp.where(
            lane == 0, below, jnp.where(lane == 1, upto, source)
        )
    mark_segments(marks, columns, seg_all)
    saves.append(move(columns, seg_out, out_sem.at[16]))
    saves.append(move(marks, kv_out.at[:, pl.ds(LANES, LANES)], out_sem.at[15]))
    for copy in weight_copies[5:]:
        copy.wait()
    saves.append(move(late, late_out, out_sem.at[12]))
    saves.append(move(early, early_out, out_sem.at[13]))
    for gap in range(1, heads):
        arriving[gap - 1].wait()
        source = lax.rem(head + heads - gap, heads) * parts + part
        block = kv_out.at[span(source, rows), pl.ds(0, LANES)]
        for at, twin in enumerate(twins):
            copies.append(push(block, block, (pass_send, pass_recv), at * heads + gap, twin))

    for copy in copies + saves:
        copy.wait()


def first_kernel(tokens, seg_row, vectors, weights, count, heads):
    rows = tokens.shape[0]
    ext = rows + 2 * EDGE
    parts = count // heads
    late = (2 * BLOCK, SMALL)
    early = (2 * BLOCK, EARLY)
    out_shape = (
        shaped(late, BF16),
        shaped(early, BF16),
        shaped((2, SMALL_ROWS, SMALL_WIDTH)),
        shaped((count, 1, rows), jnp.int32),
        shaped((heads, LANES), jnp.int32),
        shaped((HEAD_DIM, heads * rows), BF16),
        shaped((count * rows, 2 * LANES), BF16),
        shaped((rows, D)),
        shaped((rows, 2 * D)),
        shaped((rows, D)),
        shaped((rows, FF)),
        shaped((ext, HALF)),
        shaped((ext, FF)),
        shaped((rows, FF), BF16),
        shaped((rows, D)),
        shaped((rows, D)),
        shaped((4, ext, LANES)),
        shaped((TAPS, ext, LANES)),
        shaped((count * rows, LANES)),
    )
    out_specs = (
        [any_spec()] * 2 + [vmem_spec()] * 3 + [any_spec()] * 14
    )
    scratch = [
        pltpu.VMEM((BLOCK, SMALL + EARLY), F32),
        pltpu.VMEM(late, BF16),
        pltpu.VMEM(early, BF16),
        pltpu.VMEM((2, EDGE, D), BF16),
        pltpu.VMEM((2, EDGE, LANES), F32),
        pltpu.VMEM((rows, LANES), F32),
        pltpu.VMEM((SMALL_ROWS, SMALL_WIDTH), F32),
        pltpu.VMEM((ext, D), F32),
        pltpu.VMEM((ext, LANES), F32),
        pltpu.VMEM((TAPS, ext, LANES), F32),
        pltpu.VMEM((2, SMALL_ROWS, SMALL_WIDTH), F32),
        pltpu.VMEM((ext, D), BF16),
        pltpu.VMEM((rows, D), F32),
        pltpu.VMEM((ext, 2 * D), F32),
        pltpu.VMEM((rows, D), F32),
        pltpu.VMEM((rows, D), F32),
        pltpu.VMEM((3, ext, D), BF16),
        pltpu.VMEM((ext, FF), F32),
        pltpu.VMEM((ext, HALF), F32),
        pltpu.VMEM((ext, FF), F32),
        pltpu.VMEM((ext, FF), F32),
        pltpu.VMEM((rows, FF), BF16),
        pltpu.VMEM((rows, D), F32),
        pltpu.VMEM((rows, D), F32),
        pltpu.VMEM((4, ext, LANES), F32),
        pltpu.VMEM((D, rows), BF16),
        pltpu.VMEM((rows, 2 * D), BF16),
        pltpu.VMEM((count * rows, LANES), BF16),
        pltpu.VMEM((count * rows, LANES), F32),
        pltpu.SemaphoreType.DMA((sum(item[3] for item in WEIGHT_COLUMNS),)),
        pltpu.SemaphoreType.DMA((17,)),
    ]
    scratch += sem_pair(len(WEIGHT_COLUMNS) + 1) + sem_pair(4) + sem_pair(count - 1)
    scratch += sem_pair(heads - 1) + sem_pair(heads - 1) + sem_pair((parts - 1) * heads)
    return pl.pallas_call(
        functools.partial(first_body, count, heads),
        out_shape=out_shape,
        in_specs=[vmem_spec()] * (2 + len(vectors)) + [any_spec()] * 8,
        out_specs=out_specs,
        scratch_shapes=scratch,
        compiler_params=comm_params(1),
        name="first_layers",
    )(tokens, seg_row, *vectors, *weights)


def turn_keys(kv_ref, turned):
    @pl.loop(0, kv_ref.shape[0] // KEY_TILE)
    def _(tile):
        here = span(tile, KEY_TILE)
        turned[:, here] = turn(kv_ref[here, :LANES])


def other_segments(seg_q):
    number = lax.broadcasted_iota(jnp.int32, (LANES, seg_q.shape[1]), 0)
    return jnp.where(number == seg_q, 0.0, MASK_FILL).astype(BF16)


def key_tiles(plan_ref, tile):
    return plan_ref[tile, 0] // KEY_TILE, (plan_ref[tile, 1] + KEY_TILE - 1) // KEY_TILE


def attend_body(rows, plan_ref, q_ref, kv_ref, seg_ref, o_ref, low_ref, lse_ref, turned):
    turn_keys(kv_ref, turned)

    @pl.loop(0, q_ref.shape[1] // rows)
    def _(tile):
        at = span(tile, rows)
        q = q_ref[:, at] * jnp.bfloat16(HEAD_DIM**-0.5)
        others = other_segments(seg_ref[plan_ref[tile, 2]])
        q_pad = jnp.concatenate([q, jnp.zeros_like(q), others], axis=0)

        def block(key_tile, carry):
            top, total, acc = carry
            here = span(key_tile, KEY_TILE)
            scores = matmul(kv_ref[here, :], q_pad)
            new_top = jnp.maximum(top, jnp.max(scores, axis=0, keepdims=True))
            probs = jnp.exp(scores - new_top)
            shrink = jnp.exp(top - new_top)
            total = total * shrink + jnp.sum(probs, axis=0, keepdims=True)
            acc = acc * shrink + matmul(turned[HEAD_DIM:, here], probs.astype(BF16))
            return (new_top, total, acc)

        first, end = key_tiles(plan_ref, tile)
        top, total, acc = lax.fori_loop(
            first,
            end,
            block,
            (
                jnp.full((1, rows), MASK_FILL, F32),
                jnp.zeros((1, rows), F32),
                jnp.zeros((HEAD_DIM, rows), F32),
            ),
        )
        out = acc / total
        o_ref[:, at] = out
        low_ref[:, at] = out.astype(BF16)
        lse_ref[:, at] = top + jnp.log(total)


def attend(plan, q_t, kv, seg, rows):
    return pl.pallas_call(
        functools.partial(attend_body, rows),
        out_shape=(shaped(q_t.shape), shaped(q_t.shape, BF16), shaped((1, q_t.shape[1]))),
        in_specs=[smem_spec()] + [vmem_spec()] * 3,
        out_specs=(vmem_spec(),) * 3,
        scratch_shapes=[pltpu.VMEM((LANES, kv.shape[0]), BF16)],
        compiler_params=pltpu.CompilerParams(vmem_limit_bytes=VMEM_MOST),
        name="attend",
    )(plan, q_t, kv, seg)


def middle_body(
    count,
    heads,
    o_in,
    out_grad_in,
    small_in,
    x2_in,
    early_in,
    out_ref,
    small_grads,
    dx3_out,
    grads_out,
    do_out,
    out_grad,
    small_raw,
    weights,
    x2,
    small,
    o_t,
    x3,
    expand_pre,
    hidden,
    dpre,
    do_t,
    grads,
    dx3,
    load_sem,
    o_send,
    o_recv,
    do_send,
    do_recv,
):
    own, core = place()
    parts = count // heads
    head, part = own // parts, lax.rem(own, parts)
    rows = out_grad.shape[0]
    slot = o_t.at[span(head, HEAD_DIM), :]
    loads = [
        move(o_in.at[:, span(head, rows)], slot, load_sem.at[2]),
        move(small_in, small_raw, load_sem.at[3]),
        move(x2_in, x2, load_sem.at[1]),
        move(early_in, weights, load_sem.at[0]),
        move(out_grad_in, out_grad, load_sem.at[4]),
    ]
    near = [lax.rem(head + gap, heads) for gap in range(1, heads)]
    peers = [(other * parts + part, core) for other in near]
    greet(peers)
    copies = [
        push(o_in.at[:, span(other, rows)], slot, (o_send, o_recv), gap, peer)
        for gap, (other, peer) in enumerate(zip(near, peers))
    ]
    small_grads[...] = jnp.zeros_like(small_grads)
    for copy in loads:
        copy.wait()
    widened(small, small_raw)
    for copy in copies:
        copy.wait()

    state = (
        x2[...]
        + matmul(turn(o_t[...]), weights[:, ATTN : ATTN + D])
        + vector(small, ATTNB, D)
    )
    x3[...] = state
    normed, inv_std = norm_fwd(state)
    gain = vector(small, LN5G, D)
    low = (normed * gain + vector(small, LN5B, D)).astype(BF16)
    expand_bias = vector(small, EXPANDB, FF)
    for step in range(FF // 512):
        cols = slice(512 * step, 512 * (step + 1))
        pre = matmul(low, weights[:, EXPAND + 512 * step : EXPAND + 512 * (step + 1)]) + expand_bias[:, cols]
        expand_pre[:, cols] = pre
        hidden[:, cols] = jax.nn.silu(pre).astype(BF16)
    state = x3[...] + vector(small, SHRINKB, D)
    for block in range(FF // BLOCK):
        side, column = block // 4, SHRINK + D * (block % 4)
        state = state + matmul(
            hidden[:, block * BLOCK : (block + 1) * BLOCK],
            weights[side * BLOCK : (side + 1) * BLOCK, column : column + D],
        )
    out_ref[...] = state.astype(BF16)

    dz = out_grad[...]
    for block in range(FF // BLOCK):
        side, column = block // 4, SHRINK + D * (block % 4)
        cols = slice(block * BLOCK, (block + 1) * BLOCK)
        grad = back_mul(dz, weights[side * BLOCK : (side + 1) * BLOCK, column : column + D])
        dpre[:, cols] = (grad * smooth_slope(expand_pre[:, cols])).astype(BF16)
    grad = jnp.concatenate(
        [
            back_mul(dpre[...], weights[side * BLOCK : (side + 1) * BLOCK, EXPAND : EXPAND + FF])
            for side in range(2)
        ],
        axis=1,
    )
    state = dz.astype(F32) + norm_back(grad, normed, inv_std, gain)
    dx3[...] = state
    dy3 = state.astype(BF16)
    do_t[...] = back_mul(weights[:, ATTN : ATTN + D], dy3).astype(BF16)
    slot = do_out.at[:, span(head, rows)]
    copies = [
        push(do_t.at[span(other, HEAD_DIM), :], slot, (do_send, do_recv), gap, peer)
        for gap, (other, peer) in enumerate(zip(near, peers))
    ]
    copies.append(move(do_t.at[span(head, HEAD_DIM), :], slot, load_sem.at[0]))
    copies.append(move(dx3, dx3_out, load_sem.at[1]))

    put_vector(small_grads, LN5G, col_sum(grad * normed))
    put_vector(small_grads, LN5B, col_sum(grad))
    put_vector(small_grads, ATTNB, col_sum(dy3))
    put_vector(small_grads, EXPANDB, col_sum(dpre[...]))
    put_vector(small_grads, SHRINKB, col_sum(dz))
    for block in range(FF // BLOCK):
        side, column = block // 4, SHRINK + D * (block % 4)
        grads[side * BLOCK : (side + 1) * BLOCK, column : column + D] = matmul(
            turn(hidden[:, block * BLOCK : (block + 1) * BLOCK]), dz
        ).astype(BF16)
    grads[:, ATTN : ATTN + D] = matmul(o_t[...], dy3).astype(BF16)
    low_t = turn(low)
    for step in range(FF // 512):
        grads[:, EXPAND + 512 * step : EXPAND + 512 * (step + 1)] = matmul(
            low_t, dpre[:, 512 * step : 512 * (step + 1)]
        ).astype(BF16)
    copies.append(move(grads, grads_out, load_sem.at[2]))
    for copy in copies:
        copy.wait()


def middle_kernel(o_low, out_grad, small, x2, early, count, heads):
    rows = out_grad.shape[0]
    return pl.pallas_call(
        functools.partial(middle_body, count, heads),
        out_shape=(
            shaped((rows, D), BF16),
            shaped((2, SMALL_ROWS, SMALL_WIDTH)),
            shaped((rows, D)),
            shaped(early.shape, BF16),
            shaped((HEAD_DIM, heads * rows), BF16),
        ),
        in_specs=[any_spec()] * 5,
        out_specs=[vmem_spec()] * 2 + [any_spec()] * 3,
        scratch_shapes=[
            pltpu.VMEM((rows, D), BF16),
            pltpu.VMEM((2, SMALL_ROWS, SMALL_WIDTH), F32),
            pltpu.VMEM(early.shape, BF16),
            pltpu.VMEM((rows, D), F32),
            pltpu.VMEM((2, SMALL_ROWS, SMALL_WIDTH), F32),
            pltpu.VMEM((D, rows), BF16),
            pltpu.VMEM((rows, D), F32),
            pltpu.VMEM((rows, FF), F32),
            pltpu.VMEM((rows, FF), BF16),
            pltpu.VMEM((rows, FF), BF16),
            pltpu.VMEM((D, rows), BF16),
            pltpu.VMEM(early.shape, BF16),
            pltpu.VMEM((rows, D), F32),
            pltpu.SemaphoreType.DMA((5,)),
        ]
        + sem_pair(heads - 1)
        + sem_pair(heads - 1),
        compiler_params=comm_params(2),
        name="middle_layers",
    )(o_low, out_grad, small, x2, early)


def column_groups(first, width, bits):
    tiles = width // LANES
    unit = 2 ** max(0, bits - 4)
    long = max(1, round(tiles * 0.36 / unit)) * unit
    orders = [
        list(range(bits)),
        [1, 0] + list(range(2, bits)),
        list(range(2, bits)) + [0, 1],
    ]
    groups = []
    for size, order in zip([long, long, tiles - 2 * long], orders):
        if size == 0:
            continue
        groups.append((first, size * LANES, order))
        first += size * LANES
    return groups


def grad_sets(bits):
    bounds = [LATE, LATE + SHRINK, QKV, POINT, LEFT, LEFT + FF // 2, CONV, CONV + FF // 2]
    widths = [SHRINK, EARLY - SHRINK, POINT - QKV, LEFT - POINT] + [FF // 2] * 4
    return [column_groups(first, width, bits) for first, width in zip(bounds, widths)]


class Piece:
    def __init__(self, at, group, links, sums, got, total, sems):
        self.at, (self.first, self.width, self.order) = at, group
        self.core, self.sibling, self.bit_of, self.partner = links
        self.view, self.got, self.total, self.sems = sums, got, total, sems
        self.bits, self.phase, self.trail = len(self.order), 0, []
        self.since = -1
        self.copy = None

    def whole(self):
        return (0, BLOCK, self.first, self.width)

    def out(self, where):
        row, tall, col, wide = where
        return self.total.at[pl.ds(bound(row, ROW_BLOCK), tall), pl.ds(bound(col, LANES), wide)]

    def start(self, other_half):
        self.copy = push_by(
            other_half, self.out(self.whole()), self.sems[0].at[self.at], self.sems[1].at[self.at], self.sibling
        )

    def add(self, where, source, spot, last):
        row, tall, col, wide = where

        @pl.loop(0, tall // ROW_BLOCK)
        def _(step):
            gap = step * ROW_BLOCK
            here = (row + gap, ROW_BLOCK, col, wide)
            there = source.at[pl.ds(bound(spot + gap, ROW_BLOCK), ROW_BLOCK), pl.ds(self.first, wide)]
            mine = self.view(here)[...].astype(F32)
            added = (mine + there[...].astype(F32)).astype(BF16)
            if last:
                self.out(here)[...] = added
            else:
                self.view(here)[...] = added

    def halve(self, step):
        row, tall, col, wide = self.where
        bit = self.order[step]
        mine = self.bit_of[bit]
        if tall > ROW_BLOCK:
            half = tall // 2
            kept = (row + half * mine, half, col, wide)
            sent = (row + half * (1 - mine), half, col, wide)
        else:
            half = wide // 2
            kept = (row, tall, col + half * mine, half)
            sent = (row, tall, col + half * (1 - mine), half)
        self.copy = push_by(
            self.view(sent),
            self.got.at[pl.ds(self.spot, sent[1]), pl.ds(self.first, sent[3])],
            self.sems[0].at[self.at],
            self.sems[2].at[self.at * self.bits + step],
            self.partner[bit],
        )
        self.where = kept

    def double(self, step):
        place_out = self.out(self.trail[step])
        self.copy = push_by(
            place_out,
            place_out,
            self.sems[0].at[self.at],
            self.sems[3].at[self.at * self.bits + step],
            self.partner[self.order[step]],
        )

    def done(self):
        return self.phase > 2 * self.bits

    def sent_all(self):
        return self.phase >= 2 * self.bits

    def advance(self):
        if self.done():
            return
        self.copy.wait()
        if self.phase == 0:
            self.where, self.spot = self.whole(), 0
            self.add(self.where, self.total, 0, False)
            self.halve(0)
        elif self.phase <= self.bits:
            last = self.phase == self.bits
            self.add(self.where, self.got, self.spot, last)
            self.trail.append(self.where)
            self.spot += self.where[1]
            if last:
                self.double(self.bits - 1)
            else:
                self.halve(self.phase)
        elif self.phase < 2 * self.bits:
            self.double(2 * self.bits - 1 - self.phase)
        self.phase += 1


def last_body(count, heads, *refs):
    (
        q_in,
        do_in,
        o_in,
        lse_in,
        kv_in,
        seg_in,
        small_in,
        small_grads_in,
        seg_ref,
        early_grads,
        dx3_in,
        late_in,
        n1_in,
        glu_in,
        n2_in,
        left_in,
        conv_in,
        n3_in,
        depth_in,
        n4_in,
        inv_in,
        masks_in,
        total_out,
        grad_out,
        total,
        weights,
        dx3,
        n1,
        glu_pre,
        n2,
        left_pre,
        conv_pre,
        n3,
        depth,
        n4,
        inv,
        masks,
        small,
        small_grads,
        dq_t,
        dkv_own,
        q_all,
        do_all,
        o_all,
        lse,
        both,
        delta,
        kv_slots,
        seg_slots,
        turned,
        dkv_acc,
        dq_acc,
        dq_low,
        dkv_all,
        small_raw,
        shared,
        summed,
        dqkv,
        sep_own,
        sep_edges,
        sep_ext,
        depth_grad,
        g3_grad,
        row_sums,
        dleft,
        conv_grad,
        conv_taps,
        grads,
        early_own,
        got,
        load_sem,
        keep_sem,
        store_sem,
        tile_sem,
        dq_send,
        dq_recv,
        dkv_send,
        dkv_recv,
        pass_send,
        pass_recv,
        edge_send,
        edge_recv,
        piece_send,
        ws_recv,
        rs_recv,
        ag_recv,
    ) = refs
    own, core = place()
    parts = count // heads
    head, part = own // parts, lax.rem(own, parts)
    rows = dx3.shape[0]
    ext = rows + 2 * EDGE
    mid = slice(EDGE, EDGE + rows)
    sibling = (own, 1 - core)
    peers = others_of(own, core, count)
    bits = count.bit_length() - 1

    sources = (dx3_in, late_in, n4_in, inv_in, depth_in, masks_in, n3_in, left_in, conv_in, n2_in, glu_in, n1_in)
    targets = (dx3, weights, n4, inv, depth, masks, n3, left_pre, conv_pre, n2, glu_pre, n1)
    announce([sibling] + peers)
    own_rows = pl.ds(bound(core * BLOCK, BLOCK), BLOCK)
    attention_loads = [
        move(q_in, q_all, keep_sem.at[2]),
        move(do_in, do_all, keep_sem.at[5]),
        move(o_in, o_all, keep_sem.at[6]),
        move(lse_in, lse, keep_sem.at[7]),
    ]

    near_heads = max(1, KEY_TILE // (parts * rows))
    tiles_each = max(1, parts * rows // KEY_TILE)
    group_count = heads // near_heads
    key_count = count * rows
    longest = key_count // 2

    def group_first(group):
        return lax.rem(head // near_heads + group, group_count) * near_heads

    def group_head(group, at):
        mixed = lax.rem(head, near_heads)
        bit = sum(
            (lax.rem(mixed // 2**k, 2) + (at >> k & 1) - 2 * lax.rem(mixed // 2**k, 2) * (at >> k & 1)) * 2**k
            for k in range(near_heads.bit_length() - 1)
        )
        return group_first(group) + bit

    def tile_first(number):
        group, tile = number // tiles_each, number % tiles_each
        return group_first(group) * parts * rows + tile * KEY_TILE

    def fetch(number):
        here = pl.ds(bound(tile_first(number), KEY_TILE), KEY_TILE)
        return [
            move(kv_in.at[here, pl.ds(0, LANES)], kv_slots.at[number % 2], tile_sem.at[number % 2]),
            move(seg_in.at[here, :], seg_slots.at[number % 2], tile_sem.at[2 + number % 2]),
        ]

    fetched = fetch(0)

    bit_of = [lax.rem(own // 2**bit, 2) for bit in range(bits)]
    partner = [(own + 2**bit - 2 * 2**bit * bit_of[bit], core) for bit in range(bits)]
    links = (core, sibling, bit_of, partner)
    sems = (piece_send, ws_recv, rs_recv, ag_recv)

    def early_view(where):
        row, tall, col, wide = where
        return early_own.at[pl.ds(bound(row, ROW_BLOCK), tall), pl.ds(bound(col - LATE, LANES), wide)]

    def late_view(where):
        row, tall, col, wide = where
        return grads.at[pl.ds(bound(core * BLOCK + row, ROW_BLOCK), tall), pl.ds(bound(col, LANES), wide)]

    sets, at = [], 0
    for number, groups in enumerate(grad_sets(bits)):
        members = []
        for group in groups:
            view = late_view if number > 1 else early_view
            members.append(Piece(at, group, links, view, got, total, sems))
            at += 1
        sets.append(members)
    other_rows = pl.ds(bound((1 - core) * BLOCK, BLOCK), BLOCK)

    def start(members, source, shift):
        for piece in members:
            piece.start(source.at[other_rows, pl.ds(piece.first - shift, piece.width)])

    def advance(members):
        for piece in members:
            if not piece.sent_all():
                piece.advance()

    scale = HEAD_DIM**-0.5
    for copy in attention_loads:
        copy.wait()
    dq_acc[...] = jnp.zeros_like(dq_acc)

    @pl.loop(0, heads)
    def _(tile):
        at = span(tile, rows)
        q = q_all[:, at] * jnp.bfloat16(scale)
        do = do_all[:, at]
        none = jnp.zeros_like(q)
        both[tile] = jnp.concatenate(
            [jnp.concatenate([q, none], axis=1), jnp.concatenate([none, do], axis=1)], axis=0
        )
        delta[:, at] = jnp.sum(o_all[:, at] * do.astype(F32), axis=0, keepdims=True)

    def attention_tile(number):
        first, slot = tile_first(number), number % 2

        def one(tile):
            source = tile * parts + part
            apart = jnp.maximum(
                first - (source * rows + rows - 1), source * rows - (first + KEY_TILE - 1)
            )

            @pl.when(apart < longest)
            def _():
                at = span(tile, rows)
                operand = both[tile]
                pair = matmul(kv_slots[slot], operand)
                seg_k = jnp.concatenate([seg_slots[slot]] * (rows // LANES), axis=1)
                seg_q = seg_ref[source].astype(F32)
                scores = jnp.where(seg_k == seg_q, pair[:, :rows], MASK_FILL)
                probs = jnp.exp(scores - lse[:, at])
                score_grad = (probs * (pair[:, rows:] - delta[:, at])).astype(BF16)
                joined = jnp.concatenate([score_grad, probs.astype(BF16)], axis=1)
                dkv_acc[...] += back_mul(joined, operand)
                dq_acc[:, at] += matmul(turned[...], score_grad)

        return one

    collect, sharing, arrived = [], [], []

    def share_group(group):
        for at in range(near_heads):
            other = group_head(group, at)
            for gap in range(parts - 1):
                twin = lax.rem(part + gap + 1, parts)
                sharing.append(
                    push(
                        dkv_all.at[span(other * parts + twin, rows), :],
                        shared.at[gap, group * near_heads + at],
                        (pass_send, pass_recv),
                        gap * heads + group * near_heads + at,
                        (head * parts + twin, core),
                    )
                )

    def send_group(group):
        for at in range(near_heads):
            other, index = group_head(group, at), group * near_heads + at
            for copy in sharing[index * (parts - 1) : (index + 1) * (parts - 1)]:
                copy.wait()
            total_kv = dkv_all[span(other * parts + part, rows), :].astype(F32)
            for gap in range(parts - 1):
                total_kv = total_kv + shared[gap, index].astype(F32)
            if index:
                summed[index] = total_kv.astype(BF16)
                collect.append(
                    push(
                        summed.at[index],
                        dkv_own.at[:, span(head, LANES)],
                        (dkv_send, dkv_recv),
                        index - 1,
                        (other * parts + part, core),
                    )
                )
            else:
                dkv_own[:, span(head, LANES)] = total_kv.astype(BF16)

    slot = dq_t.at[span(head, HEAD_DIM), :]

    def send_dq(gap, other):
        here = span(other, rows)
        dq_low[:, here] = (dq_acc[:, here] * scale).astype(BF16)
        if gap < heads:
            collect.append(
                push(dq_low.at[:, here], slot, (dq_send, dq_recv), gap - 1, (other * parts + part, core))
            )
        else:
            collect.append(move(dq_low.at[:, here], slot, keep_sem.at[0]))

    points, keeps, loads = [], [], []

    def pump():
        at = len(points)
        points.append(at)
        if at == 0:
            all_here([sibling] + peers)
            start(sets[0] + sets[1], early_grads, LATE)
            keeps.append(move(early_grads.at[own_rows, :], early_own, keep_sem.at[1]))
            keeps.append(move(small_in, small_raw, keep_sem.at[3]))
            keeps.append(move(small_grads_in, small_grads, keep_sem.at[4]))
        elif at == 1:
            for copy in keeps:
                copy.wait()
            widened(small, small_raw)
            advance(sets[0])
            loads.extend(move(a, b, load_sem.at[k]) for k, (a, b) in enumerate(zip(sources, targets)))
        elif at in (4, 7, 9, 11, 13, 15):
            advance(sets[0])
        elif at in (2, 6, 8, 10, 12, 14):
            advance(sets[1])

    tiles = group_count * tiles_each
    for number in range(tiles):
        for copy in fetched:
            copy.wait()
        if number + 1 < tiles:
            fetched = fetch(number + 1)
        turned[...] = turn(kv_slots[number % 2, :, :HEAD_DIM])
        dkv_acc[...] = jnp.zeros_like(dkv_acc)
        group = number // tiles_each
        one = attention_tile(number)
        for turn_no in range(4):
            reach = (turn_no * heads // 4 + 1, (turn_no + 1) * heads // 4 + 1)
            pl.loop(*reach)(lambda gap: one(lax.rem(head + gap, heads)))
            if number == tiles - 1:
                for gap in range(*reach):
                    send_dq(gap, lax.rem(head + gap, heads))
            if turn_no == 2 and group and number % tiles_each == 0:
                send_group(group - 1)
            if turn_no < 3:
                pump()
        here = pl.ds(bound(tile_first(number), KEY_TILE), KEY_TILE)
        dkv_all[here, :] = dkv_acc[...].astype(BF16)
        if number % tiles_each == tiles_each - 1:
            share_group(group)
        pump()
    for copy in loads:
        copy.wait()
    send_group(group_count - 1)
    for copy in collect:
        copy.wait()

    dqkv[:, :D] = turn(dq_t[...])
    lane = lax.broadcasted_iota(jnp.int32, (rows, LANES), 1) < HEAD_DIM
    for step in range(D // LANES):
        pair = []
        for side in range(2):
            first = (2 * step + side) * LANES
            pair.append(dkv_own[:, first : first + LANES].astype(F32))
        cols = slice(D + step * LANES, D + (step + 1) * LANES)
        dqkv[:, cols] = jnp.where(lane, pair[0], pltpu.roll(pair[1], HEAD_DIM, 1)).astype(BF16)
        cols = slice(2 * D + step * LANES, 2 * D + (step + 1) * LANES)
        dqkv[:, cols] = jnp.where(lane, pltpu.roll(pair[0], HEAD_DIM, 1), pair[1]).astype(BF16)

    def through(grad, column, width):
        return jnp.concatenate(
            [
                back_mul(grad, weights[side * BLOCK : (side + 1) * BLOCK, column : column + width])
                for side in range(2)
            ],
            axis=1,
        )

    def norm_step(grad, normed, inv_std, row):
        put_vector(small_grads, row, col_sum(grad * normed))
        put_vector(small_grads, row + 1, col_sum(grad))
        return norm_back(grad, normed, inv_std, vector(small, row, D))

    grad = through(dqkv[...], QKV, 3 * D)
    dx2 = dx3[...] + norm_step(grad, n4[...], inv[3, :rows, :1], LN4G)
    dx3[...] = dx2
    sep_own[...] = dx2[:, :HALF].astype(BF16)
    right, left = (lax.rem(own + 1, count), core), (lax.rem(own + count - 1, count), core)
    edge_copies = [
        push(sep_own.at[pl.ds(rows - EDGE, EDGE), :], sep_edges.at[0], (edge_send, edge_recv), 0, right),
        push(sep_own.at[pl.ds(0, EDGE), :], sep_edges.at[1], (edge_send, edge_recv), 1, left),
    ]
    low_t = turn(n4[...] * vector(small, LN4G, D) + vector(small, LN4B, D))
    for step in range(3):
        grads[:, QKV + D * step : QKV + D * (step + 1)] = matmul(
            low_t, dqkv[:, D * step : D * (step + 1)]
        ).astype(BF16)
    start(sets[2], grads, 0)
    advance(sets[0])
    for block in range(FF // BLOCK):
        side, column = block // 4, POINT + HALF * (block % 4)
        grads[side * BLOCK : (side + 1) * BLOCK, column : column + HALF] = matmul(
            turn(depth[:, block * BLOCK : (block + 1) * BLOCK]), sep_own[...]
        ).astype(BF16)
    start(sets[3], grads, 0)
    put_vector(small_grads, POINTB, col_sum(sep_own[...]))

    for copy in edge_copies:
        copy.wait()
    sep_ext[:EDGE, :] = sep_edges[0]
    sep_ext[mid, :] = sep_own[...]
    sep_ext[EDGE + rows :, :] = sep_edges[1]
    for block in range(FF // BLOCK):
        side, column = block // 4, POINT + HALF * (block % 4)
        depth_grad[:, block * BLOCK : (block + 1) * BLOCK] = (
            back_mul(sep_ext[...], weights[side * BLOCK : (side + 1) * BLOCK, column : column + HALF])
            .astype(BF16)
            .astype(F32)
        )

    advance(sets[2])
    row_sums[...] = jnp.zeros_like(row_sums)
    half = FF // 2 // LANES

    def tap_block(step):
        cols = span(step, LANES)
        side, lanes = step // half, span(lax.rem(step, half), LANES)
        block = depth_grad[:, cols]
        normed = n3[:, cols]
        gain = small[side, LN3G : LN3G + 1, lanes]
        low = (normed[mid, :] * gain + small[side, LN3B : LN3B + 1, lanes]).astype(BF16).astype(F32)
        summed = jnp.zeros((ext, LANES), F32)
        for tap in range(TAPS):
            row = DEPTH + tap
            moved = pltpu.roll(block, (tap - REACH) % ext, 0) * masks[TAPS - 1 - tap]
            summed = summed + moved * small[side, row : row + 1, lanes]
            small_grads[side, row : row + 1, lanes] = col_sum(low * moved[mid, :])
        g3_grad[:, cols] = summed
        small_grads[side, LN3G : LN3G + 1, lanes] = col_sum(summed[mid, :] * normed[mid, :])
        small_grads[side, LN3B : LN3B + 1, lanes] = col_sum(summed[mid, :])
        scaled = summed * gain
        row_sums[0] = row_sums[0] + scaled
        row_sums[1] = row_sums[1] + scaled * normed

    for quarter, turns in enumerate((sets[1], sets[3], sets[2], sets[1])):
        pl.loop(quarter * half // 2, (quarter + 1) * half // 2)(tap_block)
        advance(turns)
    inner = jnp.sum(row_sums[0], axis=1, keepdims=True) * (1.0 / FF)
    cross = jnp.sum(row_sums[1], axis=1, keepdims=True) * (1.0 / FF)
    row_sums[0] = jnp.broadcast_to(inner, (ext, LANES))
    row_sums[1] = jnp.broadcast_to(cross, (ext, LANES))

    def left_block(step):
        cols = span(step, LANES)
        side, lanes = step // half, span(lax.rem(step, half), LANES)
        scaled = g3_grad[mid, cols] * small[side, LN3G : LN3G + 1, lanes]
        mixed_grad = inv[2, mid, :] * (scaled - row_sums[0, mid, :] - n3[mid, cols] * row_sums[1, mid, :])
        low = (mixed_grad * smooth_slope(left_pre[:, cols])).astype(BF16)
        dleft[:, cols] = low
        small_grads[side, LEFTB : LEFTB + 1, lanes] = col_sum(low)

    pl.loop(0, half)(left_block)
    advance(sets[3])
    pl.loop(half, 2 * half)(left_block)
    advance(sets[0])
    for step in range(HALF // LANES):
        cols = slice(step * LANES, (step + 1) * LANES)
        scaled = g3_grad[:, cols] * small[0, LN3G : LN3G + 1, cols]
        mixed_grad = inv[2] * (scaled - row_sums[0] - n3[:, cols] * row_sums[1])
        low = (mixed_grad * smooth_slope(conv_pre[:, cols])).astype(BF16).astype(F32)
        conv_grad[:, cols] = low
        for tap in range(3):
            moved = pltpu.roll(low, (tap - 1) % ext, 0) * masks[REACH + 1 - tap]
            conv_taps[:, HALF * tap + step * LANES : HALF * tap + (step + 1) * LANES] = moved[mid, :].astype(BF16)
    put_vector(small_grads, CONVB, col_sum(conv_grad[mid, :]))

    low_t = turn(n2[...] * vector(small, LN2G, D) + vector(small, LN2B, D))
    for step in range(FF // 512):
        grads[:, LEFT + 512 * step : LEFT + 512 * (step + 1)] = matmul(
            low_t, dleft[:, 512 * step : 512 * (step + 1)]
        ).astype(BF16)
        if step % 2:
            start(sets[4 + step // 2], grads, 0)
    advance(sets[2])
    for tap in range(3):
        grads[:, CONV + HALF * tap : CONV + HALF * (tap + 1)] = matmul(
            low_t, conv_taps[:, HALF * tap : HALF * (tap + 1)]
        ).astype(BF16)
    advance(sets[4])
    advance(sets[5])
    grad = through(dleft[...], LEFT, FF) + through(conv_taps[...], CONV, 3 * HALF)
    dx1 = dx3[...] + norm_step(grad, n2[...], inv[1, mid, :1], LN2G)
    gate = jax.nn.sigmoid(glu_pre[:, D:])
    value_grad = dx1 * gate
    dglu = jnp.concatenate([value_grad, value_grad * glu_pre[:, :D] * (1.0 - gate)], axis=1).astype(BF16)
    put_vector(small_grads, GLUB, col_sum(dglu))
    advance(sets[1])
    advance(sets[3])
    low_t = turn(n1[...] * vector(small, LN1G, D) + vector(small, LN1B, D))
    for step in range(2):
        grads[:, GLU + D * step : GLU + D * (step + 1)] = matmul(
            low_t, dglu[:, D * step : D * (step + 1)]
        ).astype(BF16)
    start(sets[6], grads, 0)
    advance(sets[2])
    grad = through(dglu, GLU, 2 * D)
    dx3[...] = dx1 + norm_step(grad, n1[...], inv[0, mid, :1], LN1G)
    keep = move(dx3, grad_out, keep_sem.at[0])
    for side in range(2):
        for block in range(SMALL_WIDTH // BLOCK):
            first = side * BLOCK + block * SMALL_ROWS
            grads[first : first + SMALL_ROWS, SMALL : SMALL + BLOCK] = small_grads[
                side, :, block * BLOCK : (block + 1) * BLOCK
            ].astype(BF16)
        first = side * BLOCK + SMALL_WIDTH // BLOCK * SMALL_ROWS
        grads[first : (side + 1) * BLOCK, SMALL : SMALL + BLOCK] = jnp.zeros(
            ((side + 1) * BLOCK - first, BLOCK), BF16
        )
    start(sets[7], grads, 0)
    advance(sets[4] + sets[5])
    pieces = [piece for number in (6, 7, 4, 5, 2, 3, 0, 1) for piece in sets[number]]
    stores, rounds = [], 0
    while not all(piece.done() for piece in pieces):
        last = all(piece.sent_all() for piece in pieces)
        for piece in pieces:
            if not piece.sent_all():
                piece.advance()
                piece.since = rounds
            elif not piece.done() and (last or piece.since < rounds - 1):
                piece.advance()
                cols = pl.ds(piece.first, piece.width)
                stores.append(move(total.at[:, cols], total_out.at[:, cols], store_sem.at[piece.at]))
        rounds += 1
    for copy in stores:
        copy.wait()
    keep.wait()


def last_kernel(attention, small, small_grads, seg, tensors, count, heads):
    rows = seg.shape[2]
    ext = rows + 2 * EDGE
    parts = count // heads
    bits = count.bit_length() - 1
    pieces = sum(len(groups) for groups in grad_sets(bits))
    scratch = [
        pltpu.VMEM((BLOCK, WIDTH), BF16),
        pltpu.VMEM(tensors[2].shape, BF16),
        pltpu.VMEM((rows, D), F32),
        pltpu.VMEM((rows, D), F32),
        pltpu.VMEM((rows, 2 * D), F32),
        pltpu.VMEM((rows, D), F32),
        pltpu.VMEM((rows, FF), F32),
        pltpu.VMEM((ext, HALF), F32),
        pltpu.VMEM((ext, FF), F32),
        pltpu.VMEM((rows, FF), BF16),
        pltpu.VMEM((rows, D), F32),
        pltpu.VMEM((4, ext, LANES), F32),
        pltpu.VMEM((TAPS, ext, LANES), F32),
        pltpu.VMEM((2, SMALL_ROWS, SMALL_WIDTH), F32),
        pltpu.VMEM((2, SMALL_ROWS, SMALL_WIDTH), F32),
        pltpu.VMEM((D, rows), BF16),
        pltpu.VMEM((rows, 2 * D), BF16),
        pltpu.VMEM((HEAD_DIM, heads * rows), BF16),
        pltpu.VMEM((HEAD_DIM, heads * rows), BF16),
        pltpu.VMEM((HEAD_DIM, heads * rows), F32),
        pltpu.VMEM((1, heads * rows), F32),
        pltpu.VMEM((heads, LANES, 2 * rows), BF16),
        pltpu.VMEM((1, heads * rows), F32),
        pltpu.VMEM((2, KEY_TILE, LANES), BF16),
        pltpu.VMEM((2, KEY_TILE, LANES), F32),
        pltpu.VMEM((HEAD_DIM, KEY_TILE), BF16),
        pltpu.VMEM((KEY_TILE, LANES), F32),
        pltpu.VMEM((HEAD_DIM, heads * rows), F32),
        pltpu.VMEM((HEAD_DIM, heads * rows), BF16),
        pltpu.VMEM((count * rows, LANES), BF16),
        pltpu.VMEM((2, SMALL_ROWS, SMALL_WIDTH), F32),
        pltpu.VMEM((parts - 1, heads, rows, LANES), BF16),
        pltpu.VMEM((heads, rows, LANES), BF16),
        pltpu.VMEM((rows, 3 * D), BF16),
        pltpu.VMEM((rows, HALF), BF16),
        pltpu.VMEM((2, EDGE, HALF), BF16),
        pltpu.VMEM((ext, HALF), BF16),
        pltpu.VMEM((ext, FF), F32),
        pltpu.VMEM((ext, FF), F32),
        pltpu.VMEM((2, ext, LANES), F32),
        pltpu.VMEM((rows, FF), BF16),
        pltpu.VMEM((ext, HALF), F32),
        pltpu.VMEM((rows, 3 * HALF), BF16),
        pltpu.VMEM((2 * BLOCK, LATE), BF16),
        pltpu.VMEM((BLOCK, EARLY), BF16),
        pltpu.VMEM((BLOCK + ROW_BLOCK * max(0, bits - 4), WIDTH), BF16),
        pltpu.SemaphoreType.DMA((12,)),
        pltpu.SemaphoreType.DMA((8,)),
        pltpu.SemaphoreType.DMA((pieces,)),
        pltpu.SemaphoreType.DMA((4,)),
    ]
    scratch += sem_pair(heads - 1) + sem_pair(heads - 1) + sem_pair((parts - 1) * heads)
    scratch += sem_pair(2) + sem_pair(pieces)
    scratch += [pltpu.SemaphoreType.DMA((pieces * bits,))] * 2
    return pl.pallas_call(
        functools.partial(last_body, count, heads),
        out_shape=(shaped((BLOCK, WIDTH), BF16), shaped((rows, D))),
        in_specs=[any_spec()] * (len(attention) + 2) + [vmem_spec()] + [any_spec()] * len(tensors),
        out_specs=[any_spec(), any_spec()],
        scratch_shapes=scratch,
        compiler_params=comm_params(3),
        name="last_layers",
    )(*attention, small, small_grads, seg, *tensors)


def unpack_body(output_in, grad_in, packed_in, *refs):
    size = len(MATRICES) + len(VECTORS) + 2
    outs, (packed, output, grad, *stages, load_sem, out_sem) = refs[:size], refs[size:]
    output_ref, grad_ref, *outs = outs
    turns = (0, 1, 6, 7, 4, 2, 3, 5)
    order = list(turns) + [len(MATRICES)]
    bounds = [(first, width * blocks) for first, width, blocks in MATRICES] + [(SMALL, BLOCK)]
    loads = {}
    for at in order:
        cols = pl.ds(*bounds[at])
        loads[at] = move(packed_in.at[:, cols], packed.at[:, cols], load_sem.at[at])
    passed = [
        move(output_in, output, load_sem.at[len(MATRICES) + 1]),
        move(grad_in, grad, load_sem.at[len(MATRICES) + 2]),
    ]
    stores = []
    for at in turns:
        first, width, blocks = MATRICES[at]
        loads[at].wait()
        stage = stages[at]
        tall = 2 * ROW_BLOCK

        @pl.loop(0, BLOCK // tall, unroll=2)
        def _(step):
            for block in range(blocks):
                value = packed[span(step, tall), first + block * width : first + (block + 1) * width].astype(F32)
                if blocks == 3:
                    stage[block, span(step, tall), :] = value
                else:
                    stage[pl.ds(bound(block * BLOCK + step * tall, tall), tall), :] = value

        stores.append(move(stage, outs[at], out_sem.at[at]))

    for copy in passed:
        copy.wait()
    stores.append(move(output, output_ref, out_sem.at[len(MATRICES)]))
    stores.append(move(grad, grad_ref, out_sem.at[len(MATRICES) + 1]))
    loads[len(MATRICES)].wait()
    small = jnp.concatenate(
        [
            packed[block * SMALL_ROWS : (block + 1) * SMALL_ROWS, SMALL : SMALL + BLOCK].astype(F32)
            for block in range(SMALL_WIDTH // BLOCK)
        ],
        axis=1,
    )
    for (row, tall, size), out in zip(VECTORS, outs[len(MATRICES) :]):
        out[...] = small[row : row + tall, :size]
    for copy in stores:
        copy.wait()


def unpack(output, grad, packed):
    shapes = []
    for _, width, blocks in MATRICES:
        shapes.append((3, BLOCK, width) if blocks == 3 else (blocks * BLOCK, width))
    vectors = [(tall, size) for _, tall, size in VECTORS]
    return pl.pallas_call(
        unpack_body,
        out_shape=(shaped(output.shape, output.dtype), shaped(grad.shape))
        + tuple(shaped(shape) for shape in shapes + vectors),
        in_specs=[any_spec()] * 3,
        out_specs=[any_spec()] * (2 + len(shapes)) + [vmem_spec()] * len(vectors),
        scratch_shapes=[
            pltpu.VMEM(packed.shape, packed.dtype),
            pltpu.VMEM(output.shape, output.dtype),
            pltpu.VMEM(grad.shape, F32),
        ]
        + [pltpu.VMEM(shape, F32) for shape in shapes]
        + [pltpu.SemaphoreType.DMA((len(shapes) + 3,)), pltpu.SemaphoreType.DMA((len(shapes) + 2,))],
        compiler_params=pltpu.CompilerParams(vmem_limit_bytes=VMEM_MOST),
        name="unpack",
    )(output, grad, packed)


def body(tokens, segment_ids, out_grad, *params):
    (
        ln1g, ln1b, glu_w, glu_b, ln2g, ln2b, left_w, left_b, conv_w, conv_b, ln3g, ln3b, depth_w,
        point_w, point_b, ln4g, ln4b, qkv_w, attn_w, attn_b, ln5g, ln5b, expand_w, expand_b,
        shrink_w, shrink_b,
    ) = params
    count = lax.axis_size("ctx")
    heads = D // HEAD_DIM
    rows = tokens.shape[1]
    vectors = [
        ln1g, ln1b, glu_b, ln2g, ln2b, left_b, conv_b, ln3g, ln3b, depth_w,
        point_b, ln4g, ln4b, attn_b, ln5g, ln5b, expand_b, shrink_b,
    ]
    vectors = [value.reshape(-1, value.shape[-1]) for value in vectors]
    weights = (glu_w, left_w, conv_w, point_w, qkv_w, attn_w, expand_w, shrink_w)
    (
        late, early, small, seg, plan, q_head, kv_head, n1, glu_pre, n2, left_pre, conv_pre, n3,
        depth, n4, x2, inv, masks, seg_cols,
    ) = first_kernel(tokens[0], segment_ids, vectors, weights, count, heads)
    o_head, o_low, log_sum = attend(plan, q_head, kv_head, seg, rows)
    output, small_grads, dx3, early_grads, do_head = middle_kernel(
        o_low, out_grad[0], small, x2, early, count, heads
    )
    tensors = (
        early_grads, dx3, late, n1, glu_pre, n2, left_pre, conv_pre, n3, depth, n4, inv, masks,
    )
    attention = (q_head, do_head, o_head, log_sum, kv_head, seg_cols)
    total, input_grad = last_kernel(attention, small, small_grads, seg, tensors, count, heads)
    output, input_grad, *pieces = unpack(output, input_grad, total)
    matrices, lines = pieces[: len(MATRICES)], pieces[len(MATRICES) :]
    lines = [line if line.shape[0] > 1 else line.reshape(-1) for line in lines]
    g_glu, g_left, g_conv, g_point, g_qkv, g_attn, g_expand, g_shrink = matrices
    (
        g_ln1g, g_ln1b, g_glu_b, g_ln2g, g_ln2b, g_left_b, g_conv_b, g_ln3g, g_ln3b, g_depth,
        g_point_b, g_ln4g, g_ln4b, g_attn_b, g_ln5g, g_ln5b, g_expand_b, g_shrink_b,
    ) = lines
    return (
        output[None], input_grad[None], g_ln1g, g_ln1b, g_glu, g_glu_b, g_ln2g, g_ln2b, g_left,
        g_left_b, g_conv, g_conv_b, g_ln3g, g_ln3b, g_depth, g_point, g_point_b, g_ln4g, g_ln4b,
        g_qkv, g_attn, g_attn_b, g_ln5g, g_ln5b, g_expand, g_expand_b, g_shrink, g_shrink_b,
    )


def solution(mesh):
    return jax.shard_map(
        body,
        mesh=mesh,
        in_specs=(
            P("ws", "ctx", None),
            P("ws", "ctx"),
            P("ws", "ctx", None),
            P("ws"),
            P("ws"),
            P("ws", None),
            P("ws"),
            P("ws"),
            P("ws"),
            P("ws", None),
            P("ws"),
            P(None, "ws", None),
            P("ws"),
            P("ws"),
            P("ws"),
            P(None, "ws"),
            P("ws", None),
            P("ws"),
            P("ws"),
            P("ws"),
            P("ws", None),
            P("ws", None),
            P("ws"),
            P("ws"),
            P("ws"),
            P("ws", None),
            P("ws"),
            P("ws", None),
            P("ws"),
        ),
        out_specs=(
            P("ws", "ctx", None),
            P("ws", "ctx", None),
            P("ws"),
            P("ws"),
            P("ws", None),
            P("ws"),
            P("ws"),
            P("ws"),
            P("ws", None),
            P("ws"),
            P(None, "ws", None),
            P("ws"),
            P("ws"),
            P("ws"),
            P(None, "ws"),
            P("ws", None),
            P("ws"),
            P("ws"),
            P("ws"),
            P("ws", None),
            P("ws", None),
            P("ws"),
            P("ws"),
            P("ws"),
            P("ws", None),
            P("ws"),
            P("ws", None),
            P("ws"),
        ),
        check_vma=False,
    )
```
